32 devices in a mesh: fsdp: 4 (over z), expert: 8 (over y, x, core).
Axes of the slice: x: 2, y: 2, z: 4, core: 2. Of those that a mesh axis runs over, the one named last changes fastest.
Arguments:
- residual_in: bfloat16 [4, 1024, 1536], P('fsdp', 'expert'), may hold values from -30 to 30
- cotangent: bfloat16 [4, 1024, 1536], P('fsdp', 'expert'), may hold values from -30 to 30
- gain_attn: bfloat16 [1536], P('fsdp'), may hold values from 0.5 to 1.5
- w_query: bfloat16 [1536, 1536], P('fsdp'), may hold values from -0.5 to 0.5
- w_key: bfloat16 [1536, 512], P('fsdp'), may hold values from -0.5 to 0.5
- w_value: bfloat16 [1536, 512], P('fsdp'), may hold values from -0.625 to 0.625
- w_out: bfloat16 [1536, 1536], P(None, 'fsdp'), may hold values from -1.5 to 1.5
- gain_ffn: bfloat16 [1536], P('fsdp'), may hold values from 0.5 to 1.5
- w_router: bfloat16 [1536, 24], P('fsdp'), may hold values from -0.078125 to 0.078125
- w_gate: bfloat16 [24, 1536, 512], P('expert'), may hold values from -0.15625 to 0.15625
- w_up: bfloat16 [24, 1536, 512], P('expert'), may hold values from -0.15625 to 0.15625
- w_down: bfloat16 [24, 512, 1536], P('expert'), may hold values from -4 to 4
- route_ids: int32 [4, 1024, 8], P('fsdp', 'expert'), may hold values from 0 to 23, all different within a row; in each aligned block of 128 rows (0 to 127, 128 to 255, ..., all dimensions but the last counted through in order) at most 64 rows name the same one
Outputs:
- output: bfloat16 [4, 1024, 1536], P('fsdp', 'expert')
- input_grad: bfloat16 [4, 1024, 1536], P('fsdp', 'expert')
- grad_gain_attn: float32 [1536], P('fsdp')
- grad_query: float32 [1536, 1536], P('fsdp')
- grad_key: float32 [1536, 512], P('fsdp')
- grad_value: float32 [1536, 512], P('fsdp')
- grad_out_proj: float32 [1536, 1536], P(None, 'fsdp')
- grad_gain_ffn: float32 [1536], P('fsdp')
- grad_router: float32 [1536, 24], P('fsdp')
- grad_gate: float32 [24, 1536, 512], P('expert', 'fsdp')
- grad_up: float32 [24, 1536, 512], P('expert', 'fsdp')
- grad_down: float32 [24, 512, 1536], P('expert', None, 'fsdp')
- residual_rms: float32 [5], replicated
The draws below stay inside these ranges and needn't reach their ends.
Inputs may be any that keep to these rules, and one draw needn't show every extreme that they name: `route_ids`: each token names 8 different experts; within the 128 tokens of one device (aligned blocks of the flattened sequences) no expert is named more than 64 times, a bound that some block reaches.
All inputs are finite; a program needn't handle non-finite values.
Results may differ from the reference program's by a relative error of at most 0.024.
Values may be sent and summed in bfloat16 or wider, within the bound.
A program may use at most 256 MiB of HBM per device.

```python
import math
from functools import partial
import jax
import jax.numpy as jnp
import numpy as np
from jax import lax

D = 1536
HEADS = 24
KV_HEADS = 8
HEAD_DIM = 64
FF_E = 512
TOPK = 8
BLOCK = 256
EXPERTS = 24
LENGTH = 1024
TOK_DEV = 128
SEQS = 4
CAP = 64


def rising_rows(key):
    scale_key, value_key = jax.random.split(key)
    row_scales = jnp.exp(jax.random.uniform(scale_key, (SEQS, LENGTH, 1), jnp.float32, math.log(0.5), math.log(2.0)))
    growth = 1.0 + 2.0 * jnp.arange(SEQS, dtype=jnp.float32)[:, None, None] / max(SEQS - 1, 1)
    entries = jnp.clip(jax.random.normal(value_key, (SEQS, LENGTH, D), jnp.float32), -5.0, 5.0)
    return (entries * row_scales * growth).astype(jnp.bfloat16)


def draw_residual_in(key, part):
    return rising_rows(jax.random.fold_in(key, 11))


def draw_cotangent(key, part):
    return rising_rows(jax.random.fold_in(key, 23))


def block_levels(stream_key, shape, shards, smallest, high):
    gain = 1.0
    for axis_at, shards_of in shards:
        steps = jax.random.uniform(jax.random.fold_in(jax.random.fold_in(stream_key, 6), axis_at), (shards_of,), jnp.float32, smallest / len(shards), high / len(shards))
        gain = gain * jnp.repeat(jnp.exp(steps), shape[axis_at] // shards_of).reshape((-1,) + (1,) * (len(shape) - 1 - axis_at))
    return gain


def routed_block(own_key, own, number, rows, amount, top, bound, skew):
    ranking = jax.random.permutation(own_key, amount)
    heavy_load, ordinary = load_shares(amount, rows * top, bound, skew, True), load_shares(amount, rows * top, bound, skew, False)
    places = jnp.arange(amount)

    def named(tallies, rotation):
        used = int((tallies > 0).sum())
        fixed = max(1, used // 4)
        passed = fixed + (places - fixed + rotation * (used - fixed)) % max(1, amount - fixed)
        return jnp.zeros((amount,), jnp.int32).at[ranking[jnp.where(places < fixed, places, passed)]].set(jnp.asarray(tallies, jnp.int32))

    tallies = jnp.where(number % 4 == 0, named(heavy_load, number // 4), named(ordinary, number - number // 4 - 1))
    mixed = jax.random.permutation(jax.random.fold_in(own, 3), amount)
    source_of, receiver = mixed[0:amount // 2 * 2:2], mixed[1:amount // 2 * 2:2]
    margin = jnp.minimum(tallies[source_of] - 1, bound - tallies[receiver]) // 2
    margin = jnp.where((source_of == ranking[0]) | (receiver == ranking[0]) | (tallies[receiver] == 0), 0, jnp.maximum(margin, 0))
    passed = jax.random.randint(jax.random.fold_in(own, 4), (amount // 2,), 0, 1 << 20) % (margin + 1)
    tallies = tallies.at[source_of].add(-passed).at[receiver].add(passed)
    items = jnp.searchsorted(jnp.cumsum(tallies), jnp.arange(rows * top), side="right").astype(jnp.int32)
    listing = items.reshape(top, rows).T
    listing = listing[jax.random.permutation(jax.random.fold_in(own, 1), rows)]
    rotation = jax.random.randint(jax.random.fold_in(own, 2), (rows, 1), 0, top)
    return jnp.take_along_axis(listing, (jnp.arange(top)[None, :] + rotation) % top, axis=1)


def load_shares(number_of, total, bound, skew, full):
    portions = [(1 << 20) // math.isqrt(grade ** skew) + 1 for grade in range(1, number_of + 1)]
    largest = bound if full else min(bound, max(-(-total // number_of), total * portions[0] // sum(portions)))
    least = 1 if total - largest >= number_of - 1 else 0
    holding, surplus = [largest] + [least] * (number_of - 1), total - largest - least * (number_of - 1)
    while surplus > 0:
        movable = [i for i in range(1, number_of) if holding[i] < largest] or [i for i in range(1, number_of) if holding[i] < bound]
        pool, remaining = sum([portions[i] for i in movable]), surplus
        for i in movable:
            addition = min(bound - holding[i], max(1, remaining * portions[i] // pool), surplus)
            holding[i] = holding[i] + addition
            surplus = surplus - addition
    return np.array(holding)


def normal_values(own_key, dims, width, limit, pieces=(), kind=jnp.bfloat16):
    array = width * jax.random.normal(own_key, dims, jnp.float32)
    if pieces:
        array = array * block_levels(own_key, dims, pieces, -0.22, 0.18)
    return jnp.clip(array, -limit, limit).astype(kind)


def setup_inputs(seed: int = 0) -> dict:
    key_of = jax.random.split(jax.random.key(seed), 14)
    residual_in = draw_residual_in(jax.random.fold_in(key_of[13], 71), 0)
    cotangent = draw_cotangent(jax.random.fold_in(key_of[13], 71), 0)
    gain_attn = jnp.clip(1.0 + 0.1 * jax.random.normal(key_of[2], (D,), jnp.float32), 0.5, 1.5).astype(jnp.bfloat16)
    w_query = normal_values(key_of[3], (D, HEADS * HEAD_DIM), (D // 12) ** -0.5, 0.5, ((0, 4),))
    w_key = normal_values(key_of[4], (D, KV_HEADS * HEAD_DIM), (D // 12) ** -0.5, 0.5, ((0, 4),))
    w_value = normal_values(key_of[5], (D, KV_HEADS * HEAD_DIM), (D // 16) ** -0.5, 0.625, ((0, 4),))
    w_out = normal_values(key_of[6], (HEADS * HEAD_DIM, D), 16 ** -0.5, 1.5, ((1, 4),))
    gain_ffn = jnp.clip(1.0 + 0.1 * jax.random.normal(key_of[7], (D,), jnp.float32), 0.5, 1.5).astype(jnp.bfloat16)
    w_router = normal_values(key_of[8], (D, EXPERTS), (4 * D) ** -0.5, 0.078125, ((0, 4),))
    w_gate = normal_values(key_of[9], (EXPERTS, D, FF_E), D ** -0.5, 0.15625, ((0, 8),))
    w_up = normal_values(key_of[10], (EXPERTS, D, FF_E), D ** -0.5, 0.15625, ((0, 8),))
    w_down = normal_values(key_of[11], (EXPERTS, FF_E, D), 2 ** -0.5, 4.0, ((0, 8),))
    route_ids_keys = jax.random.split(jax.random.fold_in(key_of[12], 1), SEQS * LENGTH // TOK_DEV)
    route_ids_turns = jax.random.permutation(jax.random.fold_in(key_of[12], 3), SEQS * LENGTH // TOK_DEV)
    route_ids = jax.vmap(lambda own, number: routed_block(jax.random.fold_in(key_of[12], 2), own, number, TOK_DEV, EXPERTS, TOPK, CAP, 2))(route_ids_keys, route_ids_turns).reshape((SEQS, LENGTH, TOPK))
    return dict(residual_in=residual_in, cotangent=cotangent, gain_attn=gain_attn, w_query=w_query, w_key=w_key, w_value=w_value, w_out=w_out, gain_ffn=gain_ffn, w_router=w_router, w_gate=w_gate, w_up=w_up, w_down=w_down, route_ids=route_ids)


EPSILON = 1e-06
RESIDUAL_SCALE = 0.22
ATTENTION_SCALE = 0.015625
ROPE_BASE = 10000.0
MASKED = -1e+30
HIGHEST = lax.Precision.HIGHEST

@jax.custom_vjp
def low(v):
    return lax.optimization_barrier(v.astype(jnp.bfloat16)).astype(jnp.float32)

@jax.custom_vjp
def low_back(v):
    return v

def low_keep(v):
    return (low(v), None)

def low_pass(kept, grad):
    return (grad,)

def back_keep(v):
    return (v, None)

def back_low(kept, grad):
    return (low(grad),)
low.defvjp(low_keep, low_pass)
low_back.defvjp(back_keep, back_low)

def product(first_matrix, second_matrix):
    return jnp.dot(first_matrix, second_matrix, precision=HIGHEST, preferred_element_type=jnp.float32)

def normalized(values):
    return values * lax.rsqrt(lax.optimization_barrier(jnp.mean(values * values, axis=-1, keepdims=True)) + EPSILON)

def rotated(values, positions):
    half_dim = HEAD_DIM // 2
    exponent = jnp.arange(half_dim, dtype=jnp.float32) * (2.0 / HEAD_DIM)
    angles = positions.astype(jnp.float32)[:, None] * jnp.power(ROPE_BASE, -exponent)[None, :]
    cosine = jnp.cos(angles)[:, None, :]
    sine_term = jnp.sin(angles)[:, None, :]
    first_half = values[..., :half_dim]
    second = values[..., half_dim:]
    return jnp.concatenate([first_half * cosine - second * sine_term, second * cosine + first_half * sine_term], axis=-1)

def attend_group(operands):
    queries, key_rows, values = operands
    scores = jnp.einsum('qgd,kd->gqk', queries, key_rows, precision=HIGHEST) * ATTENTION_SCALE
    scores = low_back(scores)
    blocks = jnp.arange(LENGTH, dtype=jnp.int32) // BLOCK
    allowed = blocks[None, :] <= blocks[:, None]
    weights = jax.nn.softmax(jnp.where(allowed[None], scores, MASKED), axis=-1)
    return jnp.einsum('gqk,kd->qgd', low(weights), values, precision=HIGHEST)

def attention(queries, key_rows, values):
    group_size = HEADS // KV_HEADS
    query_items = queries.reshape(SEQS, LENGTH, KV_HEADS, group_size, HEAD_DIM).transpose(0, 2, 1, 3, 4).reshape(SEQS * KV_HEADS, LENGTH, group_size, HEAD_DIM)
    key_items = key_rows.reshape(SEQS, LENGTH, KV_HEADS, HEAD_DIM).transpose(0, 2, 1, 3).reshape(SEQS * KV_HEADS, LENGTH, HEAD_DIM)
    value_items = values.reshape(SEQS, LENGTH, KV_HEADS, HEAD_DIM).transpose(0, 2, 1, 3).reshape(SEQS * KV_HEADS, LENGTH, HEAD_DIM)
    mixture = lax.map(jax.checkpoint(attend_group), (query_items, key_items, value_items))
    return mixture.reshape(SEQS, KV_HEADS, LENGTH, group_size, HEAD_DIM).transpose(0, 2, 1, 3, 4).reshape(SEQS * LENGTH, HEADS * HEAD_DIM)

def layer_front(flat_in, gain_attn, w_query, w_key, w_value, w_out):
    normed = low(normalized(flat_in) * gain_attn)
    positions = jnp.tile(jnp.arange(LENGTH, dtype=jnp.int32), SEQS)
    query_pre = low_back(product(normed, w_query)).reshape(SEQS * LENGTH, HEADS, HEAD_DIM)
    key_pre = low_back(product(normed, w_key)).reshape(SEQS * LENGTH, KV_HEADS, HEAD_DIM)
    values = low(low_back(product(normed, w_value)))
    queries = low(rotated(query_pre, positions))
    key_rows = low(rotated(key_pre, positions))
    mixture = low(low_back(attention(queries, key_rows, values)))
    branch = low_back(product(mixture, w_out))
    return flat_in + RESIDUAL_SCALE * branch

def expert_block(routed, token_routes, gate_probs, w_gate, w_up, w_down):
    flat_ids = token_routes.reshape(-1)
    onehot = (flat_ids[:, None] == jnp.arange(EXPERTS, dtype=jnp.int32)[None, :]).astype(jnp.int32)
    slot_index = lax.optimization_barrier(jnp.sum((jnp.cumsum(onehot, axis=0) - onehot) * onehot, axis=1))
    copies = low_back(jnp.repeat(routed, TOPK, axis=0))
    buffer = jnp.zeros((EXPERTS, CAP, D), jnp.float32).at[flat_ids, slot_index].set(copies)
    gate_pre = low_back(jnp.einsum('ecd,edf->ecf', buffer, w_gate, precision=HIGHEST))
    up_pre = low_back(jnp.einsum('ecd,edf->ecf', buffer, w_up, precision=HIGHEST))
    hidden = low(jax.nn.silu(gate_pre) * up_pre)
    produced = low(low_back(jnp.einsum('ecf,efd->ecd', hidden, w_down, precision=HIGHEST)))
    picked = produced[flat_ids, slot_index].reshape(TOK_DEV, TOPK, D)
    return jnp.einsum('tk,tkd->td', gate_probs, picked, precision=HIGHEST)

def layer_back(middle, gain_ffn, w_router, w_gate, w_up, w_down, token_routes):
    routed = low(normalized(middle) * gain_ffn)
    logits = low_back(product(routed, w_router))
    chosen = jnp.take_along_axis(logits, token_routes, axis=1)
    gate_probs = jax.nn.softmax(chosen, axis=-1)
    block_count = SEQS * LENGTH // TOK_DEV
    checked = jax.checkpoint(expert_block)
    mixture = lax.map(lambda operands: checked(operands[0], operands[1], operands[2], w_gate, w_up, w_down), (routed.reshape(block_count, TOK_DEV, D), token_routes.reshape(block_count, TOK_DEV, TOPK), gate_probs.reshape(block_count, TOK_DEV, TOPK)))
    return middle + RESIDUAL_SCALE * mixture.reshape(SEQS * LENGTH, D)

def root_mean(values):
    return jnp.sqrt(jnp.sum(values * values) / (SEQS * LENGTH * D))

def reference(residual_in, cotangent, gain_attn, w_query, w_key, w_value, w_out, gain_ffn, w_router, w_gate, w_up, w_down, route_ids):
    flat_in = residual_in.reshape(SEQS * LENGTH, D).astype(jnp.float32)
    front_weights = [weight_item.astype(jnp.float32) for weight_item in (gain_attn, w_query, w_key, w_value, w_out)]
    middle, front_vjp = jax.vjp(layer_front, flat_in, *front_weights)
    back_weights = [weight_item.astype(jnp.float32) for weight_item in (gain_ffn, w_router, w_gate, w_up, w_down)]
    token_routes = route_ids.reshape(SEQS * LENGTH, TOPK).astype(jnp.int32)
    outcome, back_vjp = jax.vjp(partial(layer_back, token_routes=token_routes), middle, *back_weights)
    grad_out = cotangent.reshape(SEQS * LENGTH, D).astype(jnp.float32)
    back_grads = back_vjp(grad_out)
    grad_middle = back_grads[0]
    front_grads = front_vjp(grad_middle)
    grad_in = front_grads[0]
    statistics = jnp.stack([root_mean(flat_in), root_mean(middle), root_mean(outcome), root_mean(grad_middle), root_mean(grad_in)])
    return (outcome.astype(jnp.bfloat16).reshape(SEQS, LENGTH, D), grad_in.astype(jnp.bfloat16).reshape(SEQS, LENGTH, D), front_grads[1], front_grads[2], front_grads[3], front_grads[4], front_grads[5], back_grads[1], back_grads[2], back_grads[3], back_grads[4], back_grads[5], statistics)
```

```python
import functools

import jax
import jax.numpy as jnp
from jax import lax
from jax.experimental import pallas as pl
from jax.experimental.pallas import tpu as pltpu
from jax.sharding import PartitionSpec as P

HEAD_DIM = 64
BLOCK = 256

EPSILON = 1e-06
RESIDUAL_SCALE = 0.22
ATTENTION_SCALE = 0.015625
ROPE_BASE = 10000.0
HIGHEST = lax.Precision.HIGHEST
MESH = pl.DeviceIdType.MESH
VMEM_LIMIT = 63_000_000
F32 = jnp.float32
BF16 = jnp.bfloat16
LANES = 128


def plane_neighbours():
    me = lax.axis_index("expert")
    core = lax.rem(me, 2)
    x_bit = lax.rem(me // 2, 2)
    y_bit = me // 4
    sibling = me + 1 - 2 * core
    x_peer = me + 2 - 4 * x_bit
    y_peer = me + 4 - 8 * y_bit
    diagonal = x_peer + 4 - 8 * y_bit
    return me, core, x_bit, y_bit, sibling, x_peer, y_peer, diagonal


def greet(axis, peers):
    barrier = pltpu.get_barrier_semaphore()
    for peer in peers:
        pl.semaphore_signal(barrier, inc=1, device_id={axis: peer}, device_id_type=MESH)
    pl.semaphore_wait(barrier, len(peers))


def gather_kernel(count, *refs):
    ins, outs = refs[:count], refs[count : 2 * count]
    own_sem, send_sem, recv_sem = refs[2 * count :]
    me, _, _, _, sibling, x_peer, y_peer, diagonal = plane_neighbours()
    greet("expert", (sibling, x_peer, y_peer))

    def remote(k, slot, source, target, peer):
        return pltpu.make_async_remote_copy(
            src_ref=source,
            dst_ref=target,
            send_sem=send_sem.at[k, slot],
            recv_sem=recv_sem.at[k, slot],
            device_id={"expert": peer},
            device_id_type=MESH,
        )

    plans = []
    for k in range(count):
        half = ins[k].shape[0] // 2
        parts = (pl.ds(0, half), pl.ds(half, half))
        out = outs[k]
        own = pltpu.make_async_copy(ins[k], out.at[me], own_sem.at[k])
        copies = [remote(k, 0, ins[k], out.at[me], sibling)]
        for h in range(2):
            copies.append(remote(k, 1 + h, ins[k].at[parts[h]], out.at[me, parts[h]], x_peer))
        for h in range(2):
            copies.append(remote(k, 3 + h, ins[k].at[parts[h]], out.at[me, parts[h]], y_peer))

        def forward(slot, block, h, peer):
            return remote(k, slot, out.at[block, parts[h]], out.at[block, parts[h]], peer)

        copies.append(forward(5, y_peer, 0, x_peer))
        copies.append(forward(6, x_peer, 1, y_peer))
        for h in range(2):
            copies.append(forward(7 + h, x_peer, h, sibling))
        for h in range(2):
            copies.append(forward(9 + h, y_peer, h, sibling))
        for h in range(2):
            copies.append(forward(11 + h, diagonal, h, sibling))
        plans.append((own, copies))
    for own, copies in plans:
        for slot in (3, 2, 1, 4, 0):
            copies[slot].start()
        own.start()
    for own, copies in plans:
        copies[3].wait_recv()
        copies[5].start()
        copies[2].wait_recv()
        copies[6].start()
        copies[9].start()
        copies[8].start()
        copies[1].wait_recv()
        copies[7].start()
        copies[4].wait_recv()
        copies[10].start()
    for own, copies in plans:
        copies[5].wait_recv()
        copies[11].start()
        copies[6].wait_recv()
        copies[12].start()
    for own, copies in plans:
        for slot in (0, 7, 8, 9, 10, 11, 12):
            copies[slot].wait_recv()
        for copy in copies:
            copy.wait_send()
        own.wait()


def plane_gather(arrays, collective_id):
    if lax.axis_size("expert") != 8:
        return [lax.all_gather(array, "expert", axis=0) for array in arrays]
    count = len(arrays)
    size = sum(array.size * array.dtype.itemsize for array in arrays)
    return pl.pallas_call(
        functools.partial(gather_kernel, count),
        out_shape=[jax.ShapeDtypeStruct((8,) + array.shape, array.dtype) for array in arrays],
        in_specs=[pl.BlockSpec(memory_space=pltpu.VMEM)] * count,
        out_specs=[pl.BlockSpec(memory_space=pl.ANY)] * count,
        scratch_shapes=[
            pltpu.SemaphoreType.DMA((count,)),
            pltpu.SemaphoreType.DMA((count, 13)),
            pltpu.SemaphoreType.DMA((count, 13)),
        ],
        compiler_params=pltpu.CompilerParams(
            collective_id=collective_id, has_side_effects=True, vmem_limit_bytes=VMEM_LIMIT
        ),
        cost_estimate=pl.CostEstimate(flops=0, bytes_accessed=16 * size, transcendentals=0),
        name="plane_gather",
    )(*arrays)


def scatter_kernel(count, *refs):
    ins, outs = refs[:count], refs[count : 2 * count]
    scratch = refs[2 * count : 2 * count + 6 * count]
    send_sem, recv_sem = refs[8 * count :]
    me, core, x_bit, y_bit, sibling, x_peer, y_peer, diagonal = plane_neighbours()
    greet("expert", (sibling, x_peer, y_peer))
    chip = me // 2
    chip_x, chip_y, chip_d = x_peer // 2, y_peer // 2, diagonal // 2
    order = (chip_d, chip_x, chip_y, chip)

    def remote(k, slot, source, target, peer):
        return pltpu.make_async_remote_copy(
            src_ref=source,
            dst_ref=target,
            send_sem=send_sem.at[k, slot],
            recv_sem=recv_sem.at[k, slot],
            device_id={"expert": peer},
            device_id_type=MESH,
        )

    stage0 = []
    for k in range(count):
        pair = scratch[6 * k]
        copies = [
            remote(k, i, ins[k].at[2 * order[i] + 1 - core], pair.at[i], sibling) for i in range(4)
        ]
        stage0.append(copies)
        for copy in copies:
            copy.start()
    later = []
    for k in range(count):
        pair, sums, first_x, first_y, second_x, second_y = scratch[6 * k : 6 * k + 6]
        rows = ins[k].shape[1]
        half = rows // 2
        parts = (pl.ds(0, half), pl.ds(half, half))
        dtype = ins[k].dtype

        def join(i):
            stage0[k][i].wait_recv()
            sums[i] = (ins[k][2 * order[i] + core].astype(F32) + pair[i].astype(F32)).astype(dtype)

        join(0)
        copies = [
            remote(k, 4, sums.at[0, parts[0]], first_x.at[1], x_peer),
            remote(k, 5, sums.at[0, parts[1]], first_y.at[1], y_peer),
        ]
        for copy in copies:
            copy.start()
        join(1)
        copies.append(remote(k, 6, sums.at[1, parts[0]], first_x.at[0], x_peer))
        copies[-1].start()
        join(2)
        copies.append(remote(k, 7, sums.at[2, parts[1]], first_y.at[0], y_peer))
        copies[-1].start()
        join(3)
        later.append(copies)
    for k in range(count):
        pair, sums, first_x, first_y, second_x, second_y = scratch[6 * k : 6 * k + 6]
        half = ins[k].shape[1] // 2
        parts = (pl.ds(0, half), pl.ds(half, half))
        dtype = ins[k].dtype
        copies = later[k]
        copies[0].wait_recv()
        pair[0, parts[0]] = (
            sums[2, parts[0]].astype(F32) + first_x[1].astype(F32)
        ).astype(dtype)
        copies.append(remote(k, 8, pair.at[0, parts[0]], second_y, y_peer))
        copies[-1].start()
        copies[1].wait_recv()
        pair[0, parts[1]] = (
            sums[1, parts[1]].astype(F32) + first_y[1].astype(F32)
        ).astype(dtype)
        copies.append(remote(k, 9, pair.at[0, parts[1]], second_x, x_peer))
        copies[-1].start()
    for k in range(count):
        pair, sums, first_x, first_y, second_x, second_y = scratch[6 * k : 6 * k + 6]
        half = ins[k].shape[1] // 2
        parts = (pl.ds(0, half), pl.ds(half, half))
        copies = later[k]
        copies[2].wait_recv()
        copies[4].wait_recv()
        outs[k][parts[0]] = (
            sums[3, parts[0]].astype(F32) + first_x[0].astype(F32) + second_y[...].astype(F32)
        )
        copies[3].wait_recv()
        copies[5].wait_recv()
        outs[k][parts[1]] = (
            sums[3, parts[1]].astype(F32) + first_y[0].astype(F32) + second_x[...].astype(F32)
        )
        for copy in stage0[k] + copies:
            copy.wait_send()


def plane_scatter(arrays, collective_id):
    if lax.axis_size("expert") != 8:
        return [
            lax.psum_scatter(array, "expert", scatter_dimension=0, tiled=False).astype(F32)
            for array in arrays
        ]
    count = len(arrays)
    scratch = []
    for array in arrays:
        _, rows, columns = array.shape
        half = rows // 2
        for shape in (
            (4, rows, columns),
            (4, rows, columns),
            (2, half, columns),
            (2, half, columns),
            (half, columns),
            (half, columns),
        ):
            scratch.append(pltpu.VMEM(shape, array.dtype))
    size = sum(array.size * array.dtype.itemsize for array in arrays)
    return pl.pallas_call(
        functools.partial(scatter_kernel, count),
        out_shape=[jax.ShapeDtypeStruct(array.shape[1:], F32) for array in arrays],
        in_specs=[pl.BlockSpec(memory_space=pltpu.VMEM)] * count,
        out_specs=[pl.BlockSpec(memory_space=pltpu.VMEM)] * count,
        scratch_shapes=scratch
        + [pltpu.SemaphoreType.DMA((count, 10)), pltpu.SemaphoreType.DMA((count, 10))],
        compiler_params=pltpu.CompilerParams(
            collective_id=collective_id, has_side_effects=True, vmem_limit_bytes=VMEM_LIMIT
        ),
        cost_estimate=pl.CostEstimate(flops=0, bytes_accessed=3 * size, transcendentals=0),
        name="plane_scatter",
    )(*arrays)


def line_greet(me, last):
    barrier = pltpu.get_barrier_semaphore()

    @pl.when(me > 0)
    def _():
        pl.semaphore_signal(barrier, inc=1, device_id={"fsdp": me - 1}, device_id_type=MESH)

    @pl.when(me < last)
    def _():
        pl.semaphore_signal(barrier, inc=1, device_id={"fsdp": me + 1}, device_id_type=MESH)

    @pl.when((me > 0) & (me < last))
    def _():
        pl.semaphore_wait(barrier, 2)

    @pl.when((me == 0) | (me == last))
    def _():
        pl.semaphore_wait(barrier, 1)


def line_gather_kernel(size, axes, *refs):
    count = len(axes)
    ins, outs = refs[:count], refs[count : 2 * count]
    own_sem, send_sem, recv_sem = refs[2 * count :]
    me = lax.axis_index("fsdp")
    last = size - 1
    line_greet(me, last)

    def place(k, owner):
        rows, columns = ins[k].shape
        if axes[k] == 0:
            return outs[k].at[pl.ds(pl.multiple_of(owner * rows, rows), rows)]
        return outs[k].at[:, pl.ds(pl.multiple_of(owner * columns, columns), columns)]

    def remote(k, side, step, owner, source=None):
        return pltpu.make_async_remote_copy(
            src_ref=place(k, owner) if source is None else source,
            dst_ref=place(k, owner),
            send_sem=send_sem.at[k, side, step],
            recv_sem=recv_sem.at[k, side, step],
            device_id={"fsdp": me + 1 - 2 * side},
            device_id_type=MESH,
        )

    own = [pltpu.make_async_copy(ins[k], place(k, me), own_sem.at[k]) for k in range(count)]
    for k in range(count):

        @pl.when(me < last)
        def _():
            remote(k, 0, 0, me, ins[k]).start()

        @pl.when(me > 0)
        def _():
            remote(k, 1, 0, me, ins[k]).start()

    for k in range(count):
        own[k].start()
    for step in range(size - 1):
        for k in range(count):
            @pl.when(me - 1 - step >= 0)
            def _():
                remote(k, 0, step, me - 1 - step).wait_recv()

                @pl.when(me < last)
                def _():
                    remote(k, 0, step + 1, me - 1 - step).start()

            @pl.when(me + 1 + step <= last)
            def _():
                remote(k, 1, step, me + 1 + step).wait_recv()

                @pl.when(me > 0)
                def _():
                    remote(k, 1, step + 1, me + 1 + step).start()

    for k in range(count):
        own[k].wait()
        for step in range(size - 1):

            @pl.when((me < last) & (me - step >= 0))
            def _():
                remote(k, 0, step, me - step).wait_send()

            @pl.when((me > 0) & (me + step <= last))
            def _():
                remote(k, 1, step, me + step).wait_send()


def line_gather(arrays, axes, collective_id):
    size = lax.axis_size("fsdp")
    if size != 4:
        return [
            lax.all_gather(array, "fsdp", axis=axis, tiled=True)
            for array, axis in zip(arrays, axes)
        ]
    count = len(arrays)
    shapes = []
    for array, axis in zip(arrays, axes):
        rows, columns = array.shape
        shapes.append((rows * size, columns) if axis == 0 else (rows, columns * size))
    return pl.pallas_call(
        functools.partial(line_gather_kernel, size, tuple(axes)),
        out_shape=[
            jax.ShapeDtypeStruct(shape, array.dtype) for shape, array in zip(shapes, arrays)
        ],
        in_specs=[pl.BlockSpec(memory_space=pltpu.VMEM)] * count,
        out_specs=[pl.BlockSpec(memory_space=pl.ANY)] * count,
        scratch_shapes=[
            pltpu.SemaphoreType.DMA((count,)),
            pltpu.SemaphoreType.DMA((count, 2, size)),
            pltpu.SemaphoreType.DMA((count, 2, size)),
        ],
        compiler_params=pltpu.CompilerParams(
            collective_id=collective_id, has_side_effects=True, vmem_limit_bytes=VMEM_LIMIT
        ),
        cost_estimate=pl.CostEstimate(flops=0, bytes_accessed=60_000_000, transcendentals=0),
        name="line_gather",
    )(*arrays)


def line_scatter_kernel(size, count, *refs):
    ins, outs = refs[: count + 1], refs[count + 1 : 2 * count + 2]
    scratch = refs[2 * count + 2 : 4 * count + 2]
    send_sem, recv_sem, note_send, note_recv, own_sem = refs[4 * count + 2 :]
    me = lax.axis_index("fsdp")
    last = size - 1
    line_greet(me, last)
    note_in, note_out = ins[count], outs[count]

    def remote(k, side, owner):
        sums, landed = scratch[2 * k], scratch[2 * k + 1]
        return pltpu.make_async_remote_copy(
            src_ref=sums.at[side, owner],
            dst_ref=landed.at[side, owner],
            send_sem=send_sem.at[k, side, owner],
            recv_sem=recv_sem.at[k, side, owner],
            device_id={"fsdp": me + 1 - 2 * side},
            device_id_type=MESH,
        )

    def note(side, hop, owner):
        return pltpu.make_async_remote_copy(
            src_ref=note_out.at[owner] if hop else note_in,
            dst_ref=note_out.at[owner],
            send_sem=note_send.at[side, hop],
            recv_sem=note_recv.at[side, hop],
            device_id={"fsdp": me + 1 - 2 * side},
            device_id_type=MESH,
        )

    own = pltpu.make_async_copy(note_in, note_out.at[me], own_sem)
    own.start()

    @pl.when(me < last)
    def _():
        note(0, 0, me).start()

    @pl.when(me > 0)
    def _():
        note(1, 0, me).start()

    def pass_on(k, side, owner, has_more):
        sums, landed = scratch[2 * k], scratch[2 * k + 1]

        @pl.when(has_more)
        def _():
            remote(k, side, owner).wait_recv()
            sums[side, owner] = (
                ins[k][owner].astype(F32) + landed[side, owner].astype(F32)
            ).astype(ins[k].dtype)

        @pl.when(jnp.logical_not(has_more))
        def _():
            sums[side, owner] = ins[k][owner]

        remote(k, side, owner).start()

    for far in range(size - 1):
        for k in range(count):
            right, left = last - far, far

            @pl.when(me < right)
            def _():
                pass_on(k, 0, right, me > 0)

            @pl.when(me > left)
            def _():
                pass_on(k, 1, left, me < last)

    for k in range(count):
        outs[k][...] = ins[k][me].astype(F32)
        for side, there in ((0, me > 0), (1, me < last)):

            @pl.when(there)
            def _():
                remote(k, side, me).wait_recv()
                outs[k][...] += scratch[2 * k + 1][side, me].astype(F32)

    for hop in range(size - 1):

        @pl.when(me - 1 - hop >= 0)
        def _():
            note(0, hop, me - 1 - hop).wait_recv()

            @pl.when(me < last)
            def _():
                note(0, hop + 1, me - 1 - hop).start()

        @pl.when(me + 1 + hop <= last)
        def _():
            note(1, hop, me + 1 + hop).wait_recv()

            @pl.when(me > 0)
            def _():
                note(1, hop + 1, me + 1 + hop).start()

    own.wait()
    for hop in range(size - 1):

        @pl.when((me < last) & (me - hop >= 0))
        def _():
            note(0, hop, me - hop).wait_send()

        @pl.when((me > 0) & (me + hop <= last))
        def _():
            note(1, hop, me + hop).wait_send()

    for k in range(count):
        for owner in range(size):

            @pl.when(me < owner)
            def _():
                remote(k, 0, owner).wait_send()

            @pl.when(me > owner)
            def _():
                remote(k, 1, owner).wait_send()


def line_scatter(arrays, notes, collective_id):
    size = lax.axis_size("fsdp")
    if size != 4:
        return [
            lax.psum_scatter(array, "fsdp", scatter_dimension=0, tiled=False).astype(F32)
            for array in arrays
        ] + [lax.all_gather(notes, "fsdp", axis=0)]
    count = len(arrays)
    scratch = []
    for array in arrays:
        scratch += [pltpu.VMEM((2,) + array.shape, array.dtype)] * 2
    return pl.pallas_call(
        functools.partial(line_scatter_kernel, size, count),
        out_shape=[jax.ShapeDtypeStruct(array.shape[1:], F32) for array in arrays]
        + [jax.ShapeDtypeStruct((size,) + notes.shape, notes.dtype)],
        in_specs=[pl.BlockSpec(memory_space=pltpu.VMEM)] * (count + 1),
        out_specs=[pl.BlockSpec(memory_space=pltpu.VMEM)] * (count + 1),
        scratch_shapes=scratch
        + [
            pltpu.SemaphoreType.DMA((count, 2, size)),
            pltpu.SemaphoreType.DMA((count, 2, size)),
            pltpu.SemaphoreType.DMA((2, size)),
            pltpu.SemaphoreType.DMA((2, size)),
            pltpu.SemaphoreType.DMA,
        ],
        compiler_params=pltpu.CompilerParams(
            collective_id=collective_id, has_side_effects=True, vmem_limit_bytes=VMEM_LIMIT
        ),
        cost_estimate=pl.CostEstimate(flops=0, bytes_accessed=60_000_000, transcendentals=0),
        name="line_scatter",
    )(*arrays, notes)


def dot(first, second, contract=(1, 0)):
    return lax.dot_general(
        first, second, (((contract[0],), (contract[1],)), ((), ())), preferred_element_type=F32
    )


def spin(values, cosine, sine):
    width = values.shape[1]
    half = HEAD_DIM // 2
    lane = lax.broadcasted_iota(jnp.int32, values.shape, 1)
    lower = lax.rem(lane, HEAD_DIM) < half
    swapped = jnp.where(
        lower, pltpu.roll(values, width - half, 1), pltpu.roll(values, half, 1)
    )
    return values * cosine + swapped * sine


def attend_kernel(
    per_group, x_ref, w_in_ref, w_out_ref, cos_ref, sin_ref,
    part_ref, a_ref, q_ref, k_ref, v_ref, o_ref, lse_ref,
):
    length, model_width = x_ref.shape
    query_width = per_group * HEAD_DIM
    turned = query_width + HEAD_DIM
    gain = w_out_ref[query_width : query_width + 1, :].astype(F32)

    def project(i, carry):
        rows = pl.ds(pl.multiple_of(i * BLOCK, BLOCK), BLOCK)
        x = x_ref[rows, :].astype(F32)
        inverse = lax.rsqrt(jnp.mean(x * x, axis=1, keepdims=True) + EPSILON)
        a = (x * inverse * gain).astype(BF16)
        a_ref[rows, :] = a
        pre = dot(a, w_in_ref[...])
        spun = spin(pre[:, :turned], cos_ref[rows, :], sin_ref[rows, :]).astype(BF16)
        for h in range(per_group):
            q_ref[h, rows, :] = spun[:, h * HEAD_DIM : (h + 1) * HEAD_DIM]
        k_ref[rows, :] = spun[:, query_width:turned]
        v_ref[rows, :] = pre[:, turned : turned + HEAD_DIM].astype(BF16)
        return carry

    lax.fori_loop(0, length // BLOCK, project, 0)
    for i in range(length // BLOCK):
        seen = (i + 1) * BLOCK
        rows = slice(i * BLOCK, seen)
        keys, values = k_ref[:seen, :], v_ref[:seen, :]
        for h in range(per_group):
            scores = dot(q_ref[h, rows, :], keys, (1, 1)) * ATTENTION_SCALE
            peak = jnp.max(scores, axis=1, keepdims=True)
            lifted = jnp.exp(scores - peak)
            total = jnp.sum(lifted, axis=1, keepdims=True)
            weights = (lifted * (1.0 / total)).astype(BF16)
            mixed = dot(weights, values)
            o_ref[rows, h * HEAD_DIM : (h + 1) * HEAD_DIM] = mixed.astype(BF16)
            lse_ref[h, rows, :] = peak + jnp.log(total)
        part_ref[rows, :] = dot(o_ref[rows, :], w_out_ref[:query_width, :]).astype(BF16)


def attend(x_all, w_in, w_out, cosine, sine, per_group):
    length, model_width = x_all.shape
    query_width = per_group * HEAD_DIM
    shapes = [
        jax.ShapeDtypeStruct((length, model_width), BF16),
        jax.ShapeDtypeStruct((length, model_width), BF16),
        jax.ShapeDtypeStruct((per_group, length, HEAD_DIM), BF16),
        jax.ShapeDtypeStruct((length, HEAD_DIM), BF16),
        jax.ShapeDtypeStruct((length, HEAD_DIM), BF16),
        jax.ShapeDtypeStruct((length, query_width), BF16),
        jax.ShapeDtypeStruct((per_group, length, 1), F32),
    ]
    return pl.pallas_call(
        functools.partial(attend_kernel, per_group),
        out_shape=shapes,
        in_specs=[pl.BlockSpec(memory_space=pltpu.VMEM)] * 5,
        out_specs=[pl.BlockSpec(memory_space=pltpu.VMEM)] * len(shapes),
        compiler_params=pltpu.CompilerParams(vmem_limit_bytes=VMEM_LIMIT),
        cost_estimate=pl.CostEstimate(
            flops=8_000_000_000, bytes_accessed=16_000_000, transcendentals=2_000_000
        ),
        name="attend",
    )(x_all, w_in, w_out, cosine, sine)


def attend_back_kernel(
    per_group, dw_ref, w_in_ref, w_out_ref, cos_ref, sin_ref,
    a_ref, q_ref, k_ref, v_ref, o_ref, lse_ref, b_ref, dl_ref,
    part_ref, gin_ref, gout_ref,
    turn_ref, dv_ref, back_ref,
):
    length, model_width = dw_ref.shape
    query_width = per_group * HEAD_DIM
    turned = query_width + HEAD_DIM
    blocks = length // BLOCK
    turn_ref[...] = jnp.zeros_like(turn_ref)
    dv_ref[...] = jnp.zeros_like(dv_ref)
    for i in range(blocks):
        seen = (i + 1) * BLOCK
        rows = slice(i * BLOCK, seen)
        keys, values = k_ref[:seen, :], v_ref[:seen, :]
        grad = dot(dw_ref[rows, :], w_out_ref[:query_width, :], (1, 1)).astype(BF16)
        for h in range(per_group):
            columns = slice(h * HEAD_DIM, (h + 1) * HEAD_DIM)
            queries = q_ref[h, rows, :]
            grad_head = grad[:, columns]
            scores = dot(queries, keys, (1, 1)) * ATTENTION_SCALE
            probs = jnp.exp(scores - lse_ref[h, rows, :])
            dv_ref[:seen, :] += dot(probs.astype(BF16), grad_head, (0, 0))
            grad_probs = dot(grad_head, values, (1, 1))
            inner = jnp.sum(probs * grad_probs, axis=1, keepdims=True)
            grad_scores = (probs * (grad_probs - inner)).astype(BF16)
            turn_ref[rows, columns] = dot(grad_scores, keys) * ATTENTION_SCALE
            turn_ref[:seen, query_width:turned] += (
                dot(grad_scores, queries, (0, 0)) * ATTENTION_SCALE
            )

    def unturn(i, carry):
        rows = pl.ds(pl.multiple_of(i * BLOCK, BLOCK), BLOCK)
        back_ref[rows, :turned] = spin(
            turn_ref[rows, :], cos_ref[rows, :], -sin_ref[rows, :]
        ).astype(BF16)
        back_ref[rows, turned : turned + HEAD_DIM] = dv_ref[rows, :].astype(BF16)
        part_ref[rows, :] = dot(
            back_ref[rows, : turned + HEAD_DIM], w_in_ref[:, : turned + HEAD_DIM], (1, 1)
        ).astype(BF16)
        return carry

    lax.fori_loop(0, blocks, unturn, 0)
    chunk = 384

    def weight_grads(i, carry):
        columns = pl.ds(pl.multiple_of(i * chunk, chunk), chunk)
        gin_ref[columns, : turned + HEAD_DIM] = dot(
            a_ref[:, columns], back_ref[:, : turned + HEAD_DIM], (0, 0)
        ).astype(BF16)
        gin_ref[columns, turned + HEAD_DIM :] = dot(
            b_ref[:, columns], dl_ref[...], (0, 0)
        )[:, : gin_ref.shape[1] - turned - HEAD_DIM].astype(BF16)
        gout_ref[:, columns] = dot(o_ref[...], dw_ref[:, columns], (0, 0)).astype(BF16)
        return carry

    lax.fori_loop(0, model_width // chunk, weight_grads, 0)


def attend_back(dw_all, w_in, w_out, cosine, sine, saved, b_all, dl_all, per_group):
    length, model_width = dw_all.shape
    query_width = per_group * HEAD_DIM
    turned = query_width + HEAD_DIM
    shapes = [
        jax.ShapeDtypeStruct((length, model_width), BF16),
        jax.ShapeDtypeStruct((model_width, w_in.shape[1]), BF16),
        jax.ShapeDtypeStruct((query_width, model_width), BF16),
    ]
    return pl.pallas_call(
        functools.partial(attend_back_kernel, per_group),
        out_shape=shapes,
        in_specs=[pl.BlockSpec(memory_space=pltpu.VMEM)] * 13,
        out_specs=[pl.BlockSpec(memory_space=pltpu.VMEM)] * len(shapes),
        scratch_shapes=[
            pltpu.VMEM((length, turned), F32),
            pltpu.VMEM((length, HEAD_DIM), F32),
            pltpu.VMEM((length, w_in.shape[1]), BF16),
        ],
        compiler_params=pltpu.CompilerParams(vmem_limit_bytes=VMEM_LIMIT),
        cost_estimate=pl.CostEstimate(
            flops=20_000_000_000, bytes_accessed=30_000_000, transcendentals=2_000_000
        ),
        name="attend_back",
    )(dw_all, w_in, w_out, cosine, sine, *saved, b_all, dl_all)


def experts_kernel(
    here, capacity, parts, lane_parts,
    me_ref, b_ref, dy_ref, g_ref, gate_ref, up_ref, down_ref,
    out_ref, db_ref, dg_ref, dgate_ref, dup_ref, ddown_ref,
    pick_ref, x_ref, y_ref, scale_ref, hidden_ref, dgp_ref, dup_s_ref, de_ref, inner_ref,
):
    step = pl.program_id(0)
    sources, tokens, model_width = b_ref.shape
    rows_all = sources * capacity
    slots = here * capacity
    first = me_ref[0, 0] * here

    @pl.when(step == 0)
    def _():
        row = lax.broadcasted_iota(jnp.int32, (tokens, tokens), 0)
        column = lax.broadcasted_iota(jnp.int32, (tokens, tokens), 1)
        earlier = (column < row).astype(BF16)
        lane = lax.broadcasted_iota(jnp.int32, (tokens, g_ref.shape[2]), 1)
        slot = lax.broadcasted_iota(jnp.int32, (tokens, slots), 1)

        def collect(j, carry):
            gates = g_ref[j]
            named = (gates >= 0.0).astype(BF16)
            rank = dot(earlier, named)
            picks = jnp.zeros((tokens, slots), F32)
            scaled = jnp.zeros((tokens, slots), F32)
            for e in range(here):
                mine = lane == first + e
                place = jnp.sum(jnp.where(mine, rank, 0.0), axis=1, keepdims=True)
                gate = jnp.sum(jnp.where(mine, gates, 0.0), axis=1, keepdims=True)
                hit = (slot - e * capacity == place.astype(jnp.int32)) & (gate >= 0.0)
                hit = hit & (slot >= e * capacity) & (slot < (e + 1) * capacity)
                picks = jnp.where(hit, 1.0, picks)
                scaled = jnp.where(hit, gate, scaled)
            pick = picks.astype(BF16)
            pick_ref[j] = pick
            ones = jnp.ones((tokens, LANES), F32)
            scales = lax.dot_general(
                scaled, ones, (((0,), (0,)), ((), ())), precision=HIGHEST,
                preferred_element_type=F32,
            )
            x = dot(pick, b_ref[j], (0, 0)).astype(BF16)
            y = dot(pick, dy_ref[j], (0, 0)).astype(BF16)
            at = pl.ds(pl.multiple_of(j * capacity, capacity), capacity)
            for e in range(here):
                piece = slice(e * capacity, (e + 1) * capacity)
                x_ref[e, at, :] = x[piece]
                y_ref[e, at, :] = y[piece]
                scale_ref[e, at, :] = scales[piece]
            return carry

        lax.fori_loop(0, sources, collect, 0)

    tile = min(256, rows_all)

    def rows_of(i, carry):
        rows = pl.ds(pl.multiple_of(i * tile, tile), tile)
        x = x_ref[step, rows, :]
        gate_pre = dot(x, gate_ref[0])
        up_pre = dot(x, up_ref[0])
        sigmoid = 1.0 / (1.0 + jnp.exp(-gate_pre))
        silu = gate_pre * sigmoid
        hidden = (silu * up_pre).astype(BF16)
        hidden_ref[rows, :] = hidden
        produced = dot(hidden, down_ref[0])
        scale = scale_ref[step, rows, 0:1]
        dy = RESIDUAL_SCALE * y_ref[step, rows, :].astype(F32)
        inner_ref[step, rows, :] = jnp.broadcast_to(
            jnp.sum(dy * produced, axis=1, keepdims=True), (tile, LANES)
        )
        grad = (scale * dy).astype(BF16)
        de_ref[rows, :] = grad
        y_ref[step, rows, :] = (scale * produced).astype(BF16)
        grad_hidden = dot(grad, down_ref[0], (1, 1))
        grad_gate = (
            grad_hidden * up_pre * sigmoid * (1.0 + gate_pre * (1.0 - sigmoid))
        ).astype(BF16)
        grad_up = (grad_hidden * silu).astype(BF16)
        dgp_ref[rows, :] = grad_gate
        dup_s_ref[rows, :] = grad_up
        return carry

    lax.fori_loop(0, rows_all // tile, rows_of, 0)
    width = model_width // parts

    def weight_grads(p, carry):
        columns = pl.ds(pl.multiple_of(p * width, width), width)
        x = x_ref[step, :, columns]
        dgate_ref[p, 0] = dot(x, dgp_ref[...], (0, 0)).astype(BF16)
        dup_ref[p, 0] = dot(x, dup_s_ref[...], (0, 0)).astype(BF16)
        return carry

    def down_grads(p, carry):
        columns = pl.ds(pl.multiple_of(p * width, width), width)
        ddown_ref[p, 0] = dot(hidden_ref[...], de_ref[:, columns], (0, 0)).astype(BF16)
        return carry

    if lane_parts:
        lax.fori_loop(0, parts, weight_grads, 0)
        lax.fori_loop(0, parts, down_grads, 0)
    else:
        for p in range(parts):
            columns = slice(p * width, (p + 1) * width)
            x = x_ref[step, :, columns]
            dgate_ref[p, 0] = dot(x, dgp_ref[...], (0, 0)).astype(BF16)
            dup_ref[p, 0] = dot(x, dup_s_ref[...], (0, 0)).astype(BF16)
        ddown_ref[0, 0] = dot(hidden_ref[...], de_ref[...], (0, 0)).astype(BF16)

    def rows_back(i, carry):
        rows = pl.ds(pl.multiple_of(i * tile, tile), tile)
        x_ref[step, rows, :] = (
            dot(dgp_ref[rows, :], gate_ref[0], (1, 1)) + dot(dup_s_ref[rows, :], up_ref[0], (1, 1))
        ).astype(BF16)
        return carry

    lax.fori_loop(0, rows_all // tile, rows_back, 0)

    @pl.when(step == here - 1)
    def _():
        lane = lax.broadcasted_iota(jnp.int32, (tokens, dg_ref.shape[2]), 1)

        def spread(j, carry):
            at = pl.ds(pl.multiple_of(j * capacity, capacity), capacity)
            pick = pick_ref[j]
            made = jnp.concatenate([y_ref[e, at, :] for e in range(here)], axis=0)
            out_ref[j] = dot(pick, made).astype(BF16)
            back = jnp.concatenate([x_ref[e, at, :] for e in range(here)], axis=0)
            db_ref[j] = dot(pick, back).astype(BF16)
            inner = jnp.concatenate([inner_ref[e, at, :] for e in range(here)], axis=0)
            place = lax.broadcasted_iota(jnp.int32, inner.shape, 0)
            target = lax.broadcasted_iota(jnp.int32, inner.shape, 1)
            owner = jnp.zeros(inner.shape, jnp.int32) + first
            for e in range(1, here):
                owner = jnp.where(place >= e * capacity, first + e, owner)
            inner = jnp.where(target == owner, inner, 0.0)
            dg_ref[j] = lax.dot_general(
                pick.astype(F32), inner, (((1,), (0,)), ((), ())), precision=HIGHEST,
                preferred_element_type=F32,
            )
            return carry

        lax.fori_loop(0, sources, spread, 0)


def experts(me, b_all, dy_all, g_all, w_gate, w_up, w_down, capacity, parts):
    sources, tokens, model_width = b_all.shape
    here, _, hidden_width = w_gate.shape
    rows_all = sources * capacity
    slots = here * capacity
    width = model_width // parts
    lane_parts = width % LANES == 0
    whole = lambda shape: pl.BlockSpec(
        shape, lambda e: (0,) * len(shape), pipeline_mode=pl.Buffered(1)
    )
    if lane_parts:
        down_shape = (parts, here, hidden_width, width)
    else:
        down_shape = (1, here, hidden_width, model_width)
    weight_shape = (parts, here, width, hidden_width)
    return pl.pallas_call(
        functools.partial(experts_kernel, here, capacity, parts, lane_parts),
        out_shape=[
            jax.ShapeDtypeStruct(b_all.shape, BF16),
            jax.ShapeDtypeStruct(b_all.shape, BF16),
            jax.ShapeDtypeStruct((sources, tokens, LANES), F32),
            jax.ShapeDtypeStruct(weight_shape, BF16),
            jax.ShapeDtypeStruct(weight_shape, BF16),
            jax.ShapeDtypeStruct(down_shape, BF16),
        ],
        grid=(here,),
        in_specs=[
            pl.BlockSpec(memory_space=pltpu.SMEM),
            whole(b_all.shape),
            whole(b_all.shape),
            whole(g_all.shape),
            pl.BlockSpec((1, model_width, hidden_width), lambda e: (e, 0, 0)),
            pl.BlockSpec((1, model_width, hidden_width), lambda e: (e, 0, 0)),
            pl.BlockSpec((1, hidden_width, model_width), lambda e: (e, 0, 0)),
        ],
        out_specs=[
            whole(b_all.shape),
            whole(b_all.shape),
            whole((sources, tokens, LANES)),
            pl.BlockSpec((parts, 1, width, hidden_width), lambda e: (0, e, 0, 0)),
            pl.BlockSpec((parts, 1, width, hidden_width), lambda e: (0, e, 0, 0)),
            pl.BlockSpec((down_shape[0], 1) + down_shape[2:], lambda e: (0, e, 0, 0)),
        ],
        scratch_shapes=[
            pltpu.VMEM((sources, tokens, slots), BF16),
            pltpu.VMEM((here, rows_all, model_width), BF16),
            pltpu.VMEM((here, rows_all, model_width), BF16),
            pltpu.VMEM((here, rows_all, LANES), F32),
            pltpu.VMEM((rows_all, hidden_width), BF16),
            pltpu.VMEM((rows_all, hidden_width), BF16),
            pltpu.VMEM((rows_all, hidden_width), BF16),
            pltpu.VMEM((rows_all, model_width), BF16),
            pltpu.VMEM((here, rows_all, LANES), F32),
        ],
        compiler_params=pltpu.CompilerParams(
            dimension_semantics=("arbitrary",), vmem_limit_bytes=VMEM_LIMIT
        ),
        cost_estimate=pl.CostEstimate(
            flops=26_000_000_000, bytes_accessed=42_000_000, transcendentals=1_000_000
        ),
        name="experts",
    )(me, b_all, dy_all, g_all, w_gate, w_up, w_down)


def norm_back(grad_normed, normed, inverse):
    return inverse * (grad_normed - normed * jnp.mean(grad_normed * normed, axis=-1, keepdims=True))


def rotary_tables(length, heads):
    half = HEAD_DIM // 2
    exponent = jnp.arange(half, dtype=F32) * (2.0 / HEAD_DIM)
    angles = jnp.arange(length, dtype=F32)[:, None] * jnp.power(ROPE_BASE, -exponent)[None, :]
    cosine, sine = jnp.cos(angles), jnp.sin(angles)
    cosine = jnp.concatenate([cosine, cosine] * heads, axis=1)
    sine = jnp.concatenate([-sine, sine] * heads, axis=1)
    return cosine, sine


def per_device(
    residual_in, cotangent, gain_attn, w_query, w_key, w_value, w_out, gain_ffn, w_router,
    w_gate, w_up, w_down, route_ids,
):
    me = lax.axis_index("expert")
    peers = lax.axis_size("expert")
    lines = lax.axis_size("fsdp")
    tokens, model_width = residual_in.shape[1:]
    length = tokens * peers
    groups = w_key.shape[1] // HEAD_DIM
    per_group = w_query.shape[1] // w_key.shape[1]
    query_width = per_group * HEAD_DIM
    experts_all = w_router.shape[1]
    here = w_gate.shape[0]
    top_count = route_ids.shape[2]
    capacity = (3 * tokens * top_count // (2 * experts_all) + 7) // 8 * 8
    shard = w_query.shape[0]
    turned = query_width + HEAD_DIM
    in_width = -(-(turned + HEAD_DIM + experts_all) // LANES) * LANES

    w_in_shard = jnp.concatenate(
        [
            lax.dynamic_slice(w_query, (0, me * query_width), (shard, query_width)),
            lax.dynamic_slice(w_key, (0, me * HEAD_DIM), (shard, HEAD_DIM)),
            lax.dynamic_slice(w_value, (0, me * HEAD_DIM), (shard, HEAD_DIM)),
            w_router,
            jnp.zeros((shard, in_width - turned - HEAD_DIM - experts_all), BF16),
        ],
        axis=1,
    )
    w_out_shard = jnp.concatenate(
        [
            lax.dynamic_slice(w_out, (me * query_width, 0), (query_width, shard)),
            gain_attn[None],
            gain_ffn[None],
            jnp.zeros((14, shard), BF16),
        ],
        axis=0,
    )
    x_all, dy_all = plane_gather([residual_in[0], cotangent[0]], 0)
    w_in, w_out_rows = line_gather([w_in_shard, w_out_shard], (0, 1), 1)
    gain_one = w_out_rows[query_width][None].astype(F32)
    gain_two = w_out_rows[query_width + 1][None].astype(F32)
    router = w_in[:, turned + HEAD_DIM : turned + HEAD_DIM + experts_all]
    cosine, sine = rotary_tables(length, per_group + 1)

    part, *saved = attend(
        x_all.reshape(length, model_width), w_in, w_out_rows, cosine, sine, per_group
    )
    (branch,) = plane_scatter([part.reshape(peers, tokens, model_width)], 2)

    rows = residual_in[0].astype(F32)
    inverse_one = lax.rsqrt(jnp.mean(rows * rows, axis=-1, keepdims=True) + EPSILON)
    normed_one = rows * inverse_one
    middle = rows + RESIDUAL_SCALE * branch
    inverse_two = lax.rsqrt(jnp.mean(middle * middle, axis=-1, keepdims=True) + EPSILON)
    normed_two = middle * inverse_two
    routed = (normed_two * gain_two).astype(BF16)
    logits = jnp.dot(routed, router, preferred_element_type=F32)
    chosen = jnp.any(
        route_ids[0][:, :, None] == jnp.arange(experts_all, dtype=jnp.int32)[None, None, :], axis=1
    )
    kept = jnp.where(chosen, logits, -jnp.inf)
    lifted = jnp.exp(kept - jnp.max(kept, axis=-1, keepdims=True))
    gates = lifted / jnp.sum(lifted, axis=-1, keepdims=True)
    marked = jnp.pad(
        jnp.where(chosen, gates, -1.0),
        ((0, 0), (0, LANES - experts_all)),
        constant_values=-1.0,
    )
    b_all, g_all = plane_gather([routed, marked], 3)

    sum_part, db_part, dg_part, dgate, dup, ddown = experts(
        me.reshape(1, 1), b_all, dy_all, g_all, w_gate, w_up, w_down, capacity, lines
    )
    if ddown.shape[0] != lines:
        ddown = ddown[0].reshape(here, -1, lines, shard).transpose(2, 0, 1, 3)
    db_sum, dg_sum = plane_scatter([db_part, dg_part], 4)

    grad_rows = cotangent[0].astype(F32)
    dg = dg_sum[:, :experts_all]
    grad_chosen = gates * (dg - jnp.sum(gates * dg, axis=-1, keepdims=True))
    grad_logits = grad_chosen.astype(BF16)
    grad_routed = (
        lax.dot_general(
            grad_logits, router, (((1,), (1,)), ((), ())), preferred_element_type=F32
        )
        + db_sum
    )
    grad_gain_two = jnp.sum(grad_routed * normed_two, axis=0)
    grad_middle = grad_rows + norm_back(grad_routed * gain_two, normed_two, inverse_two)
    grad_branch = (RESIDUAL_SCALE * grad_middle).astype(BF16)
    dw_all, dl_all = plane_gather(
        [grad_branch, jnp.pad(grad_logits, ((0, 0), (0, LANES - experts_all)))], 5
    )

    da_part, grad_in, grad_out = attend_back(
        dw_all.reshape(length, model_width), w_in, w_out_rows, cosine, sine, saved,
        b_all.reshape(length, model_width), dl_all.reshape(length, LANES), per_group,
    )
    da_sum, expert_sum = plane_scatter(
        [da_part.reshape(peers, tokens, model_width), sum_part], 6
    )

    outcome = middle + RESIDUAL_SCALE * expert_sum
    grad_gain_one = jnp.sum(da_sum * normed_one, axis=0)
    grad_input = grad_middle + norm_back(da_sum * gain_one, normed_one, inverse_one)
    squares = jnp.stack(
        [jnp.sum(v * v) for v in (rows, middle, outcome, grad_middle, grad_input)]
    )
    notes = jnp.broadcast_to(jnp.pad(squares, (0, 3))[:, None], (8, LANES))

    grad_out = jnp.concatenate(
        [
            grad_out,
            grad_gain_one.astype(BF16)[None],
            grad_gain_two.astype(BF16)[None],
            jnp.zeros((14, model_width), BF16),
        ],
        axis=0,
    )
    in_sum, out_sum, line_notes = line_scatter(
        [
            grad_in.reshape(lines, shard, in_width),
            grad_out.reshape(-1, lines, shard).transpose(1, 0, 2),
        ],
        notes,
        7,
    )
    in_all, out_all, notes_all = plane_gather(
        [in_sum.astype(BF16), out_sum.astype(BF16), jnp.sum(line_notes, axis=0)], 8
    )

    def columns_of(start, stop):
        return in_all[:, :, start:stop].transpose(1, 0, 2).reshape(shard, -1).astype(F32)

    count = tokens * model_width * lines * peers
    root_means = jnp.sqrt(jnp.sum(notes_all, axis=0)[:5, 0] / count)
    reduced = [
        lax.psum_scatter(array, "fsdp", scatter_dimension=0, tiled=False).astype(F32)
        for array in (dgate, dup, ddown)
    ]
    gain_rows = jnp.sum(out_all[:, query_width : query_width + 2, :].astype(F32), axis=0)
    return (
        outcome.astype(BF16)[None],
        grad_input.astype(BF16)[None],
        gain_rows[0],
        columns_of(0, query_width),
        columns_of(query_width, turned),
        columns_of(turned, turned + HEAD_DIM),
        out_all[:, :query_width, :].reshape(groups * query_width, shard).astype(F32),
        gain_rows[1],
        in_all[0, :, turned + HEAD_DIM : turned + HEAD_DIM + experts_all].astype(F32),
        reduced[0],
        reduced[1],
        reduced[2],
        root_means,
    )


def solution(mesh):
    in_specs = (
        P("fsdp", "expert", None),
        P("fsdp", "expert", None),
        P("fsdp"),
        P("fsdp", None),
        P("fsdp", None),
        P("fsdp", None),
        P(None, "fsdp"),
        P("fsdp"),
        P("fsdp", None),
        P("expert", None, None),
        P("expert", None, None),
        P("expert", None, None),
        P("fsdp", "expert", None),
    )
    out_specs = (
        P("fsdp", "expert", None),
        P("fsdp", "expert", None),
        P("fsdp"),
        P("fsdp", None),
        P("fsdp", None),
        P("fsdp", None),
        P(None, "fsdp"),
        P("fsdp"),
        P("fsdp", None),
        P("expert", "fsdp", None),
        P("expert", "fsdp", None),
        P("expert", None, "fsdp"),
        P(),
    )
    return jax.shard_map(
        per_device, mesh=mesh, in_specs=in_specs, out_specs=out_specs, check_vma=False
    )
```

```python
import functools

import jax
import jax.numpy as jnp
from jax import lax
from jax.experimental import pallas as pl
from jax.experimental.pallas import tpu as pltpu
from jax.sharding import PartitionSpec as P

HEAD_DIM = 64
BLOCK = 256

EPSILON = 1e-06
RESIDUAL_SCALE = 0.22
ATTENTION_SCALE = 0.015625
ROPE_BASE = 10000.0
HIGHEST = lax.Precision.HIGHEST
MESH = pl.DeviceIdType.MESH
VMEM_LIMIT = 63_000_000
F32 = jnp.float32
BF16 = jnp.bfloat16
LANES = 128


def plane_neighbours():
    me = lax.axis_index("expert")
    core = lax.rem(me, 2)
    x_bit = lax.rem(me // 2, 2)
    y_bit = me // 4
    sibling = me + 1 - 2 * core
    x_peer = me + 2 - 4 * x_bit
    y_peer = me + 4 - 8 * y_bit
    diagonal = x_peer + 4 - 8 * y_bit
    return me, core, x_bit, y_bit, sibling, x_peer, y_peer, diagonal


def greet(axis, peers):
    barrier = pltpu.get_barrier_semaphore()
    for peer in peers:
        pl.semaphore_signal(barrier, inc=1, device_id={axis: peer}, device_id_type=MESH)
    pl.semaphore_wait(barrier, len(peers))


def gather_kernel(count, *refs):
    ins, outs = refs[:count], refs[count : 2 * count]
    own_sem, send_sem, recv_sem = refs[2 * count :]
    me, _, _, _, sibling, x_peer, y_peer, diagonal = plane_neighbours()
    greet("expert", (sibling, x_peer, y_peer))

    def remote(k, slot, source, target, peer):
        return pltpu.make_async_remote_copy(
            src_ref=source,
            dst_ref=target,
            send_sem=send_sem.at[k, slot],
            recv_sem=recv_sem.at[k, slot],
            device_id={"expert": peer},
            device_id_type=MESH,
        )

    plans = []
    for k in range(count):
        half = ins[k].shape[0] // 2
        parts = (pl.ds(0, half), pl.ds(half, half))
        out = outs[k]
        own = pltpu.make_async_copy(ins[k], out.at[me], own_sem.at[k])
        copies = [remote(k, 0, ins[k], out.at[me], sibling)]
        for h in range(2):
            copies.append(remote(k, 1 + h, ins[k].at[parts[h]], out.at[me, parts[h]], x_peer))
        for h in range(2):
            copies.append(remote(k, 3 + h, ins[k].at[parts[h]], out.at[me, parts[h]], y_peer))

        def forward(slot, block, h, peer):
            return remote(k, slot, out.at[block, parts[h]], out.at[block, parts[h]], peer)

        copies.append(forward(5, y_peer, 0, x_peer))
        copies.append(forward(6, x_peer, 1, y_peer))
        for h in range(2):
            copies.append(forward(7 + h, x_peer, h, sibling))
        for h in range(2):
            copies.append(forward(9 + h, y_peer, h, sibling))
        for h in range(2):
            copies.append(forward(11 + h, diagonal, h, sibling))
        plans.append((own, copies))
    for own, copies in plans:
        for slot in (3, 2, 1, 4, 0):
            copies[slot].start()
        own.start()
    for own, copies in plans:
        copies[3].wait_recv()
        copies[5].start()
        copies[2].wait_recv()
        copies[6].start()
        copies[9].start()
        copies[8].start()
        copies[1].wait_recv()
        copies[7].start()
        copies[4].wait_recv()
        copies[10].start()
    for own, copies in plans:
        copies[5].wait_recv()
        copies[11].start()
        copies[6].wait_recv()
        copies[12].start()
    for own, copies in plans:
        for slot in (0, 7, 8, 9, 10, 11, 12):
            copies[slot].wait_recv()
        for copy in copies:
            copy.wait_send()
        own.wait()


def plane_gather(arrays, collective_id):
    if lax.axis_size("expert") != 8:
        return [lax.all_gather(array, "expert", axis=0) for array in arrays]
    count = len(arrays)
    size = sum(array.size * array.dtype.itemsize for array in arrays)
    return pl.pallas_call(
        functools.partial(gather_kernel, count),
        out_shape=[jax.ShapeDtypeStruct((8,) + array.shape, array.dtype) for array in arrays],
        in_specs=[pl.BlockSpec(memory_space=pltpu.VMEM)] * count,
        out_specs=[pl.BlockSpec(memory_space=pl.ANY)] * count,
        scratch_shapes=[
            pltpu.SemaphoreType.DMA((count,)),
            pltpu.SemaphoreType.DMA((count, 13)),
            pltpu.SemaphoreType.DMA((count, 13)),
        ],
        compiler_params=pltpu.CompilerParams(
            collective_id=collective_id, has_side_effects=True, vmem_limit_bytes=VMEM_LIMIT
        ),
        cost_estimate=pl.CostEstimate(flops=0, bytes_accessed=16 * size, transcendentals=0),
        name="plane_gather",
    )(*arrays)


def scatter_kernel(count, *refs):
    ins, outs = refs[:count], refs[count : 2 * count]
    scratch = refs[2 * count : 2 * count + 6 * count]
    send_sem, recv_sem = refs[8 * count :]
    me, core, x_bit, y_bit, sibling, x_peer, y_peer, diagonal = plane_neighbours()
    greet("expert", (sibling, x_peer, y_peer))
    chip = me // 2
    chip_x, chip_y, chip_d = x_peer // 2, y_peer // 2, diagonal // 2
    order = (chip_d, chip_x, chip_y, chip)

    def remote(k, slot, source, target, peer):
        return pltpu.make_async_remote_copy(
            src_ref=source,
            dst_ref=target,
            send_sem=send_sem.at[k, slot],
            recv_sem=recv_sem.at[k, slot],
            device_id={"expert": peer},
            device_id_type=MESH,
        )

    stage0 = []
    for k in range(count):
        pair = scratch[6 * k]
        copies = [
            remote(k, i, ins[k].at[2 * order[i] + 1 - core], pair.at[i], sibling) for i in range(4)
        ]
        stage0.append(copies)
        for copy in copies:
            copy.start()
    later = []
    for k in range(count):
        pair, sums, first_x, first_y, second_x, second_y = scratch[6 * k : 6 * k + 6]
        rows = ins[k].shape[1]
        half = rows // 2
        parts = (pl.ds(0, half), pl.ds(half, half))
        dtype = ins[k].dtype

        def join(i):
            stage0[k][i].wait_recv()
            sums[i] = (ins[k][2 * order[i] + core].astype(F32) + pair[i].astype(F32)).astype(dtype)

        join(0)
        copies = [
            remote(k, 4, sums.at[0, parts[0]], first_x.at[1], x_peer),
            remote(k, 5, sums.at[0, parts[1]], first_y.at[1], y_peer),
        ]
        for copy in copies:
            copy.start()
        join(1)
        copies.append(remote(k, 6, sums.at[1, parts[0]], first_x.at[0], x_peer))
        copies[-1].start()
        join(2)
        copies.append(remote(k, 7, sums.at[2, parts[1]], first_y.at[0], y_peer))
        copies[-1].start()
        join(3)
        later.append(copies)
    for k in range(count):
        pair, sums, first_x, first_y, second_x, second_y = scratch[6 * k : 6 * k + 6]
        half = ins[k].shape[1] // 2
        parts = (pl.ds(0, half), pl.ds(half, half))
        dtype = ins[k].dtype
        copies = later[k]
        copies[0].wait_recv()
        pair[0, parts[0]] = (
            sums[2, parts[0]].astype(F32) + first_x[1].astype(F32)
        ).astype(dtype)
        copies.append(remote(k, 8, pair.at[0, parts[0]], second_y, y_peer))
        copies[-1].start()
        copies[1].wait_recv()
        pair[0, parts[1]] = (
            sums[1, parts[1]].astype(F32) + first_y[1].astype(F32)
        ).astype(dtype)
        copies.append(remote(k, 9, pair.at[0, parts[1]], second_x, x_peer))
        copies[-1].start()
    for k in range(count):
        pair, sums, first_x, first_y, second_x, second_y = scratch[6 * k : 6 * k + 6]
        half = ins[k].shape[1] // 2
        parts = (pl.ds(0, half), pl.ds(half, half))
        copies = later[k]
        copies[2].wait_recv()
        copies[4].wait_recv()
        outs[k][parts[0]] = (
            sums[3, parts[0]].astype(F32) + first_x[0].astype(F32) + second_y[...].astype(F32)
        )
        copies[3].wait_recv()
        copies[5].wait_recv()
        outs[k][parts[1]] = (
            sums[3, parts[1]].astype(F32) + first_y[0].astype(F32) + second_x[...].astype(F32)
        )
        for copy in stage0[k] + copies:
            copy.wait_send()


def plane_scatter(arrays, collective_id):
    if lax.axis_size("expert") != 8:
        return [
            lax.psum_scatter(array, "expert", scatter_dimension=0, tiled=False).astype(F32)
            for array in arrays
        ]
    count = len(arrays)
    scratch = []
    for array in arrays:
        _, rows, columns = array.shape
        half = rows // 2
        for shape in (
            (4, rows, columns),
            (4, rows, columns),
            (2, half, columns),
            (2, half, columns),
            (half, columns),
            (half, columns),
        ):
            scratch.append(pltpu.VMEM(shape, array.dtype))
    size = sum(array.size * array.dtype.itemsize for array in arrays)
    return pl.pallas_call(
        functools.partial(scatter_kernel, count),
        out_shape=[jax.ShapeDtypeStruct(array.shape[1:], F32) for array in arrays],
        in_specs=[pl.BlockSpec(memory_space=pltpu.VMEM)] * count,
        out_specs=[pl.BlockSpec(memory_space=pltpu.VMEM)] * count,
        scratch_shapes=scratch
        + [pltpu.SemaphoreType.DMA((count, 10)), pltpu.SemaphoreType.DMA((count, 10))],
        compiler_params=pltpu.CompilerParams(
            collective_id=collective_id, has_side_effects=True, vmem_limit_bytes=VMEM_LIMIT
        ),
        cost_estimate=pl.CostEstimate(flops=0, bytes_accessed=3 * size, transcendentals=0),
        name="plane_scatter",
    )(*arrays)


def push(source, target, send_sem, recv_sem, axis, peer):
    return pltpu.make_async_remote_copy(
        src_ref=source,
        dst_ref=target,
        send_sem=send_sem,
        recv_sem=recv_sem,
        device_id={axis: peer},
        device_id_type=MESH,
    )


def meet(plane, line, size, with_line):
    barrier = pltpu.get_barrier_semaphore()
    me, _, _, _, sibling, x_peer, y_peer, _ = plane
    for peer in (sibling, x_peer, y_peer):
        pl.semaphore_signal(barrier, inc=1, device_id={"expert": peer}, device_id_type=MESH)
    pl.semaphore_signal(
        barrier, inc=1, device_id={"fsdp": pair_of(line)}, device_id_type=MESH
    )
    if not with_line:
        pl.semaphore_signal(
            barrier, inc=1, device_id={"fsdp": beside(line)}, device_id_type=MESH
        )
        pl.semaphore_wait(barrier, 5)
        return

    @pl.when(line > 0)
    def _():
        pl.semaphore_signal(barrier, inc=1, device_id={"fsdp": line - 1}, device_id_type=MESH)

    @pl.when(line < size - 1)
    def _():
        pl.semaphore_signal(barrier, inc=1, device_id={"fsdp": line + 1}, device_id_type=MESH)

    @pl.when((line > 0) & (line < size - 1))
    def _():
        pl.semaphore_wait(barrier, 6)

    @pl.when((line == 0) | (line == size - 1))
    def _():
        pl.semaphore_wait(barrier, 5)


def pair_of(line):
    return line + 2 - 4 * (line // 2)


def beside(line):
    return line + 1 - 2 * lax.rem(line, 2)


def norm_back(grad_normed, normed, inverse):
    return inverse * (grad_normed - normed * jnp.mean(grad_normed * normed, axis=-1, keepdims=True))


class Gather:
    def __init__(self, plane, k, source, out, base, own_sem, send_sem, recv_sem):
        me, _, _, _, sibling, x_peer, y_peer, diagonal = plane
        half = source.shape[0] // 2
        parts = (pl.ds(0, half), pl.ds(half, half))

        def copy(slot, src, dst, peer):
            return push(src, dst, send_sem.at[k, slot], recv_sem.at[k, slot], "expert", peer)

        def forward(slot, block, h, peer):
            ref = out.at[base + block, parts[h]]
            return copy(slot, ref, ref, peer)

        self.own = pltpu.make_async_copy(source, out.at[base + me], own_sem.at[k])
        copies = [copy(0, source, out.at[base + me], sibling)]
        for slot, peer in ((1, x_peer), (3, y_peer)):
            for h in range(2):
                copies.append(
                    copy(slot + h, source.at[parts[h]], out.at[base + me, parts[h]], peer)
                )
        copies.append(forward(5, y_peer, 0, x_peer))
        copies.append(forward(6, x_peer, 1, y_peer))
        for slot, block in ((7, x_peer), (9, y_peer), (11, diagonal)):
            for h in range(2):
                copies.append(forward(slot + h, block, h, sibling))
        self.copies = copies

    def begin(self):
        for slot in (3, 2, 1, 4, 0):
            self.copies[slot].start()
        self.own.start()

    def relay(self):
        copies = self.copies
        for landed, onward in ((3, (5, 9)), (2, (6, 8)), (1, (7,)), (4, (10,))):
            copies[landed].wait_recv()
            for slot in onward:
                copies[slot].start()

    def relay_diagonal(self):
        for landed, onward in ((5, 11), (6, 12)):
            self.copies[landed].wait_recv()
            self.copies[onward].start()

    def finish(self):
        for slot in (0, 7, 8, 9, 10, 11, 12):
            self.copies[slot].wait_recv()
        for copy in self.copies:
            copy.wait_send()
        self.own.wait()


def gather_sems(count):
    return [
        pltpu.SemaphoreType.DMA((count,)),
        pltpu.SemaphoreType.DMA((count, 13)),
        pltpu.SemaphoreType.DMA((count, 13)),
    ]


class Scatter:
    def __init__(self, plane, k, source, base, scratch, send_sem, recv_sem):
        me, core, _, _, sibling, x_peer, y_peer, diagonal = plane
        self.source, self.base, self.core = source, base, core
        self.pair, self.first_x, self.first_y, self.second_x, self.second_y = scratch[:5]
        self.order = (diagonal // 2, x_peer // 2, y_peer // 2, me // 2)
        self.sums = [
            scratch[5].at[i] if len(scratch) > 5 else source.at[base + 2 * self.order[i] + core]
            for i in range(4)
        ]
        self.dtype = source.dtype
        half = source.shape[1] // 2
        self.parts = parts = (pl.ds(0, half), pl.ds(half, half))

        def copy(slot, src, dst, peer):
            return push(src, dst, send_sem.at[k, slot], recv_sem.at[k, slot], "expert", peer)

        self.stage0 = [
            copy(i, source.at[base + 2 * self.order[i] + 1 - core], self.pair.at[i], sibling)
            for i in range(4)
        ]
        self.stage1 = [
            copy(4, self.sums[0].at[parts[0]], self.first_x.at[1], x_peer),
            copy(5, self.sums[0].at[parts[1]], self.first_y.at[1], y_peer),
            copy(6, self.sums[1].at[parts[0]], self.first_x.at[0], x_peer),
            copy(7, self.sums[2].at[parts[1]], self.first_y.at[0], y_peer),
        ]
        self.stage2 = [
            copy(8, self.pair.at[0, parts[0]], self.second_y, y_peer),
            copy(9, self.pair.at[0, parts[1]], self.second_x, x_peer),
        ]

    def begin(self):
        for copy in self.stage0:
            copy.start()

    def join(self, i):
        self.stage0[i].wait_recv()
        mine = self.source[self.base + 2 * self.order[i] + self.core]
        self.sums[i][...] = (mine.astype(F32) + self.pair[i].astype(F32)).astype(self.dtype)

    def first(self):
        self.join(0)
        self.stage1[0].start()
        self.stage1[1].start()
        self.join(1)
        self.stage1[2].start()
        self.join(2)
        self.stage1[3].start()
        self.join(3)

    def second(self):
        for h, block, landed in ((0, 2, self.first_x), (1, 1, self.first_y)):
            self.stage1[h].wait_recv()
            rows = self.parts[h]
            self.pair[0, rows] = (
                self.sums[block][rows].astype(F32) + landed[1].astype(F32)
            ).astype(self.dtype)
            self.stage2[h].start()

    def total(self, h):
        self.stage1[2 + h].wait_recv()
        self.stage2[h].wait_recv()
        near, far = ((self.first_x, self.second_y), (self.first_y, self.second_x))[h]
        return (
            self.sums[3][self.parts[h]].astype(F32)
            + near[0].astype(F32)
            + far[...].astype(F32)
        )

    def finish(self):
        for copy in self.stage0 + self.stage1 + self.stage2:
            copy.wait_send()


def scatter_scratch(rows, columns, dtype, in_place=False):
    half = rows // 2
    shapes = [
        (4, rows, columns),
        (2, half, columns),
        (2, half, columns),
        (half, columns),
        (half, columns),
        (4, rows, columns),
    ]
    return [pltpu.VMEM(shape, dtype) for shape in shapes[: 5 if in_place else 6]]


def scatter_sems(count):
    return [pltpu.SemaphoreType.DMA((count, 10)), pltpu.SemaphoreType.DMA((count, 10))]


class LineGather:
    def __init__(self, line, size, k, source, out, axis, own_sem, send_sem, recv_sem):
        self.line, self.size, self.k, self.source, self.out = line, size, k, source, out
        self.axis, self.send_sem, self.recv_sem = axis, send_sem, recv_sem
        self.own = pltpu.make_async_copy(source, self.place(line), own_sem.at[k])

    def place(self, owner):
        extent = self.source.shape[self.axis]
        span = pl.ds(pl.multiple_of(owner * extent, extent), extent)
        return self.out.at[span] if self.axis == 0 else self.out.at[:, span]

    def hop(self, side, step, owner, source=None):
        target = self.place(owner)
        return push(
            target if source is None else source,
            target,
            self.send_sem.at[self.k, side, step],
            self.recv_sem.at[self.k, side, step],
            "fsdp",
            self.line + 1 - 2 * side,
        )

    def begin(self):
        for side, there in ((0, self.line < self.size - 1), (1, self.line > 0)):

            @pl.when(there)
            def _():
                self.hop(side, 0, self.line, self.source).start()

        self.own.start()

    def step(self, step):
        line, last = self.line, self.size - 1
        for side, owner in ((0, line - 1 - step), (1, line + 1 + step)):

            @pl.when((owner >= 0) & (owner <= last))
            def _():
                self.hop(side, step, owner).wait_recv()

                @pl.when((line < last) if side == 0 else (line > 0))
                def _():
                    self.hop(side, step + 1, owner).start()

    def finish(self):
        line, last = self.line, self.size - 1
        self.own.wait()
        for step in range(self.size - 1):
            for side, owner, there in ((0, line - step, line < last), (1, line + step, line > 0)):

                @pl.when(there & (owner >= 0) & (owner <= last))
                def _():
                    self.hop(side, step, owner).wait_send()


def line_gather_sems(count, size):
    return [
        pltpu.SemaphoreType.DMA((count,)),
        pltpu.SemaphoreType.DMA((count, 2, size)),
        pltpu.SemaphoreType.DMA((count, 2, size)),
    ]


class LineScatter:
    def __init__(self, line, size, k, source, sums, landed, send_sem, recv_sem):
        self.line, self.size, self.k = line, size, k
        self.source, self.sums, self.landed = source, sums, landed
        self.send_sem, self.recv_sem = send_sem, recv_sem

    def hop(self, side, owner):
        return push(
            self.sums.at[side, owner],
            self.landed.at[side, owner],
            self.send_sem.at[self.k, side, owner],
            self.recv_sem.at[self.k, side, owner],
            "fsdp",
            self.line + 1 - 2 * side,
        )

    def begin(self):
        last = self.size - 1
        for far in range(last):
            for side, owner, end in ((0, last - far, 0), (1, far, last)):

                @pl.when(self.line == end)
                def _():
                    self.sums[side, owner] = self.source[owner]
                    self.hop(side, owner).start()

    def pass_on(self, side, owner):
        self.hop(side, owner).wait_recv()
        self.sums[side, owner] = (
            self.source[owner].astype(F32) + self.landed[side, owner].astype(F32)
        ).astype(self.source.dtype)
        self.hop(side, owner).start()

    def step(self, far):
        line, last = self.line, self.size - 1

        @pl.when((line < last - far) & (line > 0))
        def _():
            self.pass_on(0, last - far)

        @pl.when((line > far) & (line < last))
        def _():
            self.pass_on(1, far)

    def total(self, out):
        line, last = self.line, self.size - 1
        out[...] = self.source[line].astype(F32)
        for side, there in ((0, line > 0), (1, line < last)):

            @pl.when(there)
            def _():
                self.hop(side, line).wait_recv()
                out[...] += self.landed[side, line].astype(F32)

    def finish(self):
        for owner in range(self.size):

            @pl.when(self.line < owner)
            def _():
                self.hop(0, owner).wait_send()

            @pl.when(self.line > owner)
            def _():
                self.hop(1, owner).wait_send()


def line_scatter_sems(count, size):
    return [
        pltpu.SemaphoreType.DMA((count, 2, size)),
        pltpu.SemaphoreType.DMA((count, 2, size)),
    ]


def in_vmem(count):
    return [pl.BlockSpec(memory_space=pltpu.VMEM)] * count


def anywhere(count):
    return [pl.BlockSpec(memory_space=pl.ANY)] * count


def talk_params(collective_id):
    return pltpu.CompilerParams(
        collective_id=collective_id, has_side_effects=True, vmem_limit_bytes=VMEM_LIMIT
    )


def open_kernel(
    size, x_ref, dy_ref, win_ref, wout_ref,
    x_out, dy_out, win_out, wout_out,
    landed, swap_sems, own_sem, send_sem, recv_sem, line_own, line_send, line_recv,
):
    plane, line = plane_neighbours(), lax.axis_index("fsdp")
    meet(plane, line, size, True)
    swap = push(dy_ref, landed, swap_sems.at[0], swap_sems.at[1], "fsdp", pair_of(line))
    sems = (own_sem, send_sem, recv_sem)
    line_sems = (line_own, line_send, line_recv)
    x = Gather(plane, 0, x_ref, x_out, 0, *sems)
    dy = Gather(plane, 1, dy_ref, dy_out, 0, *sems)
    other = Gather(plane, 2, landed, dy_out, 8, *sems)
    win = LineGather(line, size, 0, win_ref, win_out, 0, *line_sems)
    wout = LineGather(line, size, 1, wout_ref, wout_out, 1, *line_sems)
    win.begin()
    x.begin()
    swap.start()
    wout.begin()
    dy.begin()
    x.relay()
    win.step(0)
    x.relay_diagonal()
    wout.step(0)
    win.step(1)
    dy.relay()
    swap.wait_recv()
    other.begin()
    wout.step(1)
    dy.relay_diagonal()
    win.step(2)
    wout.step(2)
    other.relay()
    other.relay_diagonal()
    for part in (x, dy, other, win, wout):
        part.finish()
    swap.wait_send()


def open_transfers(x, dy, w_in_shard, w_out_shard, size, collective_id):
    tokens, model_width = x.shape
    rows, columns = w_in_shard.shape
    out_rows, out_columns = w_out_shard.shape
    return pl.pallas_call(
        functools.partial(open_kernel, size),
        out_shape=[
            jax.ShapeDtypeStruct((8, tokens, model_width), BF16),
            jax.ShapeDtypeStruct((16, tokens, model_width), BF16),
            jax.ShapeDtypeStruct((rows * size, columns), BF16),
            jax.ShapeDtypeStruct((out_rows, out_columns * size), BF16),
        ],
        in_specs=in_vmem(4),
        out_specs=anywhere(4),
        scratch_shapes=[pltpu.VMEM((tokens, model_width), BF16), pltpu.SemaphoreType.DMA((2,))]
        + gather_sems(3)
        + line_gather_sems(2, size),
        compiler_params=talk_params(collective_id),
        cost_estimate=pl.CostEstimate(flops=0, bytes_accessed=120_000_000, transcendentals=0),
        name="open_transfers",
    )(x, dy, w_in_shard, w_out_shard)


def middle_kernel(
    query_width, router_at, part_ref, x_ref, win_ref, wout_ref, chosen_ref,
    b_out, g_out, middle_ref, marked_ref,
    routed, b_landed, g_landed, *rest,
):
    scratch, rest = rest[:6], rest[6:]
    swap_sems, scatter_send, scatter_recv, own_sem, send_sem, recv_sem = rest
    plane, line = plane_neighbours(), lax.axis_index("fsdp")
    meet(plane, line, 4, False)
    scatter = Scatter(plane, 0, part_ref, 0, scratch, scatter_send, scatter_recv)
    scatter.begin()
    scatter.first()
    scatter.second()
    half = x_ref.shape[0] // 2
    gain = wout_ref[query_width + 1 : query_width + 2, :].astype(F32)
    router = win_ref[:, router_at : router_at + LANES]
    for h in range(2):
        rows = pl.ds(h * half, half)
        middle = x_ref[rows].astype(F32) + RESIDUAL_SCALE * scatter.total(h)
        middle_ref[rows] = middle
        inverse = lax.rsqrt(jnp.mean(middle * middle, axis=1, keepdims=True) + EPSILON)
        b = (middle * inverse * gain).astype(BF16)
        routed[rows] = b
        chosen = chosen_ref[rows] > 0.0
        logits = jnp.where(chosen, dot(b, router), -1e30)
        lifted = jnp.where(chosen, jnp.exp(logits - jnp.max(logits, axis=1, keepdims=True)), 0.0)
        gates = lifted / jnp.sum(lifted, axis=1, keepdims=True)
        marked_ref[rows] = jnp.where(chosen, gates, -1.0)
    swap_b = push(routed, b_landed, swap_sems.at[0], swap_sems.at[1], "fsdp", pair_of(line))
    swap_g = push(marked_ref, g_landed, swap_sems.at[2], swap_sems.at[3], "fsdp", pair_of(line))
    swap_b.start()
    swap_g.start()
    sems = (own_sem, send_sem, recv_sem)
    b = Gather(plane, 0, routed, b_out, 0, *sems)
    g = Gather(plane, 1, marked_ref, g_out, 0, *sems)
    b_other = Gather(plane, 2, b_landed, b_out, 8, *sems)
    g_other = Gather(plane, 3, g_landed, g_out, 8, *sems)
    b.begin()
    g.begin()
    b.relay()
    g.relay()
    b.relay_diagonal()
    g.relay_diagonal()
    swap_b.wait_recv()
    swap_g.wait_recv()
    b_other.begin()
    g_other.begin()
    b_other.relay()
    g_other.relay()
    b_other.relay_diagonal()
    g_other.relay_diagonal()
    for item in (b, g, b_other, g_other, scatter):
        item.finish()
    swap_b.wait_send()
    swap_g.wait_send()


def middle_transfers(part, x, w_in, w_out, chosen, query_width, router_at, collective_id):
    tokens, model_width = x.shape
    return pl.pallas_call(
        functools.partial(middle_kernel, query_width, router_at),
        out_shape=[
            jax.ShapeDtypeStruct((16, tokens, model_width), BF16),
            jax.ShapeDtypeStruct((16, tokens, LANES), F32),
            jax.ShapeDtypeStruct((tokens, model_width), F32),
            jax.ShapeDtypeStruct((tokens, LANES), F32),
        ],
        in_specs=in_vmem(5),
        out_specs=anywhere(2) + in_vmem(2),
        scratch_shapes=[
            pltpu.VMEM((tokens, model_width), BF16),
            pltpu.VMEM((tokens, model_width), BF16),
            pltpu.VMEM((tokens, LANES), F32),
        ]
        + scatter_scratch(tokens, model_width, BF16)
        + [pltpu.SemaphoreType.DMA((4,))]
        + scatter_sems(1)
        + gather_sems(4),
        compiler_params=talk_params(collective_id),
        cost_estimate=pl.CostEstimate(flops=0, bytes_accessed=150_000_000, transcendentals=0),
        name="middle_transfers",
    )(part, x, w_in, w_out, chosen)


def close_kernel(
    size, query_width, da_ref, sum_ref, x_ref, middle_ref, grad_ref, gain_two_ref, wout_ref,
    gin_ref, gout_ref,
    outcome_ref, input_grad_ref, in_out, out_out, gains_out, notes_out,
    e_total, e_landed, gains, notes, notes_line, in_sum, out_sum, gain_sum,
    in_low, out_low, gain_low, notes_low, *rest,
):
    scratch, rest = rest[:18], rest[18:]
    line_scratch, rest = rest[:6], rest[6:]
    (
        swap_sems, scatter_send, scatter_recv, sum_send, sum_recv,
        line_own, line_send, line_recv, own_sem, send_sem, recv_sem,
    ) = rest
    plane, line = plane_neighbours(), lax.axis_index("fsdp")
    meet(plane, line, size, True)
    sums = (scatter_send, scatter_recv)
    da = Scatter(plane, 0, da_ref, 0, scratch[:6], *sums)
    other = Scatter(plane, 1, sum_ref, 8, scratch[6:12], *sums)
    mine = Scatter(plane, 2, sum_ref, 0, scratch[12:], *sums)
    gin = LineScatter(line, size, 0, gin_ref, *line_scratch[0:2], sum_send, sum_recv)
    gout = LineScatter(line, size, 1, gout_ref, *line_scratch[2:4], sum_send, sum_recv)
    gain = LineScatter(line, size, 2, gains, *line_scratch[4:6], sum_send, sum_recv)
    gin.begin()
    gout.begin()
    other.begin()
    da.begin()
    mine.begin()
    other.first()
    da.first()
    gin.step(0)
    other.second()
    half = x_ref.shape[0] // 2
    for h in range(2):
        e_total[pl.ds(h * half, half)] = other.total(h).astype(BF16)
    swap = push(e_total, e_landed, swap_sems.at[0], swap_sems.at[1], "fsdp", pair_of(line))
    da.second()
    gin.step(1)
    mine.first()
    gin.step(2)
    gout.step(0)
    swap.start()
    mine.second()
    gain_one = wout_ref[query_width : query_width + 1, :].astype(F32)
    grad_gain = jnp.zeros((1, x_ref.shape[1]), F32)
    squares = [jnp.zeros((1, 1), F32)] * 5

    def add_square(i, values):
        squares[i] = squares[i] + jnp.sum(
            jnp.sum(values * values, axis=1, keepdims=True), axis=0, keepdims=True
        )

    for h in range(2):
        rows = pl.ds(h * half, half)
        x = x_ref[rows].astype(F32)
        inverse = lax.rsqrt(jnp.mean(x * x, axis=1, keepdims=True) + EPSILON)
        normed = x * inverse
        grad_a = da.total(h)
        grad_gain += jnp.sum(grad_a * normed, axis=0, keepdims=True)
        grad_middle = grad_ref[rows]
        grad_input = grad_middle + norm_back(grad_a * gain_one, normed, inverse)
        input_grad_ref[rows] = grad_input.astype(BF16)
        add_square(0, x)
        add_square(1, middle_ref[rows])
        add_square(3, grad_middle)
        add_square(4, grad_input)
    width = x_ref.shape[1] // size
    row = lax.broadcasted_iota(jnp.int32, gains.shape[1:], 0)
    for p in range(size):
        columns = slice(p * width, (p + 1) * width)
        gains[p] = jnp.where(
            row == 0, grad_gain[:, columns],
            jnp.where(row == 1, gain_two_ref[0:1, columns], 0.0),
        ).astype(BF16)
    gain.begin()
    gout.step(1)
    gout.step(2)
    gain.step(0)
    gain.step(1)
    swap.wait_recv()
    for h in range(2):
        rows = pl.ds(h * half, half)
        outcome = middle_ref[rows] + mine.total(h) + e_landed[rows].astype(F32)
        outcome_ref[rows] = outcome.astype(BF16)
        add_square(2, outcome)
    row = lax.broadcasted_iota(jnp.int32, notes.shape, 0)
    told = jnp.zeros(notes.shape, F32)
    for i in range(5):
        told = jnp.where(row == i, squares[i], told)
    notes[...] = told
    spread = LineGather(line, size, 0, notes, notes_line, 0, line_own, line_send, line_recv)
    spread.begin()
    gathers = (own_sem, send_sem, recv_sem)
    gin.total(in_sum)
    in_low[...] = in_sum[...].astype(BF16)
    in_all = Gather(plane, 0, in_low, in_out, 0, *gathers)
    in_all.begin()
    gain.step(2)
    spread.step(0)
    gout.total(out_sum)
    out_low[...] = out_sum[...].astype(BF16)
    out_all = Gather(plane, 1, out_low, out_out, 0, *gathers)
    out_all.begin()
    spread.step(1)
    spread.step(2)
    gain.total(gain_sum)
    gain_low[...] = gain_sum[...].astype(BF16)
    gain_all = Gather(plane, 2, gain_low, gains_out, 0, *gathers)
    gain_all.begin()
    spread.finish()
    count = notes.shape[0]
    notes_low[...] = (
        notes_line[pl.ds(0, count)] + notes_line[pl.ds(count, count)]
        + notes_line[pl.ds(2 * count, count)] + notes_line[pl.ds(3 * count, count)]
    )
    notes_all = Gather(plane, 3, notes_low, notes_out, 0, *gathers)
    notes_all.begin()
    last = (in_all, out_all, gain_all, notes_all)
    for item in last:
        item.relay()
    for item in last:
        item.relay_diagonal()
    for item in last + (da, other, mine, gin, gout, gain):
        item.finish()
    swap.wait_send()


def close_transfers(
    da_part, sum_part, x, middle, grad_middle, gain_two, w_out, grad_in, grad_out,
    query_width, collective_id,
):
    tokens, model_width = x.shape
    size, in_rows, in_columns = grad_in.shape
    _, out_rows, out_columns = grad_out.shape
    wide = (tokens, model_width)
    gain_shape, note_shape = (16, out_columns), (16, LANES)
    line_scratch = []
    for shape in (grad_in.shape, grad_out.shape, (size,) + gain_shape):
        line_scratch += [pltpu.VMEM((2,) + shape, BF16)] * 2
    return pl.pallas_call(
        functools.partial(close_kernel, size, query_width),
        out_shape=[
            jax.ShapeDtypeStruct(wide, BF16),
            jax.ShapeDtypeStruct(wide, BF16),
            jax.ShapeDtypeStruct((8, in_rows, in_columns), BF16),
            jax.ShapeDtypeStruct((8, out_rows, out_columns), BF16),
            jax.ShapeDtypeStruct((8,) + gain_shape, BF16),
            jax.ShapeDtypeStruct((8,) + note_shape, F32),
        ],
        in_specs=in_vmem(9),
        out_specs=in_vmem(2) + anywhere(4),
        scratch_shapes=[
            pltpu.VMEM(wide, BF16),
            pltpu.VMEM(wide, BF16),
            pltpu.VMEM((size,) + gain_shape, BF16),
            pltpu.VMEM(note_shape, F32),
            pltpu.VMEM((size * note_shape[0], LANES), F32),
            pltpu.VMEM((in_rows, in_columns), F32),
            pltpu.VMEM((out_rows, out_columns), F32),
            pltpu.VMEM(gain_shape, F32),
            pltpu.VMEM((in_rows, in_columns), BF16),
            pltpu.VMEM((out_rows, out_columns), BF16),
            pltpu.VMEM(gain_shape, BF16),
            pltpu.VMEM(note_shape, F32),
        ]
        + scatter_scratch(*wide, BF16) * 3
        + line_scratch
        + [pltpu.SemaphoreType.DMA((2,))]
        + scatter_sems(3)
        + line_scatter_sems(3, size)
        + line_gather_sems(1, size)
        + gather_sems(4),
        compiler_params=talk_params(collective_id),
        cost_estimate=pl.CostEstimate(flops=0, bytes_accessed=200_000_000, transcendentals=0),
        name="close_transfers",
    )(da_part, sum_part, x, middle, grad_middle, gain_two, w_out, grad_in, grad_out)


def dot(first, second, contract=(1, 0)):
    return lax.dot_general(
        first, second, (((contract[0],), (contract[1],)), ((), ())), preferred_element_type=F32
    )


def spin(values, cosine, sine):
    width = values.shape[1]
    half = HEAD_DIM // 2
    cosine = jnp.concatenate([cosine] * (width // LANES), axis=1)
    sine = jnp.concatenate([sine] * (width // LANES), axis=1)
    lane = lax.broadcasted_iota(jnp.int32, values.shape, 1)
    lower = lax.rem(lane, HEAD_DIM) < half
    swapped = jnp.where(
        lower, pltpu.roll(values, width - half, 1), pltpu.roll(values, half, 1)
    )
    return values * cosine + swapped * sine


def attend_kernel(
    per_group, x_ref, w_in_ref, w_out_ref, cos_ref, sin_ref,
    part_ref, a_ref, q_ref, k_ref, v_ref, o_ref, lse_ref,
):
    length, model_width = x_ref.shape
    query_width = per_group * HEAD_DIM
    turned = query_width + HEAD_DIM
    gain = w_out_ref[query_width : query_width + 1, :].astype(F32)

    def project(i, carry):
        rows = pl.ds(pl.multiple_of(i * BLOCK, BLOCK), BLOCK)
        x = x_ref[rows, :].astype(F32)
        inverse = lax.rsqrt(jnp.mean(x * x, axis=1, keepdims=True) + EPSILON)
        a = (x * inverse * gain).astype(BF16)
        a_ref[rows, :] = a
        pre = dot(a, w_in_ref[...])
        spun = spin(pre[:, :turned], cos_ref[rows, :], sin_ref[rows, :]).astype(BF16)
        for h in range(per_group):
            q_ref[h, rows, :] = spun[:, h * HEAD_DIM : (h + 1) * HEAD_DIM]
        k_ref[rows, :] = spun[:, query_width:turned]
        v_ref[rows, :] = pre[:, turned : turned + HEAD_DIM].astype(BF16)
        return carry

    lax.fori_loop(0, length // BLOCK, project, 0)
    for i in range(length // BLOCK):
        seen = (i + 1) * BLOCK
        rows = slice(i * BLOCK, seen)
        keys, values = k_ref[:seen, :], v_ref[:seen, :]
        for h in range(per_group):
            scores = dot(q_ref[h, rows, :], keys, (1, 1)) * ATTENTION_SCALE
            peak = jnp.max(scores, axis=1, keepdims=True)
            lifted = jnp.exp(scores - peak)
            total = jnp.sum(lifted, axis=1, keepdims=True)
            weights = (lifted * (1.0 / total)).astype(BF16)
            mixed = dot(weights, values)
            o_ref[rows, h * HEAD_DIM : (h + 1) * HEAD_DIM] = mixed.astype(BF16)
            lse_ref[h, rows, :] = peak + jnp.log(total)
        part_ref[rows, :] = dot(o_ref[rows, :], w_out_ref[:query_width, :]).astype(BF16)


def attend(x_all, w_in, w_out, cosine, sine, per_group):
    length, model_width = x_all.shape
    query_width = per_group * HEAD_DIM
    shapes = [
        jax.ShapeDtypeStruct((length, model_width), BF16),
        jax.ShapeDtypeStruct((length, model_width), BF16),
        jax.ShapeDtypeStruct((per_group, length, HEAD_DIM), BF16),
        jax.ShapeDtypeStruct((length, HEAD_DIM), BF16),
        jax.ShapeDtypeStruct((length, HEAD_DIM), BF16),
        jax.ShapeDtypeStruct((length, query_width), BF16),
        jax.ShapeDtypeStruct((per_group, length, 1), F32),
    ]
    return pl.pallas_call(
        functools.partial(attend_kernel, per_group),
        out_shape=shapes,
        in_specs=[pl.BlockSpec(memory_space=pltpu.VMEM)] * 5,
        out_specs=[pl.BlockSpec(memory_space=pltpu.VMEM)] * len(shapes),
        compiler_params=pltpu.CompilerParams(vmem_limit_bytes=VMEM_LIMIT),
        cost_estimate=pl.CostEstimate(
            flops=8_000_000_000, bytes_accessed=16_000_000, transcendentals=2_000_000
        ),
        name="attend",
    )(x_all, w_in, w_out, cosine, sine)


def attend_back_kernel(
    per_group, dw_ref, w_in_ref, w_out_ref, cos_ref, sin_ref,
    a_ref, q_ref, k_ref, v_ref, o_ref, lse_ref, b_all_ref, dl_ref,
    part_ref, gin_ref, gout_ref,
    turn_ref, dv_ref, back_ref, b_ref, b_sem,
):
    length, model_width = dw_ref.shape
    fetch = pltpu.make_async_copy(b_all_ref.at[pl.ds(0, length)], b_ref, b_sem)
    fetch.start()
    query_width = per_group * HEAD_DIM
    turned = query_width + HEAD_DIM
    blocks = length // BLOCK
    turn_ref[...] = jnp.zeros_like(turn_ref)
    dv_ref[...] = jnp.zeros_like(dv_ref)
    for i in range(blocks):
        seen = (i + 1) * BLOCK
        rows = slice(i * BLOCK, seen)
        keys, values = k_ref[:seen, :], v_ref[:seen, :]
        grad = dot(dw_ref[rows, :], w_out_ref[:query_width, :], (1, 1)).astype(BF16)
        for h in range(per_group):
            columns = slice(h * HEAD_DIM, (h + 1) * HEAD_DIM)
            queries = q_ref[h, rows, :]
            grad_head = grad[:, columns]
            scores = dot(queries, keys, (1, 1)) * ATTENTION_SCALE
            probs = jnp.exp(scores - lse_ref[h, rows, :])
            dv_ref[:seen, :] += dot(probs.astype(BF16), grad_head, (0, 0))
            grad_probs = dot(grad_head, values, (1, 1))
            inner = jnp.sum(probs * grad_probs, axis=1, keepdims=True)
            grad_scores = (probs * (grad_probs - inner)).astype(BF16)
            turn_ref[rows, columns] = dot(grad_scores, keys) * ATTENTION_SCALE
            turn_ref[:seen, query_width:turned] += (
                dot(grad_scores, queries, (0, 0)) * ATTENTION_SCALE
            )

    def unturn(i, carry):
        rows = pl.ds(pl.multiple_of(i * BLOCK, BLOCK), BLOCK)
        back_ref[rows, :turned] = spin(
            turn_ref[rows, :], cos_ref[rows, :], -sin_ref[rows, :]
        ).astype(BF16)
        back_ref[rows, turned:] = jnp.concatenate(
            [dv_ref[rows, :].astype(BF16), jnp.zeros((BLOCK, LANES - HEAD_DIM), BF16)], axis=1
        )
        part_ref[rows, :] = dot(
            back_ref[rows, : turned + HEAD_DIM], w_in_ref[:, : turned + HEAD_DIM], (1, 1)
        ).astype(BF16)
        return carry

    lax.fori_loop(0, blocks, unturn, 0)
    chunk = 384
    fetch.wait()

    def weight_grads(i, carry):
        columns = pl.ds(pl.multiple_of(i * chunk, chunk), chunk)
        a = a_ref[:, columns]
        gin_ref[columns, :turned] = dot(a, back_ref[:, :turned], (0, 0)).astype(BF16)
        gin_ref[columns, turned:] = (
            dot(a, back_ref[:, turned:], (0, 0)) + dot(b_ref[:, columns], dl_ref[...], (0, 0))
        ).astype(BF16)
        gout_ref[i] = dot(o_ref[...], dw_ref[:, columns], (0, 0)).astype(BF16)
        return carry

    lax.fori_loop(0, model_width // chunk, weight_grads, 0)


def attend_back(dw_all, w_in, w_out, cosine, sine, saved, b_all, dl_all, per_group):
    length, model_width = dw_all.shape
    query_width = per_group * HEAD_DIM
    turned = query_width + HEAD_DIM
    shapes = [
        jax.ShapeDtypeStruct((length, model_width), BF16),
        jax.ShapeDtypeStruct((model_width, w_in.shape[1]), BF16),
        jax.ShapeDtypeStruct((model_width // 384, query_width, 384), BF16),
    ]
    return pl.pallas_call(
        functools.partial(attend_back_kernel, per_group),
        out_shape=shapes,
        in_specs=in_vmem(11) + anywhere(1) + in_vmem(1),
        out_specs=in_vmem(len(shapes)),
        scratch_shapes=[
            pltpu.VMEM((length, turned), F32),
            pltpu.VMEM((length, HEAD_DIM), F32),
            pltpu.VMEM((length, w_in.shape[1]), BF16),
            pltpu.VMEM((length, model_width), BF16),
            pltpu.SemaphoreType.DMA,
        ],
        compiler_params=pltpu.CompilerParams(vmem_limit_bytes=VMEM_LIMIT),
        cost_estimate=pl.CostEstimate(
            flops=20_000_000_000, bytes_accessed=30_000_000, transcendentals=2_000_000
        ),
        name="attend_back",
    )(dw_all, w_in, w_out, cosine, sine, *saved, b_all, dl_all)


def experts_kernel(
    here, tile,
    place_ref, b_hbm, dy_hbm, g_ref, gate_hbm, up_hbm, down_hbm, *rest,
):
    out_hbm, db_hbm, dg_ref = rest[:3]
    grad_hbm, rest = rest[3:6], rest[6:]
    (
        b_ref, dy_ref, in_ref, down_ref, hidden_ref, back_ref, out_ref, db_ref,
        gate_stage, up_stage, down_stage, weight_sem, tile_sem, out_sem, grad_sem,
    ) = rest
    rows_all, model_width = b_ref.shape
    width = down_ref.shape[0] // here
    tiles = rows_all // tile
    first = place_ref[0]

    def columns_of(e):
        return slice(e * width, (e + 1) * width)

    loads = []
    for e in range(here):
        loads.append((gate_hbm.at[e], in_ref.at[:, columns_of(e)]))
        loads.append((up_hbm.at[e], in_ref.at[:, columns_of(here + e)]))
    for e in range(here):
        loads.append((down_hbm.at[e], down_ref.at[columns_of(e), :]))
    loads = [
        pltpu.make_async_copy(source, target, weight_sem.at[i])
        for i, (source, target) in enumerate(loads)
    ]

    def tile_rows(i):
        return pl.ds(pl.multiple_of(i * tile, tile), tile)

    def tile_load(i, k):
        source, target = ((b_hbm, b_ref), (dy_hbm, dy_ref))[k]
        return pltpu.make_async_copy(
            source.at[tile_rows(i)], target.at[tile_rows(i)], tile_sem.at[k, i]
        )

    def tile_store(i, k):
        source, target = ((out_ref, out_hbm), (db_ref, db_hbm))[k]
        return pltpu.make_async_copy(
            source.at[tile_rows(i)], target.at[tile_rows(i)], out_sem.at[k, i]
        )

    for k in range(2):
        tile_load(0, k).start()
    for load in loads:
        load.start()
    for i in range(1, tiles):
        for k in range(2):
            tile_load(i, k).start()
    for load in loads:
        load.wait()

    def forward_back(i, carry):
        rows = tile_rows(i)
        tile_load(i, 0).wait()
        tile_load(i, 1).wait()
        pre = dot(b_ref[rows, :], in_ref[...])
        grad_mixed = dot(dy_ref[rows, :], down_ref[...], (1, 1))
        gates = g_ref[rows, :]
        lane = lax.broadcasted_iota(jnp.int32, gates.shape, 1)
        inner = jnp.zeros(gates.shape, F32)
        for e in range(here):
            mine = lane == first + e
            gate = jnp.sum(jnp.where(mine, jnp.maximum(gates, 0.0), 0.0), axis=1, keepdims=True)
            scale = RESIDUAL_SCALE * gate
            gate_pre, up_pre = pre[:, columns_of(e)], pre[:, columns_of(here + e)]
            sigmoid = 1.0 / (1.0 + jnp.exp(-gate_pre))
            silu = gate_pre * sigmoid
            hidden = silu * up_pre
            grad = grad_mixed[:, columns_of(e)]
            share = jnp.sum(hidden * grad, axis=1, keepdims=True)
            inner = jnp.where(mine, RESIDUAL_SCALE * share, inner)
            hidden_ref[rows, columns_of(e)] = (scale * hidden).astype(BF16)
            grad = scale * grad
            back_ref[rows, columns_of(e)] = (
                grad * up_pre * sigmoid * (1.0 + gate_pre * (1.0 - sigmoid))
            ).astype(BF16)
            back_ref[rows, columns_of(here + e)] = (grad * silu).astype(BF16)
        dg_ref[rows, :] = inner
        db_ref[rows, :] = dot(back_ref[rows, :], in_ref[...], (1, 1)).astype(BF16)
        tile_store(i, 1).start()
        out_ref[rows, :] = dot(hidden_ref[rows, :], down_ref[...]).astype(BF16)
        tile_store(i, 0).start()
        return carry

    lax.fori_loop(0, tiles, forward_back, 0)
    parts = 4
    part = model_width // parts

    def part_columns(i):
        return pl.ds(pl.multiple_of(i * part, part), part)

    def down_grad(i, carry):
        grad = dot(hidden_ref[...], dy_ref[:, part_columns(i)], (0, 0))
        for e in range(here):
            down_stage[i, e] = grad[columns_of(e), :].astype(BF16)
        return carry

    def in_grad(i, carry):
        grad = dot(b_ref[:, part_columns(i)], back_ref[...], (0, 0))
        for e in range(here):
            gate_stage[i, e] = grad[:, columns_of(e)].astype(BF16)
            up_stage[i, e] = grad[:, columns_of(here + e)].astype(BF16)
        return carry

    stores = []

    def store(k, stage):
        copy = pltpu.make_async_copy(stage, grad_hbm[k], grad_sem.at[k])
        copy.start()
        stores.append(copy)

    lax.fori_loop(0, parts, down_grad, 0)
    store(2, down_stage)
    lax.fori_loop(0, parts, in_grad, 0)
    store(0, gate_stage)
    store(1, up_stage)
    for copy in stores:
        copy.wait()
    for i in range(tiles):
        for k in range(2):
            tile_store(i, k).wait()


def experts(place, b_all, dy_all, g_all, w_gate, w_up, w_down):
    sources, tokens, model_width = b_all.shape
    here, _, hidden_width = w_gate.shape
    rows_all = sources * tokens
    width = hidden_width
    part = model_width // 4
    tile = 256
    tiles = rows_all // tile
    in_stage, down_stage = (4, here, part, width), (4, here, width, part)
    shapes = [in_stage, in_stage, down_stage]
    flat = (rows_all, model_width)
    out = pl.pallas_call(
        functools.partial(experts_kernel, here, tile),
        out_shape=[
            jax.ShapeDtypeStruct(flat, BF16),
            jax.ShapeDtypeStruct(flat, BF16),
            jax.ShapeDtypeStruct((rows_all, LANES), F32),
        ]
        + [jax.ShapeDtypeStruct(shape, BF16) for shape in shapes],
        in_specs=[pl.BlockSpec(memory_space=pltpu.SMEM)] + anywhere(2) + in_vmem(1) + anywhere(3),
        out_specs=anywhere(2) + in_vmem(1) + anywhere(len(shapes)),
        scratch_shapes=[
            pltpu.VMEM(flat, BF16),
            pltpu.VMEM(flat, BF16),
            pltpu.VMEM((model_width, 2 * here * width), BF16),
            pltpu.VMEM((here * width, model_width), BF16),
            pltpu.VMEM((rows_all, here * width), BF16),
            pltpu.VMEM((rows_all, 2 * here * width), BF16),
            pltpu.VMEM(flat, BF16),
            pltpu.VMEM(flat, BF16),
            pltpu.VMEM(in_stage, BF16),
            pltpu.VMEM(in_stage, BF16),
            pltpu.VMEM(down_stage, BF16),
            pltpu.SemaphoreType.DMA((3 * here,)),
            pltpu.SemaphoreType.DMA((2, tiles)),
            pltpu.SemaphoreType.DMA((2, tiles)),
            pltpu.SemaphoreType.DMA((3,)),
        ],
        compiler_params=pltpu.CompilerParams(vmem_limit_bytes=VMEM_LIMIT),
        cost_estimate=pl.CostEstimate(
            flops=43_000_000_000, bytes_accessed=42_000_000, transcendentals=1_000_000
        ),
        name="experts",
    )(
        place, b_all.reshape(flat), dy_all.reshape(flat), g_all.reshape(rows_all, LANES),
        w_gate, w_up, w_down,
    )
    return [
        out[0].reshape(b_all.shape), out[1].reshape(b_all.shape),
        out[2].reshape(sources, tokens, LANES), *out[3:],
    ]


class Trade:
    def __init__(self, line, stages, nears, came, far, sems):
        self.beside, self.across = beside(line), pair_of(line)
        self.stages, self.nears, self.came, self.far, self.sems = stages, nears, came, far, sems

    def copies(self, e, hop):
        made = []
        for k in range(3):
            source = self.stages[k].at[e, (1, 0, 3)[hop]]
            target = (self.nears, self.came, self.far)[hop][k].at[e]
            peer = self.across if hop == 2 else self.beside
            made.append(
                push(source, target, self.sems.at[0, hop, k, e], self.sems.at[1, hop, k, e], "fsdp", peer)
            )
        return made

    def send(self, e, hop):
        for copy in self.copies(e, hop):
            copy.start()

    def cross(self, e):
        for k, copy in enumerate(self.copies(e, 0)):
            copy.wait_recv()
            self.stages[k][e, 3] = (
                self.stages[k][e, 3].astype(F32) + self.nears[k][e].astype(F32)
            ).astype(BF16)
        self.send(e, 2)

    def finish(self, count):
        for e in range(count):
            for hop in range(3):
                for copy in self.copies(e, hop):
                    copy.wait_send()
                    if hop:
                        copy.wait_recv()


def experts_back_kernel(
    here, tile, lane_of, query_width, router_at,
    b_hbm, dy_hbm, g_ref, gate_hbm, up_hbm, down_hbm,
    middle_ref, marked_ref, win_ref, wout_ref,
    out_hbm, dw_out, dl_out, grad_ref, gain_ref, *rest,
):
    kept_hbm, came_hbm, far_hbm, rest = rest[0:3], rest[3:6], rest[6:9], rest[9:]
    (
        b_ref, dy_ref, in_ref, down_ref, hidden_ref, back_ref, out_ref, db_ref, dg_ref,
        down_stage, gate_stage, up_stage, down_near, gate_near, up_near,
        dw_own, dl_own, db_total, dg_total, db_landed, dg_landed,
    ) = rest[:21]
    scratch, rest = rest[21:41], rest[41:]
    (
        weight_sem, tile_sem, out_sem, kept_sem, trade_sems, swap_sems,
        scatter_send, scatter_recv, own_sem, send_sem, recv_sem,
    ) = rest
    rows_all, model_width = b_ref.shape
    width = down_ref.shape[1]
    tiles = rows_all // tile
    tokens = middle_ref.shape[0]
    per_tile = tile // tokens
    plane, line = plane_neighbours(), lax.axis_index("fsdp")
    me = plane[0]
    first = me * here + lane_of
    high, low = line // 2, lax.rem(line, 2)
    span = pl.ds(pl.multiple_of(high * width, width), width)

    def weight_loads(e):
        pairs = (
            (gate_hbm.at[e, :, span], in_ref.at[e, :, pl.ds(0, width)]),
            (up_hbm.at[e, :, span], in_ref.at[e, :, pl.ds(width, width)]),
            (down_hbm.at[e, span, :], down_ref.at[e]),
        )
        return [
            pltpu.make_async_copy(source, target, weight_sem.at[e, i])
            for i, (source, target) in enumerate(pairs)
        ]

    def tile_rows(j):
        return pl.ds(pl.multiple_of(j * tile, tile), tile)

    def tile_loads(j):
        return [
            pltpu.make_async_copy(
                source.at[tile_rows(j)], target.at[tile_rows(j)], tile_sem.at[k, j]
            )
            for k, (source, target) in enumerate(((b_hbm, b_ref), (dy_hbm, dy_ref)))
        ]

    def tile_store(j):
        return pltpu.make_async_copy(
            out_ref.at[tile_rows(j)], out_hbm.at[tile_rows(j)], out_sem.at[j]
        )

    def place_of(i):
        return lax.rem(i + tiles // 2, tiles)

    def start_loads(i, carry):
        for load in tile_loads(place_of(i)):
            load.start()
        return carry

    start_loads(0, 0)
    for load in weight_loads(0):
        load.start()
    lax.fori_loop(1, tiles, start_loads, 0)
    for e in range(1, here):
        for load in weight_loads(e):
            load.start()
    meet(plane, line, 4, False)
    trade = Trade(
        line, (down_stage, gate_stage, up_stage), (down_near, gate_near, up_near),
        came_hbm, far_hbm, trade_sems,
    )
    sums = (scatter_send, scatter_recv)
    db_other = Scatter(plane, 0, db_ref, 8, scratch[:5], *sums)
    dg_other = Scatter(plane, 1, dg_ref, 8, scratch[5:10], *sums)
    db = Scatter(plane, 2, db_ref, 0, scratch[10:15], *sums)
    dg = Scatter(plane, 3, dg_ref, 0, scratch[15:20], *sums)
    swap_g = push(dg_total, dg_landed, swap_sems.at[0], swap_sems.at[1], "fsdp", pair_of(line))
    swap_b = push(db_total, db_landed, swap_sems.at[2], swap_sems.at[3], "fsdp", pair_of(line))
    half = tokens // 2
    part = model_width // 4

    def one_expert(e, carry):
        for load in weight_loads(e):
            load.wait()
        last = e == here - 1

        def forward_back(i, carry):
            j = place_of(i)
            rows = tile_rows(j)

            @pl.when(e == 0)
            def _():
                for load in tile_loads(j):
                    load.wait()

            pre = dot(b_ref[rows, :], in_ref[e])
            grad = dot(dy_ref[rows, :], down_ref[e], (1, 1))
            gates = g_ref[rows, :]
            mine = lax.broadcasted_iota(jnp.int32, gates.shape, 1) == first + e
            gate = jnp.sum(jnp.where(mine, jnp.maximum(gates, 0.0), 0.0), axis=1, keepdims=True)
            scale = RESIDUAL_SCALE * gate
            gate_pre, up_pre = pre[:, :width], pre[:, width:]
            sigmoid = 1.0 / (1.0 + jnp.exp(-gate_pre))
            silu = gate_pre * sigmoid
            hidden = silu * up_pre
            share = jnp.sum(hidden * grad, axis=1, keepdims=True)
            inner = jnp.where(mine, RESIDUAL_SCALE * share, 0.0)
            hidden_ref[rows, :] = (scale * hidden).astype(BF16)
            grad = scale * grad
            back_ref[rows, :width] = (
                grad * up_pre * sigmoid * (1.0 + gate_pre * (1.0 - sigmoid))
            ).astype(BF16)
            back_ref[rows, width:] = (grad * silu).astype(BF16)
            made = dot(hidden_ref[rows, :], down_ref[e])
            back = dot(back_ref[rows, :], in_ref[e], (1, 1))

            @pl.when(e == 0)
            def _():
                out_ref[rows, :] = made.astype(BF16)
                for t in range(per_tile):
                    piece = slice(t * tokens, (t + 1) * tokens)
                    db_ref[per_tile * j + t] = back[piece].astype(BF16)
                    dg_ref[per_tile * j + t] = inner[piece]

            @pl.when(e > 0)
            def _():
                out_ref[rows, :] = (out_ref[rows, :].astype(F32) + made).astype(BF16)
                for t in range(per_tile):
                    piece = slice(t * tokens, (t + 1) * tokens)
                    block = per_tile * j + t
                    db_ref[block] = (db_ref[block].astype(F32) + back[piece]).astype(BF16)
                    dg_ref[block] += inner[piece]

            @pl.when(last)
            def _():
                tile_store(j).start()

            @pl.when((e > 0) & (i == tiles - 3))
            def _():
                trade.cross(e - 1)

            @pl.when(last & (i == tiles // 2 - 1))
            def _():
                dg_other.begin()
                db_other.begin()

            @pl.when(last & (i == tiles - 2))
            def _():
                dg_other.first()
                db_other.first()

            return carry

        lax.fori_loop(0, tiles, forward_back, 0)

        @pl.when(last)
        def _():
            dg.begin()
            db.begin()
            dg_other.second()
            db_other.second()

        def weight_grads(p, carry):
            i = p + 1 - 2 * lax.rem(p, 2)
            parity = jnp.where(p < 2, 1 - low, low)
            side = jnp.where(lax.rem(i, 2) == 0, high, 1 - high)
            columns = pl.ds(pl.multiple_of((2 * side + parity) * part, part), part)
            down_stage[e, i] = dot(hidden_ref[...], dy_ref[:, columns], (0, 0)).astype(BF16)
            grad = dot(b_ref[:, columns], back_ref[...], (0, 0))
            gate_stage[e, i] = grad[:, :width].astype(BF16)
            up_stage[e, i] = grad[:, width:].astype(BF16)

            @pl.when(p == 0)
            def _():
                trade.send(e, 0)

            @pl.when(p == 1)
            def _():
                trade.send(e, 1)

            @pl.when(last & (p == 1))
            def _():
                for h in range(2):
                    rows = pl.ds(h * half, half)
                    dg_total[rows] = dg_other.total(h)
                    db_total[rows] = db_other.total(h).astype(BF16)
                swap_g.start()
                swap_b.start()

            @pl.when(last & (p == 2))
            def _():
                dg.first()
                db.first()

            return carry

        lax.fori_loop(0, 4, weight_grads, 0)
        return carry

    lax.fori_loop(0, here, one_expert, 0)
    stores = [
        pltpu.make_async_copy(stage.at[e, 2], kept_hbm[k].at[e], kept_sem.at[k, e])
        for k, stage in enumerate((down_stage, gate_stage, up_stage))
        for e in range(here)
    ]
    for store in stores:
        store.start()
    dg.second()
    db.second()
    trade.cross(here - 1)
    gain = wout_ref[query_width + 1 : query_width + 2, :].astype(F32)
    router = win_ref[:, router_at : router_at + LANES]
    gain_grad = jnp.zeros((1, model_width), F32)
    sums_g = [dg.total(h) for h in range(2)]
    swap_g.wait_recv()
    swap_b.wait_recv()
    for h in range(2):
        rows = pl.ds(h * half, half)
        gates = jnp.maximum(marked_ref[rows], 0.0)
        grad_gates = sums_g[h] + dg_landed[rows]
        grad_chosen = gates * (
            grad_gates - jnp.sum(gates * grad_gates, axis=1, keepdims=True)
        )
        grad_logits = grad_chosen.astype(BF16)
        dl_own[rows] = grad_logits
        grad_b = dot(grad_logits, router, (1, 1)) + db.total(h) + db_landed[rows].astype(F32)
        middle = middle_ref[rows]
        inverse = lax.rsqrt(jnp.mean(middle * middle, axis=1, keepdims=True) + EPSILON)
        normed = middle * inverse
        gain_grad += jnp.sum(grad_b * normed, axis=0, keepdims=True)
        own = pl.ds(pl.multiple_of(me * tokens + h * half, half), half)
        grad = dy_ref[own].astype(F32) + norm_back(grad_b * gain, normed, inverse)
        grad_ref[rows] = grad
        dw_own[rows] = (RESIDUAL_SCALE * grad).astype(BF16)
    gain_ref[...] = jnp.broadcast_to(gain_grad, gain_ref.shape)
    gathers = (own_sem, send_sem, recv_sem)
    dw = Gather(plane, 0, dw_own, dw_out, 0, *gathers)
    dl = Gather(plane, 1, dl_own, dl_out, 0, *gathers)
    dw.begin()
    dl.begin()
    dw.relay()
    dl.relay()
    dw.relay_diagonal()
    dl.relay_diagonal()
    for item in (dg_other, db_other, dg, db, dw, dl):
        item.finish()
    swap_b.wait_send()
    swap_g.wait_send()
    for store in stores:
        store.wait()
    for j in range(tiles):
        tile_store(j).wait()
    trade.finish(here)


def experts_back(
    b_all, dy_all, g_all, w_gate, w_up, w_down, middle, marked, w_in, w_out,
    lane_of, query_width, router_at, collective_id,
):
    sources, tokens, model_width = b_all.shape
    here, _, hidden_width = w_gate.shape
    rows_all = sources * tokens
    width, part, tile = hidden_width // 2, model_width // 4, 256
    tiles = rows_all // tile
    flat, wide, narrow = (rows_all, model_width), (tokens, model_width), (tokens, LANES)
    slices = [(width, part), (part, width), (part, width)]
    out = pl.pallas_call(
        functools.partial(experts_back_kernel, here, tile, lane_of, query_width, router_at),
        out_shape=[
            jax.ShapeDtypeStruct(flat, BF16),
            jax.ShapeDtypeStruct((8,) + wide, BF16),
            jax.ShapeDtypeStruct((8,) + narrow, BF16),
            jax.ShapeDtypeStruct(wide, F32),
            jax.ShapeDtypeStruct((8, model_width), F32),
        ]
        + [jax.ShapeDtypeStruct((here,) + shape, BF16) for shape in slices * 3],
        in_specs=anywhere(2) + in_vmem(1) + anywhere(3) + in_vmem(4),
        out_specs=anywhere(3) + in_vmem(2) + anywhere(9),
        scratch_shapes=[
            pltpu.VMEM(flat, BF16),
            pltpu.VMEM(flat, BF16),
            pltpu.VMEM((here, model_width, 2 * width), BF16),
            pltpu.VMEM((here, width, model_width), BF16),
            pltpu.VMEM((rows_all, width), BF16),
            pltpu.VMEM((rows_all, 2 * width), BF16),
            pltpu.VMEM(flat, BF16),
            pltpu.VMEM((sources,) + wide, BF16),
            pltpu.VMEM((sources,) + narrow, F32),
        ]
        + [pltpu.VMEM((here, 4) + shape, BF16) for shape in slices]
        + [pltpu.VMEM((here,) + shape, BF16) for shape in slices]
        + [
            pltpu.VMEM(wide, BF16),
            pltpu.VMEM(narrow, BF16),
            pltpu.VMEM(wide, BF16),
            pltpu.VMEM(narrow, F32),
            pltpu.VMEM(wide, BF16),
            pltpu.VMEM(narrow, F32),
        ]
        + (scatter_scratch(*wide, BF16, True) + scatter_scratch(*narrow, F32, True)) * 2
        + [
            pltpu.SemaphoreType.DMA((here, 3)),
            pltpu.SemaphoreType.DMA((2, tiles)),
            pltpu.SemaphoreType.DMA((tiles,)),
            pltpu.SemaphoreType.DMA((3, here)),
            pltpu.SemaphoreType.DMA((2, 3, 3, here)),
            pltpu.SemaphoreType.DMA((4,)),
        ]
        + scatter_sems(4)
        + gather_sems(2),
        compiler_params=pltpu.CompilerParams(
            collective_id=collective_id, has_side_effects=True, vmem_limit_bytes=67_000_000
        ),
        cost_estimate=pl.CostEstimate(
            flops=43_000_000_000, bytes_accessed=42_000_000, transcendentals=1_000_000
        ),
        name="experts_back",
    )(
        b_all.reshape(flat), dy_all.reshape(flat), g_all.reshape(rows_all, LANES),
        w_gate, w_up, w_down, middle, marked, w_in, w_out,
    )
    return [out[0].reshape(b_all.shape), *out[1:5], out[5:8], out[8:11], out[11:14]]


def rotary_tables(length):
    lane = lax.broadcasted_iota(jnp.int32, (length, LANES), 1) % HEAD_DIM
    half = HEAD_DIM // 2
    exponent = (lane % half).astype(F32) * (2.0 / HEAD_DIM)
    position = lax.broadcasted_iota(jnp.int32, (length, LANES), 0).astype(F32)
    angles = position * jnp.power(ROPE_BASE, -exponent)
    return jnp.cos(angles), jnp.where(lane < half, -jnp.sin(angles), jnp.sin(angles))


def join_halves(kept, came, far, line, axis):
    upper = line >= 2
    near, far = kept.astype(F32) + came.astype(F32), far.astype(F32)
    return jnp.concatenate(
        [jnp.where(upper, far, near), jnp.where(upper, near, far)], axis=axis
    )


def per_device(
    residual_in, cotangent, gain_attn, w_query, w_key, w_value, w_out, gain_ffn, w_router,
    w_gate, w_up, w_down, route_ids,
):
    me = lax.axis_index("expert")
    line = lax.axis_index("fsdp")
    peers = lax.axis_size("expert")
    lines = lax.axis_size("fsdp")
    tokens, model_width = residual_in.shape[1:]
    length = tokens * peers
    groups = w_key.shape[1] // HEAD_DIM
    per_group = w_query.shape[1] // w_key.shape[1]
    query_width = per_group * HEAD_DIM
    experts_all = w_router.shape[1]
    here = w_gate.shape[0]
    shard = w_query.shape[0]
    turned = query_width + HEAD_DIM
    router_at = turned
    lane_of = HEAD_DIM
    in_width = turned + LANES
    paired = lines == 4 and peers == 8

    w_in_shard = jnp.concatenate(
        [
            lax.dynamic_slice(w_query, (0, me * query_width), (shard, query_width)),
            lax.dynamic_slice(w_key, (0, me * HEAD_DIM), (shard, HEAD_DIM)),
            lax.dynamic_slice(w_value, (0, me * HEAD_DIM), (shard, HEAD_DIM)),
            w_router,
            jnp.zeros((shard, in_width - turned - HEAD_DIM - experts_all), BF16),
        ],
        axis=1,
    )
    w_out_shard = jnp.concatenate(
        [
            lax.dynamic_slice(w_out, (me * query_width, 0), (query_width, shard)),
            gain_attn[None],
            gain_ffn[None],
            jnp.zeros((14, shard), BF16),
        ],
        axis=0,
    )
    chosen = jnp.any(
        route_ids[0][:, :, None]
        == jnp.arange(LANES, dtype=jnp.int32)[None, None, :] - lane_of,
        axis=1,
    ).astype(F32)
    cosine, sine = rotary_tables(length)
    place = jnp.full((1,), me * here + lane_of, jnp.int32)
    own_rows, own_grad = residual_in[0], cotangent[0]
    wide = (peers, tokens, model_width)

    if paired:
        x_all, dy_all, w_in, w_out_rows = open_transfers(
            own_rows, own_grad, w_in_shard, w_out_shard, lines, 0
        )
    else:
        x_all, dy_all = plane_gather([own_rows, own_grad], 0)
        w_in, w_out_rows = (
            lax.all_gather(w_in_shard, "fsdp", axis=0, tiled=True),
            lax.all_gather(w_out_shard, "fsdp", axis=1, tiled=True),
        )
    part, *saved = attend(
        x_all.reshape(length, model_width), w_in, w_out_rows, cosine, sine, per_group
    )
    if paired:
        b_all, g_all, middle, marked = middle_transfers(
            part.reshape(wide), own_rows, w_in, w_out_rows, chosen, query_width, router_at, 1
        )
        sum_part, dw_all, dl_all, grad_middle, gain_two_grad, kept, came, far = experts_back(
            b_all, dy_all, g_all, w_gate, w_up, w_down, middle, marked, w_in, w_out_rows,
            lane_of, query_width, router_at, 2,
        )
        da_part, grad_in, grad_out = attend_back(
            dw_all.reshape(length, model_width), w_in, w_out_rows, cosine, sine, saved,
            b_all.reshape(2 * length, model_width), dl_all.reshape(length, LANES), per_group,
        )
        outcome, grad_input, in_all, out_all, gains_all, notes_all = close_transfers(
            da_part.reshape(wide), sum_part, own_rows, middle, grad_middle, gain_two_grad,
            w_out_rows, grad_in.reshape(lines, shard, in_width), grad_out, query_width, 3,
        )
        squares = jnp.sum(notes_all, axis=0)[:5, 0]
        down, gate, up = (
            join_halves(*slices, line, axis)
            for *slices, axis in zip(kept, came, far, (1, 2, 2))
        )
        reduced = [gate, up, down]
        gain_rows = jnp.sum(gains_all[:, :2].astype(F32), axis=0)
    else:
        (branch,) = plane_scatter([part.reshape(wide)], 1)
        gain_one = w_out_rows[query_width][None].astype(F32)
        gain_two = w_out_rows[query_width + 1][None].astype(F32)
        router = w_in[:, router_at:]
        rows = own_rows.astype(F32)
        inverse_one = lax.rsqrt(jnp.mean(rows * rows, axis=-1, keepdims=True) + EPSILON)
        normed_one = rows * inverse_one
        middle = rows + RESIDUAL_SCALE * branch
        inverse_two = lax.rsqrt(jnp.mean(middle * middle, axis=-1, keepdims=True) + EPSILON)
        normed_two = middle * inverse_two
        routed = (normed_two * gain_two).astype(BF16)
        logits = jnp.where(chosen > 0, dot(routed, router), -1e30)
        lifted = jnp.exp(logits - jnp.max(logits, axis=-1, keepdims=True))
        lifted = jnp.where(chosen > 0, lifted, 0.0)
        gates = lifted / jnp.sum(lifted, axis=-1, keepdims=True)
        b_all, g_all = plane_gather([routed, jnp.where(chosen > 0, gates, -1.0)], 2)
        sum_part, db_part, dg_part, *grads = experts(
            place, b_all, dy_all, g_all, w_gate, w_up, w_down
        )
        db_sum, dg_sum = plane_scatter([db_part, dg_part], 3)
        grad_rows = own_grad.astype(F32)
        grad_chosen = gates * (dg_sum - jnp.sum(gates * dg_sum, axis=-1, keepdims=True))
        grad_logits = grad_chosen.astype(BF16)
        grad_routed = dot(grad_logits, router, (1, 1)) + db_sum
        grad_gain_two = jnp.sum(grad_routed * normed_two, axis=0)
        grad_middle = grad_rows + norm_back(grad_routed * gain_two, normed_two, inverse_two)
        grad_branch = (RESIDUAL_SCALE * grad_middle).astype(BF16)
        dw_all, dl_all = plane_gather([grad_branch, grad_logits], 4)
        da_part, grad_in, grad_out = attend_back(
            dw_all.reshape(length, model_width), w_in, w_out_rows, cosine, sine, saved,
            b_all.reshape(length, model_width), dl_all.reshape(length, LANES), per_group,
        )
        da_sum, expert_sum = plane_scatter([da_part.reshape(wide), sum_part], 5)
        outcome = middle + expert_sum
        grad_gain_one = jnp.sum(da_sum * normed_one, axis=0)
        grad_input = grad_middle + norm_back(da_sum * gain_one, normed_one, inverse_one)
        squares = lax.psum(
            jnp.stack(
                [jnp.sum(v * v) for v in (rows, middle, outcome, grad_middle, grad_input)]
            ),
            ("fsdp", "expert"),
        )
        in_sum = lax.psum_scatter(grad_in, "fsdp", scatter_dimension=0, tiled=True)
        out_sum = lax.psum_scatter(
            grad_out.transpose(1, 0, 2).reshape(query_width, model_width), "fsdp",
            scatter_dimension=1, tiled=True,
        )
        gain_rows = lax.psum_scatter(
            lax.psum(jnp.stack([grad_gain_one, grad_gain_two]), "expert"),
            "fsdp", scatter_dimension=1, tiled=True,
        )
        in_all = lax.all_gather(in_sum, "expert", axis=0)
        out_all = lax.all_gather(out_sum, "expert", axis=0)
        outcome, grad_input = outcome.astype(BF16), grad_input.astype(BF16)
        grads = [
            grads[0].transpose(1, 0, 2, 3).reshape(w_gate.shape),
            grads[1].transpose(1, 0, 2, 3).reshape(w_up.shape),
            grads[2].transpose(1, 2, 0, 3).reshape(w_down.shape),
        ]
        reduced = [
            lax.psum_scatter(array, "fsdp", scatter_dimension=axis, tiled=True).astype(F32)
            for array, axis in zip(grads, (1, 1, 2))
        ]

    def columns_of(start, stop):
        return in_all[:, :, start:stop].transpose(1, 0, 2).reshape(shard, -1).astype(F32)

    root_means = jnp.sqrt(squares / (tokens * model_width * lines * peers))
    return (
        outcome[None],
        grad_input[None],
        gain_rows[0],
        columns_of(0, query_width),
        columns_of(query_width, turned),
        columns_of(turned, turned + HEAD_DIM),
        out_all.reshape(groups * query_width, shard).astype(F32),
        gain_rows[1],
        in_all[0, :, turned + HEAD_DIM : turned + HEAD_DIM + experts_all].astype(F32),
        reduced[0],
        reduced[1],
        reduced[2],
        root_means,
    )


def solution(mesh):
    in_specs = (
        P("fsdp", "expert", None),
        P("fsdp", "expert", None),
        P("fsdp"),
        P("fsdp", None),
        P("fsdp", None),
        P("fsdp", None),
        P(None, "fsdp"),
        P("fsdp"),
        P("fsdp", None),
        P("expert", None, None),
        P("expert", None, None),
        P("expert", None, None),
        P("fsdp", "expert", None),
    )
    out_specs = (
        P("fsdp", "expert", None),
        P("fsdp", "expert", None),
        P("fsdp"),
        P("fsdp", None),
        P("fsdp", None),
        P("fsdp", None),
        P(None, "fsdp"),
        P("fsdp"),
        P("fsdp", None),
        P("expert", "fsdp", None),
        P("expert", "fsdp", None),
        P("expert", None, "fsdp"),
        P(),
    )
    return jax.shard_map(
        per_device, mesh=mesh, in_specs=in_specs, out_specs=out_specs, check_vma=False
    )
```

```python
import functools

import jax
import jax.numpy as jnp
from jax import lax
from jax.experimental import pallas as pl
from jax.experimental.pallas import tpu as pltpu
from jax.sharding import PartitionSpec as P

HEAD_DIM = 64
BLOCK = 256

EPSILON = 1e-06
RESIDUAL_SCALE = 0.22
ATTENTION_SCALE = 0.015625
ROPE_BASE = 10000.0
HIGHEST = lax.Precision.HIGHEST
MESH = pl.DeviceIdType.MESH
VMEM_LIMIT = 63_000_000
F32 = jnp.float32
BF16 = jnp.bfloat16
LANES = 128


def plane_neighbours():
    me = lax.axis_index("expert")
    core = lax.rem(me, 2)
    x_bit = lax.rem(me // 2, 2)
    y_bit = me // 4
    sibling = me + 1 - 2 * core
    x_peer = me + 2 - 4 * x_bit
    y_peer = me + 4 - 8 * y_bit
    diagonal = x_peer + 4 - 8 * y_bit
    return me, core, x_bit, y_bit, sibling, x_peer, y_peer, diagonal


def greet(axis, peers):
    barrier = pltpu.get_barrier_semaphore()
    for peer in peers:
        pl.semaphore_signal(barrier, inc=1, device_id={axis: peer}, device_id_type=MESH)
    pl.semaphore_wait(barrier, len(peers))


def gather_kernel(count, *refs):
    ins, outs = refs[:count], refs[count : 2 * count]
    own_sem, send_sem, recv_sem = refs[2 * count :]
    me, _, _, _, sibling, x_peer, y_peer, diagonal = plane_neighbours()
    greet("expert", (sibling, x_peer, y_peer))

    def remote(k, slot, source, target, peer):
        return pltpu.make_async_remote_copy(
            src_ref=source,
            dst_ref=target,
            send_sem=send_sem.at[k, slot],
            recv_sem=recv_sem.at[k, slot],
            device_id={"expert": peer},
            device_id_type=MESH,
        )

    plans = []
    for k in range(count):
        half = ins[k].shape[0] // 2
        parts = (pl.ds(0, half), pl.ds(half, half))
        out = outs[k]
        own = pltpu.make_async_copy(ins[k], out.at[me], own_sem.at[k])
        copies = [remote(k, 0, ins[k], out.at[me], sibling)]
        for h in range(2):
            copies.append(remote(k, 1 + h, ins[k].at[parts[h]], out.at[me, parts[h]], x_peer))
        for h in range(2):
            copies.append(remote(k, 3 + h, ins[k].at[parts[h]], out.at[me, parts[h]], y_peer))

        def forward(slot, block, h, peer):
            return remote(k, slot, out.at[block, parts[h]], out.at[block, parts[h]], peer)

        copies.append(forward(5, y_peer, 0, x_peer))
        copies.append(forward(6, x_peer, 1, y_peer))
        for h in range(2):
            copies.append(forward(7 + h, x_peer, h, sibling))
        for h in range(2):
            copies.append(forward(9 + h, y_peer, h, sibling))
        for h in range(2):
            copies.append(forward(11 + h, diagonal, h, sibling))
        plans.append((own, copies))
    for own, copies in plans:
        for slot in (3, 2, 1, 4, 0):
            copies[slot].start()
        own.start()
    for own, copies in plans:
        copies[3].wait_recv()
        copies[5].start()
        copies[2].wait_recv()
        copies[6].start()
        copies[9].start()
        copies[8].start()
        copies[1].wait_recv()
        copies[7].start()
        copies[4].wait_recv()
        copies[10].start()
    for own, copies in plans:
        copies[5].wait_recv()
        copies[11].start()
        copies[6].wait_recv()
        copies[12].start()
    for own, copies in plans:
        for slot in (0, 7, 8, 9, 10, 11, 12):
            copies[slot].wait_recv()
        for copy in copies:
            copy.wait_send()
        own.wait()


def plane_gather(arrays, collective_id):
    if lax.axis_size("expert") != 8:
        return [lax.all_gather(array, "expert", axis=0) for array in arrays]
    count = len(arrays)
    size = sum(array.size * array.dtype.itemsize for array in arrays)
    return pl.pallas_call(
        functools.partial(gather_kernel, count),
        out_shape=[jax.ShapeDtypeStruct((8,) + array.shape, array.dtype) for array in arrays],
        in_specs=[pl.BlockSpec(memory_space=pltpu.VMEM)] * count,
        out_specs=[pl.BlockSpec(memory_space=pl.ANY)] * count,
        scratch_shapes=[
            pltpu.SemaphoreType.DMA((count,)),
            pltpu.SemaphoreType.DMA((count, 13)),
            pltpu.SemaphoreType.DMA((count, 13)),
        ],
        compiler_params=pltpu.CompilerParams(
            collective_id=collective_id, has_side_effects=True, vmem_limit_bytes=VMEM_LIMIT
        ),
        cost_estimate=pl.CostEstimate(flops=0, bytes_accessed=16 * size, transcendentals=0),
        name="plane_gather",
    )(*arrays)


def scatter_kernel(count, *refs):
    ins, outs = refs[:count], refs[count : 2 * count]
    scratch = refs[2 * count : 2 * count + 6 * count]
    send_sem, recv_sem = refs[8 * count :]
    me, core, x_bit, y_bit, sibling, x_peer, y_peer, diagonal = plane_neighbours()
    greet("expert", (sibling, x_peer, y_peer))
    chip = me // 2
    chip_x, chip_y, chip_d = x_peer // 2, y_peer // 2, diagonal // 2
    order = (chip_d, chip_x, chip_y, chip)

    def remote(k, slot, source, target, peer):
        return pltpu.make_async_remote_copy(
            src_ref=source,
            dst_ref=target,
            send_sem=send_sem.at[k, slot],
            recv_sem=recv_sem.at[k, slot],
            device_id={"expert": peer},
            device_id_type=MESH,
        )

    stage0 = []
    for k in range(count):
        pair = scratch[6 * k]
        copies = [
            remote(k, i, ins[k].at[2 * order[i] + 1 - core], pair.at[i], sibling) for i in range(4)
        ]
        stage0.append(copies)
        for copy in copies:
            copy.start()
    later = []
    for k in range(count):
        pair, sums, first_x, first_y, second_x, second_y = scratch[6 * k : 6 * k + 6]
        rows = ins[k].shape[1]
        half = rows // 2
        parts = (pl.ds(0, half), pl.ds(half, half))
        dtype = ins[k].dtype

        def join(i):
            stage0[k][i].wait_recv()
            sums[i] = (ins[k][2 * order[i] + core].astype(F32) + pair[i].astype(F32)).astype(dtype)

        join(0)
        copies = [
            remote(k, 4, sums.at[0, parts[0]], first_x.at[1], x_peer),
            remote(k, 5, sums.at[0, parts[1]], first_y.at[1], y_peer),
        ]
        for copy in copies:
            copy.start()
        join(1)
        copies.append(remote(k, 6, sums.at[1, parts[0]], first_x.at[0], x_peer))
        copies[-1].start()
        join(2)
        copies.append(remote(k, 7, sums.at[2, parts[1]], first_y.at[0], y_peer))
        copies[-1].start()
        join(3)
        later.append(copies)
    for k in range(count):
        pair, sums, first_x, first_y, second_x, second_y = scratch[6 * k : 6 * k + 6]
        half = ins[k].shape[1] // 2
        parts = (pl.ds(0, half), pl.ds(half, half))
        dtype = ins[k].dtype
        copies = later[k]
        copies[0].wait_recv()
        pair[0, parts[0]] = (
            sums[2, parts[0]].astype(F32) + first_x[1].astype(F32)
        ).astype(dtype)
        copies.append(remote(k, 8, pair.at[0, parts[0]], second_y, y_peer))
        copies[-1].start()
        copies[1].wait_recv()
        pair[0, parts[1]] = (
            sums[1, parts[1]].astype(F32) + first_y[1].astype(F32)
        ).astype(dtype)
        copies.append(remote(k, 9, pair.at[0, parts[1]], second_x, x_peer))
        copies[-1].start()
    for k in range(count):
        pair, sums, first_x, first_y, second_x, second_y = scratch[6 * k : 6 * k + 6]
        half = ins[k].shape[1] // 2
        parts = (pl.ds(0, half), pl.ds(half, half))
        copies = later[k]
        copies[2].wait_recv()
        copies[4].wait_recv()
        outs[k][parts[0]] = (
            sums[3, parts[0]].astype(F32) + first_x[0].astype(F32) + second_y[...].astype(F32)
        )
        copies[3].wait_recv()
        copies[5].wait_recv()
        outs[k][parts[1]] = (
            sums[3, parts[1]].astype(F32) + first_y[0].astype(F32) + second_x[...].astype(F32)
        )
        for copy in stage0[k] + copies:
            copy.wait_send()


def plane_scatter(arrays, collective_id):
    if lax.axis_size("expert") != 8:
        return [
            lax.psum_scatter(array, "expert", scatter_dimension=0, tiled=False).astype(F32)
            for array in arrays
        ]
    count = len(arrays)
    scratch = []
    for array in arrays:
        _, rows, columns = array.shape
        half = rows // 2
        for shape in (
            (4, rows, columns),
            (4, rows, columns),
            (2, half, columns),
            (2, half, columns),
            (half, columns),
            (half, columns),
        ):
            scratch.append(pltpu.VMEM(shape, array.dtype))
    size = sum(array.size * array.dtype.itemsize for array in arrays)
    return pl.pallas_call(
        functools.partial(scatter_kernel, count),
        out_shape=[jax.ShapeDtypeStruct(array.shape[1:], F32) for array in arrays],
        in_specs=[pl.BlockSpec(memory_space=pltpu.VMEM)] * count,
        out_specs=[pl.BlockSpec(memory_space=pltpu.VMEM)] * count,
        scratch_shapes=scratch
        + [pltpu.SemaphoreType.DMA((count, 10)), pltpu.SemaphoreType.DMA((count, 10))],
        compiler_params=pltpu.CompilerParams(
            collective_id=collective_id, has_side_effects=True, vmem_limit_bytes=VMEM_LIMIT
        ),
        cost_estimate=pl.CostEstimate(flops=0, bytes_accessed=3 * size, transcendentals=0),
        name="plane_scatter",
    )(*arrays)


def push(source, target, send_sem, recv_sem, axis, peer):
    return pltpu.make_async_remote_copy(
        src_ref=source,
        dst_ref=target,
        send_sem=send_sem,
        recv_sem=recv_sem,
        device_id={axis: peer},
        device_id_type=MESH,
    )


def meet(plane, line, size, with_line):
    barrier = pltpu.get_barrier_semaphore()
    me, _, _, _, sibling, x_peer, y_peer, _ = plane
    for peer in (sibling, x_peer, y_peer):
        pl.semaphore_signal(barrier, inc=1, device_id={"expert": peer}, device_id_type=MESH)
    pl.semaphore_signal(
        barrier, inc=1, device_id={"fsdp": pair_of(line)}, device_id_type=MESH
    )
    if not with_line:
        pl.semaphore_signal(
            barrier, inc=1, device_id={"fsdp": beside(line)}, device_id_type=MESH
        )
        pl.semaphore_wait(barrier, 5)
        return

    @pl.when(line > 0)
    def _():
        pl.semaphore_signal(barrier, inc=1, device_id={"fsdp": line - 1}, device_id_type=MESH)

    @pl.when(line < size - 1)
    def _():
        pl.semaphore_signal(barrier, inc=1, device_id={"fsdp": line + 1}, device_id_type=MESH)

    @pl.when((line > 0) & (line < size - 1))
    def _():
        pl.semaphore_wait(barrier, 6)

    @pl.when((line == 0) | (line == size - 1))
    def _():
        pl.semaphore_wait(barrier, 5)


def pair_of(line):
    return line + 2 - 4 * (line // 2)


def beside(line):
    return line + 1 - 2 * lax.rem(line, 2)


def norm_back(grad_normed, normed, inverse):
    return inverse * (grad_normed - normed * jnp.mean(grad_normed * normed, axis=-1, keepdims=True))


class Gather:
    def __init__(self, plane, k, source, out, base, own_sem, send_sem, recv_sem):
        me, _, _, _, sibling, x_peer, y_peer, diagonal = plane
        half = source.shape[0] // 2
        parts = (pl.ds(0, half), pl.ds(half, half))

        def copy(slot, src, dst, peer):
            return push(src, dst, send_sem.at[k, slot], recv_sem.at[k, slot], "expert", peer)

        def forward(slot, block, h, peer):
            ref = out.at[base + block, parts[h]]
            return copy(slot, ref, ref, peer)

        self.own = pltpu.make_async_copy(source, out.at[base + me], own_sem.at[k])
        copies = [copy(0, source, out.at[base + me], sibling)]
        for slot, peer in ((1, x_peer), (3, y_peer)):
            for h in range(2):
                copies.append(
                    copy(slot + h, source.at[parts[h]], out.at[base + me, parts[h]], peer)
                )
        copies.append(forward(5, y_peer, 0, x_peer))
        copies.append(forward(6, x_peer, 1, y_peer))
        for slot, block in ((7, x_peer), (9, y_peer), (11, diagonal)):
            for h in range(2):
                copies.append(forward(slot + h, block, h, sibling))
        self.copies = copies

    def begin(self):
        for slot in (3, 2, 1, 4, 0):
            self.copies[slot].start()
        self.own.start()

    def relay(self):
        copies = self.copies
        for landed, onward in ((3, (5, 9)), (2, (6, 8)), (1, (7,)), (4, (10,))):
            copies[landed].wait_recv()
            for slot in onward:
                copies[slot].start()

    def relay_diagonal(self):
        for landed, onward in ((5, 11), (6, 12)):
            self.copies[landed].wait_recv()
            self.copies[onward].start()

    def finish(self):
        for slot in (0, 7, 8, 9, 10, 11, 12):
            self.copies[slot].wait_recv()
        for copy in self.copies:
            copy.wait_send()
        self.own.wait()


def gather_sems(count):
    return [
        pltpu.SemaphoreType.DMA((count,)),
        pltpu.SemaphoreType.DMA((count, 13)),
        pltpu.SemaphoreType.DMA((count, 13)),
    ]


class Scatter:
    def __init__(self, plane, k, source, base, scratch, send_sem, recv_sem):
        me, core, _, _, sibling, x_peer, y_peer, diagonal = plane
        self.source, self.base, self.core = source, base, core
        self.pair, self.first_x, self.first_y, self.second_x, self.second_y = scratch[:5]
        self.order = (diagonal // 2, x_peer // 2, y_peer // 2, me // 2)
        self.sums = [
            scratch[5].at[i] if len(scratch) > 5 else source.at[base + 2 * self.order[i] + core]
            for i in range(4)
        ]
        self.dtype = source.dtype
        half = source.shape[1] // 2
        self.parts = parts = (pl.ds(0, half), pl.ds(half, half))

        def copy(slot, src, dst, peer):
            return push(src, dst, send_sem.at[k, slot], recv_sem.at[k, slot], "expert", peer)

        self.stage0 = [
            copy(i, source.at[base + 2 * self.order[i] + 1 - core], self.pair.at[i], sibling)
            for i in range(4)
        ]
        self.stage1 = [
            copy(4, self.sums[0].at[parts[0]], self.first_x.at[1], x_peer),
            copy(5, self.sums[0].at[parts[1]], self.first_y.at[1], y_peer),
            copy(6, self.sums[1].at[parts[0]], self.first_x.at[0], x_peer),
            copy(7, self.sums[2].at[parts[1]], self.first_y.at[0], y_peer),
        ]
        self.stage2 = [
            copy(8, self.pair.at[0, parts[0]], self.second_y, y_peer),
            copy(9, self.pair.at[0, parts[1]], self.second_x, x_peer),
        ]

    def begin(self):
        for copy in self.stage0:
            copy.start()

    def join(self, i):
        self.stage0[i].wait_recv()
        mine = self.source[self.base + 2 * self.order[i] + self.core]
        self.sums[i][...] = (mine.astype(F32) + self.pair[i].astype(F32)).astype(self.dtype)

    def first(self):
        self.join(0)
        self.stage1[0].start()
        self.stage1[1].start()
        self.join(1)
        self.stage1[2].start()
        self.join(2)
        self.stage1[3].start()
        self.join(3)

    def second(self):
        for h, block, landed in ((0, 2, self.first_x), (1, 1, self.first_y)):
            self.stage1[h].wait_recv()
            rows = self.parts[h]
            self.pair[0, rows] = (
                self.sums[block][rows].astype(F32) + landed[1].astype(F32)
            ).astype(self.dtype)
            self.stage2[h].start()

    def total(self, h):
        self.stage1[2 + h].wait_recv()
        self.stage2[h].wait_recv()
        near, far = ((self.first_x, self.second_y), (self.first_y, self.second_x))[h]
        return (
            self.sums[3][self.parts[h]].astype(F32)
            + near[0].astype(F32)
            + far[...].astype(F32)
        )

    def finish(self):
        for copy in self.stage0 + self.stage1 + self.stage2:
            copy.wait_send()


def scatter_scratch(rows, columns, dtype, in_place=False):
    half = rows // 2
    shapes = [
        (4, rows, columns),
        (2, half, columns),
        (2, half, columns),
        (half, columns),
        (half, columns),
        (4, rows, columns),
    ]
    return [pltpu.VMEM(shape, dtype) for shape in shapes[: 5 if in_place else 6]]


def scatter_sems(count):
    return [pltpu.SemaphoreType.DMA((count, 10)), pltpu.SemaphoreType.DMA((count, 10))]


class LineGather:
    def __init__(self, line, size, k, source, out, axis, own_sem, send_sem, recv_sem):
        self.line, self.size, self.k, self.source, self.out = line, size, k, source, out
        self.axis, self.send_sem, self.recv_sem = axis, send_sem, recv_sem
        self.own = pltpu.make_async_copy(source, self.place(line), own_sem.at[k])

    def place(self, owner):
        extent = self.source.shape[self.axis]
        span = pl.ds(pl.multiple_of(owner * extent, extent), extent)
        return self.out.at[span] if self.axis == 0 else self.out.at[:, span]

    def hop(self, side, step, owner, source=None):
        target = self.place(owner)
        return push(
            target if source is None else source,
            target,
            self.send_sem.at[self.k, side, step],
            self.recv_sem.at[self.k, side, step],
            "fsdp",
            self.line + 1 - 2 * side,
        )

    def begin(self):
        for side, there in ((0, self.line < self.size - 1), (1, self.line > 0)):

            @pl.when(there)
            def _():
                self.hop(side, 0, self.line, self.source).start()

        self.own.start()

    def step(self, step):
        line, last = self.line, self.size - 1
        for side, owner in ((0, line - 1 - step), (1, line + 1 + step)):

            @pl.when((owner >= 0) & (owner <= last))
            def _():
                self.hop(side, step, owner).wait_recv()

                @pl.when((line < last) if side == 0 else (line > 0))
                def _():
                    self.hop(side, step + 1, owner).start()

    def finish(self):
        line, last = self.line, self.size - 1
        self.own.wait()
        for step in range(self.size - 1):
            for side, owner, there in ((0, line - step, line < last), (1, line + step, line > 0)):

                @pl.when(there & (owner >= 0) & (owner <= last))
                def _():
                    self.hop(side, step, owner).wait_send()


def line_gather_sems(count, size):
    return [
        pltpu.SemaphoreType.DMA((count,)),
        pltpu.SemaphoreType.DMA((count, 2, size)),
        pltpu.SemaphoreType.DMA((count, 2, size)),
    ]


class LineScatter:
    def __init__(self, line, size, k, source, sums, landed, send_sem, recv_sem):
        self.line, self.size, self.k = line, size, k
        self.source, self.sums, self.landed = source, sums, landed
        self.send_sem, self.recv_sem = send_sem, recv_sem

    def hop(self, side, owner):
        return push(
            self.sums.at[side, owner],
            self.landed.at[side, owner],
            self.send_sem.at[self.k, side, owner],
            self.recv_sem.at[self.k, side, owner],
            "fsdp",
            self.line + 1 - 2 * side,
        )

    def begin(self):
        last = self.size - 1
        for far in range(last):
            for side, owner, end in ((0, last - far, 0), (1, far, last)):

                @pl.when(self.line == end)
                def _():
                    self.sums[side, owner] = self.source[owner]
                    self.hop(side, owner).start()

    def pass_on(self, side, owner):
        self.hop(side, owner).wait_recv()
        self.sums[side, owner] = (
            self.source[owner].astype(F32) + self.landed[side, owner].astype(F32)
        ).astype(self.source.dtype)
        self.hop(side, owner).start()

    def step(self, far):
        line, last = self.line, self.size - 1

        @pl.when((line < last - far) & (line > 0))
        def _():
            self.pass_on(0, last - far)

        @pl.when((line > far) & (line < last))
        def _():
            self.pass_on(1, far)

    def total(self):
        line, last = self.line, self.size - 1
        for side, there, beyond in ((0, line > 0, line == 0), (1, line < last, line == last)):

            @pl.when(there)
            def _():
                self.hop(side, line).wait_recv()

            @pl.when(beyond)
            def _():
                self.landed[side, line] = jnp.zeros(self.source.shape[1:], self.source.dtype)

        return (
            self.source[line].astype(F32)
            + self.landed[0, line].astype(F32)
            + self.landed[1, line].astype(F32)
        )

    def finish(self):
        for owner in range(self.size):

            @pl.when(self.line < owner)
            def _():
                self.hop(0, owner).wait_send()

            @pl.when(self.line > owner)
            def _():
                self.hop(1, owner).wait_send()


def line_scatter_sems(count, size):
    return [
        pltpu.SemaphoreType.DMA((count, 2, size)),
        pltpu.SemaphoreType.DMA((count, 2, size)),
    ]


def in_vmem(count):
    return [pl.BlockSpec(memory_space=pltpu.VMEM)] * count


def anywhere(count):
    return [pl.BlockSpec(memory_space=pl.ANY)] * count


def talk_params(collective_id):
    return pltpu.CompilerParams(
        collective_id=collective_id, has_side_effects=True, vmem_limit_bytes=VMEM_LIMIT
    )


def open_kernel(
    size, x_ref, dy_ref, win_ref, wout_ref,
    x_out, dy_out, win_out, wout_out,
    landed, swap_sems, own_sem, send_sem, recv_sem, line_own, line_send, line_recv,
):
    plane, line = plane_neighbours(), lax.axis_index("fsdp")
    meet(plane, line, size, True)
    swap = push(dy_ref, landed, swap_sems.at[0], swap_sems.at[1], "fsdp", pair_of(line))
    sems = (own_sem, send_sem, recv_sem)
    line_sems = (line_own, line_send, line_recv)
    x = Gather(plane, 0, x_ref, x_out, 0, *sems)
    dy = Gather(plane, 1, dy_ref, dy_out, 0, *sems)
    other = Gather(plane, 2, landed, dy_out, 8, *sems)
    win = LineGather(line, size, 0, win_ref, win_out, 0, *line_sems)
    wout = LineGather(line, size, 1, wout_ref, wout_out, 1, *line_sems)
    win.begin()
    x.begin()
    swap.start()
    wout.begin()
    dy.begin()
    x.relay()
    win.step(0)
    x.relay_diagonal()
    wout.step(0)
    win.step(1)
    dy.relay()
    swap.wait_recv()
    other.begin()
    wout.step(1)
    dy.relay_diagonal()
    win.step(2)
    wout.step(2)
    other.relay()
    other.relay_diagonal()
    for part in (x, dy, other, win, wout):
        part.finish()
    swap.wait_send()


def open_transfers(x, dy, w_in_shard, w_out_shard, size, collective_id):
    tokens, model_width = x.shape
    rows, columns = w_in_shard.shape
    out_rows, out_columns = w_out_shard.shape
    return pl.pallas_call(
        functools.partial(open_kernel, size),
        out_shape=[
            jax.ShapeDtypeStruct((8, tokens, model_width), BF16),
            jax.ShapeDtypeStruct((16, tokens, model_width), BF16),
            jax.ShapeDtypeStruct((rows * size, columns), BF16),
            jax.ShapeDtypeStruct((out_rows, out_columns * size), BF16),
        ],
        in_specs=in_vmem(4),
        out_specs=anywhere(4),
        scratch_shapes=[pltpu.VMEM((tokens, model_width), BF16), pltpu.SemaphoreType.DMA((2,))]
        + gather_sems(3)
        + line_gather_sems(2, size),
        compiler_params=talk_params(collective_id),
        cost_estimate=pl.CostEstimate(flops=0, bytes_accessed=120_000_000, transcendentals=0),
        name="open_transfers",
    )(x, dy, w_in_shard, w_out_shard)


def middle_kernel(
    query_width, router_at, part_ref, x_ref, win_ref, wout_ref, chosen_ref,
    b_out, g_out, middle_ref, marked_ref,
    routed, b_landed, g_landed, *rest,
):
    scratch, rest = rest[:6], rest[6:]
    swap_sems, scatter_send, scatter_recv, own_sem, send_sem, recv_sem = rest
    plane, line = plane_neighbours(), lax.axis_index("fsdp")
    meet(plane, line, 4, False)
    scatter = Scatter(plane, 0, part_ref, 0, scratch, scatter_send, scatter_recv)
    scatter.begin()
    scatter.first()
    scatter.second()
    half = x_ref.shape[0] // 2
    gain = wout_ref[query_width + 1 : query_width + 2, :].astype(F32)
    router = win_ref[:, router_at : router_at + LANES]
    for h in range(2):
        rows = pl.ds(h * half, half)
        middle = x_ref[rows].astype(F32) + RESIDUAL_SCALE * scatter.total(h)
        middle_ref[rows] = middle
        inverse = lax.rsqrt(jnp.mean(middle * middle, axis=1, keepdims=True) + EPSILON)
        b = (middle * inverse * gain).astype(BF16)
        routed[rows] = b
        chosen = chosen_ref[rows] > 0.0
        logits = jnp.where(chosen, dot(b, router), -1e30)
        lifted = jnp.where(chosen, jnp.exp(logits - jnp.max(logits, axis=1, keepdims=True)), 0.0)
        gates = lifted / jnp.sum(lifted, axis=1, keepdims=True)
        marked_ref[rows] = jnp.where(chosen, gates, -1.0)
    swap_b = push(routed, b_landed, swap_sems.at[0], swap_sems.at[1], "fsdp", pair_of(line))
    swap_g = push(marked_ref, g_landed, swap_sems.at[2], swap_sems.at[3], "fsdp", pair_of(line))
    swap_b.start()
    swap_g.start()
    sems = (own_sem, send_sem, recv_sem)
    b = Gather(plane, 0, routed, b_out, 0, *sems)
    g = Gather(plane, 1, marked_ref, g_out, 0, *sems)
    b_other = Gather(plane, 2, b_landed, b_out, 8, *sems)
    g_other = Gather(plane, 3, g_landed, g_out, 8, *sems)
    b.begin()
    g.begin()
    b.relay()
    g.relay()
    b.relay_diagonal()
    g.relay_diagonal()
    swap_b.wait_recv()
    swap_g.wait_recv()
    b_other.begin()
    g_other.begin()
    b_other.relay()
    g_other.relay()
    b_other.relay_diagonal()
    g_other.relay_diagonal()
    for item in (b, g, b_other, g_other, scatter):
        item.finish()
    swap_b.wait_send()
    swap_g.wait_send()


def middle_transfers(part, x, w_in, w_out, chosen, query_width, router_at, collective_id):
    tokens, model_width = x.shape
    return pl.pallas_call(
        functools.partial(middle_kernel, query_width, router_at),
        out_shape=[
            jax.ShapeDtypeStruct((16, tokens, model_width), BF16),
            jax.ShapeDtypeStruct((16, tokens, LANES), F32),
            jax.ShapeDtypeStruct((tokens, model_width), F32),
            jax.ShapeDtypeStruct((tokens, LANES), F32),
        ],
        in_specs=in_vmem(5),
        out_specs=anywhere(2) + in_vmem(2),
        scratch_shapes=[
            pltpu.VMEM((tokens, model_width), BF16),
            pltpu.VMEM((tokens, model_width), BF16),
            pltpu.VMEM((tokens, LANES), F32),
        ]
        + scatter_scratch(tokens, model_width, BF16)
        + [pltpu.SemaphoreType.DMA((4,))]
        + scatter_sems(1)
        + gather_sems(4),
        compiler_params=talk_params(collective_id),
        cost_estimate=pl.CostEstimate(flops=0, bytes_accessed=150_000_000, transcendentals=0),
        name="middle_transfers",
    )(part, x, w_in, w_out, chosen)


def close_kernel(
    size, query_width, swaps, da_ref, e_own, e_total, x_ref, middle_ref, grad_ref, gain_two_ref, wout_ref,
    gin_ref, out_low, *rest,
):
    sent, rest = rest[:swaps], rest[swaps:]
    outcome_ref, input_grad_ref, in_out, out_out, gains_out, notes_out, *rest = rest
    came, rest = rest[:swaps], rest[swaps:]
    close_steps(
        size, query_width, sent, came, da_ref, e_own, e_total, x_ref, middle_ref, grad_ref,
        gain_two_ref, wout_ref, gin_ref, out_low,
        outcome_ref, input_grad_ref, in_out, out_out, gains_out, notes_out, *rest,
    )


def close_steps(
    size, query_width, sent, came, da_ref, e_own, e_total, x_ref, middle_ref, grad_ref,
    gain_two_ref, wout_ref, gin_ref, out_low,
    outcome_ref, input_grad_ref, in_out, out_out, gains_out, notes_out,
    e_landed, gains, notes, notes_line, in_low, gain_low, notes_low, *rest,
):
    scratch, rest = rest[:6], rest[6:]
    line_scratch, rest = rest[:4], rest[4:]
    (
        across_sems, swap_sems, scatter_send, scatter_recv, sum_send, sum_recv,
        line_own, line_send, line_recv, own_sem, send_sem, recv_sem,
    ) = rest
    plane, line = plane_neighbours(), lax.axis_index("fsdp")
    meet(plane, line, size, True)
    sums = (scatter_send, scatter_recv)
    da = Scatter(plane, 0, da_ref, 0, scratch[:6], *sums)
    across = [
        push(source, target, across_sems.at[0, i], across_sems.at[1, i], "fsdp", pair_of(line))
        for i, (source, target) in enumerate(zip(sent, came))
    ]
    swap = push(e_total, e_landed, swap_sems.at[0], swap_sems.at[1], "fsdp", pair_of(line))
    gin = LineScatter(line, size, 0, gin_ref, *line_scratch[0:2], sum_send, sum_recv)
    gain = LineScatter(line, size, 1, gains, *line_scratch[2:4], sum_send, sum_recv)
    gathers = (own_sem, send_sem, recv_sem)
    out_all = Gather(plane, 1, out_low, out_out, 0, *gathers)
    half = x_ref.shape[0] // 2
    gin.begin()
    da.begin()
    da.first()
    gin.step(0)
    swap.start()
    da.second()
    gin.step(1)
    gin.step(2)
    for copy in across[:1]:
        copy.start()
    out_all.begin()
    gain_one = wout_ref[query_width : query_width + 1, :].astype(F32)
    grad_gain = jnp.zeros((1, x_ref.shape[1]), F32)
    squares = [jnp.zeros((1, 1), F32)] * 5

    def add_square(i, values):
        squares[i] = squares[i] + jnp.sum(
            jnp.sum(values * values, axis=1, keepdims=True), axis=0, keepdims=True
        )

    for h in range(2):
        rows = pl.ds(h * half, half)
        x = x_ref[rows].astype(F32)
        inverse = lax.rsqrt(jnp.mean(x * x, axis=1, keepdims=True) + EPSILON)
        normed = x * inverse
        grad_a = da.total(h)
        grad_gain += jnp.sum(grad_a * normed, axis=0, keepdims=True)
        grad_middle = grad_ref[rows]
        grad_input = grad_middle + norm_back(grad_a * gain_one, normed, inverse)
        input_grad_ref[rows] = grad_input.astype(BF16)
        add_square(0, x)
        add_square(1, middle_ref[rows])
        add_square(3, grad_middle)
        add_square(4, grad_input)
    width = x_ref.shape[1] // size
    row = lax.broadcasted_iota(jnp.int32, gains.shape[1:], 0)
    for p in range(size):
        columns = slice(p * width, (p + 1) * width)
        gains[p] = jnp.where(
            row == 0, grad_gain[:, columns],
            jnp.where(row == 1, gain_two_ref[0:1, columns], 0.0),
        ).astype(BF16)
    gain.begin()
    for copy in across[1:2]:
        copy.start()
    gain.step(0)
    gain.step(1)
    gain.step(2)
    for copy in across[2:]:
        copy.start()
    out_all.relay()
    swap.wait_recv()
    for h in range(2):
        rows = pl.ds(h * half, half)
        outcome = middle_ref[rows] + e_own[rows] + e_landed[rows].astype(F32)
        outcome_ref[rows] = outcome.astype(BF16)
        add_square(2, outcome)
    row = lax.broadcasted_iota(jnp.int32, notes.shape, 0)
    told = jnp.zeros(notes.shape, F32)
    for i in range(5):
        told = jnp.where(row == i, squares[i], told)
    notes[...] = told
    spread = LineGather(line, size, 0, notes, notes_line, 0, line_own, line_send, line_recv)
    spread.begin()
    in_low[...] = gin.total().astype(BF16)
    in_all = Gather(plane, 0, in_low, in_out, 0, *gathers)
    in_all.begin()
    spread.step(0)
    out_all.relay_diagonal()
    spread.step(1)
    spread.step(2)
    gain_low[...] = gain.total().astype(BF16)
    gain_all = Gather(plane, 2, gain_low, gains_out, 0, *gathers)
    gain_all.begin()
    spread.finish()
    count = notes.shape[0]
    notes_low[...] = (
        notes_line[pl.ds(0, count)] + notes_line[pl.ds(count, count)]
        + notes_line[pl.ds(2 * count, count)] + notes_line[pl.ds(3 * count, count)]
    )
    notes_all = Gather(plane, 3, notes_low, notes_out, 0, *gathers)
    notes_all.begin()
    last = (in_all, gain_all, notes_all)
    for item in last:
        item.relay()
    for item in last:
        item.relay_diagonal()
    for item in last + (out_all, da, gin, gain):
        item.finish()
    swap.wait_send()
    for copy in across:
        copy.wait()


def close_transfers(
    da_part, e_own, e_total, x, middle, grad_middle, gain_two, w_out, grad_in, out_low, sent,
    query_width, collective_id,
):
    tokens, model_width = x.shape
    size, in_rows, in_columns = grad_in.shape
    out_rows, out_columns = out_low.shape
    wide = (tokens, model_width)
    gain_shape, note_shape = (16, out_columns), (16, LANES)
    line_scratch = []
    for shape in (grad_in.shape, (size,) + gain_shape):
        line_scratch += [pltpu.VMEM((2,) + shape, BF16)] * 2
    return pl.pallas_call(
        functools.partial(close_kernel, size, query_width, len(sent)),
        out_shape=[
            jax.ShapeDtypeStruct(wide, BF16),
            jax.ShapeDtypeStruct(wide, BF16),
            jax.ShapeDtypeStruct((8, in_rows, in_columns), BF16),
            jax.ShapeDtypeStruct((8, out_rows, out_columns), BF16),
            jax.ShapeDtypeStruct((8,) + gain_shape, BF16),
            jax.ShapeDtypeStruct((8,) + note_shape, F32),
        ]
        + [jax.ShapeDtypeStruct(array.shape, array.dtype) for array in sent],
        in_specs=in_vmem(10) + anywhere(len(sent)),
        out_specs=in_vmem(2) + anywhere(4 + len(sent)),
        scratch_shapes=[
            pltpu.VMEM(wide, BF16),
            pltpu.VMEM((size,) + gain_shape, BF16),
            pltpu.VMEM(note_shape, F32),
            pltpu.VMEM((size * note_shape[0], LANES), F32),
            pltpu.VMEM((in_rows, in_columns), BF16),
            pltpu.VMEM(gain_shape, BF16),
            pltpu.VMEM(note_shape, F32),
        ]
        + scatter_scratch(*wide, BF16)
        + line_scratch
        + [pltpu.SemaphoreType.DMA((2, len(sent))), pltpu.SemaphoreType.DMA((2,))]
        + scatter_sems(1)
        + line_scatter_sems(2, size)
        + line_gather_sems(1, size)
        + gather_sems(4),
        compiler_params=talk_params(collective_id),
        cost_estimate=pl.CostEstimate(flops=0, bytes_accessed=200_000_000, transcendentals=0),
        name="close_transfers",
    )(da_part, e_own, e_total, x, middle, grad_middle, gain_two, w_out, grad_in, out_low, *sent)


def dot(first, second, contract=(1, 0)):
    return lax.dot_general(
        first, second, (((contract[0],), (contract[1],)), ((), ())), preferred_element_type=F32
    )


def spin(values, cosine, sine):
    width = values.shape[1]
    half = HEAD_DIM // 2
    cosine = jnp.concatenate([cosine] * (width // LANES), axis=1)
    sine = jnp.concatenate([sine] * (width // LANES), axis=1)
    lane = lax.broadcasted_iota(jnp.int32, values.shape, 1)
    lower = lax.rem(lane, HEAD_DIM) < half
    swapped = jnp.where(
        lower, pltpu.roll(values, width - half, 1), pltpu.roll(values, half, 1)
    )
    return values * cosine + swapped * sine


def attend_kernel(
    per_group, x_ref, w_in_ref, w_out_ref, cos_ref, sin_ref,
    part_ref, a_ref, q_ref, k_ref, v_ref, o_ref, lse_ref,
):
    length, model_width = x_ref.shape
    query_width = per_group * HEAD_DIM
    turned = query_width + HEAD_DIM
    gain = w_out_ref[query_width : query_width + 1, :].astype(F32)

    def project(i, carry):
        rows = pl.ds(pl.multiple_of(i * BLOCK, BLOCK), BLOCK)
        x = x_ref[rows, :].astype(F32)
        inverse = lax.rsqrt(jnp.mean(x * x, axis=1, keepdims=True) + EPSILON)
        a = (x * inverse * gain).astype(BF16)
        a_ref[rows, :] = a
        pre = dot(a, w_in_ref[...])
        spun = spin(pre[:, :turned], cos_ref[rows, :], sin_ref[rows, :]).astype(BF16)
        for h in range(per_group):
            q_ref[h, rows, :] = spun[:, h * HEAD_DIM : (h + 1) * HEAD_DIM]
        k_ref[rows, :] = spun[:, query_width:turned]
        v_ref[rows, :] = pre[:, turned : turned + HEAD_DIM].astype(BF16)
        return carry

    lax.fori_loop(0, length // BLOCK, project, 0)
    for i in range(length // BLOCK):
        seen = (i + 1) * BLOCK
        rows = slice(i * BLOCK, seen)
        keys, values = k_ref[:seen, :], v_ref[:seen, :]
        for h in range(per_group):
            scores = dot(q_ref[h, rows, :], keys, (1, 1)) * ATTENTION_SCALE
            peak = jnp.max(scores, axis=1, keepdims=True)
            lifted = jnp.exp(scores - peak)
            total = jnp.sum(lifted, axis=1, keepdims=True)
            weights = (lifted * (1.0 / total)).astype(BF16)
            mixed = dot(weights, values)
            o_ref[rows, h * HEAD_DIM : (h + 1) * HEAD_DIM] = mixed.astype(BF16)
            lse_ref[h, rows, :] = peak + jnp.log(total)
        part_ref[rows, :] = dot(o_ref[rows, :], w_out_ref[:query_width, :]).astype(BF16)


def attend(x_all, w_in, w_out, cosine, sine, per_group):
    length, model_width = x_all.shape
    query_width = per_group * HEAD_DIM
    shapes = [
        jax.ShapeDtypeStruct((length, model_width), BF16),
        jax.ShapeDtypeStruct((length, model_width), BF16),
        jax.ShapeDtypeStruct((per_group, length, HEAD_DIM), BF16),
        jax.ShapeDtypeStruct((length, HEAD_DIM), BF16),
        jax.ShapeDtypeStruct((length, HEAD_DIM), BF16),
        jax.ShapeDtypeStruct((length, query_width), BF16),
        jax.ShapeDtypeStruct((per_group, length, 1), F32),
    ]
    return pl.pallas_call(
        functools.partial(attend_kernel, per_group),
        out_shape=shapes,
        in_specs=[pl.BlockSpec(memory_space=pltpu.VMEM)] * 5,
        out_specs=[pl.BlockSpec(memory_space=pltpu.VMEM)] * len(shapes),
        compiler_params=pltpu.CompilerParams(vmem_limit_bytes=VMEM_LIMIT),
        cost_estimate=pl.CostEstimate(
            flops=8_000_000_000, bytes_accessed=16_000_000, transcendentals=2_000_000
        ),
        name="attend",
    )(x_all, w_in, w_out, cosine, sine)


def attend_back_kernel(per_group, *refs):
    attend_back_steps(per_group, lambda step: None, *refs)


def attend_back_talk_kernel(per_group, size, swaps, *refs):
    ins, refs = refs[:13], refs[13:]
    sum_ref, sent, refs = refs[0], refs[1 : 1 + swaps], refs[1 + swaps :]
    part_ref, gin_ref, out_low, e_own, e_other = refs[:5]
    came, refs = refs[5 : 5 + swaps], refs[5 + swaps :]
    scratch, stage_a, stage_b, refs = refs[:5], refs[5:11], refs[11:17], refs[17:]
    gout_ref, line_sums, line_landed, sends, receives, swap_sems, line_send, line_recv = refs
    plane, line = plane_neighbours(), lax.axis_index("fsdp")
    other = Scatter(plane, 0, sum_ref, 8, stage_a, sends, receives)
    mine = Scatter(plane, 1, sum_ref, 0, stage_b, sends, receives)
    gout = LineScatter(line, size, 0, gout_ref, line_sums, line_landed, line_send, line_recv)
    across = [
        push(source, target, swap_sems.at[0, i], swap_sems.at[1, i], "fsdp", pair_of(line))
        for i, (source, target) in enumerate(zip(sent, came))
    ]
    half = e_own.shape[0] // 2

    def hook(step):
        if step == 0:
            meet(plane, line, size, True)
            other.begin()
            mine.begin()
            gout.begin()
            across[0].start()
        elif step == 1:
            other.first()
            gout.step(0)
            for copy in across[1:2]:
                copy.start()
        elif step == 2:
            mine.first()
            gout.step(1)
            for copy in across[2:]:
                copy.start()
        elif step == 3:
            other.second()
            gout.step(2)
        elif step == 4:
            mine.second()
        elif step == 6:
            for h in range(2):
                e_other[pl.ds(h * half, half)] = other.total(h).astype(BF16)
                e_own[pl.ds(h * half, half)] = mine.total(h)
            out_low[...] = gout.total().astype(BF16)
            for item in (other, mine, gout):
                item.finish()
            for copy in across:
                copy.wait()

    attend_back_steps(per_group, hook, *ins, part_ref, gin_ref, gout_ref, *scratch)


def attend_back_steps(
    per_group, hook, dw_ref, w_in_ref, w_out_ref, cos_ref, sin_ref,
    a_ref, q_ref, k_ref, v_ref, o_ref, lse_ref, b_all_ref, dl_ref,
    part_ref, gin_ref, gout_ref,
    turn_ref, dv_ref, back_ref, b_ref, b_sem,
):
    length, model_width = dw_ref.shape
    fetch = pltpu.make_async_copy(b_all_ref.at[pl.ds(0, length)], b_ref, b_sem)
    fetch.start()
    query_width = per_group * HEAD_DIM
    turned = query_width + HEAD_DIM
    blocks = length // BLOCK
    chunk = 384

    def out_grads(i, carry):
        columns = pl.ds(pl.multiple_of(i * chunk, chunk), chunk)
        gout_ref[i] = dot(o_ref[...], dw_ref[:, columns], (0, 0)).astype(BF16)
        return carry

    lax.fori_loop(0, model_width // chunk, out_grads, 0)
    hook(0)
    turn_ref[...] = jnp.zeros_like(turn_ref)
    dv_ref[...] = jnp.zeros_like(dv_ref)
    for i in range(blocks):
        seen = (i + 1) * BLOCK
        rows = slice(i * BLOCK, seen)
        keys, values = k_ref[:seen, :], v_ref[:seen, :]
        grad = dot(dw_ref[rows, :], w_out_ref[:query_width, :], (1, 1)).astype(BF16)
        for h in range(per_group):
            columns = slice(h * HEAD_DIM, (h + 1) * HEAD_DIM)
            queries = q_ref[h, rows, :]
            grad_head = grad[:, columns]
            scores = dot(queries, keys, (1, 1)) * ATTENTION_SCALE
            probs = jnp.exp(scores - lse_ref[h, rows, :])
            dv_ref[:seen, :] += dot(probs.astype(BF16), grad_head, (0, 0))
            grad_probs = dot(grad_head, values, (1, 1))
            inner = jnp.sum(probs * grad_probs, axis=1, keepdims=True)
            grad_scores = (probs * (grad_probs - inner)).astype(BF16)
            turn_ref[rows, columns] = dot(grad_scores, keys) * ATTENTION_SCALE
            turn_ref[:seen, query_width:turned] += (
                dot(grad_scores, queries, (0, 0)) * ATTENTION_SCALE
            )
        hook(1 + i)

    def unturn(i, carry):
        rows = pl.ds(pl.multiple_of(i * BLOCK, BLOCK), BLOCK)
        back_ref[rows, :turned] = spin(
            turn_ref[rows, :], cos_ref[rows, :], -sin_ref[rows, :]
        ).astype(BF16)
        back_ref[rows, turned:] = jnp.concatenate(
            [dv_ref[rows, :].astype(BF16), jnp.zeros((BLOCK, LANES - HEAD_DIM), BF16)], axis=1
        )
        part_ref[rows, :] = dot(
            back_ref[rows, : turned + HEAD_DIM], w_in_ref[:, : turned + HEAD_DIM], (1, 1)
        ).astype(BF16)
        return carry

    lax.fori_loop(0, blocks, unturn, 0)
    hook(5)
    fetch.wait()

    def weight_grads(i, carry):
        columns = pl.ds(pl.multiple_of(i * chunk, chunk), chunk)
        a = a_ref[:, columns]
        gin_ref[columns, :turned] = dot(a, back_ref[:, :turned], (0, 0)).astype(BF16)
        gin_ref[columns, turned:] = (
            dot(a, back_ref[:, turned:], (0, 0)) + dot(b_ref[:, columns], dl_ref[...], (0, 0))
        ).astype(BF16)
        return carry

    lax.fori_loop(0, model_width // chunk, weight_grads, 0)
    hook(6)


def attend_back(
    dw_all, w_in, w_out, cosine, sine, saved, b_all, dl_all, per_group, talk=None, collective_id=None
):
    length, model_width = dw_all.shape
    query_width = per_group * HEAD_DIM
    turned = query_width + HEAD_DIM
    shapes = [
        jax.ShapeDtypeStruct((length, model_width), BF16),
        jax.ShapeDtypeStruct((model_width, w_in.shape[1]), BF16),
        jax.ShapeDtypeStruct((model_width // 384, query_width, 384), BF16),
    ]
    scratch = [
        pltpu.VMEM((length, turned), F32),
        pltpu.VMEM((length, HEAD_DIM), F32),
        pltpu.VMEM((length, w_in.shape[1]), BF16),
        pltpu.VMEM((length, model_width), BF16),
        pltpu.SemaphoreType.DMA,
    ]
    operands = (dw_all, w_in, w_out, cosine, sine, *saved, b_all, dl_all)
    in_specs, out_specs = in_vmem(11) + anywhere(1) + in_vmem(1), in_vmem(len(shapes))
    kernel = functools.partial(attend_back_kernel, per_group)
    params = pltpu.CompilerParams(vmem_limit_bytes=VMEM_LIMIT)
    if talk is not None:
        sum_part, sent = talk
        wide = sum_part.shape[1:]
        shapes = shapes + [jax.ShapeDtypeStruct(wide, F32), jax.ShapeDtypeStruct(wide, BF16)]
        shapes += [jax.ShapeDtypeStruct(array.shape, array.dtype) for array in sent]
        gout_shape, size = shapes[2].shape, lax.axis_size("fsdp")
        shapes[2] = jax.ShapeDtypeStruct(gout_shape[1:], BF16)
        scratch = scratch + scatter_scratch(*wide, BF16) * 2
        scratch += [pltpu.VMEM(gout_shape, BF16)] + [pltpu.VMEM((2,) + gout_shape, BF16)] * 2
        scratch += scatter_sems(2) + [pltpu.SemaphoreType.DMA((2, len(sent)))]
        scratch += line_scatter_sems(1, size)
        operands += (sum_part, *sent)
        in_specs = in_specs + in_vmem(1) + anywhere(len(sent))
        out_specs = out_specs + in_vmem(2) + anywhere(len(sent))
        kernel = functools.partial(attend_back_talk_kernel, per_group, size, len(sent))
        params = talk_params(collective_id)
    return pl.pallas_call(
        kernel,
        out_shape=shapes,
        in_specs=in_specs,
        out_specs=out_specs,
        scratch_shapes=scratch,
        compiler_params=params,
        cost_estimate=pl.CostEstimate(
            flops=20_000_000_000, bytes_accessed=30_000_000, transcendentals=2_000_000
        ),
        name="attend_back",
    )(*operands)


def experts_kernel(
    here, tile,
    place_ref, b_hbm, dy_hbm, g_ref, gate_hbm, up_hbm, down_hbm, *rest,
):
    out_hbm, db_hbm, dg_ref = rest[:3]
    grad_hbm, rest = rest[3:6], rest[6:]
    (
        b_ref, dy_ref, in_ref, down_ref, hidden_ref, back_ref, out_ref, db_ref,
        gate_stage, up_stage, down_stage, weight_sem, tile_sem, out_sem, grad_sem,
    ) = rest
    rows_all, model_width = b_ref.shape
    width = down_ref.shape[0] // here
    tiles = rows_all // tile
    first = place_ref[0]

    def columns_of(e):
        return slice(e * width, (e + 1) * width)

    loads = []
    for e in range(here):
        loads.append((gate_hbm.at[e], in_ref.at[:, columns_of(e)]))
        loads.append((up_hbm.at[e], in_ref.at[:, columns_of(here + e)]))
    for e in range(here):
        loads.append((down_hbm.at[e], down_ref.at[columns_of(e), :]))
    loads = [
        pltpu.make_async_copy(source, target, weight_sem.at[i])
        for i, (source, target) in enumerate(loads)
    ]

    def tile_rows(i):
        return pl.ds(pl.multiple_of(i * tile, tile), tile)

    def tile_load(i, k):
        source, target = ((b_hbm, b_ref), (dy_hbm, dy_ref))[k]
        return pltpu.make_async_copy(
            source.at[tile_rows(i)], target.at[tile_rows(i)], tile_sem.at[k, i]
        )

    def tile_store(i, k):
        source, target = ((out_ref, out_hbm), (db_ref, db_hbm))[k]
        return pltpu.make_async_copy(
            source.at[tile_rows(i)], target.at[tile_rows(i)], out_sem.at[k, i]
        )

    for k in range(2):
        tile_load(0, k).start()
    for load in loads:
        load.start()
    for i in range(1, tiles):
        for k in range(2):
            tile_load(i, k).start()
    for load in loads:
        load.wait()

    def forward_back(i, carry):
        rows = tile_rows(i)
        tile_load(i, 0).wait()
        tile_load(i, 1).wait()
        pre = dot(b_ref[rows, :], in_ref[...])
        grad_mixed = dot(dy_ref[rows, :], down_ref[...], (1, 1))
        gates = g_ref[rows, :]
        lane = lax.broadcasted_iota(jnp.int32, gates.shape, 1)
        inner = jnp.zeros(gates.shape, F32)
        for e in range(here):
            mine = lane == first + e
            gate = jnp.sum(jnp.where(mine, jnp.maximum(gates, 0.0), 0.0), axis=1, keepdims=True)
            scale = RESIDUAL_SCALE * gate
            gate_pre, up_pre = pre[:, columns_of(e)], pre[:, columns_of(here + e)]
            sigmoid = 1.0 / (1.0 + jnp.exp(-gate_pre))
            silu = gate_pre * sigmoid
            hidden = silu * up_pre
            grad = grad_mixed[:, columns_of(e)]
            share = jnp.sum(hidden * grad, axis=1, keepdims=True)
            inner = jnp.where(mine, RESIDUAL_SCALE * share, inner)
            hidden_ref[rows, columns_of(e)] = (scale * hidden).astype(BF16)
            grad = scale * grad
            back_ref[rows, columns_of(e)] = (
                grad * up_pre * sigmoid * (1.0 + gate_pre * (1.0 - sigmoid))
            ).astype(BF16)
            back_ref[rows, columns_of(here + e)] = (grad * silu).astype(BF16)
        dg_ref[rows, :] = inner
        db_ref[rows, :] = dot(back_ref[rows, :], in_ref[...], (1, 1)).astype(BF16)
        tile_store(i, 1).start()
        out_ref[rows, :] = dot(hidden_ref[rows, :], down_ref[...]).astype(BF16)
        tile_store(i, 0).start()
        return carry

    lax.fori_loop(0, tiles, forward_back, 0)
    parts = 4
    part = model_width // parts

    def part_columns(i):
        return pl.ds(pl.multiple_of(i * part, part), part)

    def down_grad(i, carry):
        grad = dot(hidden_ref[...], dy_ref[:, part_columns(i)], (0, 0))
        for e in range(here):
            down_stage[i, e] = grad[columns_of(e), :].astype(BF16)
        return carry

    def in_grad(i, carry):
        grad = dot(b_ref[:, part_columns(i)], back_ref[...], (0, 0))
        for e in range(here):
            gate_stage[i, e] = grad[:, columns_of(e)].astype(BF16)
            up_stage[i, e] = grad[:, columns_of(here + e)].astype(BF16)
        return carry

    stores = []

    def store(k, stage):
        copy = pltpu.make_async_copy(stage, grad_hbm[k], grad_sem.at[k])
        copy.start()
        stores.append(copy)

    lax.fori_loop(0, parts, down_grad, 0)
    store(2, down_stage)
    lax.fori_loop(0, parts, in_grad, 0)
    store(0, gate_stage)
    store(1, up_stage)
    for copy in stores:
        copy.wait()
    for i in range(tiles):
        for k in range(2):
            tile_store(i, k).wait()


def experts(place, b_all, dy_all, g_all, w_gate, w_up, w_down):
    sources, tokens, model_width = b_all.shape
    here, _, hidden_width = w_gate.shape
    rows_all = sources * tokens
    width = hidden_width
    part = model_width // 4
    tile = 256
    tiles = rows_all // tile
    in_stage, down_stage = (4, here, part, width), (4, here, width, part)
    shapes = [in_stage, in_stage, down_stage]
    flat = (rows_all, model_width)
    out = pl.pallas_call(
        functools.partial(experts_kernel, here, tile),
        out_shape=[
            jax.ShapeDtypeStruct(flat, BF16),
            jax.ShapeDtypeStruct(flat, BF16),
            jax.ShapeDtypeStruct((rows_all, LANES), F32),
        ]
        + [jax.ShapeDtypeStruct(shape, BF16) for shape in shapes],
        in_specs=[pl.BlockSpec(memory_space=pltpu.SMEM)] + anywhere(2) + in_vmem(1) + anywhere(3),
        out_specs=anywhere(2) + in_vmem(1) + anywhere(len(shapes)),
        scratch_shapes=[
            pltpu.VMEM(flat, BF16),
            pltpu.VMEM(flat, BF16),
            pltpu.VMEM((model_width, 2 * here * width), BF16),
            pltpu.VMEM((here * width, model_width), BF16),
            pltpu.VMEM((rows_all, here * width), BF16),
            pltpu.VMEM((rows_all, 2 * here * width), BF16),
            pltpu.VMEM(flat, BF16),
            pltpu.VMEM(flat, BF16),
            pltpu.VMEM(in_stage, BF16),
            pltpu.VMEM(in_stage, BF16),
            pltpu.VMEM(down_stage, BF16),
            pltpu.SemaphoreType.DMA((3 * here,)),
            pltpu.SemaphoreType.DMA((2, tiles)),
            pltpu.SemaphoreType.DMA((2, tiles)),
            pltpu.SemaphoreType.DMA((3,)),
        ],
        compiler_params=pltpu.CompilerParams(vmem_limit_bytes=VMEM_LIMIT),
        cost_estimate=pl.CostEstimate(
            flops=43_000_000_000, bytes_accessed=42_000_000, transcendentals=1_000_000
        ),
        name="experts",
    )(
        place, b_all.reshape(flat), dy_all.reshape(flat), g_all.reshape(rows_all, LANES),
        w_gate, w_up, w_down,
    )
    return [
        out[0].reshape(b_all.shape), out[1].reshape(b_all.shape),
        out[2].reshape(sources, tokens, LANES), *out[3:],
    ]


class Trade:
    def __init__(self, line, stages, nears, came, far, sems):
        self.beside, self.across = beside(line), pair_of(line)
        self.stages, self.nears, self.came, self.far, self.sems = stages, nears, came, far, sems

    def copies(self, e, hop):
        made = []
        for k in range(3):
            source = self.stages[k].at[e, (1, 0, 3)[hop]]
            target = self.far[k] if hop == 2 else (self.nears, self.came)[hop][k].at[e]
            peer = self.across if hop == 2 else self.beside
            made.append(
                push(source, target, self.sems.at[0, hop, k, e], self.sems.at[1, hop, k, e], "fsdp", peer)
            )
        return made

    def send(self, e, hop):
        for copy in self.copies(e, hop):
            copy.start()

    def add(self, e):
        for k, copy in enumerate(self.copies(e, 0)):
            copy.wait_recv()
            self.stages[k][e, 3] = (
                self.stages[k][e, 3].astype(F32) + self.nears[k][e].astype(F32)
            ).astype(BF16)

    def finish(self, count):
        for e in range(count):
            for hop in range(3 if e == 0 else 2):
                for copy in self.copies(e, hop):
                    copy.wait_send()
                    if hop:
                        copy.wait_recv()


def experts_back_kernel(
    here, tile, lane_of, query_width, router_at,
    b_hbm, dy_hbm, g_ref, gate_hbm, up_hbm, down_hbm,
    middle_ref, marked_ref, win_ref, wout_ref,
    out_hbm, dw_out, dl_out, grad_ref, gain_ref, *rest,
):
    kept_hbm, came_hbm, far_hbm, rest = rest[0:3], rest[3:6], rest[6:9], rest[9:]
    other_hbm, rest = rest[: 3 * (here - 1)], rest[3 * (here - 1) :]
    (
        b_ref, dy_ref, in_ref, down_ref, hidden_ref, back_ref, out_ref, db_ref, dg_ref,
        down_stage, gate_stage, up_stage, down_near, gate_near, up_near,
        dw_own, dl_own, db_total, dg_total, db_landed, dg_landed,
    ) = rest[:21]
    scratch, rest = rest[21:41], rest[41:]
    (
        weight_sem, tile_sem, out_sem, kept_sem, other_sem, trade_sems, swap_sems,
        scatter_send, scatter_recv, own_sem, send_sem, recv_sem,
    ) = rest
    rows_all, model_width = b_ref.shape
    width = down_ref.shape[1]
    tiles = rows_all // tile
    tokens = middle_ref.shape[0]
    per_tile = tile // tokens
    plane, line = plane_neighbours(), lax.axis_index("fsdp")
    me = plane[0]
    first = me * here + lane_of
    high, low = line // 2, lax.rem(line, 2)
    span = pl.ds(pl.multiple_of(high * width, width), width)

    def weight_loads(e):
        pairs = (
            (gate_hbm.at[e, :, span], in_ref.at[e, :, pl.ds(0, width)]),
            (up_hbm.at[e, :, span], in_ref.at[e, :, pl.ds(width, width)]),
            (down_hbm.at[e, span, :], down_ref.at[e]),
        )
        return [
            pltpu.make_async_copy(source, target, weight_sem.at[e, i])
            for i, (source, target) in enumerate(pairs)
        ]

    def tile_rows(j):
        return pl.ds(pl.multiple_of(j * tile, tile), tile)

    def tile_loads(j):
        return [
            pltpu.make_async_copy(
                source.at[tile_rows(j)], target.at[tile_rows(j)], tile_sem.at[k, j]
            )
            for k, (source, target) in enumerate(((b_hbm, b_ref), (dy_hbm, dy_ref)))
        ]

    def tile_store(j):
        return pltpu.make_async_copy(
            out_ref.at[tile_rows(j)], out_hbm.at[tile_rows(j)], out_sem.at[j]
        )

    def place_of(i):
        return lax.rem(i + tiles // 2, tiles)

    def start_loads(i, carry):
        for load in tile_loads(place_of(i)):
            load.start()
        return carry

    start_loads(0, 0)
    for load in weight_loads(0):
        load.start()
    lax.fori_loop(1, tiles, start_loads, 0)
    for e in range(1, here):
        for load in weight_loads(e):
            load.start()
    meet(plane, line, 4, False)
    trade = Trade(
        line, (down_stage, gate_stage, up_stage), (down_near, gate_near, up_near),
        came_hbm, far_hbm, trade_sems,
    )
    sums = (scatter_send, scatter_recv)
    db_other = Scatter(plane, 0, db_ref, 8, scratch[:5], *sums)
    dg_other = Scatter(plane, 1, dg_ref, 8, scratch[5:10], *sums)
    db = Scatter(plane, 2, db_ref, 0, scratch[10:15], *sums)
    dg = Scatter(plane, 3, dg_ref, 0, scratch[15:20], *sums)
    swap_g = push(dg_total, dg_landed, swap_sems.at[0], swap_sems.at[1], "fsdp", pair_of(line))
    swap_b = push(db_total, db_landed, swap_sems.at[2], swap_sems.at[3], "fsdp", pair_of(line))
    half = tokens // 2
    part = model_width // 4

    def one_expert(e, carry):
        for load in weight_loads(e):
            load.wait()
        last = e == here - 1

        def forward_back(i, carry):
            j = place_of(i)
            rows = tile_rows(j)

            @pl.when(e == 0)
            def _():
                for load in tile_loads(j):
                    load.wait()

            pre = dot(b_ref[rows, :], in_ref[e])
            grad = dot(dy_ref[rows, :], down_ref[e], (1, 1))
            gates = g_ref[rows, :]
            mine = lax.broadcasted_iota(jnp.int32, gates.shape, 1) == first + e
            gate = jnp.sum(jnp.where(mine, jnp.maximum(gates, 0.0), 0.0), axis=1, keepdims=True)
            scale = RESIDUAL_SCALE * gate
            gate_pre, up_pre = pre[:, :width], pre[:, width:]
            sigmoid = 1.0 / (1.0 + jnp.exp(-gate_pre))
            silu = gate_pre * sigmoid
            hidden = silu * up_pre
            share = jnp.sum(hidden * grad, axis=1, keepdims=True)
            inner = jnp.where(mine, RESIDUAL_SCALE * share, 0.0)
            hidden_ref[rows, :] = (scale * hidden).astype(BF16)
            grad = scale * grad
            back_ref[rows, :width] = (
                grad * up_pre * sigmoid * (1.0 + gate_pre * (1.0 - sigmoid))
            ).astype(BF16)
            back_ref[rows, width:] = (grad * silu).astype(BF16)
            made = dot(hidden_ref[rows, :], down_ref[e])
            back = dot(back_ref[rows, :], in_ref[e], (1, 1))

            @pl.when(e == 0)
            def _():
                out_ref[rows, :] = made.astype(BF16)
                for t in range(per_tile):
                    piece = slice(t * tokens, (t + 1) * tokens)
                    db_ref[per_tile * j + t] = back[piece].astype(BF16)
                    dg_ref[per_tile * j + t] = inner[piece]

            @pl.when(e > 0)
            def _():
                out_ref[rows, :] = (out_ref[rows, :].astype(F32) + made).astype(BF16)
                for t in range(per_tile):
                    piece = slice(t * tokens, (t + 1) * tokens)
                    block = per_tile * j + t
                    db_ref[block] = (db_ref[block].astype(F32) + back[piece]).astype(BF16)
                    dg_ref[block] += inner[piece]

            @pl.when(last)
            def _():
                tile_store(j).start()

            @pl.when((e == 1) & (i == tiles - 3))
            def _():
                trade.add(0)
                trade.send(0, 2)

            @pl.when(last & (i == tiles // 2 - 1))
            def _():
                dg_other.begin()
                db_other.begin()

            @pl.when(last & (i == tiles - 2))
            def _():
                dg_other.first()
                db_other.first()

            return carry

        lax.fori_loop(0, tiles, forward_back, 0)

        @pl.when(last)
        def _():
            dg.begin()
            db.begin()
            dg_other.second()
            db_other.second()

        def weight_grads(p, carry):
            i = p + 1 - 2 * lax.rem(p, 2)
            parity = jnp.where(p < 2, 1 - low, low)
            side = jnp.where(lax.rem(i, 2) == 0, high, 1 - high)
            columns = pl.ds(pl.multiple_of((2 * side + parity) * part, part), part)
            down_stage[e, i] = dot(hidden_ref[...], dy_ref[:, columns], (0, 0)).astype(BF16)
            grad = dot(b_ref[:, columns], back_ref[...], (0, 0))
            gate_stage[e, i] = grad[:, :width].astype(BF16)
            up_stage[e, i] = grad[:, width:].astype(BF16)

            @pl.when((p == 0) & (e < here - 1))
            def _():
                trade.send(e, 0)

            @pl.when((p == 1) & (e < here - 2))
            def _():
                trade.send(e, 1)

            @pl.when(last & (p == 1))
            def _():
                for h in range(2):
                    rows = pl.ds(h * half, half)
                    dg_total[rows] = dg_other.total(h)
                    db_total[rows] = db_other.total(h).astype(BF16)
                swap_g.start()
                swap_b.start()
                trade.send(here - 2, 1)
                trade.send(here - 1, 0)
                trade.send(here - 1, 1)

            @pl.when(last & (p == 2))
            def _():
                dg.first()
                db.first()

            return carry

        lax.fori_loop(0, 4, weight_grads, 0)
        return carry

    lax.fori_loop(0, here, one_expert, 0)
    stores = [
        pltpu.make_async_copy(stage.at[e, 2], kept_hbm[k].at[e], kept_sem.at[k, e])
        for k, stage in enumerate((down_stage, gate_stage, up_stage))
        for e in range(here)
    ]
    for store in stores:
        store.start()
    dg.second()
    db.second()
    others = []

    def give_other(e):
        trade.add(e)
        for k, stage in enumerate((down_stage, gate_stage, up_stage)):
            target = other_hbm[3 * (e - 1) + k]
            others.append(pltpu.make_async_copy(stage.at[e, 3], target, other_sem.at[e - 1, k]))
            others[-1].start()

    for e in range(1, here - 1):
        give_other(e)
    gain = wout_ref[query_width + 1 : query_width + 2, :].astype(F32)
    router = win_ref[:, router_at : router_at + LANES]
    gain_grad = jnp.zeros((1, model_width), F32)
    sums_g = [dg.total(h) for h in range(2)]
    swap_g.wait_recv()
    swap_b.wait_recv()
    for h in range(2):
        rows = pl.ds(h * half, half)
        gates = jnp.maximum(marked_ref[rows], 0.0)
        grad_gates = sums_g[h] + dg_landed[rows]
        grad_chosen = gates * (
            grad_gates - jnp.sum(gates * grad_gates, axis=1, keepdims=True)
        )
        grad_logits = grad_chosen.astype(BF16)
        dl_own[rows] = grad_logits
        grad_b = dot(grad_logits, router, (1, 1)) + db.total(h) + db_landed[rows].astype(F32)
        middle = middle_ref[rows]
        inverse = lax.rsqrt(jnp.mean(middle * middle, axis=1, keepdims=True) + EPSILON)
        normed = middle * inverse
        gain_grad += jnp.sum(grad_b * normed, axis=0, keepdims=True)
        own = pl.ds(pl.multiple_of(me * tokens + h * half, half), half)
        grad = dy_ref[own].astype(F32) + norm_back(grad_b * gain, normed, inverse)
        grad_ref[rows] = grad
        dw_own[rows] = (RESIDUAL_SCALE * grad).astype(BF16)
    gain_ref[...] = jnp.broadcast_to(gain_grad, gain_ref.shape)
    gathers = (own_sem, send_sem, recv_sem)
    dw = Gather(plane, 0, dw_own, dw_out, 0, *gathers)
    dl = Gather(plane, 1, dl_own, dl_out, 0, *gathers)
    dw.begin()
    dl.begin()
    dw.relay()
    dl.relay()
    dw.relay_diagonal()
    dl.relay_diagonal()
    give_other(here - 1)
    for item in (dg_other, db_other, dg, db, dw, dl):
        item.finish()
    swap_b.wait_send()
    swap_g.wait_send()
    for store in stores + others:
        store.wait()
    for j in range(tiles):
        tile_store(j).wait()
    trade.finish(here)


def experts_back(
    b_all, dy_all, g_all, w_gate, w_up, w_down, middle, marked, w_in, w_out,
    lane_of, query_width, router_at, collective_id,
):
    sources, tokens, model_width = b_all.shape
    here, _, hidden_width = w_gate.shape
    rows_all = sources * tokens
    width, part, tile = hidden_width // 2, model_width // 4, 256
    tiles = rows_all // tile
    flat, wide, narrow = (rows_all, model_width), (tokens, model_width), (tokens, LANES)
    slices = [(width, part), (part, width), (part, width)]
    out = pl.pallas_call(
        functools.partial(experts_back_kernel, here, tile, lane_of, query_width, router_at),
        out_shape=[
            jax.ShapeDtypeStruct(flat, BF16),
            jax.ShapeDtypeStruct((8,) + wide, BF16),
            jax.ShapeDtypeStruct((8,) + narrow, BF16),
            jax.ShapeDtypeStruct(wide, F32),
            jax.ShapeDtypeStruct((8, model_width), F32),
        ]
        + [jax.ShapeDtypeStruct((here,) + shape, BF16) for shape in slices * 2]
        + [jax.ShapeDtypeStruct(shape, BF16) for shape in slices * here],
        in_specs=anywhere(2) + in_vmem(1) + anywhere(3) + in_vmem(4),
        out_specs=anywhere(3) + in_vmem(2) + anywhere(6 + 3 * here),
        scratch_shapes=[
            pltpu.VMEM(flat, BF16),
            pltpu.VMEM(flat, BF16),
            pltpu.VMEM((here, model_width, 2 * width), BF16),
            pltpu.VMEM((here, width, model_width), BF16),
            pltpu.VMEM((rows_all, width), BF16),
            pltpu.VMEM((rows_all, 2 * width), BF16),
            pltpu.VMEM(flat, BF16),
            pltpu.VMEM((sources,) + wide, BF16),
            pltpu.VMEM((sources,) + narrow, F32),
        ]
        + [pltpu.VMEM((here, 4) + shape, BF16) for shape in slices]
        + [pltpu.VMEM((here,) + shape, BF16) for shape in slices]
        + [
            pltpu.VMEM(wide, BF16),
            pltpu.VMEM(narrow, BF16),
            pltpu.VMEM(wide, BF16),
            pltpu.VMEM(narrow, F32),
            pltpu.VMEM(wide, BF16),
            pltpu.VMEM(narrow, F32),
        ]
        + (scatter_scratch(*wide, BF16, True) + scatter_scratch(*narrow, F32, True)) * 2
        + [
            pltpu.SemaphoreType.DMA((here, 3)),
            pltpu.SemaphoreType.DMA((2, tiles)),
            pltpu.SemaphoreType.DMA((tiles,)),
            pltpu.SemaphoreType.DMA((3, here)),
            pltpu.SemaphoreType.DMA((here - 1, 3)),
            pltpu.SemaphoreType.DMA((2, 3, 3, here)),
            pltpu.SemaphoreType.DMA((4,)),
        ]
        + scatter_sems(4)
        + gather_sems(2),
        compiler_params=pltpu.CompilerParams(
            collective_id=collective_id, has_side_effects=True, vmem_limit_bytes=67_000_000
        ),
        cost_estimate=pl.CostEstimate(
            flops=43_000_000_000, bytes_accessed=42_000_000, transcendentals=1_000_000
        ),
        name="experts_back",
    )(
        b_all.reshape(flat), dy_all.reshape(flat), g_all.reshape(rows_all, LANES),
        w_gate, w_up, w_down, middle, marked, w_in, w_out,
    )
    others = [out[at : at + 3] for at in range(14, 11 + 3 * here, 3)]
    return [out[0].reshape(b_all.shape), *out[1:5], out[5:8], out[8:11], out[11:14], others]


def rotary_tables(length):
    lane = lax.broadcasted_iota(jnp.int32, (length, LANES), 1) % HEAD_DIM
    half = HEAD_DIM // 2
    exponent = (lane % half).astype(F32) * (2.0 / HEAD_DIM)
    position = lax.broadcasted_iota(jnp.int32, (length, LANES), 0).astype(F32)
    angles = position * jnp.power(ROPE_BASE, -exponent)
    return jnp.cos(angles), jnp.where(lane < half, -jnp.sin(angles), jnp.sin(angles))


def finish_kernel(per_group, here, in_ref, out_ref, *refs):
    kept, came, far, refs = refs[:3], refs[3:6], refs[6 : 6 + 3 * here], refs[6 + 3 * here :]
    query_ref, key_ref, value_ref, router_ref, proj_ref, *expert_refs = refs
    query_width = per_group * HEAD_DIM
    groups, out_rows, _ = out_ref.shape
    for j in range(0, groups, 2):
        pair = (in_ref[j].astype(F32), in_ref[j + 1].astype(F32))
        at = 0
        for target, width in ((query_ref, query_width), (key_ref, HEAD_DIM), (value_ref, HEAD_DIM)):
            target[:, j * width : (j + 2) * width] = jnp.concatenate(
                [block[:, at : at + width] for block in pair], axis=1
            )
            at += width
    router_ref[...] = in_ref[0][:, at : at + router_ref.shape[1]].astype(F32)
    for j in range(groups):
        proj_ref[j * out_rows : (j + 1) * out_rows, :] = out_ref[j].astype(F32)
    high = lax.axis_index("fsdp") // 2
    for k, target in enumerate(expert_refs):
        width = kept[k].shape[1 if k == 0 else 2]
        near = pl.ds(pl.multiple_of(high * width, width), width)
        beyond = pl.ds(pl.multiple_of((1 - high) * width, width), width)
        for e in range(here):
            near_sum = kept[k][e].astype(F32) + came[k][e].astype(F32)
            far_sum = far[3 * e + k][...].astype(F32)
            if k == 0:
                target[e, near, :] = near_sum
                target[e, beyond, :] = far_sum
            else:
                target[e, :, near] = near_sum
                target[e, :, beyond] = far_sum


def finish(in_all, out_all, kept, came, far, per_group, experts_all):
    groups, shard, _ = in_all.shape
    here, width, part = kept[0].shape
    query_width = per_group * HEAD_DIM
    shapes = [
        (shard, groups * query_width),
        (shard, groups * HEAD_DIM),
        (shard, groups * HEAD_DIM),
        (shard, experts_all),
        (groups * out_all.shape[1], out_all.shape[2]),
        (here, 2 * width, part),
        (here, part, 2 * width),
        (here, part, 2 * width),
    ]
    operands = (in_all, out_all, *kept, *came, *far)
    return pl.pallas_call(
        functools.partial(finish_kernel, per_group, here),
        out_shape=[jax.ShapeDtypeStruct(shape, F32) for shape in shapes],
        in_specs=in_vmem(len(operands)),
        out_specs=in_vmem(len(shapes)),
        compiler_params=pltpu.CompilerParams(vmem_limit_bytes=VMEM_LIMIT),
        cost_estimate=pl.CostEstimate(flops=0, bytes_accessed=25_000_000, transcendentals=0),
        name="finish",
    )(*operands)


def per_device(
    residual_in, cotangent, gain_attn, w_query, w_key, w_value, w_out, gain_ffn, w_router,
    w_gate, w_up, w_down, route_ids,
):
    me = lax.axis_index("expert")
    line = lax.axis_index("fsdp")
    peers = lax.axis_size("expert")
    lines = lax.axis_size("fsdp")
    tokens, model_width = residual_in.shape[1:]
    length = tokens * peers
    groups = w_key.shape[1] // HEAD_DIM
    per_group = w_query.shape[1] // w_key.shape[1]
    query_width = per_group * HEAD_DIM
    experts_all = w_router.shape[1]
    here = w_gate.shape[0]
    shard = w_query.shape[0]
    turned = query_width + HEAD_DIM
    router_at = turned
    lane_of = HEAD_DIM
    in_width = turned + LANES
    paired = lines == 4 and peers == 8

    w_in_shard = jnp.concatenate(
        [
            lax.dynamic_slice(w_query, (0, me * query_width), (shard, query_width)),
            lax.dynamic_slice(w_key, (0, me * HEAD_DIM), (shard, HEAD_DIM)),
            lax.dynamic_slice(w_value, (0, me * HEAD_DIM), (shard, HEAD_DIM)),
            w_router,
            jnp.zeros((shard, in_width - turned - HEAD_DIM - experts_all), BF16),
        ],
        axis=1,
    )
    w_out_shard = jnp.concatenate(
        [
            lax.dynamic_slice(w_out, (me * query_width, 0), (query_width, shard)),
            gain_attn[None],
            gain_ffn[None],
            jnp.zeros((14, shard), BF16),
        ],
        axis=0,
    )
    chosen = jnp.any(
        route_ids[0][:, :, None]
        == jnp.arange(LANES, dtype=jnp.int32)[None, None, :] - lane_of,
        axis=1,
    ).astype(F32)
    cosine, sine = rotary_tables(length)
    place = jnp.full((1,), me * here + lane_of, jnp.int32)
    own_rows, own_grad = residual_in[0], cotangent[0]
    wide = (peers, tokens, model_width)

    if paired:
        x_all, dy_all, w_in, w_out_rows = open_transfers(
            own_rows, own_grad, w_in_shard, w_out_shard, lines, 0
        )
    else:
        x_all, dy_all = plane_gather([own_rows, own_grad], 0)
        w_in, w_out_rows = (
            lax.all_gather(w_in_shard, "fsdp", axis=0, tiled=True),
            lax.all_gather(w_out_shard, "fsdp", axis=1, tiled=True),
        )
    part, *saved = attend(
        x_all.reshape(length, model_width), w_in, w_out_rows, cosine, sine, per_group
    )
    if paired:
        b_all, g_all, middle, marked = middle_transfers(
            part.reshape(wide), own_rows, w_in, w_out_rows, chosen, query_width, router_at, 1
        )
        sum_part, dw_all, dl_all, grad_middle, gain_two_grad, kept, came, far, others = experts_back(
            b_all, dy_all, g_all, w_gate, w_up, w_down, middle, marked, w_in, w_out_rows,
            lane_of, query_width, router_at, 2,
        )
        early = [array for given in others[:-1] for array in given]
        da_part, grad_in, out_low, e_own, e_total, *crossed = attend_back(
            dw_all.reshape(length, model_width), w_in, w_out_rows, cosine, sine, saved,
            b_all.reshape(2 * length, model_width), dl_all.reshape(length, LANES), per_group,
            (sum_part, early), 4,
        )
        outcome, grad_input, in_all, out_all, gains_all, notes_all, *crossed_last = close_transfers(
            da_part.reshape(wide), e_own, e_total, own_rows, middle, grad_middle, gain_two_grad,
            w_out_rows, grad_in.reshape(lines, shard, in_width), out_low, others[-1],
            query_width, 3,
        )
        squares = jnp.sum(notes_all, axis=0)[:5, 0]
        query, key, value, router_grad, proj, down, gate, up = finish(
            in_all, out_all, kept, came, [*far, *crossed, *crossed_last], per_group, experts_all
        )
        reduced = [gate, up, down]
        gain_rows = jnp.sum(gains_all[:, :2].astype(F32), axis=0)
    else:
        (branch,) = plane_scatter([part.reshape(wide)], 1)
        gain_one = w_out_rows[query_width][None].astype(F32)
        gain_two = w_out_rows[query_width + 1][None].astype(F32)
        router = w_in[:, router_at:]
        rows = own_rows.astype(F32)
        inverse_one = lax.rsqrt(jnp.mean(rows * rows, axis=-1, keepdims=True) + EPSILON)
        normed_one = rows * inverse_one
        middle = rows + RESIDUAL_SCALE * branch
        inverse_two = lax.rsqrt(jnp.mean(middle * middle, axis=-1, keepdims=True) + EPSILON)
        normed_two = middle * inverse_two
        routed = (normed_two * gain_two).astype(BF16)
        logits = jnp.where(chosen > 0, dot(routed, router), -1e30)
        lifted = jnp.exp(logits - jnp.max(logits, axis=-1, keepdims=True))
        lifted = jnp.where(chosen > 0, lifted, 0.0)
        gates = lifted / jnp.sum(lifted, axis=-1, keepdims=True)
        b_all, g_all = plane_gather([routed, jnp.where(chosen > 0, gates, -1.0)], 2)
        sum_part, db_part, dg_part, *grads = experts(
            place, b_all, dy_all, g_all, w_gate, w_up, w_down
        )
        db_sum, dg_sum = plane_scatter([db_part, dg_part], 3)
        grad_rows = own_grad.astype(F32)
        grad_chosen = gates * (dg_sum - jnp.sum(gates * dg_sum, axis=-1, keepdims=True))
        grad_logits = grad_chosen.astype(BF16)
        grad_routed = dot(grad_logits, router, (1, 1)) + db_sum
        grad_gain_two = jnp.sum(grad_routed * normed_two, axis=0)
        grad_middle = grad_rows + norm_back(grad_routed * gain_two, normed_two, inverse_two)
        grad_branch = (RESIDUAL_SCALE * grad_middle).astype(BF16)
        dw_all, dl_all = plane_gather([grad_branch, grad_logits], 4)
        da_part, grad_in, grad_out = attend_back(
            dw_all.reshape(length, model_width), w_in, w_out_rows, cosine, sine, saved,
            b_all.reshape(length, model_width), dl_all.reshape(length, LANES), per_group,
        )
        da_sum, expert_sum = plane_scatter([da_part.reshape(wide), sum_part], 5)
        outcome = middle + expert_sum
        grad_gain_one = jnp.sum(da_sum * normed_one, axis=0)
        grad_input = grad_middle + norm_back(da_sum * gain_one, normed_one, inverse_one)
        squares = lax.psum(
            jnp.stack(
                [jnp.sum(v * v) for v in (rows, middle, outcome, grad_middle, grad_input)]
            ),
            ("fsdp", "expert"),
        )
        in_sum = lax.psum_scatter(grad_in, "fsdp", scatter_dimension=0, tiled=True)
        out_sum = lax.psum_scatter(
            grad_out.transpose(1, 0, 2).reshape(query_width, model_width), "fsdp",
            scatter_dimension=1, tiled=True,
        )
        gain_rows = lax.psum_scatter(
            lax.psum(jnp.stack([grad_gain_one, grad_gain_two]), "expert"),
            "fsdp", scatter_dimension=1, tiled=True,
        )
        in_all = lax.all_gather(in_sum, "expert", axis=0)
        out_all = lax.all_gather(out_sum, "expert", axis=0)
        outcome, grad_input = outcome.astype(BF16), grad_input.astype(BF16)
        grads = [
            grads[0].transpose(1, 0, 2, 3).reshape(w_gate.shape),
            grads[1].transpose(1, 0, 2, 3).reshape(w_up.shape),
            grads[2].transpose(1, 2, 0, 3).reshape(w_down.shape),
        ]
        reduced = [
            lax.psum_scatter(array, "fsdp", scatter_dimension=axis, tiled=True).astype(F32)
            for array, axis in zip(grads, (1, 1, 2))
        ]

        def columns_of(start, stop):
            return in_all[:, :, start:stop].transpose(1, 0, 2).reshape(shard, -1).astype(F32)

        query, key = columns_of(0, query_width), columns_of(query_width, turned)
        value = columns_of(turned, turned + HEAD_DIM)
        proj = out_all.reshape(groups * query_width, shard).astype(F32)
        at = turned + HEAD_DIM
        router_grad = in_all[0, :, at : at + experts_all].astype(F32)

    root_means = jnp.sqrt(squares / (tokens * model_width * lines * peers))
    return (
        outcome[None],
        grad_input[None],
        gain_rows[0],
        query,
        key,
        value,
        proj,
        gain_rows[1],
        router_grad,
        reduced[0],
        reduced[1],
        reduced[2],
        root_means,
    )


def solution(mesh):
    in_specs = (
        P("fsdp", "expert", None),
        P("fsdp", "expert", None),
        P("fsdp"),
        P("fsdp", None),
        P("fsdp", None),
        P("fsdp", None),
        P(None, "fsdp"),
        P("fsdp"),
        P("fsdp", None),
        P("expert", None, None),
        P("expert", None, None),
        P("expert", None, None),
        P("fsdp", "expert", None),
    )
    out_specs = (
        P("fsdp", "expert", None),
        P("fsdp", "expert", None),
        P("fsdp"),
        P("fsdp", None),
        P("fsdp", None),
        P("fsdp", None),
        P(None, "fsdp"),
        P("fsdp"),
        P("fsdp", None),
        P("expert", "fsdp", None),
        P("expert", "fsdp", None),
        P("expert", None, "fsdp"),
        P(),
    )
    return jax.shard_map(
        per_device, mesh=mesh, in_specs=in_specs, out_specs=out_specs, check_vma=False
    )
```

```python
import functools

import jax
import jax.numpy as jnp
from jax import lax
from jax.experimental import pallas as pl
from jax.experimental.pallas import tpu as pltpu
from jax.sharding import PartitionSpec as P

HEAD_DIM = 64
BLOCK = 256

EPSILON = 1e-06
RESIDUAL_SCALE = 0.22
ATTENTION_SCALE = 0.015625
ROPE_BASE = 10000.0
HIGHEST = lax.Precision.HIGHEST
MESH = pl.DeviceIdType.MESH
VMEM_LIMIT = 63_000_000
F32 = jnp.float32
BF16 = jnp.bfloat16
LANES = 128


def plane_neighbours():
    me = lax.axis_index("expert")
    core = lax.rem(me, 2)
    x_bit = lax.rem(me // 2, 2)
    y_bit = me // 4
    sibling = me + 1 - 2 * core
    x_peer = me + 2 - 4 * x_bit
    y_peer = me + 4 - 8 * y_bit
    diagonal = x_peer + 4 - 8 * y_bit
    return me, core, x_bit, y_bit, sibling, x_peer, y_peer, diagonal


def greet(axis, peers):
    barrier = pltpu.get_barrier_semaphore()
    for peer in peers:
        pl.semaphore_signal(barrier, inc=1, device_id={axis: peer}, device_id_type=MESH)
    pl.semaphore_wait(barrier, len(peers))


def gather_kernel(count, *refs):
    ins, outs = refs[:count], refs[count : 2 * count]
    own_sem, send_sem, recv_sem = refs[2 * count :]
    me, _, _, _, sibling, x_peer, y_peer, diagonal = plane_neighbours()
    greet("expert", (sibling, x_peer, y_peer))

    def remote(k, slot, source, target, peer):
        return pltpu.make_async_remote_copy(
            src_ref=source,
            dst_ref=target,
            send_sem=send_sem.at[k, slot],
            recv_sem=recv_sem.at[k, slot],
            device_id={"expert": peer},
            device_id_type=MESH,
        )

    plans = []
    for k in range(count):
        half = ins[k].shape[0] // 2
        parts = (pl.ds(0, half), pl.ds(half, half))
        out = outs[k]
        own = pltpu.make_async_copy(ins[k], out.at[me], own_sem.at[k])
        copies = [remote(k, 0, ins[k], out.at[me], sibling)]
        for h in range(2):
            copies.append(remote(k, 1 + h, ins[k].at[parts[h]], out.at[me, parts[h]], x_peer))
        for h in range(2):
            copies.append(remote(k, 3 + h, ins[k].at[parts[h]], out.at[me, parts[h]], y_peer))

        def forward(slot, block, h, peer):
            return remote(k, slot, out.at[block, parts[h]], out.at[block, parts[h]], peer)

        copies.append(forward(5, y_peer, 0, x_peer))
        copies.append(forward(6, x_peer, 1, y_peer))
        for h in range(2):
            copies.append(forward(7 + h, x_peer, h, sibling))
        for h in range(2):
            copies.append(forward(9 + h, y_peer, h, sibling))
        for h in range(2):
            copies.append(forward(11 + h, diagonal, h, sibling))
        plans.append((own, copies))
    for own, copies in plans:
        for slot in (3, 2, 1, 4, 0):
            copies[slot].start()
        own.start()
    for own, copies in plans:
        copies[3].wait_recv()
        copies[5].start()
        copies[2].wait_recv()
        copies[6].start()
        copies[9].start()
        copies[8].start()
        copies[1].wait_recv()
        copies[7].start()
        copies[4].wait_recv()
        copies[10].start()
    for own, copies in plans:
        copies[5].wait_recv()
        copies[11].start()
        copies[6].wait_recv()
        copies[12].start()
    for own, copies in plans:
        for slot in (0, 7, 8, 9, 10, 11, 12):
            copies[slot].wait_recv()
        for copy in copies:
            copy.wait_send()
        own.wait()


def plane_gather(arrays, collective_id):
    if lax.axis_size("expert") != 8:
        return [lax.all_gather(array, "expert", axis=0) for array in arrays]
    count = len(arrays)
    size = sum(array.size * array.dtype.itemsize for array in arrays)
    return pl.pallas_call(
        functools.partial(gather_kernel, count),
        out_shape=[jax.ShapeDtypeStruct((8,) + array.shape, array.dtype) for array in arrays],
        in_specs=[pl.BlockSpec(memory_space=pltpu.VMEM)] * count,
        out_specs=[pl.BlockSpec(memory_space=pl.ANY)] * count,
        scratch_shapes=[
            pltpu.SemaphoreType.DMA((count,)),
            pltpu.SemaphoreType.DMA((count, 13)),
            pltpu.SemaphoreType.DMA((count, 13)),
        ],
        compiler_params=pltpu.CompilerParams(
            collective_id=collective_id, has_side_effects=True, vmem_limit_bytes=VMEM_LIMIT
        ),
        cost_estimate=pl.CostEstimate(flops=0, bytes_accessed=16 * size, transcendentals=0),
        name="plane_gather",
    )(*arrays)


def scatter_kernel(count, *refs):
    ins, outs = refs[:count], refs[count : 2 * count]
    scratch = refs[2 * count : 2 * count + 6 * count]
    send_sem, recv_sem = refs[8 * count :]
    me, core, x_bit, y_bit, sibling, x_peer, y_peer, diagonal = plane_neighbours()
    greet("expert", (sibling, x_peer, y_peer))
    chip = me // 2
    chip_x, chip_y, chip_d = x_peer // 2, y_peer // 2, diagonal // 2
    order = (chip_d, chip_x, chip_y, chip)

    def remote(k, slot, source, target, peer):
        return pltpu.make_async_remote_copy(
            src_ref=source,
            dst_ref=target,
            send_sem=send_sem.at[k, slot],
            recv_sem=recv_sem.at[k, slot],
            device_id={"expert": peer},
            device_id_type=MESH,
        )

    stage0 = []
    for k in range(count):
        pair = scratch[6 * k]
        copies = [
            remote(k, i, ins[k].at[2 * order[i] + 1 - core], pair.at[i], sibling) for i in range(4)
        ]
        stage0.append(copies)
        for copy in copies:
            copy.start()
    later = []
    for k in range(count):
        pair, sums, first_x, first_y, second_x, second_y = scratch[6 * k : 6 * k + 6]
        rows = ins[k].shape[1]
        half = rows // 2
        parts = (pl.ds(0, half), pl.ds(half, half))
        dtype = ins[k].dtype

        def join(i):
            stage0[k][i].wait_recv()
            sums[i] = (ins[k][2 * order[i] + core].astype(F32) + pair[i].astype(F32)).astype(dtype)

        join(0)
        copies = [
            remote(k, 4, sums.at[0, parts[0]], first_x.at[1], x_peer),
            remote(k, 5, sums.at[0, parts[1]], first_y.at[1], y_peer),
        ]
        for copy in copies:
            copy.start()
        join(1)
        copies.append(remote(k, 6, sums.at[1, parts[0]], first_x.at[0], x_peer))
        copies[-1].start()
        join(2)
        copies.append(remote(k, 7, sums.at[2, parts[1]], first_y.at[0], y_peer))
        copies[-1].start()
        join(3)
        later.append(copies)
    for k in range(count):
        pair, sums, first_x, first_y, second_x, second_y = scratch[6 * k : 6 * k + 6]
        half = ins[k].shape[1] // 2
        parts = (pl.ds(0, half), pl.ds(half, half))
        dtype = ins[k].dtype
        copies = later[k]
        copies[0].wait_recv()
        pair[0, parts[0]] = (
            sums[2, parts[0]].astype(F32) + first_x[1].astype(F32)
        ).astype(dtype)
        copies.append(remote(k, 8, pair.at[0, parts[0]], second_y, y_peer))
        copies[-1].start()
        copies[1].wait_recv()
        pair[0, parts[1]] = (
            sums[1, parts[1]].astype(F32) + first_y[1].astype(F32)
        ).astype(dtype)
        copies.append(remote(k, 9, pair.at[0, parts[1]], second_x, x_peer))
        copies[-1].start()
    for k in range(count):
        pair, sums, first_x, first_y, second_x, second_y = scratch[6 * k : 6 * k + 6]
        half = ins[k].shape[1] // 2
        parts = (pl.ds(0, half), pl.ds(half, half))
        copies = later[k]
        copies[2].wait_recv()
        copies[4].wait_recv()
        outs[k][parts[0]] = (
            sums[3, parts[0]].astype(F32) + first_x[0].astype(F32) + second_y[...].astype(F32)
        )
        copies[3].wait_recv()
        copies[5].wait_recv()
        outs[k][parts[1]] = (
            sums[3, parts[1]].astype(F32) + first_y[0].astype(F32) + second_x[...].astype(F32)
        )
        for copy in stage0[k] + copies:
            copy.wait_send()


def plane_scatter(arrays, collective_id):
    if lax.axis_size("expert") != 8:
        return [
            lax.psum_scatter(array, "expert", scatter_dimension=0, tiled=False).astype(F32)
            for array in arrays
        ]
    count = len(arrays)
    scratch = []
    for array in arrays:
        _, rows, columns = array.shape
        half = rows // 2
        for shape in (
            (4, rows, columns),
            (4, rows, columns),
            (2, half, columns),
            (2, half, columns),
            (half, columns),
            (half, columns),
        ):
            scratch.append(pltpu.VMEM(shape, array.dtype))
    size = sum(array.size * array.dtype.itemsize for array in arrays)
    return pl.pallas_call(
        functools.partial(scatter_kernel, count),
        out_shape=[jax.ShapeDtypeStruct(array.shape[1:], F32) for array in arrays],
        in_specs=[pl.BlockSpec(memory_space=pltpu.VMEM)] * count,
        out_specs=[pl.BlockSpec(memory_space=pltpu.VMEM)] * count,
        scratch_shapes=scratch
        + [pltpu.SemaphoreType.DMA((count, 10)), pltpu.SemaphoreType.DMA((count, 10))],
        compiler_params=pltpu.CompilerParams(
            collective_id=collective_id, has_side_effects=True, vmem_limit_bytes=VMEM_LIMIT
        ),
        cost_estimate=pl.CostEstimate(flops=0, bytes_accessed=3 * size, transcendentals=0),
        name="plane_scatter",
    )(*arrays)


def push(source, target, send_sem, recv_sem, axis, peer):
    return pltpu.make_async_remote_copy(
        src_ref=source,
        dst_ref=target,
        send_sem=send_sem,
        recv_sem=recv_sem,
        device_id={axis: peer},
        device_id_type=MESH,
    )


def meet(plane, line, size, with_line):
    barrier = pltpu.get_barrier_semaphore()
    me, _, _, _, sibling, x_peer, y_peer, _ = plane
    for peer in (sibling, x_peer, y_peer):
        pl.semaphore_signal(barrier, inc=1, device_id={"expert": peer}, device_id_type=MESH)
    pl.semaphore_signal(
        barrier, inc=1, device_id={"fsdp": pair_of(line)}, device_id_type=MESH
    )
    if not with_line:
        pl.semaphore_signal(
            barrier, inc=1, device_id={"fsdp": beside(line)}, device_id_type=MESH
        )
        pl.semaphore_wait(barrier, 5)
        return

    @pl.when(line > 0)
    def _():
        pl.semaphore_signal(barrier, inc=1, device_id={"fsdp": line - 1}, device_id_type=MESH)

    @pl.when(line < size - 1)
    def _():
        pl.semaphore_signal(barrier, inc=1, device_id={"fsdp": line + 1}, device_id_type=MESH)

    @pl.when((line > 0) & (line < size - 1))
    def _():
        pl.semaphore_wait(barrier, 6)

    @pl.when((line == 0) | (line == size - 1))
    def _():
        pl.semaphore_wait(barrier, 5)


def pair_of(line):
    return line + 2 - 4 * (line // 2)


def beside(line):
    return line + 1 - 2 * lax.rem(line, 2)


def norm_back(grad_normed, normed, inverse):
    return inverse * (grad_normed - normed * jnp.mean(grad_normed * normed, axis=-1, keepdims=True))


class Gather:
    def __init__(self, plane, k, source, out, base, own_sem, send_sem, recv_sem):
        me, _, _, _, sibling, x_peer, y_peer, diagonal = plane
        half = source.shape[0] // 2
        parts = (pl.ds(0, half), pl.ds(half, half))

        def copy(slot, src, dst, peer):
            return push(src, dst, send_sem.at[k, slot], recv_sem.at[k, slot], "expert", peer)

        def forward(slot, block, h, peer):
            ref = out.at[base + block, parts[h]]
            return copy(slot, ref, ref, peer)

        self.own = pltpu.make_async_copy(source, out.at[base + me], own_sem.at[k])
        copies = [copy(0, source, out.at[base + me], sibling)]
        for slot, peer in ((1, x_peer), (3, y_peer)):
            for h in range(2):
                copies.append(
                    copy(slot + h, source.at[parts[h]], out.at[base + me, parts[h]], peer)
                )
        copies.append(forward(5, y_peer, 0, x_peer))
        copies.append(forward(6, x_peer, 1, y_peer))
        for slot, block in ((7, x_peer), (9, y_peer), (11, diagonal)):
            for h in range(2):
                copies.append(forward(slot + h, block, h, sibling))
        self.copies = copies

    def begin(self):
        for slot in (3, 2, 1, 4, 0):
            self.copies[slot].start()
        self.own.start()

    def relay(self):
        copies = self.copies
        for landed, onward in ((3, (5, 9)), (2, (6, 8)), (1, (7,)), (4, (10,))):
            copies[landed].wait_recv()
            for slot in onward:
                copies[slot].start()

    def relay_diagonal(self):
        for landed, onward in ((5, 11), (6, 12)):
            self.copies[landed].wait_recv()
            self.copies[onward].start()

    def finish(self):
        for slot in (0, 7, 8, 9, 10, 11, 12):
            self.copies[slot].wait_recv()
        for copy in self.copies:
            copy.wait_send()
        self.own.wait()


def gather_sems(count):
    return [
        pltpu.SemaphoreType.DMA((count,)),
        pltpu.SemaphoreType.DMA((count, 13)),
        pltpu.SemaphoreType.DMA((count, 13)),
    ]


class Scatter:
    def __init__(self, plane, k, source, base, scratch, send_sem, recv_sem):
        me, core, _, _, sibling, x_peer, y_peer, diagonal = plane
        self.source, self.base, self.core = source, base, core
        self.pair, self.first_x, self.first_y, self.second_x, self.second_y = scratch[:5]
        self.order = (diagonal // 2, x_peer // 2, y_peer // 2, me // 2)
        self.sums = [
            scratch[5].at[i] if len(scratch) > 5 else source.at[base + 2 * self.order[i] + core]
            for i in range(4)
        ]
        self.dtype = source.dtype
        half = source.shape[1] // 2
        self.parts = parts = (pl.ds(0, half), pl.ds(half, half))

        def copy(slot, src, dst, peer):
            return push(src, dst, send_sem.at[k, slot], recv_sem.at[k, slot], "expert", peer)

        self.stage0 = [
            copy(i, source.at[base + 2 * self.order[i] + 1 - core], self.pair.at[i], sibling)
            for i in range(4)
        ]
        self.stage1 = [
            copy(4, self.sums[0].at[parts[0]], self.first_x.at[1], x_peer),
            copy(5, self.sums[0].at[parts[1]], self.first_y.at[1], y_peer),
            copy(6, self.sums[1].at[parts[0]], self.first_x.at[0], x_peer),
            copy(7, self.sums[2].at[parts[1]], self.first_y.at[0], y_peer),
        ]
        self.stage2 = [
            copy(8, self.pair.at[0, parts[0]], self.second_y, y_peer),
            copy(9, self.pair.at[0, parts[1]], self.second_x, x_peer),
        ]

    def begin(self):
        for copy in self.stage0:
            copy.start()

    def join(self, i):
        self.stage0[i].wait_recv()
        mine = self.source[self.base + 2 * self.order[i] + self.core]
        self.sums[i][...] = (mine.astype(F32) + self.pair[i].astype(F32)).astype(self.dtype)

    def first(self):
        self.join(0)
        self.stage1[0].start()
        self.stage1[1].start()
        self.join(1)
        self.stage1[2].start()
        self.join(2)
        self.stage1[3].start()
        self.join(3)

    def second(self):
        for h, block, landed in ((0, 2, self.first_x), (1, 1, self.first_y)):
            self.stage1[h].wait_recv()
            rows = self.parts[h]
            self.pair[0, rows] = (
                self.sums[block][rows].astype(F32) + landed[1].astype(F32)
            ).astype(self.dtype)
            self.stage2[h].start()

    def total(self, h):
        self.stage1[2 + h].wait_recv()
        self.stage2[h].wait_recv()
        near, far = ((self.first_x, self.second_y), (self.first_y, self.second_x))[h]
        return (
            self.sums[3][self.parts[h]].astype(F32)
            + near[0].astype(F32)
            + far[...].astype(F32)
        )

    def finish(self):
        for copy in self.stage0 + self.stage1 + self.stage2:
            copy.wait_send()


def scatter_scratch(rows, columns, dtype, in_place=False):
    half = rows // 2
    shapes = [
        (4, rows, columns),
        (2, half, columns),
        (2, half, columns),
        (half, columns),
        (half, columns),
        (4, rows, columns),
    ]
    return [pltpu.VMEM(shape, dtype) for shape in shapes[: 5 if in_place else 6]]


def scatter_sems(count):
    return [pltpu.SemaphoreType.DMA((count, 10)), pltpu.SemaphoreType.DMA((count, 10))]


class LineGather:
    def __init__(self, line, size, k, source, out, axis, own_sem, send_sem, recv_sem):
        self.line, self.size, self.k, self.source, self.out = line, size, k, source, out
        self.axis, self.send_sem, self.recv_sem = axis, send_sem, recv_sem
        self.own = pltpu.make_async_copy(source, self.place(line), own_sem.at[k])

    def place(self, owner):
        extent = self.source.shape[self.axis]
        span = pl.ds(pl.multiple_of(owner * extent, extent), extent)
        return self.out.at[span] if self.axis == 0 else self.out.at[:, span]

    def hop(self, side, step, owner, source=None):
        target = self.place(owner)
        return push(
            target if source is None else source,
            target,
            self.send_sem.at[self.k, side, step],
            self.recv_sem.at[self.k, side, step],
            "fsdp",
            self.line + 1 - 2 * side,
        )

    def begin(self):
        for side, there in ((0, self.line < self.size - 1), (1, self.line > 0)):

            @pl.when(there)
            def _():
                self.hop(side, 0, self.line, self.source).start()

        self.own.start()

    def step(self, step):
        line, last = self.line, self.size - 1
        for side, owner in ((0, line - 1 - step), (1, line + 1 + step)):

            @pl.when((owner >= 0) & (owner <= last))
            def _():
                self.hop(side, step, owner).wait_recv()

                @pl.when((line < last) if side == 0 else (line > 0))
                def _():
                    self.hop(side, step + 1, owner).start()

    def finish(self):
        line, last = self.line, self.size - 1
        self.own.wait()
        for step in range(self.size - 1):
            for side, owner, there in ((0, line - step, line < last), (1, line + step, line > 0)):

                @pl.when(there & (owner >= 0) & (owner <= last))
                def _():
                    self.hop(side, step, owner).wait_send()


def line_gather_sems(count, size):
    return [
        pltpu.SemaphoreType.DMA((count,)),
        pltpu.SemaphoreType.DMA((count, 2, size)),
        pltpu.SemaphoreType.DMA((count, 2, size)),
    ]


class LineScatter:
    def __init__(self, line, size, k, source, sums, landed, send_sem, recv_sem):
        self.line, self.size, self.k = line, size, k
        self.source, self.sums, self.landed = source, sums, landed
        self.send_sem, self.recv_sem = send_sem, recv_sem

    def hop(self, side, owner):
        return push(
            self.sums.at[side, owner],
            self.landed.at[side, owner],
            self.send_sem.at[self.k, side, owner],
            self.recv_sem.at[self.k, side, owner],
            "fsdp",
            self.line + 1 - 2 * side,
        )

    def begin(self):
        last = self.size - 1
        for far in range(last):
            for side, owner, end in ((0, last - far, 0), (1, far, last)):

                @pl.when(self.line == end)
                def _():
                    self.sums[side, owner] = self.source[owner]
                    self.hop(side, owner).start()

    def pass_on(self, side, owner):
        self.hop(side, owner).wait_recv()
        self.sums[side, owner] = (
            self.source[owner].astype(F32) + self.landed[side, owner].astype(F32)
        ).astype(self.source.dtype)
        self.hop(side, owner).start()

    def step(self, far):
        line, last = self.line, self.size - 1

        @pl.when((line < last - far) & (line > 0))
        def _():
            self.pass_on(0, last - far)

        @pl.when((line > far) & (line < last))
        def _():
            self.pass_on(1, far)

    def total(self):
        line, last = self.line, self.size - 1
        for side, there, beyond in ((0, line > 0, line == 0), (1, line < last, line == last)):

            @pl.when(there)
            def _():
                self.hop(side, line).wait_recv()

            @pl.when(beyond)
            def _():
                self.landed[side, line] = jnp.zeros(self.source.shape[1:], self.source.dtype)

        return (
            self.source[line].astype(F32)
            + self.landed[0, line].astype(F32)
            + self.landed[1, line].astype(F32)
        )

    def finish(self):
        for owner in range(self.size):

            @pl.when(self.line < owner)
            def _():
                self.hop(0, owner).wait_send()

            @pl.when(self.line > owner)
            def _():
                self.hop(1, owner).wait_send()


def line_scatter_sems(count, size):
    return [
        pltpu.SemaphoreType.DMA((count, 2, size)),
        pltpu.SemaphoreType.DMA((count, 2, size)),
    ]


def in_vmem(count):
    return [pl.BlockSpec(memory_space=pltpu.VMEM)] * count


def anywhere(count):
    return [pl.BlockSpec(memory_space=pl.ANY)] * count


def talk_params(collective_id):
    return pltpu.CompilerParams(
        collective_id=collective_id, has_side_effects=True, vmem_limit_bytes=VMEM_LIMIT
    )


def open_kernel(
    size, x_ref, dy_ref, win_ref, wout_ref,
    x_out, dy_out, win_out, wout_out,
    landed, swap_sems, own_sem, send_sem, recv_sem, line_own, line_send, line_recv,
):
    plane, line = plane_neighbours(), lax.axis_index("fsdp")
    meet(plane, line, size, True)
    swap = push(dy_ref, landed, swap_sems.at[0], swap_sems.at[1], "fsdp", pair_of(line))
    sems = (own_sem, send_sem, recv_sem)
    line_sems = (line_own, line_send, line_recv)
    x = Gather(plane, 0, x_ref, x_out, 0, *sems)
    dy = Gather(plane, 1, dy_ref, dy_out, 0, *sems)
    other = Gather(plane, 2, landed, dy_out, 8, *sems)
    win = LineGather(line, size, 0, win_ref, win_out, 0, *line_sems)
    wout = LineGather(line, size, 1, wout_ref, wout_out, 1, *line_sems)
    win.begin()
    x.begin()
    swap.start()
    wout.begin()
    dy.begin()
    x.relay()
    win.step(0)
    x.relay_diagonal()
    wout.step(0)
    win.step(1)
    dy.relay()
    swap.wait_recv()
    other.begin()
    wout.step(1)
    dy.relay_diagonal()
    win.step(2)
    wout.step(2)
    other.relay()
    other.relay_diagonal()
    for part in (x, dy, other, win, wout):
        part.finish()
    swap.wait_send()


def open_transfers(x, dy, w_in_shard, w_out_shard, size, collective_id):
    tokens, model_width = x.shape
    rows, columns = w_in_shard.shape
    out_rows, out_columns = w_out_shard.shape
    return pl.pallas_call(
        functools.partial(open_kernel, size),
        out_shape=[
            jax.ShapeDtypeStruct((8, tokens, model_width), BF16),
            jax.ShapeDtypeStruct((16, tokens, model_width), BF16),
            jax.ShapeDtypeStruct((rows * size, columns), BF16),
            jax.ShapeDtypeStruct((out_rows, out_columns * size), BF16),
        ],
        in_specs=in_vmem(4),
        out_specs=anywhere(4),
        scratch_shapes=[pltpu.VMEM((tokens, model_width), BF16), pltpu.SemaphoreType.DMA((2,))]
        + gather_sems(3)
        + line_gather_sems(2, size),
        compiler_params=talk_params(collective_id),
        cost_estimate=pl.CostEstimate(flops=0, bytes_accessed=120_000_000, transcendentals=0),
        name="open_transfers",
    )(x, dy, w_in_shard, w_out_shard)


def middle_kernel(
    query_width, router_at, part_ref, x_ref, win_ref, wout_ref, chosen_ref,
    b_out, g_out, middle_ref, marked_ref,
    routed, b_landed, g_landed, *rest,
):
    scratch, rest = rest[:6], rest[6:]
    swap_sems, scatter_send, scatter_recv, own_sem, send_sem, recv_sem = rest
    plane, line = plane_neighbours(), lax.axis_index("fsdp")
    meet(plane, line, 4, False)
    scatter = Scatter(plane, 0, part_ref, 0, scratch, scatter_send, scatter_recv)
    scatter.begin()
    scatter.first()
    scatter.second()
    half = x_ref.shape[0] // 2
    gain = wout_ref[query_width + 1 : query_width + 2, :].astype(F32)
    router = win_ref[:, router_at : router_at + LANES]
    for h in range(2):
        rows = pl.ds(h * half, half)
        middle = x_ref[rows].astype(F32) + RESIDUAL_SCALE * scatter.total(h)
        middle_ref[rows] = middle
        inverse = lax.rsqrt(jnp.mean(middle * middle, axis=1, keepdims=True) + EPSILON)
        b = (middle * inverse * gain).astype(BF16)
        routed[rows] = b
        chosen = chosen_ref[rows] > 0.0
        logits = jnp.where(chosen, dot(b, router), -1e30)
        lifted = jnp.where(chosen, jnp.exp(logits - jnp.max(logits, axis=1, keepdims=True)), 0.0)
        gates = lifted / jnp.sum(lifted, axis=1, keepdims=True)
        marked_ref[rows] = jnp.where(chosen, gates, -1.0)
    swap_b = push(routed, b_landed, swap_sems.at[0], swap_sems.at[1], "fsdp", pair_of(line))
    swap_g = push(marked_ref, g_landed, swap_sems.at[2], swap_sems.at[3], "fsdp", pair_of(line))
    swap_b.start()
    swap_g.start()
    sems = (own_sem, send_sem, recv_sem)
    b = Gather(plane, 0, routed, b_out, 0, *sems)
    g = Gather(plane, 1, marked_ref, g_out, 0, *sems)
    b_other = Gather(plane, 2, b_landed, b_out, 8, *sems)
    g_other = Gather(plane, 3, g_landed, g_out, 8, *sems)
    b.begin()
    g.begin()
    b.relay()
    g.relay()
    b.relay_diagonal()
    g.relay_diagonal()
    swap_b.wait_recv()
    swap_g.wait_recv()
    b_other.begin()
    g_other.begin()
    b_other.relay()
    g_other.relay()
    b_other.relay_diagonal()
    g_other.relay_diagonal()
    for item in (b, g, b_other, g_other, scatter):
        item.finish()
    swap_b.wait_send()
    swap_g.wait_send()


def middle_transfers(part, x, w_in, w_out, chosen, query_width, router_at, collective_id):
    tokens, model_width = x.shape
    return pl.pallas_call(
        functools.partial(middle_kernel, query_width, router_at),
        out_shape=[
            jax.ShapeDtypeStruct((16, tokens, model_width), BF16),
            jax.ShapeDtypeStruct((16, tokens, LANES), F32),
            jax.ShapeDtypeStruct((tokens, model_width), F32),
            jax.ShapeDtypeStruct((tokens, LANES), F32),
        ],
        in_specs=in_vmem(5),
        out_specs=anywhere(2) + in_vmem(2),
        scratch_shapes=[
            pltpu.VMEM((tokens, model_width), BF16),
            pltpu.VMEM((tokens, model_width), BF16),
            pltpu.VMEM((tokens, LANES), F32),
        ]
        + scatter_scratch(tokens, model_width, BF16)
        + [pltpu.SemaphoreType.DMA((4,))]
        + scatter_sems(1)
        + gather_sems(4),
        compiler_params=talk_params(collective_id),
        cost_estimate=pl.CostEstimate(flops=0, bytes_accessed=150_000_000, transcendentals=0),
        name="middle_transfers",
    )(part, x, w_in, w_out, chosen)


def close_kernel(
    size, query_width, da_ref, e_own, e_total, x_ref, middle_ref, grad_ref,
    gain_two_ref, wout_ref, gin_ref, out_low,
    outcome_ref, input_grad_ref, in_out, out_out, gains_out, notes_out,
    e_landed, gains, notes, notes_line, in_low, gain_low, notes_low, *rest,
):
    scratch, rest = rest[:6], rest[6:]
    line_scratch, rest = rest[:4], rest[4:]
    (
        swap_sems, scatter_send, scatter_recv, sum_send, sum_recv,
        line_own, line_send, line_recv, own_sem, send_sem, recv_sem,
    ) = rest
    plane, line = plane_neighbours(), lax.axis_index("fsdp")
    meet(plane, line, size, True)
    sums = (scatter_send, scatter_recv)
    da = Scatter(plane, 0, da_ref, 0, scratch[:6], *sums)
    swap = push(e_total, e_landed, swap_sems.at[0], swap_sems.at[1], "fsdp", pair_of(line))
    gin = LineScatter(line, size, 0, gin_ref, *line_scratch[0:2], sum_send, sum_recv)
    gain = LineScatter(line, size, 1, gains, *line_scratch[2:4], sum_send, sum_recv)
    gathers = (own_sem, send_sem, recv_sem)
    out_all = Gather(plane, 1, out_low, out_out, 0, *gathers)
    half = x_ref.shape[0] // 2
    gin.begin()
    da.begin()
    da.first()
    gin.step(0)
    swap.start()
    da.second()
    gin.step(1)
    gin.step(2)
    out_all.begin()
    gain_one = wout_ref[query_width : query_width + 1, :].astype(F32)
    grad_gain = jnp.zeros((1, x_ref.shape[1]), F32)
    squares = [jnp.zeros((1, 1), F32)] * 5

    def add_square(i, values):
        squares[i] = squares[i] + jnp.sum(
            jnp.sum(values * values, axis=1, keepdims=True), axis=0, keepdims=True
        )

    for h in range(2):
        rows = pl.ds(h * half, half)
        x = x_ref[rows].astype(F32)
        inverse = lax.rsqrt(jnp.mean(x * x, axis=1, keepdims=True) + EPSILON)
        normed = x * inverse
        grad_a = da.total(h)
        grad_gain += jnp.sum(grad_a * normed, axis=0, keepdims=True)
        grad_middle = grad_ref[rows]
        grad_input = grad_middle + norm_back(grad_a * gain_one, normed, inverse)
        input_grad_ref[rows] = grad_input.astype(BF16)
        add_square(0, x)
        add_square(1, middle_ref[rows])
        add_square(3, grad_middle)
        add_square(4, grad_input)
    width = x_ref.shape[1] // size
    row = lax.broadcasted_iota(jnp.int32, gains.shape[1:], 0)
    for p in range(size):
        columns = slice(p * width, (p + 1) * width)
        gains[p] = jnp.where(
            row == 0, grad_gain[:, columns],
            jnp.where(row == 1, gain_two_ref[0:1, columns], 0.0),
        ).astype(BF16)
    gain.begin()
    gain.step(0)
    gain.step(1)
    gain.step(2)
    out_all.relay()
    swap.wait_recv()
    for h in range(2):
        rows = pl.ds(h * half, half)
        outcome = middle_ref[rows] + e_own[rows] + e_landed[rows].astype(F32)
        outcome_ref[rows] = outcome.astype(BF16)
        add_square(2, outcome)
    row = lax.broadcasted_iota(jnp.int32, notes.shape, 0)
    told = jnp.zeros(notes.shape, F32)
    for i in range(5):
        told = jnp.where(row == i, squares[i], told)
    notes[...] = told
    spread = LineGather(line, size, 0, notes, notes_line, 0, line_own, line_send, line_recv)
    spread.begin()
    in_low[...] = gin.total().astype(BF16)
    in_all = Gather(plane, 0, in_low, in_out, 0, *gathers)
    in_all.begin()
    spread.step(0)
    out_all.relay_diagonal()
    spread.step(1)
    spread.step(2)
    gain_low[...] = gain.total().astype(BF16)
    gain_all = Gather(plane, 2, gain_low, gains_out, 0, *gathers)
    gain_all.begin()
    spread.finish()
    count = notes.shape[0]
    notes_low[...] = (
        notes_line[pl.ds(0, count)] + notes_line[pl.ds(count, count)]
        + notes_line[pl.ds(2 * count, count)] + notes_line[pl.ds(3 * count, count)]
    )
    notes_all = Gather(plane, 3, notes_low, notes_out, 0, *gathers)
    notes_all.begin()
    last = (in_all, gain_all, notes_all)
    for item in last:
        item.relay()
    for item in last:
        item.relay_diagonal()
    for item in last + (out_all, da, gin, gain):
        item.finish()
    swap.wait_send()


def close_transfers(
    da_part, e_own, e_total, x, middle, grad_middle, gain_two, w_out, grad_in, out_low,
    query_width, collective_id,
):
    tokens, model_width = x.shape
    size, in_rows, in_columns = grad_in.shape
    out_rows, out_columns = out_low.shape
    wide = (tokens, model_width)
    gain_shape, note_shape = (16, out_columns), (16, LANES)
    line_scratch = []
    for shape in (grad_in.shape, (size,) + gain_shape):
        line_scratch += [pltpu.VMEM((2,) + shape, BF16)] * 2
    return pl.pallas_call(
        functools.partial(close_kernel, size, query_width),
        out_shape=[
            jax.ShapeDtypeStruct(wide, BF16),
            jax.ShapeDtypeStruct(wide, BF16),
            jax.ShapeDtypeStruct((8, in_rows, in_columns), BF16),
            jax.ShapeDtypeStruct((8, out_rows, out_columns), BF16),
            jax.ShapeDtypeStruct((8,) + gain_shape, BF16),
            jax.ShapeDtypeStruct((8,) + note_shape, F32),
        ],
        in_specs=in_vmem(10),
        out_specs=in_vmem(2) + anywhere(4),
        scratch_shapes=[
            pltpu.VMEM(wide, BF16),
            pltpu.VMEM((size,) + gain_shape, BF16),
            pltpu.VMEM(note_shape, F32),
            pltpu.VMEM((size * note_shape[0], LANES), F32),
            pltpu.VMEM((in_rows, in_columns), BF16),
            pltpu.VMEM(gain_shape, BF16),
            pltpu.VMEM(note_shape, F32),
        ]
        + scatter_scratch(*wide, BF16)
        + line_scratch
        + [pltpu.SemaphoreType.DMA((2,))]
        + scatter_sems(1)
        + line_scatter_sems(2, size)
        + line_gather_sems(1, size)
        + gather_sems(4),
        compiler_params=talk_params(collective_id),
        cost_estimate=pl.CostEstimate(flops=0, bytes_accessed=200_000_000, transcendentals=0),
        name="close_transfers",
    )(da_part, e_own, e_total, x, middle, grad_middle, gain_two, w_out, grad_in, out_low)


def dot(first, second, contract=(1, 0)):
    return lax.dot_general(
        first, second, (((contract[0],), (contract[1],)), ((), ())), preferred_element_type=F32
    )


def spin(values, cosine, sine):
    width = values.shape[1]
    half = HEAD_DIM // 2
    cosine = jnp.concatenate([cosine] * (width // LANES), axis=1)
    sine = jnp.concatenate([sine] * (width // LANES), axis=1)
    lane = lax.broadcasted_iota(jnp.int32, values.shape, 1)
    lower = lax.rem(lane, HEAD_DIM) < half
    swapped = jnp.where(
        lower, pltpu.roll(values, width - half, 1), pltpu.roll(values, half, 1)
    )
    return values * cosine + swapped * sine


def attend_kernel(
    per_group, x_ref, w_in_ref, w_out_ref, cos_ref, sin_ref,
    part_ref, a_ref, q_ref, k_ref, v_ref, o_ref, lse_ref,
):
    length, model_width = x_ref.shape
    query_width = per_group * HEAD_DIM
    turned = query_width + HEAD_DIM
    gain = w_out_ref[query_width : query_width + 1, :].astype(F32)

    def project(i, carry):
        rows = pl.ds(pl.multiple_of(i * BLOCK, BLOCK), BLOCK)
        x = x_ref[rows, :].astype(F32)
        inverse = lax.rsqrt(jnp.mean(x * x, axis=1, keepdims=True) + EPSILON)
        a = (x * inverse * gain).astype(BF16)
        a_ref[rows, :] = a
        pre = dot(a, w_in_ref[...])
        spun = spin(pre[:, :turned], cos_ref[rows, :], sin_ref[rows, :]).astype(BF16)
        for h in range(per_group):
            q_ref[h, rows, :] = spun[:, h * HEAD_DIM : (h + 1) * HEAD_DIM]
        k_ref[rows, :] = spun[:, query_width:turned]
        v_ref[rows, :] = pre[:, turned : turned + HEAD_DIM].astype(BF16)
        return carry

    lax.fori_loop(0, length // BLOCK, project, 0)
    for i in range(length // BLOCK):
        seen = (i + 1) * BLOCK
        rows = slice(i * BLOCK, seen)
        keys, values = k_ref[:seen, :], v_ref[:seen, :]
        for h in range(per_group):
            scores = dot(q_ref[h, rows, :], keys, (1, 1)) * ATTENTION_SCALE
            peak = jnp.max(scores, axis=1, keepdims=True)
            lifted = jnp.exp(scores - peak)
            total = jnp.sum(lifted, axis=1, keepdims=True)
            weights = (lifted * (1.0 / total)).astype(BF16)
            mixed = dot(weights, values)
            o_ref[rows, h * HEAD_DIM : (h + 1) * HEAD_DIM] = mixed.astype(BF16)
            lse_ref[h, rows, :] = peak + jnp.log(total)
        part_ref[rows, :] = dot(o_ref[rows, :], w_out_ref[:query_width, :]).astype(BF16)


def attend(x_all, w_in, w_out, cosine, sine, per_group):
    length, model_width = x_all.shape
    query_width = per_group * HEAD_DIM
    shapes = [
        jax.ShapeDtypeStruct((length, model_width), BF16),
        jax.ShapeDtypeStruct((length, model_width), BF16),
        jax.ShapeDtypeStruct((per_group, length, HEAD_DIM), BF16),
        jax.ShapeDtypeStruct((length, HEAD_DIM), BF16),
        jax.ShapeDtypeStruct((length, HEAD_DIM), BF16),
        jax.ShapeDtypeStruct((length, query_width), BF16),
        jax.ShapeDtypeStruct((per_group, length, 1), F32),
    ]
    return pl.pallas_call(
        functools.partial(attend_kernel, per_group),
        out_shape=shapes,
        in_specs=[pl.BlockSpec(memory_space=pltpu.VMEM)] * 5,
        out_specs=[pl.BlockSpec(memory_space=pltpu.VMEM)] * len(shapes),
        compiler_params=pltpu.CompilerParams(vmem_limit_bytes=VMEM_LIMIT),
        cost_estimate=pl.CostEstimate(
            flops=8_000_000_000, bytes_accessed=16_000_000, transcendentals=2_000_000
        ),
        name="attend",
    )(x_all, w_in, w_out, cosine, sine)


def attend_back_kernel(per_group, *refs):
    attend_back_steps(per_group, lambda step: None, *refs)


def attend_back_talk_kernel(per_group, size, swaps, *refs):
    ins, refs = refs[:13], refs[13:]
    sum_ref, sent, refs = refs[0], refs[1 : 1 + swaps], refs[1 + swaps :]
    part_ref, gin_ref, out_low, e_own, e_other = refs[:5]
    came, refs = refs[5 : 5 + swaps], refs[5 + swaps :]
    scratch, stage_a, stage_b, refs = refs[:5], refs[5:11], refs[11:17], refs[17:]
    gout_ref, line_sums, line_landed, sends, receives, swap_sems, line_send, line_recv = refs
    plane, line = plane_neighbours(), lax.axis_index("fsdp")
    other = Scatter(plane, 0, sum_ref, 8, stage_a, sends, receives)
    mine = Scatter(plane, 1, sum_ref, 0, stage_b, sends, receives)
    gout = LineScatter(line, size, 0, gout_ref, line_sums, line_landed, line_send, line_recv)
    across = [
        push(source, target, swap_sems.at[0, i], swap_sems.at[1, i], "fsdp", pair_of(line))
        for i, (source, target) in enumerate(zip(sent, came))
    ]
    half = e_own.shape[0] // 2

    def hook(step):
        if step == 0:
            meet(plane, line, size, True)
            other.begin()
            mine.begin()
            gout.begin()
            across[0].start()
        elif step == 1:
            other.first()
            gout.step(0)
            for copy in across[1:2]:
                copy.start()
        elif step == 2:
            mine.first()
            gout.step(1)
            for copy in across[2:]:
                copy.start()
        elif step == 3:
            other.second()
            gout.step(2)
        elif step == 4:
            mine.second()
        elif step == 6:
            for h in range(2):
                e_other[pl.ds(h * half, half)] = other.total(h).astype(BF16)
                e_own[pl.ds(h * half, half)] = mine.total(h)
            out_low[...] = gout.total().astype(BF16)
            for item in (other, mine, gout):
                item.finish()
            for copy in across:
                copy.wait()

    attend_back_steps(per_group, hook, *ins, part_ref, gin_ref, gout_ref, *scratch)


def attend_back_steps(
    per_group, hook, dw_ref, w_in_ref, w_out_ref, cos_ref, sin_ref,
    a_ref, q_ref, k_ref, v_ref, o_ref, lse_ref, b_all_ref, dl_ref,
    part_ref, gin_ref, gout_ref,
    turn_ref, dv_ref, back_ref, b_ref, b_sem,
):
    length, model_width = dw_ref.shape
    fetch = pltpu.make_async_copy(b_all_ref.at[pl.ds(0, length)], b_ref, b_sem)
    fetch.start()
    query_width = per_group * HEAD_DIM
    turned = query_width + HEAD_DIM
    blocks = length // BLOCK
    chunk = 384

    def out_grads(i, carry):
        columns = pl.ds(pl.multiple_of(i * chunk, chunk), chunk)
        gout_ref[i] = dot(o_ref[...], dw_ref[:, columns], (0, 0)).astype(BF16)
        return carry

    lax.fori_loop(0, model_width // chunk, out_grads, 0)
    hook(0)
    turn_ref[...] = jnp.zeros_like(turn_ref)
    dv_ref[...] = jnp.zeros_like(dv_ref)
    for i in range(blocks):
        seen = (i + 1) * BLOCK
        rows = slice(i * BLOCK, seen)
        keys, values = k_ref[:seen, :], v_ref[:seen, :]
        grad = dot(dw_ref[rows, :], w_out_ref[:query_width, :], (1, 1)).astype(BF16)
        for h in range(per_group):
            columns = slice(h * HEAD_DIM, (h + 1) * HEAD_DIM)
            queries = q_ref[h, rows, :]
            grad_head = grad[:, columns]
            scores = dot(queries, keys, (1, 1)) * ATTENTION_SCALE
            probs = jnp.exp(scores - lse_ref[h, rows, :])
            dv_ref[:seen, :] += dot(probs.astype(BF16), grad_head, (0, 0))
            grad_probs = dot(grad_head, values, (1, 1))
            inner = jnp.sum(probs * grad_probs, axis=1, keepdims=True)
            grad_scores = (probs * (grad_probs - inner)).astype(BF16)
            turn_ref[rows, columns] = dot(grad_scores, keys) * ATTENTION_SCALE
            turn_ref[:seen, query_width:turned] += (
                dot(grad_scores, queries, (0, 0)) * ATTENTION_SCALE
            )
        hook(1 + i)

    def unturn(i, carry):
        rows = pl.ds(pl.multiple_of(i * BLOCK, BLOCK), BLOCK)
        back_ref[rows, :turned] = spin(
            turn_ref[rows, :], cos_ref[rows, :], -sin_ref[rows, :]
        ).astype(BF16)
        back_ref[rows, turned:] = jnp.concatenate(
            [dv_ref[rows, :].astype(BF16), jnp.zeros((BLOCK, LANES - HEAD_DIM), BF16)], axis=1
        )
        part_ref[rows, :] = dot(
            back_ref[rows, : turned + HEAD_DIM], w_in_ref[:, : turned + HEAD_DIM], (1, 1)
        ).astype(BF16)
        return carry

    lax.fori_loop(0, blocks, unturn, 0)
    hook(5)
    fetch.wait()

    def weight_grads(i, carry):
        columns = pl.ds(pl.multiple_of(i * chunk, chunk), chunk)
        a = a_ref[:, columns]
        gin_ref[columns, :turned] = dot(a, back_ref[:, :turned], (0, 0)).astype(BF16)
        gin_ref[columns, turned:] = (
            dot(a, back_ref[:, turned:], (0, 0)) + dot(b_ref[:, columns], dl_ref[...], (0, 0))
        ).astype(BF16)
        return carry

    lax.fori_loop(0, model_width // chunk, weight_grads, 0)
    hook(6)


def attend_back(
    dw_all, w_in, w_out, cosine, sine, saved, b_all, dl_all, per_group, talk=None, collective_id=None
):
    length, model_width = dw_all.shape
    query_width = per_group * HEAD_DIM
    turned = query_width + HEAD_DIM
    shapes = [
        jax.ShapeDtypeStruct((length, model_width), BF16),
        jax.ShapeDtypeStruct((model_width, w_in.shape[1]), BF16),
        jax.ShapeDtypeStruct((model_width // 384, query_width, 384), BF16),
    ]
    scratch = [
        pltpu.VMEM((length, turned), F32),
        pltpu.VMEM((length, HEAD_DIM), F32),
        pltpu.VMEM((length, w_in.shape[1]), BF16),
        pltpu.VMEM((length, model_width), BF16),
        pltpu.SemaphoreType.DMA,
    ]
    operands = (dw_all, w_in, w_out, cosine, sine, *saved, b_all, dl_all)
    in_specs, out_specs = in_vmem(11) + anywhere(1) + in_vmem(1), in_vmem(len(shapes))
    kernel = functools.partial(attend_back_kernel, per_group)
    params = pltpu.CompilerParams(vmem_limit_bytes=VMEM_LIMIT)
    if talk is not None:
        sum_part, sent = talk
        wide = sum_part.shape[1:]
        shapes = shapes + [jax.ShapeDtypeStruct(wide, F32), jax.ShapeDtypeStruct(wide, BF16)]
        shapes += [jax.ShapeDtypeStruct(array.shape, array.dtype) for array in sent]
        gout_shape, size = shapes[2].shape, lax.axis_size("fsdp")
        shapes[2] = jax.ShapeDtypeStruct(gout_shape[1:], BF16)
        scratch = scratch + scatter_scratch(*wide, BF16) * 2
        scratch += [pltpu.VMEM(gout_shape, BF16)] + [pltpu.VMEM((2,) + gout_shape, BF16)] * 2
        scratch += scatter_sems(2) + [pltpu.SemaphoreType.DMA((2, len(sent)))]
        scratch += line_scatter_sems(1, size)
        operands += (sum_part, *sent)
        in_specs = in_specs + in_vmem(1) + anywhere(len(sent))
        out_specs = out_specs + in_vmem(2) + anywhere(len(sent))
        kernel = functools.partial(attend_back_talk_kernel, per_group, size, len(sent))
        params = talk_params(collective_id)
    return pl.pallas_call(
        kernel,
        out_shape=shapes,
        in_specs=in_specs,
        out_specs=out_specs,
        scratch_shapes=scratch,
        compiler_params=params,
        cost_estimate=pl.CostEstimate(
            flops=20_000_000_000, bytes_accessed=30_000_000, transcendentals=2_000_000
        ),
        name="attend_back",
    )(*operands)


def experts_kernel(
    here, tile,
    place_ref, b_hbm, dy_hbm, g_ref, gate_hbm, up_hbm, down_hbm, *rest,
):
    out_hbm, db_hbm, dg_ref = rest[:3]
    grad_hbm, rest = rest[3:6], rest[6:]
    (
        b_ref, dy_ref, in_ref, down_ref, hidden_ref, back_ref, out_ref, db_ref,
        gate_stage, up_stage, down_stage, weight_sem, tile_sem, out_sem, grad_sem,
    ) = rest
    rows_all, model_width = b_ref.shape
    width = down_ref.shape[0] // here
    tiles = rows_all // tile
    first = place_ref[0]

    def columns_of(e):
        return slice(e * width, (e + 1) * width)

    loads = []
    for e in range(here):
        loads.append((gate_hbm.at[e], in_ref.at[:, columns_of(e)]))
        loads.append((up_hbm.at[e], in_ref.at[:, columns_of(here + e)]))
    for e in range(here):
        loads.append((down_hbm.at[e], down_ref.at[columns_of(e), :]))
    loads = [
        pltpu.make_async_copy(source, target, weight_sem.at[i])
        for i, (source, target) in enumerate(loads)
    ]

    def tile_rows(i):
        return pl.ds(pl.multiple_of(i * tile, tile), tile)

    def tile_load(i, k):
        source, target = ((b_hbm, b_ref), (dy_hbm, dy_ref))[k]
        return pltpu.make_async_copy(
            source.at[tile_rows(i)], target.at[tile_rows(i)], tile_sem.at[k, i]
        )

    def tile_store(i, k):
        source, target = ((out_ref, out_hbm), (db_ref, db_hbm))[k]
        return pltpu.make_async_copy(
            source.at[tile_rows(i)], target.at[tile_rows(i)], out_sem.at[k, i]
        )

    for k in range(2):
        tile_load(0, k).start()
    for load in loads:
        load.start()
    for i in range(1, tiles):
        for k in range(2):
            tile_load(i, k).start()
    for load in loads:
        load.wait()

    def forward_back(i, carry):
        rows = tile_rows(i)
        tile_load(i, 0).wait()
        tile_load(i, 1).wait()
        pre = dot(b_ref[rows, :], in_ref[...])
        grad_mixed = dot(dy_ref[rows, :], down_ref[...], (1, 1))
        gates = g_ref[rows, :]
        lane = lax.broadcasted_iota(jnp.int32, gates.shape, 1)
        inner = jnp.zeros(gates.shape, F32)
        for e in range(here):
            mine = lane == first + e
            gate = jnp.sum(jnp.where(mine, jnp.maximum(gates, 0.0), 0.0), axis=1, keepdims=True)
            scale = RESIDUAL_SCALE * gate
            gate_pre, up_pre = pre[:, columns_of(e)], pre[:, columns_of(here + e)]
            sigmoid = 1.0 / (1.0 + jnp.exp(-gate_pre))
            silu = gate_pre * sigmoid
            hidden = silu * up_pre
            grad = grad_mixed[:, columns_of(e)]
            share = jnp.sum(hidden * grad, axis=1, keepdims=True)
            inner = jnp.where(mine, RESIDUAL_SCALE * share, inner)
            hidden_ref[rows, columns_of(e)] = (scale * hidden).astype(BF16)
            grad = scale * grad
            back_ref[rows, columns_of(e)] = (
                grad * up_pre * sigmoid * (1.0 + gate_pre * (1.0 - sigmoid))
            ).astype(BF16)
            back_ref[rows, columns_of(here + e)] = (grad * silu).astype(BF16)
        dg_ref[rows, :] = inner
        db_ref[rows, :] = dot(back_ref[rows, :], in_ref[...], (1, 1)).astype(BF16)
        tile_store(i, 1).start()
        out_ref[rows, :] = dot(hidden_ref[rows, :], down_ref[...]).astype(BF16)
        tile_store(i, 0).start()
        return carry

    lax.fori_loop(0, tiles, forward_back, 0)
    parts = 4
    part = model_width // parts

    def part_columns(i):
        return pl.ds(pl.multiple_of(i * part, part), part)

    def down_grad(i, carry):
        grad = dot(hidden_ref[...], dy_ref[:, part_columns(i)], (0, 0))
        for e in range(here):
            down_stage[i, e] = grad[columns_of(e), :].astype(BF16)
        return carry

    def in_grad(i, carry):
        grad = dot(b_ref[:, part_columns(i)], back_ref[...], (0, 0))
        for e in range(here):
            gate_stage[i, e] = grad[:, columns_of(e)].astype(BF16)
            up_stage[i, e] = grad[:, columns_of(here + e)].astype(BF16)
        return carry

    stores = []

    def store(k, stage):
        copy = pltpu.make_async_copy(stage, grad_hbm[k], grad_sem.at[k])
        copy.start()
        stores.append(copy)

    lax.fori_loop(0, parts, down_grad, 0)
    store(2, down_stage)
    lax.fori_loop(0, parts, in_grad, 0)
    store(0, gate_stage)
    store(1, up_stage)
    for copy in stores:
        copy.wait()
    for i in range(tiles):
        for k in range(2):
            tile_store(i, k).wait()


def experts(place, b_all, dy_all, g_all, w_gate, w_up, w_down):
    sources, tokens, model_width = b_all.shape
    here, _, hidden_width = w_gate.shape
    rows_all = sources * tokens
    width = hidden_width
    part = model_width // 4
    tile = 256
    tiles = rows_all // tile
    in_stage, down_stage = (4, here, part, width), (4, here, width, part)
    shapes = [in_stage, in_stage, down_stage]
    flat = (rows_all, model_width)
    out = pl.pallas_call(
        functools.partial(experts_kernel, here, tile),
        out_shape=[
            jax.ShapeDtypeStruct(flat, BF16),
            jax.ShapeDtypeStruct(flat, BF16),
            jax.ShapeDtypeStruct((rows_all, LANES), F32),
        ]
        + [jax.ShapeDtypeStruct(shape, BF16) for shape in shapes],
        in_specs=[pl.BlockSpec(memory_space=pltpu.SMEM)] + anywhere(2) + in_vmem(1) + anywhere(3),
        out_specs=anywhere(2) + in_vmem(1) + anywhere(len(shapes)),
        scratch_shapes=[
            pltpu.VMEM(flat, BF16),
            pltpu.VMEM(flat, BF16),
            pltpu.VMEM((model_width, 2 * here * width), BF16),
            pltpu.VMEM((here * width, model_width), BF16),
            pltpu.VMEM((rows_all, here * width), BF16),
            pltpu.VMEM((rows_all, 2 * here * width), BF16),
            pltpu.VMEM(flat, BF16),
            pltpu.VMEM(flat, BF16),
            pltpu.VMEM(in_stage, BF16),
            pltpu.VMEM(in_stage, BF16),
            pltpu.VMEM(down_stage, BF16),
            pltpu.SemaphoreType.DMA((3 * here,)),
            pltpu.SemaphoreType.DMA((2, tiles)),
            pltpu.SemaphoreType.DMA((2, tiles)),
            pltpu.SemaphoreType.DMA((3,)),
        ],
        compiler_params=pltpu.CompilerParams(vmem_limit_bytes=VMEM_LIMIT),
        cost_estimate=pl.CostEstimate(
            flops=43_000_000_000, bytes_accessed=42_000_000, transcendentals=1_000_000
        ),
        name="experts",
    )(
        place, b_all.reshape(flat), dy_all.reshape(flat), g_all.reshape(rows_all, LANES),
        w_gate, w_up, w_down,
    )
    return [
        out[0].reshape(b_all.shape), out[1].reshape(b_all.shape),
        out[2].reshape(sources, tokens, LANES), *out[3:],
    ]


class Trade:
    def __init__(self, line, stages, nears, came, far, sems):
        self.beside, self.across = beside(line), pair_of(line)
        self.stages, self.nears, self.came, self.far, self.sems = stages, nears, came, far, sems

    def copies(self, e, hop):
        made = []
        for k in range(3):
            source = self.stages[k].at[e, (1, 0, 3)[hop]]
            target = self.far[3 * e + k] if hop == 2 else (self.nears, self.came)[hop][k].at[e]
            peer = self.across if hop == 2 else self.beside
            made.append(
                push(source, target, self.sems.at[0, hop, k, e], self.sems.at[1, hop, k, e], "fsdp", peer)
            )
        return made

    def send(self, e, hop):
        for copy in self.copies(e, hop):
            copy.start()

    def add(self, e):
        for k, copy in enumerate(self.copies(e, 0)):
            copy.wait_recv()
            self.stages[k][e, 3] = (
                self.stages[k][e, 3].astype(F32) + self.nears[k][e].astype(F32)
            ).astype(BF16)

    def finish(self, count):
        for e in range(count):
            for hop in range(3 if e < count - 1 else 2):
                for copy in self.copies(e, hop):
                    copy.wait_send()
                    if hop:
                        copy.wait_recv()


def experts_back_kernel(
    here, tile, lane_of, query_width, router_at,
    b_hbm, dy_hbm, g_ref, gate_hbm, up_hbm, down_hbm,
    middle_ref, marked_ref, win_ref, wout_ref,
    out_hbm, dw_out, dl_out, grad_ref, gain_ref, *rest,
):
    kept_hbm, came_hbm, rest = rest[0:3], rest[3:6], rest[6:]
    far_hbm, rest = rest[: 3 * (here - 1)], rest[3 * (here - 1) :]
    other_hbm, rest = rest[:3], rest[3:]
    (
        b_ref, dy_ref, in_ref, down_ref, hidden_ref, back_ref, out_ref, db_ref, dg_ref,
        down_stage, gate_stage, up_stage, down_near, gate_near, up_near,
        dw_own, dl_own, db_total, dg_total, db_landed, dg_landed,
    ) = rest[:21]
    scratch, rest = rest[21:41], rest[41:]
    (
        weight_sem, tile_sem, out_sem, kept_sem, other_sem, trade_sems, swap_sems,
        scatter_send, scatter_recv, own_sem, send_sem, recv_sem,
    ) = rest
    rows_all, model_width = b_ref.shape
    width = down_ref.shape[1]
    tiles = rows_all // tile
    tokens = middle_ref.shape[0]
    per_tile = tile // tokens
    plane, line = plane_neighbours(), lax.axis_index("fsdp")
    me = plane[0]
    first = me * here + lane_of
    high, low = line // 2, lax.rem(line, 2)
    span = pl.ds(pl.multiple_of(high * width, width), width)

    def weight_loads(e):
        pairs = (
            (gate_hbm.at[e, :, span], in_ref.at[e, :, pl.ds(0, width)]),
            (up_hbm.at[e, :, span], in_ref.at[e, :, pl.ds(width, width)]),
            (down_hbm.at[e, span, :], down_ref.at[e]),
        )
        return [
            pltpu.make_async_copy(source, target, weight_sem.at[e, i])
            for i, (source, target) in enumerate(pairs)
        ]

    def tile_rows(j):
        return pl.ds(pl.multiple_of(j * tile, tile), tile)

    def tile_loads(j):
        return [
            pltpu.make_async_copy(
                source.at[tile_rows(j)], target.at[tile_rows(j)], tile_sem.at[k, j]
            )
            for k, (source, target) in enumerate(((b_hbm, b_ref), (dy_hbm, dy_ref)))
        ]

    def tile_store(j):
        return pltpu.make_async_copy(
            out_ref.at[tile_rows(j)], out_hbm.at[tile_rows(j)], out_sem.at[j]
        )

    def place_of(i):
        return lax.rem(i + tiles // 2, tiles)

    def start_loads(i, carry):
        for load in tile_loads(place_of(i)):
            load.start()
        return carry

    start_loads(0, 0)
    for load in weight_loads(0):
        load.start()
    lax.fori_loop(1, tiles, start_loads, 0)
    for e in range(1, here):
        for load in weight_loads(e):
            load.start()
    meet(plane, line, 4, False)
    trade = Trade(
        line, (down_stage, gate_stage, up_stage), (down_near, gate_near, up_near),
        came_hbm, far_hbm, trade_sems,
    )
    sums = (scatter_send, scatter_recv)
    db_other = Scatter(plane, 0, db_ref, 8, scratch[:5], *sums)
    dg_other = Scatter(plane, 1, dg_ref, 8, scratch[5:10], *sums)
    db = Scatter(plane, 2, db_ref, 0, scratch[10:15], *sums)
    dg = Scatter(plane, 3, dg_ref, 0, scratch[15:20], *sums)
    swap_g = push(dg_total, dg_landed, swap_sems.at[0], swap_sems.at[1], "fsdp", pair_of(line))
    swap_b = push(db_total, db_landed, swap_sems.at[2], swap_sems.at[3], "fsdp", pair_of(line))
    half = tokens // 2
    part = model_width // 4

    def one_expert(e, carry):
        for load in weight_loads(e):
            load.wait()
        last = e == here - 1

        def forward_back(i, carry):
            j = place_of(i)
            rows = tile_rows(j)

            @pl.when(e == 0)
            def _():
                for load in tile_loads(j):
                    load.wait()

            pre = dot(b_ref[rows, :], in_ref[e])
            grad = dot(dy_ref[rows, :], down_ref[e], (1, 1))
            gates = g_ref[rows, :]
            mine = lax.broadcasted_iota(jnp.int32, gates.shape, 1) == first + e
            gate = jnp.sum(jnp.where(mine, jnp.maximum(gates, 0.0), 0.0), axis=1, keepdims=True)
            scale = RESIDUAL_SCALE * gate
            gate_pre, up_pre = pre[:, :width], pre[:, width:]
            sigmoid = 1.0 / (1.0 + jnp.exp(-gate_pre))
            silu = gate_pre * sigmoid
            hidden = silu * up_pre
            share = jnp.sum(hidden * grad, axis=1, keepdims=True)
            inner = jnp.where(mine, RESIDUAL_SCALE * share, 0.0)
            hidden_ref[rows, :] = (scale * hidden).astype(BF16)
            grad = scale * grad
            back_ref[rows, :width] = (
                grad * up_pre * sigmoid * (1.0 + gate_pre * (1.0 - sigmoid))
            ).astype(BF16)
            back_ref[rows, width:] = (grad * silu).astype(BF16)
            made = dot(hidden_ref[rows, :], down_ref[e])
            back = dot(back_ref[rows, :], in_ref[e], (1, 1))

            @pl.when(e == 0)
            def _():
                out_ref[rows, :] = made.astype(BF16)
                for t in range(per_tile):
                    piece = slice(t * tokens, (t + 1) * tokens)
                    db_ref[per_tile * j + t] = back[piece].astype(BF16)
                    dg_ref[per_tile * j + t] = inner[piece]

            @pl.when(e > 0)
            def _():
                out_ref[rows, :] = (out_ref[rows, :].astype(F32) + made).astype(BF16)
                for t in range(per_tile):
                    piece = slice(t * tokens, (t + 1) * tokens)
                    block = per_tile * j + t
                    db_ref[block] = (db_ref[block].astype(F32) + back[piece]).astype(BF16)
                    dg_ref[block] += inner[piece]

            @pl.when(last)
            def _():
                tile_store(j).start()

            @pl.when((e == 1) & (i == tiles - 3))
            def _():
                trade.add(0)
                trade.send(0, 2)

            @pl.when(last & (i == tiles // 2 - 1))
            def _():
                dg_other.begin()
                db_other.begin()

            @pl.when(last & (i == tiles - 2))
            def _():
                dg_other.first()
                db_other.first()

            return carry

        lax.fori_loop(0, tiles, forward_back, 0)

        @pl.when(last)
        def _():
            dg.begin()
            db.begin()
            dg_other.second()
            db_other.second()

        def weight_grads(p, carry):
            i = p + 1 - 2 * lax.rem(p, 2)
            parity = jnp.where(p < 2, 1 - low, low)
            side = jnp.where(lax.rem(i, 2) == 0, high, 1 - high)
            columns = pl.ds(pl.multiple_of((2 * side + parity) * part, part), part)
            down_stage[e, i] = dot(hidden_ref[...], dy_ref[:, columns], (0, 0)).astype(BF16)
            grad = dot(b_ref[:, columns], back_ref[...], (0, 0))
            gate_stage[e, i] = grad[:, :width].astype(BF16)
            up_stage[e, i] = grad[:, width:].astype(BF16)

            @pl.when((p == 0) & (e < here - 1))
            def _():
                trade.send(e, 0)

            @pl.when((p == 1) & (e < here - 2))
            def _():
                trade.send(e, 1)

            @pl.when(last & (p == 1))
            def _():
                for h in range(2):
                    rows = pl.ds(h * half, half)
                    dg_total[rows] = dg_other.total(h)
                    db_total[rows] = db_other.total(h).astype(BF16)
                swap_g.start()
                swap_b.start()

            @pl.when(last & (p == 2))
            def _():
                dg.first()
                db.first()
                trade.add(here - 2)
                trade.send(here - 2, 2)
                trade.send(here - 2, 1)
                trade.send(here - 1, 0)
                trade.send(here - 1, 1)

            return carry

        lax.fori_loop(0, 4, weight_grads, 0)
        return carry

    lax.fori_loop(0, here, one_expert, 0)
    stores = [
        pltpu.make_async_copy(stage.at[e, 2], kept_hbm[k].at[e], kept_sem.at[k, e])
        for k, stage in enumerate((down_stage, gate_stage, up_stage))
        for e in range(here)
    ]
    for store in stores:
        store.start()
    dg.second()
    db.second()
    gain = wout_ref[query_width + 1 : query_width + 2, :].astype(F32)
    router = win_ref[:, router_at : router_at + LANES]
    gain_grad = jnp.zeros((1, model_width), F32)
    sums_g = [dg.total(h) for h in range(2)]
    swap_g.wait_recv()
    swap_b.wait_recv()
    for h in range(2):
        rows = pl.ds(h * half, half)
        gates = jnp.maximum(marked_ref[rows], 0.0)
        grad_gates = sums_g[h] + dg_landed[rows]
        grad_chosen = gates * (
            grad_gates - jnp.sum(gates * grad_gates, axis=1, keepdims=True)
        )
        grad_logits = grad_chosen.astype(BF16)
        dl_own[rows] = grad_logits
        grad_b = dot(grad_logits, router, (1, 1)) + db.total(h) + db_landed[rows].astype(F32)
        middle = middle_ref[rows]
        inverse = lax.rsqrt(jnp.mean(middle * middle, axis=1, keepdims=True) + EPSILON)
        normed = middle * inverse
        gain_grad += jnp.sum(grad_b * normed, axis=0, keepdims=True)
        own = pl.ds(pl.multiple_of(me * tokens + h * half, half), half)
        grad = dy_ref[own].astype(F32) + norm_back(grad_b * gain, normed, inverse)
        grad_ref[rows] = grad
        dw_own[rows] = (RESIDUAL_SCALE * grad).astype(BF16)
    gain_ref[...] = jnp.broadcast_to(gain_grad, gain_ref.shape)
    gathers = (own_sem, send_sem, recv_sem)
    dw = Gather(plane, 0, dw_own, dw_out, 0, *gathers)
    dl = Gather(plane, 1, dl_own, dl_out, 0, *gathers)
    dw.begin()
    dl.begin()
    dw.relay()
    dl.relay()
    dw.relay_diagonal()
    dl.relay_diagonal()
    trade.add(here - 1)
    others = [
        pltpu.make_async_copy(stage.at[here - 1, 3], other_hbm[k], other_sem.at[k])
        for k, stage in enumerate((down_stage, gate_stage, up_stage))
    ]
    for copy in others:
        copy.start()
    for item in (dg_other, db_other, dg, db, dw, dl):
        item.finish()
    swap_b.wait_send()
    swap_g.wait_send()
    for store in stores + others:
        store.wait()
    for j in range(tiles):
        tile_store(j).wait()
    trade.finish(here)


def experts_back(
    b_all, dy_all, g_all, w_gate, w_up, w_down, middle, marked, w_in, w_out,
    lane_of, query_width, router_at, collective_id,
):
    sources, tokens, model_width = b_all.shape
    here, _, hidden_width = w_gate.shape
    rows_all = sources * tokens
    width, part, tile = hidden_width // 2, model_width // 4, 256
    tiles = rows_all // tile
    flat, wide, narrow = (rows_all, model_width), (tokens, model_width), (tokens, LANES)
    slices = [(width, part), (part, width), (part, width)]
    out = pl.pallas_call(
        functools.partial(experts_back_kernel, here, tile, lane_of, query_width, router_at),
        out_shape=[
            jax.ShapeDtypeStruct(flat, BF16),
            jax.ShapeDtypeStruct((8,) + wide, BF16),
            jax.ShapeDtypeStruct((8,) + narrow, BF16),
            jax.ShapeDtypeStruct(wide, F32),
            jax.ShapeDtypeStruct((8, model_width), F32),
        ]
        + [jax.ShapeDtypeStruct((here,) + shape, BF16) for shape in slices * 2]
        + [jax.ShapeDtypeStruct(shape, BF16) for shape in slices * here],
        in_specs=anywhere(2) + in_vmem(1) + anywhere(3) + in_vmem(4),
        out_specs=anywhere(3) + in_vmem(2) + anywhere(6 + 3 * here),
        scratch_shapes=[
            pltpu.VMEM(flat, BF16),
            pltpu.VMEM(flat, BF16),
            pltpu.VMEM((here, model_width, 2 * width), BF16),
            pltpu.VMEM((here, width, model_width), BF16),
            pltpu.VMEM((rows_all, width), BF16),
            pltpu.VMEM((rows_all, 2 * width), BF16),
            pltpu.VMEM(flat, BF16),
            pltpu.VMEM((sources,) + wide, BF16),
            pltpu.VMEM((sources,) + narrow, F32),
        ]
        + [pltpu.VMEM((here, 4) + shape, BF16) for shape in slices]
        + [pltpu.VMEM((here,) + shape, BF16) for shape in slices]
        + [
            pltpu.VMEM(wide, BF16),
            pltpu.VMEM(narrow, BF16),
            pltpu.VMEM(wide, BF16),
            pltpu.VMEM(narrow, F32),
            pltpu.VMEM(wide, BF16),
            pltpu.VMEM(narrow, F32),
        ]
        + (scatter_scratch(*wide, BF16, True) + scatter_scratch(*narrow, F32, True)) * 2
        + [
            pltpu.SemaphoreType.DMA((here, 3)),
            pltpu.SemaphoreType.DMA((2, tiles)),
            pltpu.SemaphoreType.DMA((tiles,)),
            pltpu.SemaphoreType.DMA((3, here)),
            pltpu.SemaphoreType.DMA((3,)),
            pltpu.SemaphoreType.DMA((2, 3, 3, here)),
            pltpu.SemaphoreType.DMA((4,)),
        ]
        + scatter_sems(4)
        + gather_sems(2),
        compiler_params=pltpu.CompilerParams(
            collective_id=collective_id, has_side_effects=True, vmem_limit_bytes=67_000_000
        ),
        cost_estimate=pl.CostEstimate(
            flops=43_000_000_000, bytes_accessed=42_000_000, transcendentals=1_000_000
        ),
        name="experts_back",
    )(
        b_all.reshape(flat), dy_all.reshape(flat), g_all.reshape(rows_all, LANES),
        w_gate, w_up, w_down, middle, marked, w_in, w_out,
    )
    return [out[0].reshape(b_all.shape), *out[1:5], out[5:8], out[8:11], out[11:-3], out[-3:]]


def rotary_tables(length):
    lane = lax.broadcasted_iota(jnp.int32, (length, LANES), 1) % HEAD_DIM
    half = HEAD_DIM // 2
    exponent = (lane % half).astype(F32) * (2.0 / HEAD_DIM)
    position = lax.broadcasted_iota(jnp.int32, (length, LANES), 0).astype(F32)
    angles = position * jnp.power(ROPE_BASE, -exponent)
    return jnp.cos(angles), jnp.where(lane < half, -jnp.sin(angles), jnp.sin(angles))


def finish_kernel(per_group, here, in_ref, out_ref, *refs):
    kept, came, far, refs = refs[:3], refs[3:6], refs[6 : 6 + 3 * here], refs[6 + 3 * here :]
    query_ref, key_ref, value_ref, router_ref, proj_ref, *expert_refs = refs
    query_width = per_group * HEAD_DIM
    groups, out_rows, _ = out_ref.shape
    for j in range(0, groups, 2):
        pair = (in_ref[j].astype(F32), in_ref[j + 1].astype(F32))
        at = 0
        for target, width in ((query_ref, query_width), (key_ref, HEAD_DIM), (value_ref, HEAD_DIM)):
            target[:, j * width : (j + 2) * width] = jnp.concatenate(
                [block[:, at : at + width] for block in pair], axis=1
            )
            at += width
    router_ref[...] = in_ref[0][:, at : at + router_ref.shape[1]].astype(F32)
    for j in range(groups):
        proj_ref[j * out_rows : (j + 1) * out_rows, :] = out_ref[j].astype(F32)
    high = lax.axis_index("fsdp") // 2
    for k, target in enumerate(expert_refs):
        width = kept[k].shape[1 if k == 0 else 2]
        near = pl.ds(pl.multiple_of(high * width, width), width)
        beyond = pl.ds(pl.multiple_of((1 - high) * width, width), width)
        for e in range(here):
            near_sum = kept[k][e].astype(F32) + came[k][e].astype(F32)
            far_sum = far[3 * e + k][...].astype(F32)
            if k == 0:
                target[e, near, :] = near_sum
                target[e, beyond, :] = far_sum
            else:
                target[e, :, near] = near_sum
                target[e, :, beyond] = far_sum


def finish(in_all, out_all, kept, came, far, per_group, experts_all):
    groups, shard, _ = in_all.shape
    here, width, part = kept[0].shape
    query_width = per_group * HEAD_DIM
    shapes = [
        (shard, groups * query_width),
        (shard, groups * HEAD_DIM),
        (shard, groups * HEAD_DIM),
        (shard, experts_all),
        (groups * out_all.shape[1], out_all.shape[2]),
        (here, 2 * width, part),
        (here, part, 2 * width),
        (here, part, 2 * width),
    ]
    operands = (in_all, out_all, *kept, *came, *far)
    return pl.pallas_call(
        functools.partial(finish_kernel, per_group, here),
        out_shape=[jax.ShapeDtypeStruct(shape, F32) for shape in shapes],
        in_specs=in_vmem(len(operands)),
        out_specs=in_vmem(len(shapes)),
        compiler_params=pltpu.CompilerParams(vmem_limit_bytes=VMEM_LIMIT),
        cost_estimate=pl.CostEstimate(flops=0, bytes_accessed=25_000_000, transcendentals=0),
        name="finish",
    )(*operands)


def per_device(
    residual_in, cotangent, gain_attn, w_query, w_key, w_value, w_out, gain_ffn, w_router,
    w_gate, w_up, w_down, route_ids,
):
    me = lax.axis_index("expert")
    line = lax.axis_index("fsdp")
    peers = lax.axis_size("expert")
    lines = lax.axis_size("fsdp")
    tokens, model_width = residual_in.shape[1:]
    length = tokens * peers
    groups = w_key.shape[1] // HEAD_DIM
    per_group = w_query.shape[1] // w_key.shape[1]
    query_width = per_group * HEAD_DIM
    experts_all = w_router.shape[1]
    here = w_gate.shape[0]
    shard = w_query.shape[0]
    turned = query_width + HEAD_DIM
    router_at = turned
    lane_of = HEAD_DIM
    in_width = turned + LANES
    paired = lines == 4 and peers == 8

    w_in_shard = jnp.concatenate(
        [
            lax.dynamic_slice(w_query, (0, me * query_width), (shard, query_width)),
            lax.dynamic_slice(w_key, (0, me * HEAD_DIM), (shard, HEAD_DIM)),
            lax.dynamic_slice(w_value, (0, me * HEAD_DIM), (shard, HEAD_DIM)),
            w_router,
            jnp.zeros((shard, in_width - turned - HEAD_DIM - experts_all), BF16),
        ],
        axis=1,
    )
    w_out_shard = jnp.concatenate(
        [
            lax.dynamic_slice(w_out, (me * query_width, 0), (query_width, shard)),
            gain_attn[None],
            gain_ffn[None],
            jnp.zeros((14, shard), BF16),
        ],
        axis=0,
    )
    chosen = jnp.any(
        route_ids[0][:, :, None]
        == jnp.arange(LANES, dtype=jnp.int32)[None, None, :] - lane_of,
        axis=1,
    ).astype(F32)
    cosine, sine = rotary_tables(length)
    place = jnp.full((1,), me * here + lane_of, jnp.int32)
    own_rows, own_grad = residual_in[0], cotangent[0]
    wide = (peers, tokens, model_width)

    if paired:
        x_all, dy_all, w_in, w_out_rows = open_transfers(
            own_rows, own_grad, w_in_shard, w_out_shard, lines, 0
        )
    else:
        x_all, dy_all = plane_gather([own_rows, own_grad], 0)
        w_in, w_out_rows = (
            lax.all_gather(w_in_shard, "fsdp", axis=0, tiled=True),
            lax.all_gather(w_out_shard, "fsdp", axis=1, tiled=True),
        )
    part, *saved = attend(
        x_all.reshape(length, model_width), w_in, w_out_rows, cosine, sine, per_group
    )
    if paired:
        b_all, g_all, middle, marked = middle_transfers(
            part.reshape(wide), own_rows, w_in, w_out_rows, chosen, query_width, router_at, 1
        )
        sum_part, dw_all, dl_all, grad_middle, gain_two_grad, kept, came, far, others = experts_back(
            b_all, dy_all, g_all, w_gate, w_up, w_down, middle, marked, w_in, w_out_rows,
            lane_of, query_width, router_at, 2,
        )
        da_part, grad_in, out_low, e_own, e_total, *crossed = attend_back(
            dw_all.reshape(length, model_width), w_in, w_out_rows, cosine, sine, saved,
            b_all.reshape(2 * length, model_width), dl_all.reshape(length, LANES), per_group,
            (sum_part, others), 4,
        )
        outcome, grad_input, in_all, out_all, gains_all, notes_all = close_transfers(
            da_part.reshape(wide), e_own, e_total, own_rows, middle, grad_middle, gain_two_grad,
            w_out_rows, grad_in.reshape(lines, shard, in_width), out_low,
            query_width, 3,
        )
        squares = jnp.sum(notes_all, axis=0)[:5, 0]
        query, key, value, router_grad, proj, down, gate, up = finish(
            in_all, out_all, kept, came, [*far, *crossed], per_group, experts_all
        )
        reduced = [gate, up, down]
        gain_rows = jnp.sum(gains_all[:, :2].astype(F32), axis=0)
    else:
        (branch,) = plane_scatter([part.reshape(wide)], 1)
        gain_one = w_out_rows[query_width][None].astype(F32)
        gain_two = w_out_rows[query_width + 1][None].astype(F32)
        router = w_in[:, router_at:]
        rows = own_rows.astype(F32)
        inverse_one = lax.rsqrt(jnp.mean(rows * rows, axis=-1, keepdims=True) + EPSILON)
        normed_one = rows * inverse_one
        middle = rows + RESIDUAL_SCALE * branch
        inverse_two = lax.rsqrt(jnp.mean(middle * middle, axis=-1, keepdims=True) + EPSILON)
        normed_two = middle * inverse_two
        routed = (normed_two * gain_two).astype(BF16)
        logits = jnp.where(chosen > 0, dot(routed, router), -1e30)
        lifted = jnp.exp(logits - jnp.max(logits, axis=-1, keepdims=True))
        lifted = jnp.where(chosen > 0, lifted, 0.0)
        gates = lifted / jnp.sum(lifted, axis=-1, keepdims=True)
        b_all, g_all = plane_gather([routed, jnp.where(chosen > 0, gates, -1.0)], 2)
        sum_part, db_part, dg_part, *grads = experts(
            place, b_all, dy_all, g_all, w_gate, w_up, w_down
        )
        db_sum, dg_sum = plane_scatter([db_part, dg_part], 3)
        grad_rows = own_grad.astype(F32)
        grad_chosen = gates * (dg_sum - jnp.sum(gates * dg_sum, axis=-1, keepdims=True))
        grad_logits = grad_chosen.astype(BF16)
        grad_routed = dot(grad_logits, router, (1, 1)) + db_sum
        grad_gain_two = jnp.sum(grad_routed * normed_two, axis=0)
        grad_middle = grad_rows + norm_back(grad_routed * gain_two, normed_two, inverse_two)
        grad_branch = (RESIDUAL_SCALE * grad_middle).astype(BF16)
        dw_all, dl_all = plane_gather([grad_branch, grad_logits], 4)
        da_part, grad_in, grad_out = attend_back(
            dw_all.reshape(length, model_width), w_in, w_out_rows, cosine, sine, saved,
            b_all.reshape(length, model_width), dl_all.reshape(length, LANES), per_group,
        )
        da_sum, expert_sum = plane_scatter([da_part.reshape(wide), sum_part], 5)
        outcome = middle + expert_sum
        grad_gain_one = jnp.sum(da_sum * normed_one, axis=0)
        grad_input = grad_middle + norm_back(da_sum * gain_one, normed_one, inverse_one)
        squares = lax.psum(
            jnp.stack(
                [jnp.sum(v * v) for v in (rows, middle, outcome, grad_middle, grad_input)]
            ),
            ("fsdp", "expert"),
        )
        in_sum = lax.psum_scatter(grad_in, "fsdp", scatter_dimension=0, tiled=True)
        out_sum = lax.psum_scatter(
            grad_out.transpose(1, 0, 2).reshape(query_width, model_width), "fsdp",
            scatter_dimension=1, tiled=True,
        )
        gain_rows = lax.psum_scatter(
            lax.psum(jnp.stack([grad_gain_one, grad_gain_two]), "expert"),
            "fsdp", scatter_dimension=1, tiled=True,
        )
        in_all = lax.all_gather(in_sum, "expert", axis=0)
        out_all = lax.all_gather(out_sum, "expert", axis=0)
        outcome, grad_input = outcome.astype(BF16), grad_input.astype(BF16)
        grads = [
            grads[0].transpose(1, 0, 2, 3).reshape(w_gate.shape),
            grads[1].transpose(1, 0, 2, 3).reshape(w_up.shape),
            grads[2].transpose(1, 2, 0, 3).reshape(w_down.shape),
        ]
        reduced = [
            lax.psum_scatter(array, "fsdp", scatter_dimension=axis, tiled=True).astype(F32)
            for array, axis in zip(grads, (1, 1, 2))
        ]

        def columns_of(start, stop):
            return in_all[:, :, start:stop].transpose(1, 0, 2).reshape(shard, -1).astype(F32)

        query, key = columns_of(0, query_width), columns_of(query_width, turned)
        value = columns_of(turned, turned + HEAD_DIM)
        proj = out_all.reshape(groups * query_width, shard).astype(F32)
        at = turned + HEAD_DIM
        router_grad = in_all[0, :, at : at + experts_all].astype(F32)

    root_means = jnp.sqrt(squares / (tokens * model_width * lines * peers))
    return (
        outcome[None],
        grad_input[None],
        gain_rows[0],
        query,
        key,
        value,
        proj,
        gain_rows[1],
        router_grad,
        reduced[0],
        reduced[1],
        reduced[2],
        root_means,
    )


def solution(mesh):
    in_specs = (
        P("fsdp", "expert", None),
        P("fsdp", "expert", None),
        P("fsdp"),
        P("fsdp", None),
        P("fsdp", None),
        P("fsdp", None),
        P(None, "fsdp"),
        P("fsdp"),
        P("fsdp", None),
        P("expert", None, None),
        P("expert", None, None),
        P("expert", None, None),
        P("fsdp", "expert", None),
    )
    out_specs = (
        P("fsdp", "expert", None),
        P("fsdp", "expert", None),
        P("fsdp"),
        P("fsdp", None),
        P("fsdp", None),
        P("fsdp", None),
        P(None, "fsdp"),
        P("fsdp"),
        P("fsdp", None),
        P("expert", "fsdp", None),
        P("expert", "fsdp", None),
        P("expert", None, "fsdp"),
        P(),
    )
    return jax.shard_map(
        per_device, mesh=mesh, in_specs=in_specs, out_specs=out_specs, check_vma=False
    )
```

```python
import functools

import jax
import jax.numpy as jnp
from jax import lax
from jax.experimental import pallas as pl
from jax.experimental.pallas import tpu as pltpu
from jax.sharding import PartitionSpec as P

HEAD_DIM = 64
BLOCK = 256

EPSILON = 1e-06
RESIDUAL_SCALE = 0.22
ATTENTION_SCALE = 0.015625
ROPE_BASE = 10000.0
HIGHEST = lax.Precision.HIGHEST
MESH = pl.DeviceIdType.MESH
VMEM_LIMIT = 63_000_000
F32 = jnp.float32
BF16 = jnp.bfloat16
LANES = 128


def plane_neighbours():
    me = lax.axis_index("expert")
    core = lax.rem(me, 2)
    x_bit = lax.rem(me // 2, 2)
    y_bit = me // 4
    sibling = me + 1 - 2 * core
    x_peer = me + 2 - 4 * x_bit
    y_peer = me + 4 - 8 * y_bit
    diagonal = x_peer + 4 - 8 * y_bit
    return me, core, x_bit, y_bit, sibling, x_peer, y_peer, diagonal


def greet(axis, peers):
    barrier = pltpu.get_barrier_semaphore()
    for peer in peers:
        pl.semaphore_signal(barrier, inc=1, device_id={axis: peer}, device_id_type=MESH)
    pl.semaphore_wait(barrier, len(peers))


def gather_kernel(count, *refs):
    ins, outs = refs[:count], refs[count : 2 * count]
    own_sem, send_sem, recv_sem = refs[2 * count :]
    me, _, _, _, sibling, x_peer, y_peer, diagonal = plane_neighbours()
    greet("expert", (sibling, x_peer, y_peer))

    def remote(k, slot, source, target, peer):
        return pltpu.make_async_remote_copy(
            src_ref=source,
            dst_ref=target,
            send_sem=send_sem.at[k, slot],
            recv_sem=recv_sem.at[k, slot],
            device_id={"expert": peer},
            device_id_type=MESH,
        )

    plans = []
    for k in range(count):
        half = ins[k].shape[0] // 2
        parts = (pl.ds(0, half), pl.ds(half, half))
        out = outs[k]
        own = pltpu.make_async_copy(ins[k], out.at[me], own_sem.at[k])
        copies = [remote(k, 0, ins[k], out.at[me], sibling)]
        for h in range(2):
            copies.append(remote(k, 1 + h, ins[k].at[parts[h]], out.at[me, parts[h]], x_peer))
        for h in range(2):
            copies.append(remote(k, 3 + h, ins[k].at[parts[h]], out.at[me, parts[h]], y_peer))

        def forward(slot, block, h, peer):
            return remote(k, slot, out.at[block, parts[h]], out.at[block, parts[h]], peer)

        copies.append(forward(5, y_peer, 0, x_peer))
        copies.append(forward(6, x_peer, 1, y_peer))
        for h in range(2):
            copies.append(forward(7 + h, x_peer, h, sibling))
        for h in range(2):
            copies.append(forward(9 + h, y_peer, h, sibling))
        for h in range(2):
            copies.append(forward(11 + h, diagonal, h, sibling))
        plans.append((own, copies))
    for own, copies in plans:
        for slot in (3, 2, 1, 4, 0):
            copies[slot].start()
        own.start()
    for own, copies in plans:
        copies[3].wait_recv()
        copies[5].start()
        copies[2].wait_recv()
        copies[6].start()
        copies[9].start()
        copies[8].start()
        copies[1].wait_recv()
        copies[7].start()
        copies[4].wait_recv()
        copies[10].start()
    for own, copies in plans:
        copies[5].wait_recv()
        copies[11].start()
        copies[6].wait_recv()
        copies[12].start()
    for own, copies in plans:
        for slot in (0, 7, 8, 9, 10, 11, 12):
            copies[slot].wait_recv()
        for copy in copies:
            copy.wait_send()
        own.wait()


def plane_gather(arrays, collective_id):
    if lax.axis_size("expert") != 8:
        return [lax.all_gather(array, "expert", axis=0) for array in arrays]
    count = len(arrays)
    size = sum(array.size * array.dtype.itemsize for array in arrays)
    return pl.pallas_call(
        functools.partial(gather_kernel, count),
        out_shape=[jax.ShapeDtypeStruct((8,) + array.shape, array.dtype) for array in arrays],
        in_specs=[pl.BlockSpec(memory_space=pltpu.VMEM)] * count,
        out_specs=[pl.BlockSpec(memory_space=pl.ANY)] * count,
        scratch_shapes=[
            pltpu.SemaphoreType.DMA((count,)),
            pltpu.SemaphoreType.DMA((count, 13)),
            pltpu.SemaphoreType.DMA((count, 13)),
        ],
        compiler_params=pltpu.CompilerParams(
            collective_id=collective_id, has_side_effects=True, vmem_limit_bytes=VMEM_LIMIT
        ),
        cost_estimate=pl.CostEstimate(flops=0, bytes_accessed=16 * size, transcendentals=0),
        name="plane_gather",
    )(*arrays)


def scatter_kernel(count, *refs):
    ins, outs = refs[:count], refs[count : 2 * count]
    scratch = refs[2 * count : 2 * count + 6 * count]
    send_sem, recv_sem = refs[8 * count :]
    me, core, x_bit, y_bit, sibling, x_peer, y_peer, diagonal = plane_neighbours()
    greet("expert", (sibling, x_peer, y_peer))
    chip = me // 2
    chip_x, chip_y, chip_d = x_peer // 2, y_peer // 2, diagonal // 2
    order = (chip_d, chip_x, chip_y, chip)

    def remote(k, slot, source, target, peer):
        return pltpu.make_async_remote_copy(
            src_ref=source,
            dst_ref=target,
            send_sem=send_sem.at[k, slot],
            recv_sem=recv_sem.at[k, slot],
            device_id={"expert": peer},
            device_id_type=MESH,
        )

    stage0 = []
    for k in range(count):
        pair = scratch[6 * k]
        copies = [
            remote(k, i, ins[k].at[2 * order[i] + 1 - core], pair.at[i], sibling) for i in range(4)
        ]
        stage0.append(copies)
        for copy in copies:
            copy.start()
    later = []
    for k in range(count):
        pair, sums, first_x, first_y, second_x, second_y = scratch[6 * k : 6 * k + 6]
        rows = ins[k].shape[1]
        half = rows // 2
        parts = (pl.ds(0, half), pl.ds(half, half))
        dtype = ins[k].dtype

        def join(i):
            stage0[k][i].wait_recv()
            sums[i] = (ins[k][2 * order[i] + core].astype(F32) + pair[i].astype(F32)).astype(dtype)

        join(0)
        copies = [
            remote(k, 4, sums.at[0, parts[0]], first_x.at[1], x_peer),
            remote(k, 5, sums.at[0, parts[1]], first_y.at[1], y_peer),
        ]
        for copy in copies:
            copy.start()
        join(1)
        copies.append(remote(k, 6, sums.at[1, parts[0]], first_x.at[0], x_peer))
        copies[-1].start()
        join(2)
        copies.append(remote(k, 7, sums.at[2, parts[1]], first_y.at[0], y_peer))
        copies[-1].start()
        join(3)
        later.append(copies)
    for k in range(count):
        pair, sums, first_x, first_y, second_x, second_y = scratch[6 * k : 6 * k + 6]
        half = ins[k].shape[1] // 2
        parts = (pl.ds(0, half), pl.ds(half, half))
        dtype = ins[k].dtype
        copies = later[k]
        copies[0].wait_recv()
        pair[0, parts[0]] = (
            sums[2, parts[0]].astype(F32) + first_x[1].astype(F32)
        ).astype(dtype)
        copies.append(remote(k, 8, pair.at[0, parts[0]], second_y, y_peer))
        copies[-1].start()
        copies[1].wait_recv()
        pair[0, parts[1]] = (
            sums[1, parts[1]].astype(F32) + first_y[1].astype(F32)
        ).astype(dtype)
        copies.append(remote(k, 9, pair.at[0, parts[1]], second_x, x_peer))
        copies[-1].start()
    for k in range(count):
        pair, sums, first_x, first_y, second_x, second_y = scratch[6 * k : 6 * k + 6]
        half = ins[k].shape[1] // 2
        parts = (pl.ds(0, half), pl.ds(half, half))
        copies = later[k]
        copies[2].wait_recv()
        copies[4].wait_recv()
        outs[k][parts[0]] = (
            sums[3, parts[0]].astype(F32) + first_x[0].astype(F32) + second_y[...].astype(F32)
        )
        copies[3].wait_recv()
        copies[5].wait_recv()
        outs[k][parts[1]] = (
            sums[3, parts[1]].astype(F32) + first_y[0].astype(F32) + second_x[...].astype(F32)
        )
        for copy in stage0[k] + copies:
            copy.wait_send()


def plane_scatter(arrays, collective_id):
    if lax.axis_size("expert") != 8:
        return [
            lax.psum_scatter(array, "expert", scatter_dimension=0, tiled=False).astype(F32)
            for array in arrays
        ]
    count = len(arrays)
    scratch = []
    for array in arrays:
        _, rows, columns = array.shape
        half = rows // 2
        for shape in (
            (4, rows, columns),
            (4, rows, columns),
            (2, half, columns),
            (2, half, columns),
            (half, columns),
            (half, columns),
        ):
            scratch.append(pltpu.VMEM(shape, array.dtype))
    size = sum(array.size * array.dtype.itemsize for array in arrays)
    return pl.pallas_call(
        functools.partial(scatter_kernel, count),
        out_shape=[jax.ShapeDtypeStruct(array.shape[1:], F32) for array in arrays],
        in_specs=[pl.BlockSpec(memory_space=pltpu.VMEM)] * count,
        out_specs=[pl.BlockSpec(memory_space=pltpu.VMEM)] * count,
        scratch_shapes=scratch
        + [pltpu.SemaphoreType.DMA((count, 10)), pltpu.SemaphoreType.DMA((count, 10))],
        compiler_params=pltpu.CompilerParams(
            collective_id=collective_id, has_side_effects=True, vmem_limit_bytes=VMEM_LIMIT
        ),
        cost_estimate=pl.CostEstimate(flops=0, bytes_accessed=3 * size, transcendentals=0),
        name="plane_scatter",
    )(*arrays)


def push(source, target, send_sem, recv_sem, axis, peer):
    return pltpu.make_async_remote_copy(
        src_ref=source,
        dst_ref=target,
        send_sem=send_sem,
        recv_sem=recv_sem,
        device_id={axis: peer},
        device_id_type=MESH,
    )


def meet(plane, line, size, with_line):
    barrier = pltpu.get_barrier_semaphore()
    me, _, _, _, sibling, x_peer, y_peer, _ = plane
    for peer in (sibling, x_peer, y_peer):
        pl.semaphore_signal(barrier, inc=1, device_id={"expert": peer}, device_id_type=MESH)
    pl.semaphore_signal(
        barrier, inc=1, device_id={"fsdp": pair_of(line)}, device_id_type=MESH
    )
    if not with_line:
        pl.semaphore_signal(
            barrier, inc=1, device_id={"fsdp": beside(line)}, device_id_type=MESH
        )
        pl.semaphore_wait(barrier, 5)
        return

    @pl.when(line > 0)
    def _():
        pl.semaphore_signal(barrier, inc=1, device_id={"fsdp": line - 1}, device_id_type=MESH)

    @pl.when(line < size - 1)
    def _():
        pl.semaphore_signal(barrier, inc=1, device_id={"fsdp": line + 1}, device_id_type=MESH)

    @pl.when((line > 0) & (line < size - 1))
    def _():
        pl.semaphore_wait(barrier, 6)

    @pl.when((line == 0) | (line == size - 1))
    def _():
        pl.semaphore_wait(barrier, 5)


def pair_of(line):
    return line + 2 - 4 * (line // 2)


def beside(line):
    return line + 1 - 2 * lax.rem(line, 2)


def norm_back(grad_normed, normed, inverse):
    return inverse * (grad_normed - normed * jnp.mean(grad_normed * normed, axis=-1, keepdims=True))


class Gather:
    def __init__(self, plane, k, source, out, base, own_sem, send_sem, recv_sem):
        me, _, _, _, sibling, x_peer, y_peer, diagonal = plane
        half = source.shape[0] // 2
        parts = (pl.ds(0, half), pl.ds(half, half))

        def copy(slot, src, dst, peer):
            return push(src, dst, send_sem.at[k, slot], recv_sem.at[k, slot], "expert", peer)

        def forward(slot, block, h, peer):
            ref = out.at[base + block, parts[h]]
            return copy(slot, ref, ref, peer)

        self.own = pltpu.make_async_copy(source, out.at[base + me], own_sem.at[k])
        copies = [copy(0, source, out.at[base + me], sibling)]
        for slot, peer in ((1, x_peer), (3, y_peer)):
            for h in range(2):
                copies.append(
                    copy(slot + h, source.at[parts[h]], out.at[base + me, parts[h]], peer)
                )
        copies.append(forward(5, y_peer, 0, x_peer))
        copies.append(forward(6, x_peer, 1, y_peer))
        for slot, block in ((7, x_peer), (9, y_peer), (11, diagonal)):
            for h in range(2):
                copies.append(forward(slot + h, block, h, sibling))
        self.copies = copies

    def begin(self):
        for slot in (3, 2, 1, 4, 0):
            self.copies[slot].start()
        self.own.start()

    def relay(self):
        copies = self.copies
        for landed, onward in ((3, (5, 9)), (2, (6, 8)), (1, (7,)), (4, (10,))):
            copies[landed].wait_recv()
            for slot in onward:
                copies[slot].start()

    def relay_diagonal(self):
        for landed, onward in ((5, 11), (6, 12)):
            self.copies[landed].wait_recv()
            self.copies[onward].start()

    def finish(self):
        for slot in (0, 7, 8, 9, 10, 11, 12):
            self.copies[slot].wait_recv()
        for copy in self.copies:
            copy.wait_send()
        self.own.wait()


def gather_sems(count):
    return [
        pltpu.SemaphoreType.DMA((count,)),
        pltpu.SemaphoreType.DMA((count, 13)),
        pltpu.SemaphoreType.DMA((count, 13)),
    ]


class Scatter:
    def __init__(self, plane, k, source, base, scratch, send_sem, recv_sem):
        me, core, _, _, sibling, x_peer, y_peer, diagonal = plane
        self.source, self.base, self.core = source, base, core
        self.pair, self.first_x, self.first_y, self.second_x, self.second_y = scratch[:5]
        self.order = (diagonal // 2, x_peer // 2, y_peer // 2, me // 2)
        self.sums = [
            scratch[5].at[i] if len(scratch) > 5 else source.at[base + 2 * self.order[i] + core]
            for i in range(4)
        ]
        self.dtype = source.dtype
        half = source.shape[1] // 2
        self.parts = parts = (pl.ds(0, half), pl.ds(half, half))

        def copy(slot, src, dst, peer):
            return push(src, dst, send_sem.at[k, slot], recv_sem.at[k, slot], "expert", peer)

        self.stage0 = [
            copy(i, source.at[base + 2 * self.order[i] + 1 - core], self.pair.at[i], sibling)
            for i in range(4)
        ]
        self.stage1 = [
            copy(4, self.sums[0].at[parts[0]], self.first_x.at[1], x_peer),
            copy(5, self.sums[0].at[parts[1]], self.first_y.at[1], y_peer),
            copy(6, self.sums[1].at[parts[0]], self.first_x.at[0], x_peer),
            copy(7, self.sums[2].at[parts[1]], self.first_y.at[0], y_peer),
        ]
        self.stage2 = [
            copy(8, self.pair.at[0, parts[0]], self.second_y, y_peer),
            copy(9, self.pair.at[0, parts[1]], self.second_x, x_peer),
        ]

    def begin(self):
        for copy in self.stage0:
            copy.start()

    def join(self, i):
        self.stage0[i].wait_recv()
        mine = self.source[self.base + 2 * self.order[i] + self.core]
        self.sums[i][...] = (mine.astype(F32) + self.pair[i].astype(F32)).astype(self.dtype)

    def first(self):
        self.join(0)
        self.stage1[0].start()
        self.stage1[1].start()
        self.join(1)
        self.stage1[2].start()
        self.join(2)
        self.stage1[3].start()
        self.join(3)

    def second(self):
        for h, block, landed in ((0, 2, self.first_x), (1, 1, self.first_y)):
            self.stage1[h].wait_recv()
            rows = self.parts[h]
            self.pair[0, rows] = (
                self.sums[block][rows].astype(F32) + landed[1].astype(F32)
            ).astype(self.dtype)
            self.stage2[h].start()

    def total(self, h):
        self.stage1[2 + h].wait_recv()
        self.stage2[h].wait_recv()
        near, far = ((self.first_x, self.second_y), (self.first_y, self.second_x))[h]
        return (
            self.sums[3][self.parts[h]].astype(F32)
            + near[0].astype(F32)
            + far[...].astype(F32)
        )

    def finish(self):
        for copy in self.stage0 + self.stage1 + self.stage2:
            copy.wait_send()


def scatter_scratch(rows, columns, dtype, in_place=False):
    half = rows // 2
    shapes = [
        (4, rows, columns),
        (2, half, columns),
        (2, half, columns),
        (half, columns),
        (half, columns),
        (4, rows, columns),
    ]
    return [pltpu.VMEM(shape, dtype) for shape in shapes[: 5 if in_place else 6]]


def scatter_sems(count):
    return [pltpu.SemaphoreType.DMA((count, 10)), pltpu.SemaphoreType.DMA((count, 10))]


class LineGather:
    def __init__(self, line, size, k, source, out, axis, own_sem, send_sem, recv_sem):
        self.line, self.size, self.k, self.source, self.out = line, size, k, source, out
        self.axis, self.send_sem, self.recv_sem = axis, send_sem, recv_sem
        self.own = pltpu.make_async_copy(source, self.place(line), own_sem.at[k])

    def place(self, owner):
        extent = self.source.shape[self.axis]
        span = pl.ds(pl.multiple_of(owner * extent, extent), extent)
        return self.out.at[span] if self.axis == 0 else self.out.at[:, span]

    def hop(self, side, step, owner, source=None):
        target = self.place(owner)
        return push(
            target if source is None else source,
            target,
            self.send_sem.at[self.k, side, step],
            self.recv_sem.at[self.k, side, step],
            "fsdp",
            self.line + 1 - 2 * side,
        )

    def begin(self):
        for side, there in ((0, self.line < self.size - 1), (1, self.line > 0)):

            @pl.when(there)
            def _():
                self.hop(side, 0, self.line, self.source).start()

        self.own.start()

    def step(self, step):
        line, last = self.line, self.size - 1
        for side, owner in ((0, line - 1 - step), (1, line + 1 + step)):

            @pl.when((owner >= 0) & (owner <= last))
            def _():
                self.hop(side, step, owner).wait_recv()

                @pl.when((line < last) if side == 0 else (line > 0))
                def _():
                    self.hop(side, step + 1, owner).start()

    def finish(self):
        line, last = self.line, self.size - 1
        self.own.wait()
        for step in range(self.size - 1):
            for side, owner, there in ((0, line - step, line < last), (1, line + step, line > 0)):

                @pl.when(there & (owner >= 0) & (owner <= last))
                def _():
                    self.hop(side, step, owner).wait_send()


def line_gather_sems(count, size):
    return [
        pltpu.SemaphoreType.DMA((count,)),
        pltpu.SemaphoreType.DMA((count, 2, size)),
        pltpu.SemaphoreType.DMA((count, 2, size)),
    ]


class LineScatter:
    def __init__(self, line, size, k, source, sums, landed, send_sem, recv_sem):
        self.line, self.size, self.k = line, size, k
        self.source, self.sums, self.landed = source, sums, landed
        self.send_sem, self.recv_sem = send_sem, recv_sem

    def hop(self, side, owner):
        return push(
            self.sums.at[side, owner],
            self.landed.at[side, owner],
            self.send_sem.at[self.k, side, owner],
            self.recv_sem.at[self.k, side, owner],
            "fsdp",
            self.line + 1 - 2 * side,
        )

    def begin(self):
        last = self.size - 1
        for far in range(last):
            for side, owner, end in ((0, last - far, 0), (1, far, last)):

                @pl.when(self.line == end)
                def _():
                    self.sums[side, owner] = self.source[owner]
                    self.hop(side, owner).start()

    def pass_on(self, side, owner):
        self.hop(side, owner).wait_recv()
        self.sums[side, owner] = (
            self.source[owner].astype(F32) + self.landed[side, owner].astype(F32)
        ).astype(self.source.dtype)
        self.hop(side, owner).start()

    def step(self, far):
        line, last = self.line, self.size - 1

        @pl.when((line < last - far) & (line > 0))
        def _():
            self.pass_on(0, last - far)

        @pl.when((line > far) & (line < last))
        def _():
            self.pass_on(1, far)

    def total(self):
        line, last = self.line, self.size - 1
        for side, there, beyond in ((0, line > 0, line == 0), (1, line < last, line == last)):

            @pl.when(there)
            def _():
                self.hop(side, line).wait_recv()

            @pl.when(beyond)
            def _():
                self.landed[side, line] = jnp.zeros(self.source.shape[1:], self.source.dtype)

        return (
            self.source[line].astype(F32)
            + self.landed[0, line].astype(F32)
            + self.landed[1, line].astype(F32)
        )

    def finish(self):
        for owner in range(self.size):

            @pl.when(self.line < owner)
            def _():
                self.hop(0, owner).wait_send()

            @pl.when(self.line > owner)
            def _():
                self.hop(1, owner).wait_send()


def line_scatter_sems(count, size):
    return [
        pltpu.SemaphoreType.DMA((count, 2, size)),
        pltpu.SemaphoreType.DMA((count, 2, size)),
    ]


def in_vmem(count):
    return [pl.BlockSpec(memory_space=pltpu.VMEM)] * count


def anywhere(count):
    return [pl.BlockSpec(memory_space=pl.ANY)] * count


def talk_params(collective_id):
    return pltpu.CompilerParams(
        collective_id=collective_id, has_side_effects=True, vmem_limit_bytes=VMEM_LIMIT
    )


def close_kernel(
    size, query_width, da_ref, e_own, e_total, x_ref, middle_ref, grad_ref,
    gain_two_ref, wout_ref, gin_ref, out_low,
    outcome_ref, input_grad_ref, in_out, out_out, gains_out, notes_out,
    e_landed, gains, notes, notes_line, in_low, gain_low, notes_low, *rest,
):
    scratch, rest = rest[:6], rest[6:]
    line_scratch, rest = rest[:4], rest[4:]
    (
        swap_sems, scatter_send, scatter_recv, sum_send, sum_recv,
        line_own, line_send, line_recv, own_sem, send_sem, recv_sem,
    ) = rest
    plane, line = plane_neighbours(), lax.axis_index("fsdp")
    meet(plane, line, size, True)
    sums = (scatter_send, scatter_recv)
    da = Scatter(plane, 0, da_ref, 0, scratch[:6], *sums)
    swap = push(e_total, e_landed, swap_sems.at[0], swap_sems.at[1], "fsdp", pair_of(line))
    gin = LineScatter(line, size, 0, gin_ref, *line_scratch[0:2], sum_send, sum_recv)
    gain = LineScatter(line, size, 1, gains, *line_scratch[2:4], sum_send, sum_recv)
    gathers = (own_sem, send_sem, recv_sem)
    out_all = Gather(plane, 1, out_low, out_out, 0, *gathers)
    half = x_ref.shape[0] // 2
    gin.begin()
    da.begin()
    da.first()
    gin.step(0)
    swap.start()
    da.second()
    gin.step(1)
    gin.step(2)
    out_all.begin()
    gain_one = wout_ref[query_width : query_width + 1, :].astype(F32)
    grad_gain = jnp.zeros((1, x_ref.shape[1]), F32)
    squares = [jnp.zeros((1, 1), F32)] * 5

    def add_square(i, values):
        squares[i] = squares[i] + jnp.sum(
            jnp.sum(values * values, axis=1, keepdims=True), axis=0, keepdims=True
        )

    for h in range(2):
        rows = pl.ds(h * half, half)
        x = x_ref[rows].astype(F32)
        inverse = lax.rsqrt(jnp.mean(x * x, axis=1, keepdims=True) + EPSILON)
        normed = x * inverse
        grad_a = da.total(h)
        grad_gain += jnp.sum(grad_a * normed, axis=0, keepdims=True)
        grad_middle = grad_ref[rows]
        grad_input = grad_middle + norm_back(grad_a * gain_one, normed, inverse)
        input_grad_ref[rows] = grad_input.astype(BF16)
        add_square(0, x)
        add_square(1, middle_ref[rows])
        add_square(3, grad_middle)
        add_square(4, grad_input)
    width = x_ref.shape[1] // size
    row = lax.broadcasted_iota(jnp.int32, gains.shape[1:], 0)
    for p in range(size):
        columns = slice(p * width, (p + 1) * width)
        gains[p] = jnp.where(
            row == 0, grad_gain[:, columns],
            jnp.where(row == 1, gain_two_ref[0:1, columns], 0.0),
        ).astype(BF16)
    gain.begin()
    gain.step(0)
    gain.step(1)
    gain.step(2)
    out_all.relay()
    swap.wait_recv()
    for h in range(2):
        rows = pl.ds(h * half, half)
        outcome = middle_ref[rows] + e_own[rows] + e_landed[rows].astype(F32)
        outcome_ref[rows] = outcome.astype(BF16)
        add_square(2, outcome)
    row = lax.broadcasted_iota(jnp.int32, notes.shape, 0)
    told = jnp.zeros(notes.shape, F32)
    for i in range(5):
        told = jnp.where(row == i, squares[i], told)
    notes[...] = told
    spread = LineGather(line, size, 0, notes, notes_line, 0, line_own, line_send, line_recv)
    spread.begin()
    in_low[...] = gin.total().astype(BF16)
    in_all = Gather(plane, 0, in_low, in_out, 0, *gathers)
    in_all.begin()
    spread.step(0)
    out_all.relay_diagonal()
    spread.step(1)
    spread.step(2)
    gain_low[...] = gain.total().astype(BF16)
    gain_all = Gather(plane, 2, gain_low, gains_out, 0, *gathers)
    gain_all.begin()
    spread.finish()
    count = notes.shape[0]
    notes_low[...] = (
        notes_line[pl.ds(0, count)] + notes_line[pl.ds(count, count)]
        + notes_line[pl.ds(2 * count, count)] + notes_line[pl.ds(3 * count, count)]
    )
    notes_all = Gather(plane, 3, notes_low, notes_out, 0, *gathers)
    notes_all.begin()
    last = (in_all, gain_all, notes_all)
    for item in last:
        item.relay()
    for item in last:
        item.relay_diagonal()
    for item in last + (out_all, da, gin, gain):
        item.finish()
    swap.wait_send()


def close_transfers(
    da_part, e_own, e_total, x, middle, grad_middle, gain_two, w_out, grad_in, out_low,
    query_width, collective_id,
):
    tokens, model_width = x.shape
    size, in_rows, in_columns = grad_in.shape
    out_rows, out_columns = out_low.shape
    wide = (tokens, model_width)
    gain_shape, note_shape = (16, out_columns), (16, LANES)
    line_scratch = []
    for shape in (grad_in.shape, (size,) + gain_shape):
        line_scratch += [pltpu.VMEM((2,) + shape, BF16)] * 2
    return pl.pallas_call(
        functools.partial(close_kernel, size, query_width),
        out_shape=[
            jax.ShapeDtypeStruct(wide, BF16),
            jax.ShapeDtypeStruct(wide, BF16),
            jax.ShapeDtypeStruct((8, in_rows, in_columns), BF16),
            jax.ShapeDtypeStruct((8, out_rows, out_columns), BF16),
            jax.ShapeDtypeStruct((8,) + gain_shape, BF16),
            jax.ShapeDtypeStruct((8,) + note_shape, F32),
        ],
        in_specs=in_vmem(10),
        out_specs=in_vmem(2) + anywhere(4),
        scratch_shapes=[
            pltpu.VMEM(wide, BF16),
            pltpu.VMEM((size,) + gain_shape, BF16),
            pltpu.VMEM(note_shape, F32),
            pltpu.VMEM((size * note_shape[0], LANES), F32),
            pltpu.VMEM((in_rows, in_columns), BF16),
            pltpu.VMEM(gain_shape, BF16),
            pltpu.VMEM(note_shape, F32),
        ]
        + scatter_scratch(*wide, BF16)
        + line_scratch
        + [pltpu.SemaphoreType.DMA((2,))]
        + scatter_sems(1)
        + line_scatter_sems(2, size)
        + line_gather_sems(1, size)
        + gather_sems(4),
        compiler_params=talk_params(collective_id),
        cost_estimate=pl.CostEstimate(flops=0, bytes_accessed=200_000_000, transcendentals=0),
        name="close_transfers",
    )(da_part, e_own, e_total, x, middle, grad_middle, gain_two, w_out, grad_in, out_low)


def dot(first, second, contract=(1, 0)):
    return lax.dot_general(
        first, second, (((contract[0],), (contract[1],)), ((), ())), preferred_element_type=F32
    )


def spin(values, cosine, sine):
    width = values.shape[1]
    half = HEAD_DIM // 2
    cosine = jnp.concatenate([cosine] * (width // LANES), axis=1)
    sine = jnp.concatenate([sine] * (width // LANES), axis=1)
    lane = lax.broadcasted_iota(jnp.int32, values.shape, 1)
    lower = lax.rem(lane, HEAD_DIM) < half
    swapped = jnp.where(
        lower, pltpu.roll(values, width - half, 1), pltpu.roll(values, half, 1)
    )
    return values * cosine + swapped * sine


def attend_kernel(per_group, x_ref, w_in_ref, w_out_ref, cos_ref, sin_ref, part_ref, *outs):
    def take(rows):
        return x_ref[rows, :]

    def put(i, part):
        part_ref[i * BLOCK : (i + 1) * BLOCK, :] = part

    attend_steps(
        per_group, x_ref.shape[0], take, put, lambda step: None, w_in_ref, w_out_ref, cos_ref,
        sin_ref, *outs,
    )


def attend_steps(
    per_group, length, take, put, hook, w_in_ref, w_out_ref, cos_ref, sin_ref,
    a_ref, q_ref, k_ref, v_ref, o_ref, lse_ref,
):
    query_width = per_group * HEAD_DIM
    turned = query_width + HEAD_DIM
    gain = w_out_ref[query_width : query_width + 1, :].astype(F32)

    def project(i, carry):
        rows = pl.ds(pl.multiple_of(i * BLOCK, BLOCK), BLOCK)
        x = take(rows).astype(F32)
        inverse = lax.rsqrt(jnp.mean(x * x, axis=1, keepdims=True) + EPSILON)
        a = (x * inverse * gain).astype(BF16)
        a_ref[rows, :] = a
        pre = dot(a, w_in_ref[...])
        spun = spin(pre[:, :turned], cos_ref[rows, :], sin_ref[rows, :]).astype(BF16)
        for h in range(per_group):
            q_ref[h, rows, :] = spun[:, h * HEAD_DIM : (h + 1) * HEAD_DIM]
        k_ref[rows, :] = spun[:, query_width:turned]
        v_ref[rows, :] = pre[:, turned : turned + HEAD_DIM].astype(BF16)
        return carry

    lax.fori_loop(0, length // BLOCK, project, 0)
    hook(0)
    for i in range(length // BLOCK):
        seen = (i + 1) * BLOCK
        rows = slice(i * BLOCK, seen)
        keys, values = k_ref[:seen, :], v_ref[:seen, :]
        for h in range(per_group):
            scores = dot(q_ref[h, rows, :], keys, (1, 1)) * ATTENTION_SCALE
            peak = jnp.max(scores, axis=1, keepdims=True)
            lifted = jnp.exp(scores - peak)
            total = jnp.sum(lifted, axis=1, keepdims=True)
            weights = (lifted * (1.0 / total)).astype(BF16)
            mixed = dot(weights, values)
            o_ref[rows, h * HEAD_DIM : (h + 1) * HEAD_DIM] = mixed.astype(BF16)
            lse_ref[h, rows, :] = peak + jnp.log(total)
        put(i, dot(o_ref[rows, :], w_out_ref[:query_width, :]).astype(BF16))
        hook(1 + i)


def saved_shapes(length, model_width, per_group):
    return [
        jax.ShapeDtypeStruct((length, model_width), BF16),
        jax.ShapeDtypeStruct((per_group, length, HEAD_DIM), BF16),
        jax.ShapeDtypeStruct((length, HEAD_DIM), BF16),
        jax.ShapeDtypeStruct((length, HEAD_DIM), BF16),
        jax.ShapeDtypeStruct((length, per_group * HEAD_DIM), BF16),
        jax.ShapeDtypeStruct((per_group, length, 1), F32),
    ]


def front_kernel(
    size, per_group, router_at, x_ref, dy_ref, win_shard, wout_shard, chosen_ref, cos_ref, sin_ref,
    dy_out, win_ref, wout_ref, *rest,
):
    saved, rest = rest[:6], rest[6:]
    b_out, g_out, middle_ref, marked_ref, *rest = rest
    x_all, part_ref, dy_landed, routed, b_landed, g_landed, *rest = rest
    scratch, rest = rest[:5], rest[5:]
    (
        swap_sems, scatter_send, scatter_recv, own_sem, send_sem, recv_sem,
        line_own, line_send, line_recv,
    ) = rest
    plane, line = plane_neighbours(), lax.axis_index("fsdp")
    pair = pair_of(line)
    tokens = x_ref.shape[0]
    half, per_block = tokens // 2, BLOCK // tokens
    query_width = per_group * HEAD_DIM
    meet(plane, line, size, True)
    sems = (own_sem, send_sem, recv_sem)
    line_sems = (line_own, line_send, line_recv)
    x = Gather(plane, 0, x_ref, x_all, 0, *sems)
    dy = Gather(plane, 1, dy_ref, dy_out, 0, *sems)
    other = Gather(plane, 2, dy_landed, dy_out, 8, *sems)
    win = LineGather(line, size, 0, win_shard, win_ref, 0, *line_sems)
    wout = LineGather(line, size, 1, wout_shard, wout_ref, 1, *line_sems)
    scatter = Scatter(plane, 0, part_ref, 0, scratch, scatter_send, scatter_recv)
    swap_dy = push(dy_ref, dy_landed, swap_sems.at[0], swap_sems.at[1], "fsdp", pair)
    swap_b = push(routed, b_landed, swap_sems.at[2], swap_sems.at[3], "fsdp", pair)
    swap_g = push(marked_ref, g_landed, swap_sems.at[4], swap_sems.at[5], "fsdp", pair)
    win.begin()
    x.begin()
    wout.begin()
    x.relay()
    win.step(0)
    x.relay_diagonal()
    wout.step(0)
    dy.begin()
    win.step(1)
    swap_dy.start()
    wout.step(1)
    win.step(2)
    wout.step(2)
    for item in (x, win, wout):
        item.finish()

    def take(rows):
        block = pl.ds(rows.start // tokens, per_block)
        return x_all[block].reshape(BLOCK, x_all.shape[2])

    def put(i, part):
        for t in range(per_block):
            part_ref[per_block * i + t] = part[t * tokens : (t + 1) * tokens]

    def hook(step):
        if step == 0:
            dy.relay()
        elif step == 2:
            dy.relay_diagonal()
        elif step == 3:
            swap_dy.wait_recv()
            other.begin()

    attend_steps(
        per_group, x_all.shape[0] * tokens, take, put, hook, win_ref, wout_ref, cos_ref, sin_ref,
        *saved,
    )
    scatter.begin()
    scatter.first()
    other.relay()
    scatter.second()
    gain = wout_ref[query_width + 1 : query_width + 2, :].astype(F32)
    router = win_ref[:, router_at : router_at + LANES]
    for h in range(2):
        rows = pl.ds(h * half, half)
        middle = x_ref[rows].astype(F32) + RESIDUAL_SCALE * scatter.total(h)
        middle_ref[rows] = middle
        inverse = lax.rsqrt(jnp.mean(middle * middle, axis=1, keepdims=True) + EPSILON)
        b = (middle * inverse * gain).astype(BF16)
        routed[rows] = b
        chosen = chosen_ref[rows] > 0.0
        logits = jnp.where(chosen, dot(b, router), -1e30)
        lifted = jnp.where(chosen, jnp.exp(logits - jnp.max(logits, axis=1, keepdims=True)), 0.0)
        gates = lifted / jnp.sum(lifted, axis=1, keepdims=True)
        marked_ref[rows] = jnp.where(chosen, gates, -1.0)
    swap_b.start()
    swap_g.start()
    b = Gather(plane, 3, routed, b_out, 0, *sems)
    g = Gather(plane, 4, marked_ref, g_out, 0, *sems)
    b_other = Gather(plane, 5, b_landed, b_out, 8, *sems)
    g_other = Gather(plane, 6, g_landed, g_out, 8, *sems)
    b.begin()
    g.begin()
    other.relay_diagonal()
    b.relay()
    g.relay()
    b.relay_diagonal()
    g.relay_diagonal()
    swap_b.wait_recv()
    swap_g.wait_recv()
    b_other.begin()
    g_other.begin()
    b_other.relay()
    g_other.relay()
    b_other.relay_diagonal()
    g_other.relay_diagonal()
    for item in (dy, other, b, g, b_other, g_other, scatter):
        item.finish()
    for swap in (swap_dy, swap_b, swap_g):
        swap.wait_send()


def front(
    x, dy, w_in_shard, w_out_shard, chosen, cosine, sine, size, per_group, router_at, collective_id
):
    tokens, model_width = x.shape
    rows, columns = w_in_shard.shape
    out_rows, out_columns = w_out_shard.shape
    wide, narrow = (tokens, model_width), (tokens, LANES)
    out = pl.pallas_call(
        functools.partial(front_kernel, size, per_group, router_at),
        out_shape=[
            jax.ShapeDtypeStruct((16,) + wide, BF16),
            jax.ShapeDtypeStruct((rows * size, columns), BF16),
            jax.ShapeDtypeStruct((out_rows, out_columns * size), BF16),
        ]
        + saved_shapes(8 * tokens, model_width, per_group)
        + [
            jax.ShapeDtypeStruct((16,) + wide, BF16),
            jax.ShapeDtypeStruct((16,) + narrow, F32),
            jax.ShapeDtypeStruct(wide, F32),
            jax.ShapeDtypeStruct(narrow, F32),
        ],
        in_specs=in_vmem(7),
        out_specs=anywhere(1) + in_vmem(8) + anywhere(2) + in_vmem(2),
        scratch_shapes=[
            pltpu.VMEM((8,) + wide, BF16),
            pltpu.VMEM((8,) + wide, BF16),
            pltpu.VMEM(wide, BF16),
            pltpu.VMEM(wide, BF16),
            pltpu.VMEM(wide, BF16),
            pltpu.VMEM(narrow, F32),
        ]
        + scatter_scratch(*wide, BF16, True)
        + [pltpu.SemaphoreType.DMA((6,))]
        + scatter_sems(1)
        + gather_sems(7)
        + line_gather_sems(2, size),
        compiler_params=talk_params(collective_id),
        cost_estimate=pl.CostEstimate(
            flops=8_000_000_000, bytes_accessed=150_000_000, transcendentals=2_000_000
        ),
        name="front",
    )(x, dy, w_in_shard, w_out_shard, chosen, cosine, sine)
    return [*out[:3], out[3:9], *out[9:]]


def attend(x_all, w_in, w_out, cosine, sine, per_group):
    length, model_width = x_all.shape
    shapes = [jax.ShapeDtypeStruct((length, model_width), BF16)]
    shapes += saved_shapes(length, model_width, per_group)
    return pl.pallas_call(
        functools.partial(attend_kernel, per_group),
        out_shape=shapes,
        in_specs=[pl.BlockSpec(memory_space=pltpu.VMEM)] * 5,
        out_specs=[pl.BlockSpec(memory_space=pltpu.VMEM)] * len(shapes),
        compiler_params=pltpu.CompilerParams(vmem_limit_bytes=VMEM_LIMIT),
        cost_estimate=pl.CostEstimate(
            flops=8_000_000_000, bytes_accessed=16_000_000, transcendentals=2_000_000
        ),
        name="attend",
    )(x_all, w_in, w_out, cosine, sine)


def attend_back_kernel(per_group, *refs):
    attend_back_steps(per_group, lambda step: None, *refs)


def attend_back_talk_kernel(per_group, size, swaps, *refs):
    ins, refs = refs[:13], refs[13:]
    sum_ref, sent, refs = refs[0], refs[1 : 1 + swaps], refs[1 + swaps :]
    part_ref, gin_ref, out_low, e_own, e_other = refs[:5]
    came, refs = refs[5 : 5 + swaps], refs[5 + swaps :]
    scratch, stage_a, stage_b, refs = refs[:5], refs[5:11], refs[11:17], refs[17:]
    gout_ref, line_sums, line_landed, sends, receives, swap_sems, line_send, line_recv = refs
    plane, line = plane_neighbours(), lax.axis_index("fsdp")
    other = Scatter(plane, 0, sum_ref, 8, stage_a, sends, receives)
    mine = Scatter(plane, 1, sum_ref, 0, stage_b, sends, receives)
    gout = LineScatter(line, size, 0, gout_ref, line_sums, line_landed, line_send, line_recv)
    across = [
        push(source, target, swap_sems.at[0, i], swap_sems.at[1, i], "fsdp", pair_of(line))
        for i, (source, target) in enumerate(zip(sent, came))
    ]
    half = e_own.shape[0] // 2

    def hook(step):
        if step == 0:
            meet(plane, line, size, True)
            other.begin()
            mine.begin()
            gout.begin()
            across[0].start()
        elif step == 1:
            other.first()
            gout.step(0)
            for copy in across[1:2]:
                copy.start()
        elif step == 2:
            mine.first()
            gout.step(1)
            for copy in across[2:]:
                copy.start()
        elif step == 3:
            other.second()
            gout.step(2)
        elif step == 4:
            mine.second()
        elif step == 6:
            for h in range(2):
                e_other[pl.ds(h * half, half)] = other.total(h).astype(BF16)
                e_own[pl.ds(h * half, half)] = mine.total(h)
            out_low[...] = gout.total().astype(BF16)
            for item in (other, mine, gout):
                item.finish()
            for copy in across:
                copy.wait()

    attend_back_steps(per_group, hook, *ins, part_ref, gin_ref, gout_ref, *scratch)


def attend_back_steps(
    per_group, hook, dw_ref, w_in_ref, w_out_ref, cos_ref, sin_ref,
    a_ref, q_ref, k_ref, v_ref, o_ref, lse_ref, b_all_ref, dl_ref,
    part_ref, gin_ref, gout_ref,
    turn_ref, dv_ref, back_ref, b_ref, b_sem,
):
    length, model_width = dw_ref.shape
    fetch = pltpu.make_async_copy(b_all_ref.at[pl.ds(0, length)], b_ref, b_sem)
    fetch.start()
    query_width = per_group * HEAD_DIM
    turned = query_width + HEAD_DIM
    blocks = length // BLOCK
    chunk = 384

    def out_grads(i, carry):
        columns = pl.ds(pl.multiple_of(i * chunk, chunk), chunk)
        gout_ref[i] = dot(o_ref[...], dw_ref[:, columns], (0, 0)).astype(BF16)
        return carry

    lax.fori_loop(0, model_width // chunk, out_grads, 0)
    hook(0)
    turn_ref[...] = jnp.zeros_like(turn_ref)
    dv_ref[...] = jnp.zeros_like(dv_ref)
    for i in range(blocks):
        seen = (i + 1) * BLOCK
        rows = slice(i * BLOCK, seen)
        keys, values = k_ref[:seen, :], v_ref[:seen, :]
        grad = dot(dw_ref[rows, :], w_out_ref[:query_width, :], (1, 1)).astype(BF16)
        for h in range(per_group):
            columns = slice(h * HEAD_DIM, (h + 1) * HEAD_DIM)
            queries = q_ref[h, rows, :]
            grad_head = grad[:, columns]
            scores = dot(queries, keys, (1, 1)) * ATTENTION_SCALE
            probs = jnp.exp(scores - lse_ref[h, rows, :])
            dv_ref[:seen, :] += dot(probs.astype(BF16), grad_head, (0, 0))
            grad_probs = dot(grad_head, values, (1, 1))
            inner = jnp.sum(probs * grad_probs, axis=1, keepdims=True)
            grad_scores = (probs * (grad_probs - inner)).astype(BF16)
            turn_ref[rows, columns] = dot(grad_scores, keys) * ATTENTION_SCALE
            turn_ref[:seen, query_width:turned] += (
                dot(grad_scores, queries, (0, 0)) * ATTENTION_SCALE
            )
        hook(1 + i)

    def unturn(i, carry):
        rows = pl.ds(pl.multiple_of(i * BLOCK, BLOCK), BLOCK)
        back_ref[rows, :turned] = spin(
            turn_ref[rows, :], cos_ref[rows, :], -sin_ref[rows, :]
        ).astype(BF16)
        back_ref[rows, turned:] = jnp.concatenate(
            [dv_ref[rows, :].astype(BF16), jnp.zeros((BLOCK, LANES - HEAD_DIM), BF16)], axis=1
        )
        part_ref[rows, :] = dot(
            back_ref[rows, : turned + HEAD_DIM], w_in_ref[:, : turned + HEAD_DIM], (1, 1)
        ).astype(BF16)
        return carry

    lax.fori_loop(0, blocks, unturn, 0)
    hook(5)
    fetch.wait()

    def weight_grads(i, carry):
        columns = pl.ds(pl.multiple_of(i * chunk, chunk), chunk)
        a = a_ref[:, columns]
        gin_ref[columns, :turned] = dot(a, back_ref[:, :turned], (0, 0)).astype(BF16)
        gin_ref[columns, turned:] = (
            dot(a, back_ref[:, turned:], (0, 0)) + dot(b_ref[:, columns], dl_ref[...], (0, 0))
        ).astype(BF16)
        return carry

    lax.fori_loop(0, model_width // chunk, weight_grads, 0)
    hook(6)


def attend_back(
    dw_all, w_in, w_out, cosine, sine, saved, b_all, dl_all, per_group, talk=None, collective_id=None
):
    length, model_width = dw_all.shape
    query_width = per_group * HEAD_DIM
    turned = query_width + HEAD_DIM
    shapes = [
        jax.ShapeDtypeStruct((length, model_width), BF16),
        jax.ShapeDtypeStruct((model_width, w_in.shape[1]), BF16),
        jax.ShapeDtypeStruct((model_width // 384, query_width, 384), BF16),
    ]
    scratch = [
        pltpu.VMEM((length, turned), F32),
        pltpu.VMEM((length, HEAD_DIM), F32),
        pltpu.VMEM((length, w_in.shape[1]), BF16),
        pltpu.VMEM((length, model_width), BF16),
        pltpu.SemaphoreType.DMA,
    ]
    operands = (dw_all, w_in, w_out, cosine, sine, *saved, b_all, dl_all)
    in_specs, out_specs = in_vmem(11) + anywhere(1) + in_vmem(1), in_vmem(len(shapes))
    kernel = functools.partial(attend_back_kernel, per_group)
    params = pltpu.CompilerParams(vmem_limit_bytes=VMEM_LIMIT)
    if talk is not None:
        sum_part, sent = talk
        wide = sum_part.shape[1:]
        shapes = shapes + [jax.ShapeDtypeStruct(wide, F32), jax.ShapeDtypeStruct(wide, BF16)]
        shapes += [jax.ShapeDtypeStruct(array.shape, array.dtype) for array in sent]
        gout_shape, size = shapes[2].shape, lax.axis_size("fsdp")
        shapes[2] = jax.ShapeDtypeStruct(gout_shape[1:], BF16)
        scratch = scratch + scatter_scratch(*wide, BF16) * 2
        scratch += [pltpu.VMEM(gout_shape, BF16)] + [pltpu.VMEM((2,) + gout_shape, BF16)] * 2
        scratch += scatter_sems(2) + [pltpu.SemaphoreType.DMA((2, len(sent)))]
        scratch += line_scatter_sems(1, size)
        operands += (sum_part, *sent)
        in_specs = in_specs + in_vmem(1) + anywhere(len(sent))
        out_specs = out_specs + in_vmem(2) + anywhere(len(sent))
        kernel = functools.partial(attend_back_talk_kernel, per_group, size, len(sent))
        params = talk_params(collective_id)
    return pl.pallas_call(
        kernel,
        out_shape=shapes,
        in_specs=in_specs,
        out_specs=out_specs,
        scratch_shapes=scratch,
        compiler_params=params,
        cost_estimate=pl.CostEstimate(
            flops=20_000_000_000, bytes_accessed=30_000_000, transcendentals=2_000_000
        ),
        name="attend_back",
    )(*operands)


def experts_kernel(
    here, tile,
    place_ref, b_hbm, dy_hbm, g_ref, gate_hbm, up_hbm, down_hbm, *rest,
):
    out_hbm, db_hbm, dg_ref = rest[:3]
    grad_hbm, rest = rest[3:6], rest[6:]
    (
        b_ref, dy_ref, in_ref, down_ref, hidden_ref, back_ref, out_ref, db_ref,
        gate_stage, up_stage, down_stage, weight_sem, tile_sem, out_sem, grad_sem,
    ) = rest
    rows_all, model_width = b_ref.shape
    width = down_ref.shape[0] // here
    tiles = rows_all // tile
    first = place_ref[0]

    def columns_of(e):
        return slice(e * width, (e + 1) * width)

    loads = []
    for e in range(here):
        loads.append((gate_hbm.at[e], in_ref.at[:, columns_of(e)]))
        loads.append((up_hbm.at[e], in_ref.at[:, columns_of(here + e)]))
    for e in range(here):
        loads.append((down_hbm.at[e], down_ref.at[columns_of(e), :]))
    loads = [
        pltpu.make_async_copy(source, target, weight_sem.at[i])
        for i, (source, target) in enumerate(loads)
    ]

    def tile_rows(i):
        return pl.ds(pl.multiple_of(i * tile, tile), tile)

    def tile_load(i, k):
        source, target = ((b_hbm, b_ref), (dy_hbm, dy_ref))[k]
        return pltpu.make_async_copy(
            source.at[tile_rows(i)], target.at[tile_rows(i)], tile_sem.at[k, i]
        )

    def tile_store(i, k):
        source, target = ((out_ref, out_hbm), (db_ref, db_hbm))[k]
        return pltpu.make_async_copy(
            source.at[tile_rows(i)], target.at[tile_rows(i)], out_sem.at[k, i]
        )

    for k in range(2):
        tile_load(0, k).start()
    for load in loads:
        load.start()
    for i in range(1, tiles):
        for k in range(2):
            tile_load(i, k).start()
    for load in loads:
        load.wait()

    def forward_back(i, carry):
        rows = tile_rows(i)
        tile_load(i, 0).wait()
        tile_load(i, 1).wait()
        pre = dot(b_ref[rows, :], in_ref[...])
        grad_mixed = dot(dy_ref[rows, :], down_ref[...], (1, 1))
        gates = g_ref[rows, :]
        lane = lax.broadcasted_iota(jnp.int32, gates.shape, 1)
        inner = jnp.zeros(gates.shape, F32)
        for e in range(here):
            mine = lane == first + e
            gate = jnp.sum(jnp.where(mine, jnp.maximum(gates, 0.0), 0.0), axis=1, keepdims=True)
            scale = RESIDUAL_SCALE * gate
            gate_pre, up_pre = pre[:, columns_of(e)], pre[:, columns_of(here + e)]
            sigmoid = 1.0 / (1.0 + jnp.exp(-gate_pre))
            silu = gate_pre * sigmoid
            hidden = silu * up_pre
            grad = grad_mixed[:, columns_of(e)]
            share = jnp.sum(hidden * grad, axis=1, keepdims=True)
            inner = jnp.where(mine, RESIDUAL_SCALE * share, inner)
            hidden_ref[rows, columns_of(e)] = (scale * hidden).astype(BF16)
            grad = scale * grad
            back_ref[rows, columns_of(e)] = (
                grad * up_pre * sigmoid * (1.0 + gate_pre * (1.0 - sigmoid))
            ).astype(BF16)
            back_ref[rows, columns_of(here + e)] = (grad * silu).astype(BF16)
        dg_ref[rows, :] = inner
        db_ref[rows, :] = dot(back_ref[rows, :], in_ref[...], (1, 1)).astype(BF16)
        tile_store(i, 1).start()
        out_ref[rows, :] = dot(hidden_ref[rows, :], down_ref[...]).astype(BF16)
        tile_store(i, 0).start()
        return carry

    lax.fori_loop(0, tiles, forward_back, 0)
    parts = 4
    part = model_width // parts

    def part_columns(i):
        return pl.ds(pl.multiple_of(i * part, part), part)

    def down_grad(i, carry):
        grad = dot(hidden_ref[...], dy_ref[:, part_columns(i)], (0, 0))
        for e in range(here):
            down_stage[i, e] = grad[columns_of(e), :].astype(BF16)
        return carry

    def in_grad(i, carry):
        grad = dot(b_ref[:, part_columns(i)], back_ref[...], (0, 0))
        for e in range(here):
            gate_stage[i, e] = grad[:, columns_of(e)].astype(BF16)
            up_stage[i, e] = grad[:, columns_of(here + e)].astype(BF16)
        return carry

    stores = []

    def store(k, stage):
        copy = pltpu.make_async_copy(stage, grad_hbm[k], grad_sem.at[k])
        copy.start()
        stores.append(copy)

    lax.fori_loop(0, parts, down_grad, 0)
    store(2, down_stage)
    lax.fori_loop(0, parts, in_grad, 0)
    store(0, gate_stage)
    store(1, up_stage)
    for copy in stores:
        copy.wait()
    for i in range(tiles):
        for k in range(2):
            tile_store(i, k).wait()


def experts(place, b_all, dy_all, g_all, w_gate, w_up, w_down):
    sources, tokens, model_width = b_all.shape
    here, _, hidden_width = w_gate.shape
    rows_all = sources * tokens
    width = hidden_width
    part = model_width // 4
    tile = 256
    tiles = rows_all // tile
    in_stage, down_stage = (4, here, part, width), (4, here, width, part)
    shapes = [in_stage, in_stage, down_stage]
    flat = (rows_all, model_width)
    out = pl.pallas_call(
        functools.partial(experts_kernel, here, tile),
        out_shape=[
            jax.ShapeDtypeStruct(flat, BF16),
            jax.ShapeDtypeStruct(flat, BF16),
            jax.ShapeDtypeStruct((rows_all, LANES), F32),
        ]
        + [jax.ShapeDtypeStruct(shape, BF16) for shape in shapes],
        in_specs=[pl.BlockSpec(memory_space=pltpu.SMEM)] + anywhere(2) + in_vmem(1) + anywhere(3),
        out_specs=anywhere(2) + in_vmem(1) + anywhere(len(shapes)),
        scratch_shapes=[
            pltpu.VMEM(flat, BF16),
            pltpu.VMEM(flat, BF16),
            pltpu.VMEM((model_width, 2 * here * width), BF16),
            pltpu.VMEM((here * width, model_width), BF16),
            pltpu.VMEM((rows_all, here * width), BF16),
            pltpu.VMEM((rows_all, 2 * here * width), BF16),
            pltpu.VMEM(flat, BF16),
            pltpu.VMEM(flat, BF16),
            pltpu.VMEM(in_stage, BF16),
            pltpu.VMEM(in_stage, BF16),
            pltpu.VMEM(down_stage, BF16),
            pltpu.SemaphoreType.DMA((3 * here,)),
            pltpu.SemaphoreType.DMA((2, tiles)),
            pltpu.SemaphoreType.DMA((2, tiles)),
            pltpu.SemaphoreType.DMA((3,)),
        ],
        compiler_params=pltpu.CompilerParams(vmem_limit_bytes=VMEM_LIMIT),
        cost_estimate=pl.CostEstimate(
            flops=43_000_000_000, bytes_accessed=42_000_000, transcendentals=1_000_000
        ),
        name="experts",
    )(
        place, b_all.reshape(flat), dy_all.reshape(flat), g_all.reshape(rows_all, LANES),
        w_gate, w_up, w_down,
    )
    return [
        out[0].reshape(b_all.shape), out[1].reshape(b_all.shape),
        out[2].reshape(sources, tokens, LANES), *out[3:],
    ]


class Trade:
    def __init__(self, line, stages, nears, came, far, sems):
        self.beside, self.across = beside(line), pair_of(line)
        self.stages, self.nears, self.came, self.far, self.sems = stages, nears, came, far, sems

    def copies(self, e, hop):
        made = []
        for k in range(3):
            source = self.stages[k].at[e, (1, 0, 3)[hop]]
            target = self.far[3 * e + k] if hop == 2 else (self.nears, self.came)[hop][k].at[e]
            peer = self.across if hop == 2 else self.beside
            made.append(
                push(source, target, self.sems.at[0, hop, k, e], self.sems.at[1, hop, k, e], "fsdp", peer)
            )
        return made

    def send(self, e, hop):
        for copy in self.copies(e, hop):
            copy.start()

    def add(self, e):
        for k, copy in enumerate(self.copies(e, 0)):
            copy.wait_recv()
            self.stages[k][e, 3] = (
                self.stages[k][e, 3].astype(F32) + self.nears[k][e].astype(F32)
            ).astype(BF16)

    def finish(self, count):
        for e in range(count):
            for hop in range(3 if e < count - 1 else 2):
                for copy in self.copies(e, hop):
                    copy.wait_send()
                    if hop:
                        copy.wait_recv()


def experts_back_kernel(
    here, tile, lane_of, query_width, router_at,
    b_hbm, dy_hbm, g_ref, gate_hbm, up_hbm, down_hbm,
    middle_ref, marked_ref, win_ref, wout_ref,
    out_hbm, dw_out, dl_out, grad_ref, gain_ref, *rest,
):
    kept_hbm, came_hbm, rest = rest[0:3], rest[3:6], rest[6:]
    far_hbm, rest = rest[: 3 * (here - 1)], rest[3 * (here - 1) :]
    other_hbm, rest = rest[:3], rest[3:]
    (
        b_ref, dy_ref, in_ref, down_ref, hidden_ref, back_ref, out_ref, db_ref, dg_ref,
        down_stage, gate_stage, up_stage, down_near, gate_near, up_near,
        dw_own, dl_own, db_total, dg_total, db_landed, dg_landed,
    ) = rest[:21]
    scratch, rest = rest[21:41], rest[41:]
    (
        weight_sem, tile_sem, out_sem, kept_sem, other_sem, trade_sems, swap_sems,
        scatter_send, scatter_recv, own_sem, send_sem, recv_sem,
    ) = rest
    rows_all, model_width = b_ref.shape
    width = down_ref.shape[1]
    tiles = rows_all // tile
    tokens = middle_ref.shape[0]
    per_tile = tile // tokens
    plane, line = plane_neighbours(), lax.axis_index("fsdp")
    me = plane[0]
    first = me * here + lane_of
    high, low = line // 2, lax.rem(line, 2)
    span = pl.ds(pl.multiple_of(high * width, width), width)

    def weight_loads(e):
        pairs = (
            (gate_hbm.at[e, :, span], in_ref.at[e, :, pl.ds(0, width)]),
            (up_hbm.at[e, :, span], in_ref.at[e, :, pl.ds(width, width)]),
            (down_hbm.at[e, span, :], down_ref.at[e]),
        )
        return [
            pltpu.make_async_copy(source, target, weight_sem.at[e, i])
            for i, (source, target) in enumerate(pairs)
        ]

    def tile_rows(j):
        return pl.ds(pl.multiple_of(j * tile, tile), tile)

    def tile_loads(j):
        return [
            pltpu.make_async_copy(
                source.at[tile_rows(j)], target.at[tile_rows(j)], tile_sem.at[k, j]
            )
            for k, (source, target) in enumerate(((b_hbm, b_ref), (dy_hbm, dy_ref)))
        ]

    def tile_store(j):
        return pltpu.make_async_copy(
            out_ref.at[tile_rows(j)], out_hbm.at[tile_rows(j)], out_sem.at[j]
        )

    def place_of(i):
        return lax.rem(i + tiles // 2, tiles)

    def start_loads(i, carry):
        for load in tile_loads(place_of(i)):
            load.start()
        return carry

    start_loads(0, 0)
    for load in weight_loads(0):
        load.start()
    lax.fori_loop(1, tiles, start_loads, 0)
    for e in range(1, here):
        for load in weight_loads(e):
            load.start()
    meet(plane, line, 4, False)
    trade = Trade(
        line, (down_stage, gate_stage, up_stage), (down_near, gate_near, up_near),
        came_hbm, far_hbm, trade_sems,
    )
    sums = (scatter_send, scatter_recv)
    db_other = Scatter(plane, 0, db_ref, 8, scratch[:5], *sums)
    dg_other = Scatter(plane, 1, dg_ref, 8, scratch[5:10], *sums)
    db = Scatter(plane, 2, db_ref, 0, scratch[10:15], *sums)
    dg = Scatter(plane, 3, dg_ref, 0, scratch[15:20], *sums)
    swap_g = push(dg_total, dg_landed, swap_sems.at[0], swap_sems.at[1], "fsdp", pair_of(line))
    swap_b = push(db_total, db_landed, swap_sems.at[2], swap_sems.at[3], "fsdp", pair_of(line))
    half = tokens // 2
    part = model_width // 4

    def one_expert(e, carry):
        for load in weight_loads(e):
            load.wait()
        last = e == here - 1

        def forward_back(i, carry):
            j = place_of(i)
            rows = tile_rows(j)

            @pl.when(e == 0)
            def _():
                for load in tile_loads(j):
                    load.wait()

            pre = dot(b_ref[rows, :], in_ref[e])
            grad = dot(dy_ref[rows, :], down_ref[e], (1, 1))
            gates = g_ref[rows, :]
            mine = lax.broadcasted_iota(jnp.int32, gates.shape, 1) == first + e
            gate = jnp.sum(jnp.where(mine, jnp.maximum(gates, 0.0), 0.0), axis=1, keepdims=True)
            scale = RESIDUAL_SCALE * gate
            gate_pre, up_pre = pre[:, :width], pre[:, width:]
            sigmoid = 1.0 / (1.0 + jnp.exp(-gate_pre))
            silu = gate_pre * sigmoid
            hidden = silu * up_pre
            share = jnp.sum(hidden * grad, axis=1, keepdims=True)
            inner = jnp.where(mine, RESIDUAL_SCALE * share, 0.0)
            hidden_ref[rows, :] = (scale * hidden).astype(BF16)
            grad = scale * grad
            back_ref[rows, :width] = (
                grad * up_pre * sigmoid * (1.0 + gate_pre * (1.0 - sigmoid))
            ).astype(BF16)
            back_ref[rows, width:] = (grad * silu).astype(BF16)
            made = dot(hidden_ref[rows, :], down_ref[e])
            back = dot(back_ref[rows, :], in_ref[e], (1, 1))

            @pl.when(e == 0)
            def _():
                out_ref[rows, :] = made.astype(BF16)
                for t in range(per_tile):
                    piece = slice(t * tokens, (t + 1) * tokens)
                    db_ref[per_tile * j + t] = back[piece].astype(BF16)
                    dg_ref[per_tile * j + t] = inner[piece]

            @pl.when(e > 0)
            def _():
                out_ref[rows, :] = (out_ref[rows, :].astype(F32) + made).astype(BF16)
                for t in range(per_tile):
                    piece = slice(t * tokens, (t + 1) * tokens)
                    block = per_tile * j + t
                    db_ref[block] = (db_ref[block].astype(F32) + back[piece]).astype(BF16)
                    dg_ref[block] += inner[piece]

            @pl.when(last)
            def _():
                tile_store(j).start()

            @pl.when((e == 1) & (i == tiles - 3))
            def _():
                trade.add(0)
                trade.send(0, 2)

            @pl.when(last & (i == tiles // 2 - 1))
            def _():
                dg_other.begin()
                db_other.begin()

            @pl.when(last & (i == tiles - 2))
            def _():
                dg_other.first()
                db_other.first()

            return carry

        lax.fori_loop(0, tiles, forward_back, 0)

        @pl.when(last)
        def _():
            dg.begin()
            db.begin()
            dg_other.second()
            db_other.second()

        def weight_grads(p, carry):
            i = p + 1 - 2 * lax.rem(p, 2)
            parity = jnp.where(p < 2, 1 - low, low)
            side = jnp.where(lax.rem(i, 2) == 0, high, 1 - high)
            columns = pl.ds(pl.multiple_of((2 * side + parity) * part, part), part)
            down_stage[e, i] = dot(hidden_ref[...], dy_ref[:, columns], (0, 0)).astype(BF16)
            grad = dot(b_ref[:, columns], back_ref[...], (0, 0))
            gate_stage[e, i] = grad[:, :width].astype(BF16)
            up_stage[e, i] = grad[:, width:].astype(BF16)

            @pl.when((p == 0) & (e < here - 1))
            def _():
                trade.send(e, 0)

            @pl.when((p == 1) & (e < here - 2))
            def _():
                trade.send(e, 1)

            @pl.when(last & (p == 1))
            def _():
                for h in range(2):
                    rows = pl.ds(h * half, half)
                    dg_total[rows] = dg_other.total(h)
                    db_total[rows] = db_other.total(h).astype(BF16)
                swap_g.start()
                swap_b.start()

            @pl.when(last & (p == 2))
            def _():
                dg.first()
                db.first()
                trade.add(here - 2)
                trade.send(here - 2, 2)
                trade.send(here - 2, 1)
                trade.send(here - 1, 0)
                trade.send(here - 1, 1)

            return carry

        lax.fori_loop(0, 4, weight_grads, 0)
        return carry

    lax.fori_loop(0, here, one_expert, 0)
    stores = [
        pltpu.make_async_copy(stage.at[e, 2], kept_hbm[k].at[e], kept_sem.at[k, e])
        for k, stage in enumerate((down_stage, gate_stage, up_stage))
        for e in range(here)
    ]
    for store in stores:
        store.start()
    dg.second()
    db.second()
    gain = wout_ref[query_width + 1 : query_width + 2, :].astype(F32)
    router = win_ref[:, router_at : router_at + LANES]
    gain_grad = jnp.zeros((1, model_width), F32)
    sums_g = [dg.total(h) for h in range(2)]
    swap_g.wait_recv()
    swap_b.wait_recv()
    for h in range(2):
        rows = pl.ds(h * half, half)
        gates = jnp.maximum(marked_ref[rows], 0.0)
        grad_gates = sums_g[h] + dg_landed[rows]
        grad_chosen = gates * (
            grad_gates - jnp.sum(gates * grad_gates, axis=1, keepdims=True)
        )
        grad_logits = grad_chosen.astype(BF16)
        dl_own[rows] = grad_logits
        grad_b = dot(grad_logits, router, (1, 1)) + db.total(h) + db_landed[rows].astype(F32)
        middle = middle_ref[rows]
        inverse = lax.rsqrt(jnp.mean(middle * middle, axis=1, keepdims=True) + EPSILON)
        normed = middle * inverse
        gain_grad += jnp.sum(grad_b * normed, axis=0, keepdims=True)
        own = pl.ds(pl.multiple_of(me * tokens + h * half, half), half)
        grad = dy_ref[own].astype(F32) + norm_back(grad_b * gain, normed, inverse)
        grad_ref[rows] = grad
        dw_own[rows] = (RESIDUAL_SCALE * grad).astype(BF16)
    gain_ref[...] = jnp.broadcast_to(gain_grad, gain_ref.shape)
    gathers = (own_sem, send_sem, recv_sem)
    dw = Gather(plane, 0, dw_own, dw_out, 0, *gathers)
    dl = Gather(plane, 1, dl_own, dl_out, 0, *gathers)
    dw.begin()
    dl.begin()
    dw.relay()
    dl.relay()
    dw.relay_diagonal()
    dl.relay_diagonal()
    trade.add(here - 1)
    others = [
        pltpu.make_async_copy(stage.at[here - 1, 3], other_hbm[k], other_sem.at[k])
        for k, stage in enumerate((down_stage, gate_stage, up_stage))
    ]
    for copy in others:
        copy.start()
    for item in (dg_other, db_other, dg, db, dw, dl):
        item.finish()
    swap_b.wait_send()
    swap_g.wait_send()
    for store in stores + others:
        store.wait()
    for j in range(tiles):
        tile_store(j).wait()
    trade.finish(here)


def experts_back(
    b_all, dy_all, g_all, w_gate, w_up, w_down, middle, marked, w_in, w_out,
    lane_of, query_width, router_at, collective_id,
):
    sources, tokens, model_width = b_all.shape
    here, _, hidden_width = w_gate.shape
    rows_all = sources * tokens
    width, part, tile = hidden_width // 2, model_width // 4, 256
    tiles = rows_all // tile
    flat, wide, narrow = (rows_all, model_width), (tokens, model_width), (tokens, LANES)
    slices = [(width, part), (part, width), (part, width)]
    out = pl.pallas_call(
        functools.partial(experts_back_kernel, here, tile, lane_of, query_width, router_at),
        out_shape=[
            jax.ShapeDtypeStruct(flat, BF16),
            jax.ShapeDtypeStruct((8,) + wide, BF16),
            jax.ShapeDtypeStruct((8,) + narrow, BF16),
            jax.ShapeDtypeStruct(wide, F32),
            jax.ShapeDtypeStruct((8, model_width), F32),
        ]
        + [jax.ShapeDtypeStruct((here,) + shape, BF16) for shape in slices * 2]
        + [jax.ShapeDtypeStruct(shape, BF16) for shape in slices * here],
        in_specs=anywhere(2) + in_vmem(1) + anywhere(3) + in_vmem(4),
        out_specs=anywhere(3) + in_vmem(2) + anywhere(6 + 3 * here),
        scratch_shapes=[
            pltpu.VMEM(flat, BF16),
            pltpu.VMEM(flat, BF16),
            pltpu.VMEM((here, model_width, 2 * width), BF16),
            pltpu.VMEM((here, width, model_width), BF16),
            pltpu.VMEM((rows_all, width), BF16),
            pltpu.VMEM((rows_all, 2 * width), BF16),
            pltpu.VMEM(flat, BF16),
            pltpu.VMEM((sources,) + wide, BF16),
            pltpu.VMEM((sources,) + narrow, F32),
        ]
        + [pltpu.VMEM((here, 4) + shape, BF16) for shape in slices]
        + [pltpu.VMEM((here,) + shape, BF16) for shape in slices]
        + [
            pltpu.VMEM(wide, BF16),
            pltpu.VMEM(narrow, BF16),
            pltpu.VMEM(wide, BF16),
            pltpu.VMEM(narrow, F32),
            pltpu.VMEM(wide, BF16),
            pltpu.VMEM(narrow, F32),
        ]
        + (scatter_scratch(*wide, BF16, True) + scatter_scratch(*narrow, F32, True)) * 2
        + [
            pltpu.SemaphoreType.DMA((here, 3)),
            pltpu.SemaphoreType.DMA((2, tiles)),
            pltpu.SemaphoreType.DMA((tiles,)),
            pltpu.SemaphoreType.DMA((3, here)),
            pltpu.SemaphoreType.DMA((3,)),
            pltpu.SemaphoreType.DMA((2, 3, 3, here)),
            pltpu.SemaphoreType.DMA((4,)),
        ]
        + scatter_sems(4)
        + gather_sems(2),
        compiler_params=pltpu.CompilerParams(
            collective_id=collective_id, has_side_effects=True, vmem_limit_bytes=67_000_000
        ),
        cost_estimate=pl.CostEstimate(
            flops=43_000_000_000, bytes_accessed=42_000_000, transcendentals=1_000_000
        ),
        name="experts_back",
    )(
        b_all.reshape(flat), dy_all.reshape(flat), g_all.reshape(rows_all, LANES),
        w_gate, w_up, w_down, middle, marked, w_in, w_out,
    )
    return [out[0].reshape(b_all.shape), *out[1:5], out[5:8], out[8:11], out[11:-3], out[-3:]]


def rotary_tables(length):
    lane = lax.broadcasted_iota(jnp.int32, (length, LANES), 1) % HEAD_DIM
    half = HEAD_DIM // 2
    exponent = (lane % half).astype(F32) * (2.0 / HEAD_DIM)
    position = lax.broadcasted_iota(jnp.int32, (length, LANES), 0).astype(F32)
    angles = position * jnp.power(ROPE_BASE, -exponent)
    return jnp.cos(angles), jnp.where(lane < half, -jnp.sin(angles), jnp.sin(angles))


def finish_kernel(per_group, here, in_ref, out_ref, *refs):
    kept, came, far, refs = refs[:3], refs[3:6], refs[6 : 6 + 3 * here], refs[6 + 3 * here :]
    query_ref, key_ref, value_ref, router_ref, proj_ref, *expert_refs = refs
    query_width = per_group * HEAD_DIM
    groups, out_rows, _ = out_ref.shape
    for j in range(0, groups, 2):
        pair = (in_ref[j].astype(F32), in_ref[j + 1].astype(F32))
        at = 0
        for target, width in ((query_ref, query_width), (key_ref, HEAD_DIM), (value_ref, HEAD_DIM)):
            target[:, j * width : (j + 2) * width] = jnp.concatenate(
                [block[:, at : at + width] for block in pair], axis=1
            )
            at += width
    router_ref[...] = in_ref[0][:, at : at + router_ref.shape[1]].astype(F32)
    for j in range(groups):
        proj_ref[j * out_rows : (j + 1) * out_rows, :] = out_ref[j].astype(F32)
    high = lax.axis_index("fsdp") // 2
    for k, target in enumerate(expert_refs):
        width = kept[k].shape[1 if k == 0 else 2]
        near = pl.ds(pl.multiple_of(high * width, width), width)
        beyond = pl.ds(pl.multiple_of((1 - high) * width, width), width)
        for e in range(here):
            near_sum = kept[k][e].astype(F32) + came[k][e].astype(F32)
            far_sum = far[3 * e + k][...].astype(F32)
            if k == 0:
                target[e, near, :] = near_sum
                target[e, beyond, :] = far_sum
            else:
                target[e, :, near] = near_sum
                target[e, :, beyond] = far_sum


def finish(in_all, out_all, kept, came, far, per_group, experts_all):
    groups, shard, _ = in_all.shape
    here, width, part = kept[0].shape
    query_width = per_group * HEAD_DIM
    shapes = [
        (shard, groups * query_width),
        (shard, groups * HEAD_DIM),
        (shard, groups * HEAD_DIM),
        (shard, experts_all),
        (groups * out_all.shape[1], out_all.shape[2]),
        (here, 2 * width, part),
        (here, part, 2 * width),
        (here, part, 2 * width),
    ]
    operands = (in_all, out_all, *kept, *came, *far)
    return pl.pallas_call(
        functools.partial(finish_kernel, per_group, here),
        out_shape=[jax.ShapeDtypeStruct(shape, F32) for shape in shapes],
        in_specs=in_vmem(len(operands)),
        out_specs=in_vmem(len(shapes)),
        compiler_params=pltpu.CompilerParams(vmem_limit_bytes=VMEM_LIMIT),
        cost_estimate=pl.CostEstimate(flops=0, bytes_accessed=25_000_000, transcendentals=0),
        name="finish",
    )(*operands)


def per_device(
    residual_in, cotangent, gain_attn, w_query, w_key, w_value, w_out, gain_ffn, w_router,
    w_gate, w_up, w_down, route_ids,
):
    me = lax.axis_index("expert")
    line = lax.axis_index("fsdp")
    peers = lax.axis_size("expert")
    lines = lax.axis_size("fsdp")
    tokens, model_width = residual_in.shape[1:]
    length = tokens * peers
    groups = w_key.shape[1] // HEAD_DIM
    per_group = w_query.shape[1] // w_key.shape[1]
    query_width = per_group * HEAD_DIM
    experts_all = w_router.shape[1]
    here = w_gate.shape[0]
    shard = w_query.shape[0]
    turned = query_width + HEAD_DIM
    router_at = turned
    lane_of = HEAD_DIM
    in_width = turned + LANES
    paired = lines == 4 and peers == 8

    w_in_shard = jnp.concatenate(
        [
            lax.dynamic_slice(w_query, (0, me * query_width), (shard, query_width)),
            lax.dynamic_slice(w_key, (0, me * HEAD_DIM), (shard, HEAD_DIM)),
            lax.dynamic_slice(w_value, (0, me * HEAD_DIM), (shard, HEAD_DIM)),
            w_router,
            jnp.zeros((shard, in_width - turned - HEAD_DIM - experts_all), BF16),
        ],
        axis=1,
    )
    w_out_shard = jnp.concatenate(
        [
            lax.dynamic_slice(w_out, (me * query_width, 0), (query_width, shard)),
            gain_attn[None],
            gain_ffn[None],
            jnp.zeros((14, shard), BF16),
        ],
        axis=0,
    )
    chosen = jnp.any(
        route_ids[0][:, :, None]
        == jnp.arange(LANES, dtype=jnp.int32)[None, None, :] - lane_of,
        axis=1,
    ).astype(F32)
    cosine, sine = rotary_tables(length)
    place = jnp.full((1,), me * here + lane_of, jnp.int32)
    own_rows, own_grad = residual_in[0], cotangent[0]
    wide = (peers, tokens, model_width)

    if paired:
        dy_all, w_in, w_out_rows, saved, b_all, g_all, middle, marked = front(
            own_rows, own_grad, w_in_shard, w_out_shard, chosen, cosine, sine, lines, per_group,
            router_at, 0,
        )
        sum_part, dw_all, dl_all, grad_middle, gain_two_grad, kept, came, far, others = experts_back(
            b_all, dy_all, g_all, w_gate, w_up, w_down, middle, marked, w_in, w_out_rows,
            lane_of, query_width, router_at, 2,
        )
        da_part, grad_in, out_low, e_own, e_total, *crossed = attend_back(
            dw_all.reshape(length, model_width), w_in, w_out_rows, cosine, sine, saved,
            b_all.reshape(2 * length, model_width), dl_all.reshape(length, LANES), per_group,
            (sum_part, others), 4,
        )
        outcome, grad_input, in_all, out_all, gains_all, notes_all = close_transfers(
            da_part.reshape(wide), e_own, e_total, own_rows, middle, grad_middle, gain_two_grad,
            w_out_rows, grad_in.reshape(lines, shard, in_width), out_low,
            query_width, 3,
        )
        squares = jnp.sum(notes_all, axis=0)[:5, 0]
        query, key, value, router_grad, proj, down, gate, up = finish(
            in_all, out_all, kept, came, [*far, *crossed], per_group, experts_all
        )
        reduced = [gate, up, down]
        gain_rows = jnp.sum(gains_all[:, :2].astype(F32), axis=0)
    else:
        x_all, dy_all = plane_gather([own_rows, own_grad], 0)
        w_in, w_out_rows = (
            lax.all_gather(w_in_shard, "fsdp", axis=0, tiled=True),
            lax.all_gather(w_out_shard, "fsdp", axis=1, tiled=True),
        )
        part, *saved = attend(
            x_all.reshape(length, model_width), w_in, w_out_rows, cosine, sine, per_group
        )
        (branch,) = plane_scatter([part.reshape(wide)], 1)
        gain_one = w_out_rows[query_width][None].astype(F32)
        gain_two = w_out_rows[query_width + 1][None].astype(F32)
        router = w_in[:, router_at:]
        rows = own_rows.astype(F32)
        inverse_one = lax.rsqrt(jnp.mean(rows * rows, axis=-1, keepdims=True) + EPSILON)
        normed_one = rows * inverse_one
        middle = rows + RESIDUAL_SCALE * branch
        inverse_two = lax.rsqrt(jnp.mean(middle * middle, axis=-1, keepdims=True) + EPSILON)
        normed_two = middle * inverse_two
        routed = (normed_two * gain_two).astype(BF16)
        logits = jnp.where(chosen > 0, dot(routed, router), -1e30)
        lifted = jnp.exp(logits - jnp.max(logits, axis=-1, keepdims=True))
        lifted = jnp.where(chosen > 0, lifted, 0.0)
        gates = lifted / jnp.sum(lifted, axis=-1, keepdims=True)
        b_all, g_all = plane_gather([routed, jnp.where(chosen > 0, gates, -1.0)], 2)
        sum_part, db_part, dg_part, *grads = experts(
            place, b_all, dy_all, g_all, w_gate, w_up, w_down
        )
        db_sum, dg_sum = plane_scatter([db_part, dg_part], 3)
        grad_rows = own_grad.astype(F32)
        grad_chosen = gates * (dg_sum - jnp.sum(gates * dg_sum, axis=-1, keepdims=True))
        grad_logits = grad_chosen.astype(BF16)
        grad_routed = dot(grad_logits, router, (1, 1)) + db_sum
        grad_gain_two = jnp.sum(grad_routed * normed_two, axis=0)
        grad_middle = grad_rows + norm_back(grad_routed * gain_two, normed_two, inverse_two)
        grad_branch = (RESIDUAL_SCALE * grad_middle).astype(BF16)
        dw_all, dl_all = plane_gather([grad_branch, grad_logits], 4)
        da_part, grad_in, grad_out = attend_back(
            dw_all.reshape(length, model_width), w_in, w_out_rows, cosine, sine, saved,
            b_all.reshape(length, model_width), dl_all.reshape(length, LANES), per_group,
        )
        da_sum, expert_sum = plane_scatter([da_part.reshape(wide), sum_part], 5)
        outcome = middle + expert_sum
        grad_gain_one = jnp.sum(da_sum * normed_one, axis=0)
        grad_input = grad_middle + norm_back(da_sum * gain_one, normed_one, inverse_one)
        squares = lax.psum(
            jnp.stack(
                [jnp.sum(v * v) for v in (rows, middle, outcome, grad_middle, grad_input)]
            ),
            ("fsdp", "expert"),
        )
        in_sum = lax.psum_scatter(grad_in, "fsdp", scatter_dimension=0, tiled=True)
        out_sum = lax.psum_scatter(
            grad_out.transpose(1, 0, 2).reshape(query_width, model_width), "fsdp",
            scatter_dimension=1, tiled=True,
        )
        gain_rows = lax.psum_scatter(
            lax.psum(jnp.stack([grad_gain_one, grad_gain_two]), "expert"),
            "fsdp", scatter_dimension=1, tiled=True,
        )
        in_all = lax.all_gather(in_sum, "expert", axis=0)
        out_all = lax.all_gather(out_sum, "expert", axis=0)
        outcome, grad_input = outcome.astype(BF16), grad_input.astype(BF16)
        grads = [
            grads[0].transpose(1, 0, 2, 3).reshape(w_gate.shape),
            grads[1].transpose(1, 0, 2, 3).reshape(w_up.shape),
            grads[2].transpose(1, 2, 0, 3).reshape(w_down.shape),
        ]
        reduced = [
            lax.psum_scatter(array, "fsdp", scatter_dimension=axis, tiled=True).astype(F32)
            for array, axis in zip(grads, (1, 1, 2))
        ]

        def columns_of(start, stop):
            return in_all[:, :, start:stop].transpose(1, 0, 2).reshape(shard, -1).astype(F32)

        query, key = columns_of(0, query_width), columns_of(query_width, turned)
        value = columns_of(turned, turned + HEAD_DIM)
        proj = out_all.reshape(groups * query_width, shard).astype(F32)
        at = turned + HEAD_DIM
        router_grad = in_all[0, :, at : at + experts_all].astype(F32)

    root_means = jnp.sqrt(squares / (tokens * model_width * lines * peers))
    return (
        outcome[None],
        grad_input[None],
        gain_rows[0],
        query,
        key,
        value,
        proj,
        gain_rows[1],
        router_grad,
        reduced[0],
        reduced[1],
        reduced[2],
        root_means,
    )


def solution(mesh):
    in_specs = (
        P("fsdp", "expert", None),
        P("fsdp", "expert", None),
        P("fsdp"),
        P("fsdp", None),
        P("fsdp", None),
        P("fsdp", None),
        P(None, "fsdp"),
        P("fsdp"),
        P("fsdp", None),
        P("expert", None, None),
        P("expert", None, None),
        P("expert", None, None),
        P("fsdp", "expert", None),
    )
    out_specs = (
        P("fsdp", "expert", None),
        P("fsdp", "expert", None),
        P("fsdp"),
        P("fsdp", None),
        P("fsdp", None),
        P("fsdp", None),
        P(None, "fsdp"),
        P("fsdp"),
        P("fsdp", None),
        P("expert", "fsdp", None),
        P("expert", "fsdp", None),
        P("expert", None, "fsdp"),
        P(),
    )
    return jax.shard_map(
        per_device, mesh=mesh, in_specs=in_specs, out_specs=out_specs, check_vma=False
    )
```

```python
import functools

import jax
import jax.numpy as jnp
from jax import lax
from jax.experimental import pallas as pl
from jax.experimental.pallas import tpu as pltpu
from jax.sharding import PartitionSpec as P

HEAD_DIM = 64
BLOCK = 256

EPSILON = 1e-06
RESIDUAL_SCALE = 0.22
ATTENTION_SCALE = 0.015625
ROPE_BASE = 10000.0
HIGHEST = lax.Precision.HIGHEST
MESH = pl.DeviceIdType.MESH
VMEM_LIMIT = 63_000_000
F32 = jnp.float32
BF16 = jnp.bfloat16
LANES = 128


def plane_neighbours():
    me = lax.axis_index("expert")
    core = lax.rem(me, 2)
    x_bit = lax.rem(me // 2, 2)
    y_bit = me // 4
    sibling = me + 1 - 2 * core
    x_peer = me + 2 - 4 * x_bit
    y_peer = me + 4 - 8 * y_bit
    diagonal = x_peer + 4 - 8 * y_bit
    return me, core, x_bit, y_bit, sibling, x_peer, y_peer, diagonal


def greet(axis, peers):
    barrier = pltpu.get_barrier_semaphore()
    for peer in peers:
        pl.semaphore_signal(barrier, inc=1, device_id={axis: peer}, device_id_type=MESH)
    pl.semaphore_wait(barrier, len(peers))


def gather_kernel(count, *refs):
    ins, outs = refs[:count], refs[count : 2 * count]
    own_sem, send_sem, recv_sem = refs[2 * count :]
    me, _, _, _, sibling, x_peer, y_peer, diagonal = plane_neighbours()
    greet("expert", (sibling, x_peer, y_peer))

    def remote(k, slot, source, target, peer):
        return pltpu.make_async_remote_copy(
            src_ref=source,
            dst_ref=target,
            send_sem=send_sem.at[k, slot],
            recv_sem=recv_sem.at[k, slot],
            device_id={"expert": peer},
            device_id_type=MESH,
        )

    plans = []
    for k in range(count):
        half = ins[k].shape[0] // 2
        parts = (pl.ds(0, half), pl.ds(half, half))
        out = outs[k]
        own = pltpu.make_async_copy(ins[k], out.at[me], own_sem.at[k])
        copies = [remote(k, 0, ins[k], out.at[me], sibling)]
        for h in range(2):
            copies.append(remote(k, 1 + h, ins[k].at[parts[h]], out.at[me, parts[h]], x_peer))
        for h in range(2):
            copies.append(remote(k, 3 + h, ins[k].at[parts[h]], out.at[me, parts[h]], y_peer))

        def forward(slot, block, h, peer):
            return remote(k, slot, out.at[block, parts[h]], out.at[block, parts[h]], peer)

        copies.append(forward(5, y_peer, 0, x_peer))
        copies.append(forward(6, x_peer, 1, y_peer))
        for h in range(2):
            copies.append(forward(7 + h, x_peer, h, sibling))
        for h in range(2):
            copies.append(forward(9 + h, y_peer, h, sibling))
        for h in range(2):
            copies.append(forward(11 + h, diagonal, h, sibling))
        plans.append((own, copies))
    for own, copies in plans:
        for slot in (3, 2, 1, 4, 0):
            copies[slot].start()
        own.start()
    for own, copies in plans:
        copies[3].wait_recv()
        copies[5].start()
        copies[2].wait_recv()
        copies[6].start()
        copies[9].start()
        copies[8].start()
        copies[1].wait_recv()
        copies[7].start()
        copies[4].wait_recv()
        copies[10].start()
    for own, copies in plans:
        copies[5].wait_recv()
        copies[11].start()
        copies[6].wait_recv()
        copies[12].start()
    for own, copies in plans:
        for slot in (0, 7, 8, 9, 10, 11, 12):
            copies[slot].wait_recv()
        for copy in copies:
            copy.wait_send()
        own.wait()


def plane_gather(arrays, collective_id):
    if lax.axis_size("expert") != 8:
        return [lax.all_gather(array, "expert", axis=0) for array in arrays]
    count = len(arrays)
    size = sum(array.size * array.dtype.itemsize for array in arrays)
    return pl.pallas_call(
        functools.partial(gather_kernel, count),
        out_shape=[jax.ShapeDtypeStruct((8,) + array.shape, array.dtype) for array in arrays],
        in_specs=[pl.BlockSpec(memory_space=pltpu.VMEM)] * count,
        out_specs=[pl.BlockSpec(memory_space=pl.ANY)] * count,
        scratch_shapes=[
            pltpu.SemaphoreType.DMA((count,)),
            pltpu.SemaphoreType.DMA((count, 13)),
            pltpu.SemaphoreType.DMA((count, 13)),
        ],
        compiler_params=pltpu.CompilerParams(
            collective_id=collective_id, has_side_effects=True, vmem_limit_bytes=VMEM_LIMIT
        ),
        cost_estimate=pl.CostEstimate(flops=0, bytes_accessed=16 * size, transcendentals=0),
        name="plane_gather",
    )(*arrays)


def scatter_kernel(count, *refs):
    ins, outs = refs[:count], refs[count : 2 * count]
    scratch = refs[2 * count : 2 * count + 6 * count]
    send_sem, recv_sem = refs[8 * count :]
    me, core, x_bit, y_bit, sibling, x_peer, y_peer, diagonal = plane_neighbours()
    greet("expert", (sibling, x_peer, y_peer))
    chip = me // 2
    chip_x, chip_y, chip_d = x_peer // 2, y_peer // 2, diagonal // 2
    order = (chip_d, chip_x, chip_y, chip)

    def remote(k, slot, source, target, peer):
        return pltpu.make_async_remote_copy(
            src_ref=source,
            dst_ref=target,
            send_sem=send_sem.at[k, slot],
            recv_sem=recv_sem.at[k, slot],
            device_id={"expert": peer},
            device_id_type=MESH,
        )

    stage0 = []
    for k in range(count):
        pair = scratch[6 * k]
        copies = [
            remote(k, i, ins[k].at[2 * order[i] + 1 - core], pair.at[i], sibling) for i in range(4)
        ]
        stage0.append(copies)
        for copy in copies:
            copy.start()
    later = []
    for k in range(count):
        pair, sums, first_x, first_y, second_x, second_y = scratch[6 * k : 6 * k + 6]
        rows = ins[k].shape[1]
        half = rows // 2
        parts = (pl.ds(0, half), pl.ds(half, half))
        dtype = ins[k].dtype

        def join(i):
            stage0[k][i].wait_recv()
            sums[i] = (ins[k][2 * order[i] + core].astype(F32) + pair[i].astype(F32)).astype(dtype)

        join(0)
        copies = [
            remote(k, 4, sums.at[0, parts[0]], first_x.at[1], x_peer),
            remote(k, 5, sums.at[0, parts[1]], first_y.at[1], y_peer),
        ]
        for copy in copies:
            copy.start()
        join(1)
        copies.append(remote(k, 6, sums.at[1, parts[0]], first_x.at[0], x_peer))
        copies[-1].start()
        join(2)
        copies.append(remote(k, 7, sums.at[2, parts[1]], first_y.at[0], y_peer))
        copies[-1].start()
        join(3)
        later.append(copies)
    for k in range(count):
        pair, sums, first_x, first_y, second_x, second_y = scratch[6 * k : 6 * k + 6]
        half = ins[k].shape[1] // 2
        parts = (pl.ds(0, half), pl.ds(half, half))
        dtype = ins[k].dtype
        copies = later[k]
        copies[0].wait_recv()
        pair[0, parts[0]] = (
            sums[2, parts[0]].astype(F32) + first_x[1].astype(F32)
        ).astype(dtype)
        copies.append(remote(k, 8, pair.at[0, parts[0]], second_y, y_peer))
        copies[-1].start()
        copies[1].wait_recv()
        pair[0, parts[1]] = (
            sums[1, parts[1]].astype(F32) + first_y[1].astype(F32)
        ).astype(dtype)
        copies.append(remote(k, 9, pair.at[0, parts[1]], second_x, x_peer))
        copies[-1].start()
    for k in range(count):
        pair, sums, first_x, first_y, second_x, second_y = scratch[6 * k : 6 * k + 6]
        half = ins[k].shape[1] // 2
        parts = (pl.ds(0, half), pl.ds(half, half))
        copies = later[k]
        copies[2].wait_recv()
        copies[4].wait_recv()
        outs[k][parts[0]] = (
            sums[3, parts[0]].astype(F32) + first_x[0].astype(F32) + second_y[...].astype(F32)
        )
        copies[3].wait_recv()
        copies[5].wait_recv()
        outs[k][parts[1]] = (
            sums[3, parts[1]].astype(F32) + first_y[0].astype(F32) + second_x[...].astype(F32)
        )
        for copy in stage0[k] + copies:
            copy.wait_send()


def plane_scatter(arrays, collective_id):
    if lax.axis_size("expert") != 8:
        return [
            lax.psum_scatter(array, "expert", scatter_dimension=0, tiled=False).astype(F32)
            for array in arrays
        ]
    count = len(arrays)
    scratch = []
    for array in arrays:
        _, rows, columns = array.shape
        half = rows // 2
        for shape in (
            (4, rows, columns),
            (4, rows, columns),
            (2, half, columns),
            (2, half, columns),
            (half, columns),
            (half, columns),
        ):
            scratch.append(pltpu.VMEM(shape, array.dtype))
    size = sum(array.size * array.dtype.itemsize for array in arrays)
    return pl.pallas_call(
        functools.partial(scatter_kernel, count),
        out_shape=[jax.ShapeDtypeStruct(array.shape[1:], F32) for array in arrays],
        in_specs=[pl.BlockSpec(memory_space=pltpu.VMEM)] * count,
        out_specs=[pl.BlockSpec(memory_space=pltpu.VMEM)] * count,
        scratch_shapes=scratch
        + [pltpu.SemaphoreType.DMA((count, 10)), pltpu.SemaphoreType.DMA((count, 10))],
        compiler_params=pltpu.CompilerParams(
            collective_id=collective_id, has_side_effects=True, vmem_limit_bytes=VMEM_LIMIT
        ),
        cost_estimate=pl.CostEstimate(flops=0, bytes_accessed=3 * size, transcendentals=0),
        name="plane_scatter",
    )(*arrays)


def push(source, target, send_sem, recv_sem, axis, peer):
    return pltpu.make_async_remote_copy(
        src_ref=source,
        dst_ref=target,
        send_sem=send_sem,
        recv_sem=recv_sem,
        device_id={axis: peer},
        device_id_type=MESH,
    )


def meet(plane, line, size, with_line):
    barrier = pltpu.get_barrier_semaphore()
    me, _, _, _, sibling, x_peer, y_peer, _ = plane
    for peer in (sibling, x_peer, y_peer):
        pl.semaphore_signal(barrier, inc=1, device_id={"expert": peer}, device_id_type=MESH)
    pl.semaphore_signal(
        barrier, inc=1, device_id={"fsdp": pair_of(line)}, device_id_type=MESH
    )
    if not with_line:
        pl.semaphore_signal(
            barrier, inc=1, device_id={"fsdp": beside(line)}, device_id_type=MESH
        )
        pl.semaphore_wait(barrier, 5)
        return

    @pl.when(line > 0)
    def _():
        pl.semaphore_signal(barrier, inc=1, device_id={"fsdp": line - 1}, device_id_type=MESH)

    @pl.when(line < size - 1)
    def _():
        pl.semaphore_signal(barrier, inc=1, device_id={"fsdp": line + 1}, device_id_type=MESH)

    @pl.when((line > 0) & (line < size - 1))
    def _():
        pl.semaphore_wait(barrier, 6)

    @pl.when((line == 0) | (line == size - 1))
    def _():
        pl.semaphore_wait(barrier, 5)


def pair_of(line):
    return line + 2 - 4 * (line // 2)


def beside(line):
    return line + 1 - 2 * lax.rem(line, 2)


def norm_back(grad_normed, normed, inverse):
    return inverse * (grad_normed - normed * jnp.mean(grad_normed * normed, axis=-1, keepdims=True))


class Gather:
    def __init__(self, plane, k, source, out, base, own_sem, send_sem, recv_sem):
        me, _, _, _, sibling, x_peer, y_peer, diagonal = plane
        half = source.shape[0] // 2
        parts = (pl.ds(0, half), pl.ds(half, half))

        def copy(slot, src, dst, peer):
            return push(src, dst, send_sem.at[k, slot], recv_sem.at[k, slot], "expert", peer)

        def forward(slot, block, h, peer):
            ref = out.at[base + block, parts[h]]
            return copy(slot, ref, ref, peer)

        self.own = pltpu.make_async_copy(source, out.at[base + me], own_sem.at[k])
        copies = [copy(0, source, out.at[base + me], sibling)]
        for slot, peer in ((1, x_peer), (3, y_peer)):
            for h in range(2):
                copies.append(
                    copy(slot + h, source.at[parts[h]], out.at[base + me, parts[h]], peer)
                )
        copies.append(forward(5, y_peer, 0, x_peer))
        copies.append(forward(6, x_peer, 1, y_peer))
        for slot, block in ((7, x_peer), (9, y_peer), (11, diagonal)):
            for h in range(2):
                copies.append(forward(slot + h, block, h, sibling))
        self.copies = copies

    def begin(self):
        for slot in (3, 2, 1, 4, 0):
            self.copies[slot].start()
        self.own.start()

    def relay(self):
        copies = self.copies
        for landed, onward in ((3, (5, 9)), (2, (6, 8)), (1, (7,)), (4, (10,))):
            copies[landed].wait_recv()
            for slot in onward:
                copies[slot].start()

    def relay_diagonal(self):
        for landed, onward in ((5, 11), (6, 12)):
            self.copies[landed].wait_recv()
            self.copies[onward].start()

    def finish(self):
        for slot in (0, 7, 8, 9, 10, 11, 12):
            self.copies[slot].wait_recv()
        for copy in self.copies:
            copy.wait_send()
        self.own.wait()


def gather_sems(count):
    return [
        pltpu.SemaphoreType.DMA((count,)),
        pltpu.SemaphoreType.DMA((count, 13)),
        pltpu.SemaphoreType.DMA((count, 13)),
    ]


class Scatter:
    def __init__(self, plane, k, source, base, scratch, send_sem, recv_sem):
        me, core, _, _, sibling, x_peer, y_peer, diagonal = plane
        self.source, self.base, self.core = source, base, core
        self.pair, self.first_x, self.first_y, self.second_x, self.second_y = scratch[:5]
        self.order = (diagonal // 2, x_peer // 2, y_peer // 2, me // 2)
        self.sums = [
            scratch[5].at[i] if len(scratch) > 5 else source.at[base + 2 * self.order[i] + core]
            for i in range(4)
        ]
        self.dtype = source.dtype
        half = source.shape[1] // 2
        self.parts = parts = (pl.ds(0, half), pl.ds(half, half))

        def copy(slot, src, dst, peer):
            return push(src, dst, send_sem.at[k, slot], recv_sem.at[k, slot], "expert", peer)

        self.stage0 = [
            copy(i, source.at[base + 2 * self.order[i] + 1 - core], self.pair.at[i], sibling)
            for i in range(4)
        ]
        self.stage1 = [
            copy(4, self.sums[0].at[parts[0]], self.first_x.at[1], x_peer),
            copy(5, self.sums[0].at[parts[1]], self.first_y.at[1], y_peer),
            copy(6, self.sums[1].at[parts[0]], self.first_x.at[0], x_peer),
            copy(7, self.sums[2].at[parts[1]], self.first_y.at[0], y_peer),
        ]
        self.stage2 = [
            copy(8, self.pair.at[0, parts[0]], self.second_y, y_peer),
            copy(9, self.pair.at[0, parts[1]], self.second_x, x_peer),
        ]

    def begin(self):
        for copy in self.stage0:
            copy.start()

    def join(self, i):
        self.stage0[i].wait_recv()
        mine = self.source[self.base + 2 * self.order[i] + self.core]
        self.sums[i][...] = (mine.astype(F32) + self.pair[i].astype(F32)).astype(self.dtype)

    def first(self):
        self.join(0)
        self.stage1[0].start()
        self.stage1[1].start()
        self.join(1)
        self.stage1[2].start()
        self.join(2)
        self.stage1[3].start()
        self.join(3)

    def second(self):
        for h, block, landed in ((0, 2, self.first_x), (1, 1, self.first_y)):
            self.stage1[h].wait_recv()
            rows = self.parts[h]
            self.pair[0, rows] = (
                self.sums[block][rows].astype(F32) + landed[1].astype(F32)
            ).astype(self.dtype)
            self.stage2[h].start()

    def total(self, h):
        self.stage1[2 + h].wait_recv()
        self.stage2[h].wait_recv()
        near, far = ((self.first_x, self.second_y), (self.first_y, self.second_x))[h]
        return (
            self.sums[3][self.parts[h]].astype(F32)
            + near[0].astype(F32)
            + far[...].astype(F32)
        )

    def finish(self):
        for copy in self.stage0 + self.stage1 + self.stage2:
            copy.wait_send()


def scatter_scratch(rows, columns, dtype, in_place=False):
    half = rows // 2
    shapes = [
        (4, rows, columns),
        (2, half, columns),
        (2, half, columns),
        (half, columns),
        (half, columns),
        (4, rows, columns),
    ]
    return [pltpu.VMEM(shape, dtype) for shape in shapes[: 5 if in_place else 6]]


def scatter_sems(count):
    return [pltpu.SemaphoreType.DMA((count, 10)), pltpu.SemaphoreType.DMA((count, 10))]


class LineGather:
    def __init__(self, line, size, k, source, out, axis, own_sem, send_sem, recv_sem):
        self.line, self.size, self.k, self.source, self.out = line, size, k, source, out
        self.axis, self.send_sem, self.recv_sem = axis, send_sem, recv_sem
        self.own = pltpu.make_async_copy(source, self.place(line), own_sem.at[k])

    def place(self, owner):
        extent = self.source.shape[self.axis]
        span = pl.ds(pl.multiple_of(owner * extent, extent), extent)
        return self.out.at[span] if self.axis == 0 else self.out.at[:, span]

    def hop(self, side, step, owner, source=None):
        target = self.place(owner)
        return push(
            target if source is None else source,
            target,
            self.send_sem.at[self.k, side, step],
            self.recv_sem.at[self.k, side, step],
            "fsdp",
            self.line + 1 - 2 * side,
        )

    def begin(self):
        for side, there in ((0, self.line < self.size - 1), (1, self.line > 0)):

            @pl.when(there)
            def _():
                self.hop(side, 0, self.line, self.source).start()

        self.own.start()

    def step(self, step):
        line, last = self.line, self.size - 1
        for side, owner in ((0, line - 1 - step), (1, line + 1 + step)):

            @pl.when((owner >= 0) & (owner <= last))
            def _():
                self.hop(side, step, owner).wait_recv()

                @pl.when((line < last) if side == 0 else (line > 0))
                def _():
                    self.hop(side, step + 1, owner).start()

    def finish(self):
        line, last = self.line, self.size - 1
        self.own.wait()
        for step in range(self.size - 1):
            for side, owner, there in ((0, line - step, line < last), (1, line + step, line > 0)):

                @pl.when(there & (owner >= 0) & (owner <= last))
                def _():
                    self.hop(side, step, owner).wait_send()


def line_gather_sems(count, size):
    return [
        pltpu.SemaphoreType.DMA((count,)),
        pltpu.SemaphoreType.DMA((count, 2, size)),
        pltpu.SemaphoreType.DMA((count, 2, size)),
    ]


class LineScatter:
    def __init__(self, line, size, k, source, sums, landed, send_sem, recv_sem):
        self.line, self.size, self.k = line, size, k
        self.source, self.sums, self.landed = source, sums, landed
        self.send_sem, self.recv_sem = send_sem, recv_sem

    def hop(self, side, owner):
        return push(
            self.sums.at[side, owner],
            self.landed.at[side, owner],
            self.send_sem.at[self.k, side, owner],
            self.recv_sem.at[self.k, side, owner],
            "fsdp",
            self.line + 1 - 2 * side,
        )

    def begin(self):
        last = self.size - 1
        for far in range(last):
            for side, owner, end in ((0, last - far, 0), (1, far, last)):

                @pl.when(self.line == end)
                def _():
                    self.sums[side, owner] = self.source[owner]
                    self.hop(side, owner).start()

    def pass_on(self, side, owner):
        self.hop(side, owner).wait_recv()
        self.sums[side, owner] = (
            self.source[owner].astype(F32) + self.landed[side, owner].astype(F32)
        ).astype(self.source.dtype)
        self.hop(side, owner).start()

    def step(self, far):
        line, last = self.line, self.size - 1

        @pl.when((line < last - far) & (line > 0))
        def _():
            self.pass_on(0, last - far)

        @pl.when((line > far) & (line < last))
        def _():
            self.pass_on(1, far)

    def total(self):
        line, last = self.line, self.size - 1
        for side, there, beyond in ((0, line > 0, line == 0), (1, line < last, line == last)):

            @pl.when(there)
            def _():
                self.hop(side, line).wait_recv()

            @pl.when(beyond)
            def _():
                self.landed[side, line] = jnp.zeros(self.source.shape[1:], self.source.dtype)

        return (
            self.source[line].astype(F32)
            + self.landed[0, line].astype(F32)
            + self.landed[1, line].astype(F32)
        )

    def finish(self):
        for owner in range(self.size):

            @pl.when(self.line < owner)
            def _():
                self.hop(0, owner).wait_send()

            @pl.when(self.line > owner)
            def _():
                self.hop(1, owner).wait_send()


def line_scatter_sems(count, size):
    return [
        pltpu.SemaphoreType.DMA((count, 2, size)),
        pltpu.SemaphoreType.DMA((count, 2, size)),
    ]


def in_vmem(count):
    return [pl.BlockSpec(memory_space=pltpu.VMEM)] * count


def anywhere(count):
    return [pl.BlockSpec(memory_space=pl.ANY)] * count


def talk_params(collective_id):
    return pltpu.CompilerParams(
        collective_id=collective_id, has_side_effects=True, vmem_limit_bytes=VMEM_LIMIT
    )


def close_kernel(
    size, query_width, da_ref, e_own, e_total, x_ref, middle_ref, grad_ref,
    gain_two_ref, wout_ref, gin_ref, out_low,
    outcome_ref, input_grad_ref, in_out, out_out, gains_out, notes_out,
    e_landed, gains, notes, notes_line, in_low, gain_low, notes_low, *rest,
):
    scratch, rest = rest[:6], rest[6:]
    line_scratch, rest = rest[:4], rest[4:]
    (
        swap_sems, scatter_send, scatter_recv, sum_send, sum_recv,
        line_own, line_send, line_recv, own_sem, send_sem, recv_sem,
    ) = rest
    plane, line = plane_neighbours(), lax.axis_index("fsdp")
    meet(plane, line, size, True)
    sums = (scatter_send, scatter_recv)
    da = Scatter(plane, 0, da_ref, 0, scratch[:6], *sums)
    swap = push(e_total, e_landed, swap_sems.at[0], swap_sems.at[1], "fsdp", pair_of(line))
    gin = LineScatter(line, size, 0, gin_ref, *line_scratch[0:2], sum_send, sum_recv)
    gain = LineScatter(line, size, 1, gains, *line_scratch[2:4], sum_send, sum_recv)
    gathers = (own_sem, send_sem, recv_sem)
    out_all = Gather(plane, 1, out_low, out_out, 0, *gathers)
    half = x_ref.shape[0] // 2
    gin.begin()
    da.begin()
    da.first()
    gin.step(0)
    swap.start()
    da.second()
    gin.step(1)
    gin.step(2)
    out_all.begin()
    gain_one = wout_ref[query_width : query_width + 1, :].astype(F32)
    grad_gain = jnp.zeros((1, x_ref.shape[1]), F32)
    squares = [jnp.zeros((1, 1), F32)] * 5

    def add_square(i, values):
        squares[i] = squares[i] + jnp.sum(
            jnp.sum(values * values, axis=1, keepdims=True), axis=0, keepdims=True
        )

    for h in range(2):
        rows = pl.ds(h * half, half)
        x = x_ref[rows].astype(F32)
        inverse = lax.rsqrt(jnp.mean(x * x, axis=1, keepdims=True) + EPSILON)
        normed = x * inverse
        grad_a = da.total(h)
        grad_gain += jnp.sum(grad_a * normed, axis=0, keepdims=True)
        grad_middle = grad_ref[rows]
        grad_input = grad_middle + norm_back(grad_a * gain_one, normed, inverse)
        input_grad_ref[rows] = grad_input.astype(BF16)
        add_square(0, x)
        add_square(1, middle_ref[rows])
        add_square(3, grad_middle)
        add_square(4, grad_input)
    width = x_ref.shape[1] // size
    row = lax.broadcasted_iota(jnp.int32, gains.shape[1:], 0)
    for p in range(size):
        columns = slice(p * width, (p + 1) * width)
        gains[p] = jnp.where(
            row == 0, grad_gain[:, columns],
            jnp.where(row == 1, gain_two_ref[0:1, columns], 0.0),
        ).astype(BF16)
    gain.begin()
    gain.step(0)
    gain.step(1)
    gain.step(2)
    out_all.relay()
    swap.wait_recv()
    for h in range(2):
        rows = pl.ds(h * half, half)
        outcome = middle_ref[rows] + e_own[rows] + e_landed[rows].astype(F32)
        outcome_ref[rows] = outcome.astype(BF16)
        add_square(2, outcome)
    row = lax.broadcasted_iota(jnp.int32, notes.shape, 0)
    told = jnp.zeros(notes.shape, F32)
    for i in range(5):
        told = jnp.where(row == i, squares[i], told)
    notes[...] = told
    spread = LineGather(line, size, 0, notes, notes_line, 0, line_own, line_send, line_recv)
    spread.begin()
    in_low[...] = gin.total().astype(BF16)
    in_all = Gather(plane, 0, in_low, in_out, 0, *gathers)
    in_all.begin()
    spread.step(0)
    out_all.relay_diagonal()
    spread.step(1)
    spread.step(2)
    gain_low[...] = gain.total().astype(BF16)
    gain_all = Gather(plane, 2, gain_low, gains_out, 0, *gathers)
    gain_all.begin()
    spread.finish()
    count = notes.shape[0]
    notes_low[...] = (
        notes_line[pl.ds(0, count)] + notes_line[pl.ds(count, count)]
        + notes_line[pl.ds(2 * count, count)] + notes_line[pl.ds(3 * count, count)]
    )
    notes_all = Gather(plane, 3, notes_low, notes_out, 0, *gathers)
    notes_all.begin()
    last = (in_all, gain_all, notes_all)
    for item in last:
        item.relay()
    for item in last:
        item.relay_diagonal()
    for item in last + (out_all, da, gin, gain):
        item.finish()
    swap.wait_send()


def close_transfers(
    da_part, e_own, e_total, x, middle, grad_middle, gain_two, w_out, grad_in, out_low,
    query_width, collective_id,
):
    tokens, model_width = x.shape
    size, in_rows, in_columns = grad_in.shape
    out_rows, out_columns = out_low.shape
    wide = (tokens, model_width)
    gain_shape, note_shape = (16, out_columns), (16, LANES)
    line_scratch = []
    for shape in (grad_in.shape, (size,) + gain_shape):
        line_scratch += [pltpu.VMEM((2,) + shape, BF16)] * 2
    return pl.pallas_call(
        functools.partial(close_kernel, size, query_width),
        out_shape=[
            jax.ShapeDtypeStruct(wide, BF16),
            jax.ShapeDtypeStruct(wide, BF16),
            jax.ShapeDtypeStruct((8, in_rows, in_columns), BF16),
            jax.ShapeDtypeStruct((8, out_rows, out_columns), BF16),
            jax.ShapeDtypeStruct((8,) + gain_shape, BF16),
            jax.ShapeDtypeStruct((8,) + note_shape, F32),
        ],
        in_specs=in_vmem(10),
        out_specs=in_vmem(2) + anywhere(4),
        scratch_shapes=[
            pltpu.VMEM(wide, BF16),
            pltpu.VMEM((size,) + gain_shape, BF16),
            pltpu.VMEM(note_shape, F32),
            pltpu.VMEM((size * note_shape[0], LANES), F32),
            pltpu.VMEM((in_rows, in_columns), BF16),
            pltpu.VMEM(gain_shape, BF16),
            pltpu.VMEM(note_shape, F32),
        ]
        + scatter_scratch(*wide, BF16)
        + line_scratch
        + [pltpu.SemaphoreType.DMA((2,))]
        + scatter_sems(1)
        + line_scatter_sems(2, size)
        + line_gather_sems(1, size)
        + gather_sems(4),
        compiler_params=talk_params(collective_id),
        cost_estimate=pl.CostEstimate(flops=0, bytes_accessed=200_000_000, transcendentals=0),
        name="close_transfers",
    )(da_part, e_own, e_total, x, middle, grad_middle, gain_two, w_out, grad_in, out_low)


def dot(first, second, contract=(1, 0)):
    return lax.dot_general(
        first, second, (((contract[0],), (contract[1],)), ((), ())), preferred_element_type=F32
    )


def spin(values, cosine, sine):
    width = values.shape[1]
    half = HEAD_DIM // 2
    cosine = jnp.concatenate([cosine] * (width // LANES), axis=1)
    sine = jnp.concatenate([sine] * (width // LANES), axis=1)
    lane = lax.broadcasted_iota(jnp.int32, values.shape, 1)
    lower = lax.rem(lane, HEAD_DIM) < half
    swapped = jnp.where(
        lower, pltpu.roll(values, width - half, 1), pltpu.roll(values, half, 1)
    )
    return values * cosine + swapped * sine


def attend_kernel(per_group, x_ref, w_in_ref, w_out_ref, cos_ref, sin_ref, part_ref, *outs):
    def take(rows):
        return x_ref[rows, :]

    def put(i, part):
        part_ref[i * BLOCK : (i + 1) * BLOCK, :] = part

    attend_steps(
        per_group, x_ref.shape[0], take, put, lambda step: None, w_in_ref, w_out_ref, cos_ref,
        sin_ref, *outs,
    )


def attend_steps(
    per_group, length, take, put, hook, w_in_ref, w_out_ref, cos_ref, sin_ref,
    a_ref, q_ref, k_ref, v_ref, o_ref, lse_ref,
):
    query_width = per_group * HEAD_DIM
    turned = query_width + HEAD_DIM
    gain = w_out_ref[query_width : query_width + 1, :].astype(F32)

    def project(i, carry):
        rows = pl.ds(pl.multiple_of(i * BLOCK, BLOCK), BLOCK)
        x = take(rows).astype(F32)
        inverse = lax.rsqrt(jnp.mean(x * x, axis=1, keepdims=True) + EPSILON)
        a = (x * inverse * gain).astype(BF16)
        a_ref[rows, :] = a
        pre = dot(a, w_in_ref[...])
        spun = spin(pre[:, :turned], cos_ref[rows, :], sin_ref[rows, :]).astype(BF16)
        for h in range(per_group):
            q_ref[h, rows, :] = spun[:, h * HEAD_DIM : (h + 1) * HEAD_DIM]
        k_ref[rows, :] = spun[:, query_width:turned]
        v_ref[rows, :] = pre[:, turned : turned + HEAD_DIM].astype(BF16)
        return carry

    lax.fori_loop(0, length // BLOCK, project, 0)
    hook(0)
    for i in range(length // BLOCK):
        seen = (i + 1) * BLOCK
        rows = slice(i * BLOCK, seen)
        keys, values = k_ref[:seen, :], v_ref[:seen, :]
        for h in range(per_group):
            scores = dot(q_ref[h, rows, :], keys, (1, 1)) * ATTENTION_SCALE
            peak = jnp.max(scores, axis=1, keepdims=True)
            lifted = jnp.exp(scores - peak)
            total = jnp.sum(lifted, axis=1, keepdims=True)
            weights = (lifted * (1.0 / total)).astype(BF16)
            mixed = dot(weights, values)
            o_ref[rows, h * HEAD_DIM : (h + 1) * HEAD_DIM] = mixed.astype(BF16)
            lse_ref[h, rows, :] = peak + jnp.log(total)
        put(i, dot(o_ref[rows, :], w_out_ref[:query_width, :]).astype(BF16))
        hook(1 + i)


def saved_shapes(length, model_width, per_group):
    return [
        jax.ShapeDtypeStruct((length, model_width), BF16),
        jax.ShapeDtypeStruct((per_group, length, HEAD_DIM), BF16),
        jax.ShapeDtypeStruct((length, HEAD_DIM), BF16),
        jax.ShapeDtypeStruct((length, HEAD_DIM), BF16),
        jax.ShapeDtypeStruct((length, per_group * HEAD_DIM), BF16),
        jax.ShapeDtypeStruct((per_group, length, 1), F32),
    ]


def front_kernel(
    size, per_group, router_at, x_ref, dy_ref, win_shard, wout_shard, chosen_ref, cos_ref, sin_ref,
    dy_out, win_ref, wout_ref, *rest,
):
    saved, rest = rest[:6], rest[6:]
    b_out, g_out, middle_ref, marked_ref, *rest = rest
    x_all, part_ref, dy_landed, routed, b_landed, g_landed, *rest = rest
    scratch, rest = rest[:5], rest[5:]
    (
        swap_sems, scatter_send, scatter_recv, own_sem, send_sem, recv_sem,
        line_own, line_send, line_recv,
    ) = rest
    plane, line = plane_neighbours(), lax.axis_index("fsdp")
    pair = pair_of(line)
    tokens = x_ref.shape[0]
    half, per_block = tokens // 2, BLOCK // tokens
    query_width = per_group * HEAD_DIM
    meet(plane, line, size, True)
    sems = (own_sem, send_sem, recv_sem)
    line_sems = (line_own, line_send, line_recv)
    x = Gather(plane, 0, x_ref, x_all, 0, *sems)
    dy = Gather(plane, 1, dy_ref, dy_out, 0, *sems)
    other = Gather(plane, 2, dy_landed, dy_out, 8, *sems)
    win = LineGather(line, size, 0, win_shard, win_ref, 0, *line_sems)
    wout = LineGather(line, size, 1, wout_shard, wout_ref, 1, *line_sems)
    scatter = Scatter(plane, 0, part_ref, 0, scratch, scatter_send, scatter_recv)
    swap_dy = push(dy_ref, dy_landed, swap_sems.at[0], swap_sems.at[1], "fsdp", pair)
    swap_b = push(routed, b_landed, swap_sems.at[2], swap_sems.at[3], "fsdp", pair)
    swap_g = push(marked_ref, g_landed, swap_sems.at[4], swap_sems.at[5], "fsdp", pair)
    win.begin()
    x.begin()
    wout.begin()
    x.relay()
    win.step(0)
    x.relay_diagonal()
    wout.step(0)
    dy.begin()
    win.step(1)
    wout.step(1)
    win.step(2)
    wout.step(2)
    swap_dy.start()
    for item in (x, win, wout):
        item.finish()

    def take(rows):
        block = pl.ds(rows.start // tokens, per_block)
        return x_all[block].reshape(BLOCK, x_all.shape[2])

    def put(i, part):
        for t in range(per_block):
            part_ref[per_block * i + t] = part[t * tokens : (t + 1) * tokens]

    def hook(step):
        if step == 0:
            dy.relay()
        elif step == 2:
            dy.relay_diagonal()
        elif step == 3:
            swap_dy.wait_recv()

    attend_steps(
        per_group, x_all.shape[0] * tokens, take, put, hook, win_ref, wout_ref, cos_ref, sin_ref,
        *saved,
    )
    scatter.begin()
    scatter.first()
    scatter.second()
    gain = wout_ref[query_width + 1 : query_width + 2, :].astype(F32)
    router = win_ref[:, router_at : router_at + LANES]
    for h in range(2):
        rows = pl.ds(h * half, half)
        middle = x_ref[rows].astype(F32) + RESIDUAL_SCALE * scatter.total(h)
        middle_ref[rows] = middle
        inverse = lax.rsqrt(jnp.mean(middle * middle, axis=1, keepdims=True) + EPSILON)
        b = (middle * inverse * gain).astype(BF16)
        routed[rows] = b
        chosen = chosen_ref[rows] > 0.0
        logits = jnp.where(chosen, dot(b, router), -1e30)
        lifted = jnp.where(chosen, jnp.exp(logits - jnp.max(logits, axis=1, keepdims=True)), 0.0)
        gates = lifted / jnp.sum(lifted, axis=1, keepdims=True)
        marked_ref[rows] = jnp.where(chosen, gates, -1.0)
    swap_b.start()
    swap_g.start()
    b = Gather(plane, 3, routed, b_out, 0, *sems)
    g = Gather(plane, 4, marked_ref, g_out, 0, *sems)
    b_other = Gather(plane, 5, b_landed, b_out, 8, *sems)
    g_other = Gather(plane, 6, g_landed, g_out, 8, *sems)
    b.begin()
    g.begin()
    b.relay()
    g.relay()
    other.begin()
    b.relay_diagonal()
    g.relay_diagonal()
    other.relay()
    swap_b.wait_recv()
    swap_g.wait_recv()
    b_other.begin()
    g_other.begin()
    other.relay_diagonal()
    b_other.relay()
    g_other.relay()
    b_other.relay_diagonal()
    g_other.relay_diagonal()
    for item in (dy, other, b, g, b_other, g_other, scatter):
        item.finish()
    for swap in (swap_dy, swap_b, swap_g):
        swap.wait_send()


def front(
    x, dy, w_in_shard, w_out_shard, chosen, cosine, sine, size, per_group, router_at, collective_id
):
    tokens, model_width = x.shape
    rows, columns = w_in_shard.shape
    out_rows, out_columns = w_out_shard.shape
    wide, narrow = (tokens, model_width), (tokens, LANES)
    out = pl.pallas_call(
        functools.partial(front_kernel, size, per_group, router_at),
        out_shape=[
            jax.ShapeDtypeStruct((16,) + wide, BF16),
            jax.ShapeDtypeStruct((rows * size, columns), BF16),
            jax.ShapeDtypeStruct((out_rows, out_columns * size), BF16),
        ]
        + saved_shapes(8 * tokens, model_width, per_group)
        + [
            jax.ShapeDtypeStruct((16,) + wide, BF16),
            jax.ShapeDtypeStruct((16,) + narrow, F32),
            jax.ShapeDtypeStruct(wide, F32),
            jax.ShapeDtypeStruct(narrow, F32),
        ],
        in_specs=in_vmem(7),
        out_specs=anywhere(1) + in_vmem(8) + anywhere(2) + in_vmem(2),
        scratch_shapes=[
            pltpu.VMEM((8,) + wide, BF16),
            pltpu.VMEM((8,) + wide, BF16),
            pltpu.VMEM(wide, BF16),
            pltpu.VMEM(wide, BF16),
            pltpu.VMEM(wide, BF16),
            pltpu.VMEM(narrow, F32),
        ]
        + scatter_scratch(*wide, BF16, True)
        + [pltpu.SemaphoreType.DMA((6,))]
        + scatter_sems(1)
        + gather_sems(7)
        + line_gather_sems(2, size),
        compiler_params=talk_params(collective_id),
        cost_estimate=pl.CostEstimate(
            flops=8_000_000_000, bytes_accessed=150_000_000, transcendentals=2_000_000
        ),
        name="front",
    )(x, dy, w_in_shard, w_out_shard, chosen, cosine, sine)
    return [*out[:3], out[3:9], *out[9:]]


def attend(x_all, w_in, w_out, cosine, sine, per_group):
    length, model_width = x_all.shape
    shapes = [jax.ShapeDtypeStruct((length, model_width), BF16)]
    shapes += saved_shapes(length, model_width, per_group)
    return pl.pallas_call(
        functools.partial(attend_kernel, per_group),
        out_shape=shapes,
        in_specs=[pl.BlockSpec(memory_space=pltpu.VMEM)] * 5,
        out_specs=[pl.BlockSpec(memory_space=pltpu.VMEM)] * len(shapes),
        compiler_params=pltpu.CompilerParams(vmem_limit_bytes=VMEM_LIMIT),
        cost_estimate=pl.CostEstimate(
            flops=8_000_000_000, bytes_accessed=16_000_000, transcendentals=2_000_000
        ),
        name="attend",
    )(x_all, w_in, w_out, cosine, sine)


def attend_back_kernel(per_group, *refs):
    attend_back_steps(per_group, lambda step: None, *refs)


def attend_back_talk_kernel(per_group, size, swaps, *refs):
    ins, refs = refs[:13], refs[13:]
    sum_ref, sent, refs = refs[0], refs[1 : 1 + swaps], refs[1 + swaps :]
    part_ref, gin_ref, out_low, e_own, e_other = refs[:5]
    came, refs = refs[5 : 5 + swaps], refs[5 + swaps :]
    scratch, stage_a, stage_b, refs = refs[:5], refs[5:11], refs[11:17], refs[17:]
    gout_ref, line_sums, line_landed, sends, receives, swap_sems, line_send, line_recv = refs
    plane, line = plane_neighbours(), lax.axis_index("fsdp")
    other = Scatter(plane, 0, sum_ref, 8, stage_a, sends, receives)
    mine = Scatter(plane, 1, sum_ref, 0, stage_b, sends, receives)
    gout = LineScatter(line, size, 0, gout_ref, line_sums, line_landed, line_send, line_recv)
    across = [
        push(source, target, swap_sems.at[0, i], swap_sems.at[1, i], "fsdp", pair_of(line))
        for i, (source, target) in enumerate(zip(sent, came))
    ]
    half = e_own.shape[0] // 2

    def hook(step):
        if step == 0:
            meet(plane, line, size, True)
            other.begin()
            mine.begin()
            gout.begin()
            across[0].start()
        elif step == 1:
            other.first()
            gout.step(0)
            for copy in across[1:2]:
                copy.start()
        elif step == 2:
            mine.first()
            gout.step(1)
            for copy in across[2:]:
                copy.start()
        elif step == 3:
            other.second()
            gout.step(2)
        elif step == 4:
            mine.second()
        elif step == 6:
            for h in range(2):
                e_other[pl.ds(h * half, half)] = other.total(h).astype(BF16)
                e_own[pl.ds(h * half, half)] = mine.total(h)
            out_low[...] = gout.total().astype(BF16)
            for item in (other, mine, gout):
                item.finish()
            for copy in across:
                copy.wait()

    attend_back_steps(per_group, hook, *ins, part_ref, gin_ref, gout_ref, *scratch)


def attend_back_steps(
    per_group, hook, dw_ref, w_in_ref, w_out_ref, cos_ref, sin_ref,
    a_ref, q_ref, k_ref, v_ref, o_ref, lse_ref, b_all_ref, dl_ref,
    part_ref, gin_ref, gout_ref,
    turn_ref, dv_ref, back_ref, b_ref, b_sem,
):
    length, model_width = dw_ref.shape
    fetch = pltpu.make_async_copy(b_all_ref.at[pl.ds(0, length)], b_ref, b_sem)
    fetch.start()
    query_width = per_group * HEAD_DIM
    turned = query_width + HEAD_DIM
    blocks = length // BLOCK
    chunk = 384

    def out_grads(i, carry):
        columns = pl.ds(pl.multiple_of(i * chunk, chunk), chunk)
        gout_ref[i] = dot(o_ref[...], dw_ref[:, columns], (0, 0)).astype(BF16)
        return carry

    lax.fori_loop(0, model_width // chunk, out_grads, 0)
    hook(0)
    turn_ref[...] = jnp.zeros_like(turn_ref)
    dv_ref[...] = jnp.zeros_like(dv_ref)
    for i in range(blocks):
        seen = (i + 1) * BLOCK
        rows = slice(i * BLOCK, seen)
        keys, values = k_ref[:seen, :], v_ref[:seen, :]
        grad = dot(dw_ref[rows, :], w_out_ref[:query_width, :], (1, 1)).astype(BF16)
        for h in range(per_group):
            columns = slice(h * HEAD_DIM, (h + 1) * HEAD_DIM)
            queries = q_ref[h, rows, :]
            grad_head = grad[:, columns]
            scores = dot(queries, keys, (1, 1)) * ATTENTION_SCALE
            probs = jnp.exp(scores - lse_ref[h, rows, :])
            dv_ref[:seen, :] += dot(probs.astype(BF16), grad_head, (0, 0))
            grad_probs = dot(grad_head, values, (1, 1))
            inner = jnp.sum(probs * grad_probs, axis=1, keepdims=True)
            grad_scores = (probs * (grad_probs - inner)).astype(BF16)
            turn_ref[rows, columns] = dot(grad_scores, keys) * ATTENTION_SCALE
            turn_ref[:seen, query_width:turned] += (
                dot(grad_scores, queries, (0, 0)) * ATTENTION_SCALE
            )
        hook(1 + i)

    def unturn(i, carry):
        rows = pl.ds(pl.multiple_of(i * BLOCK, BLOCK), BLOCK)
        back_ref[rows, :turned] = spin(
            turn_ref[rows, :], cos_ref[rows, :], -sin_ref[rows, :]
        ).astype(BF16)
        back_ref[rows, turned:] = jnp.concatenate(
            [dv_ref[rows, :].astype(BF16), jnp.zeros((BLOCK, LANES - HEAD_DIM), BF16)], axis=1
        )
        part_ref[rows, :] = dot(
            back_ref[rows, : turned + HEAD_DIM], w_in_ref[:, : turned + HEAD_DIM], (1, 1)
        ).astype(BF16)
        return carry

    lax.fori_loop(0, blocks, unturn, 0)
    hook(5)
    fetch.wait()

    def weight_grads(i, carry):
        columns = pl.ds(pl.multiple_of(i * chunk, chunk), chunk)
        a = a_ref[:, columns]
        gin_ref[columns, :turned] = dot(a, back_ref[:, :turned], (0, 0)).astype(BF16)
        gin_ref[columns, turned:] = (
            dot(a, back_ref[:, turned:], (0, 0)) + dot(b_ref[:, columns], dl_ref[...], (0, 0))
        ).astype(BF16)
        return carry

    lax.fori_loop(0, model_width // chunk, weight_grads, 0)
    hook(6)


def attend_back(
    dw_all, w_in, w_out, cosine, sine, saved, b_all, dl_all, per_group, talk=None, collective_id=None
):
    length, model_width = dw_all.shape
    query_width = per_group * HEAD_DIM
    turned = query_width + HEAD_DIM
    shapes = [
        jax.ShapeDtypeStruct((length, model_width), BF16),
        jax.ShapeDtypeStruct((model_width, w_in.shape[1]), BF16),
        jax.ShapeDtypeStruct((model_width // 384, query_width, 384), BF16),
    ]
    scratch = [
        pltpu.VMEM((length, turned), F32),
        pltpu.VMEM((length, HEAD_DIM), F32),
        pltpu.VMEM((length, w_in.shape[1]), BF16),
        pltpu.VMEM((length, model_width), BF16),
        pltpu.SemaphoreType.DMA,
    ]
    operands = (dw_all, w_in, w_out, cosine, sine, *saved, b_all, dl_all)
    in_specs, out_specs = in_vmem(11) + anywhere(1) + in_vmem(1), in_vmem(len(shapes))
    kernel = functools.partial(attend_back_kernel, per_group)
    params = pltpu.CompilerParams(vmem_limit_bytes=VMEM_LIMIT)
    if talk is not None:
        sum_part, sent = talk
        wide = sum_part.shape[1:]
        shapes = shapes + [jax.ShapeDtypeStruct(wide, F32), jax.ShapeDtypeStruct(wide, BF16)]
        shapes += [jax.ShapeDtypeStruct(array.shape, array.dtype) for array in sent]
        gout_shape, size = shapes[2].shape, lax.axis_size("fsdp")
        shapes[2] = jax.ShapeDtypeStruct(gout_shape[1:], BF16)
        scratch = scratch + scatter_scratch(*wide, BF16) * 2
        scratch += [pltpu.VMEM(gout_shape, BF16)] + [pltpu.VMEM((2,) + gout_shape, BF16)] * 2
        scratch += scatter_sems(2) + [pltpu.SemaphoreType.DMA((2, len(sent)))]
        scratch += line_scatter_sems(1, size)
        operands += (sum_part, *sent)
        in_specs = in_specs + in_vmem(1) + anywhere(len(sent))
        out_specs = out_specs + in_vmem(2) + anywhere(len(sent))
        kernel = functools.partial(attend_back_talk_kernel, per_group, size, len(sent))
        params = talk_params(collective_id)
    return pl.pallas_call(
        kernel,
        out_shape=shapes,
        in_specs=in_specs,
        out_specs=out_specs,
        scratch_shapes=scratch,
        compiler_params=params,
        cost_estimate=pl.CostEstimate(
            flops=20_000_000_000, bytes_accessed=30_000_000, transcendentals=2_000_000
        ),
        name="attend_back",
    )(*operands)


def experts_kernel(
    here, tile,
    place_ref, b_hbm, dy_hbm, g_ref, gate_hbm, up_hbm, down_hbm, *rest,
):
    out_hbm, db_hbm, dg_ref = rest[:3]
    grad_hbm, rest = rest[3:6], rest[6:]
    (
        b_ref, dy_ref, in_ref, down_ref, hidden_ref, back_ref, out_ref, db_ref,
        gate_stage, up_stage, down_stage, weight_sem, tile_sem, out_sem, grad_sem,
    ) = rest
    rows_all, model_width = b_ref.shape
    width = down_ref.shape[0] // here
    tiles = rows_all // tile
    first = place_ref[0]

    def columns_of(e):
        return slice(e * width, (e + 1) * width)

    loads = []
    for e in range(here):
        loads.append((gate_hbm.at[e], in_ref.at[:, columns_of(e)]))
        loads.append((up_hbm.at[e], in_ref.at[:, columns_of(here + e)]))
    for e in range(here):
        loads.append((down_hbm.at[e], down_ref.at[columns_of(e), :]))
    loads = [
        pltpu.make_async_copy(source, target, weight_sem.at[i])
        for i, (source, target) in enumerate(loads)
    ]

    def tile_rows(i):
        return pl.ds(pl.multiple_of(i * tile, tile), tile)

    def tile_load(i, k):
        source, target = ((b_hbm, b_ref), (dy_hbm, dy_ref))[k]
        return pltpu.make_async_copy(
            source.at[tile_rows(i)], target.at[tile_rows(i)], tile_sem.at[k, i]
        )

    def tile_store(i, k):
        source, target = ((out_ref, out_hbm), (db_ref, db_hbm))[k]
        return pltpu.make_async_copy(
            source.at[tile_rows(i)], target.at[tile_rows(i)], out_sem.at[k, i]
        )

    for k in range(2):
        tile_load(0, k).start()
    for load in loads:
        load.start()
    for i in range(1, tiles):
        for k in range(2):
            tile_load(i, k).start()
    for load in loads:
        load.wait()

    def forward_back(i, carry):
        rows = tile_rows(i)
        tile_load(i, 0).wait()
        tile_load(i, 1).wait()
        pre = dot(b_ref[rows, :], in_ref[...])
        grad_mixed = dot(dy_ref[rows, :], down_ref[...], (1, 1))
        gates = g_ref[rows, :]
        lane = lax.broadcasted_iota(jnp.int32, gates.shape, 1)
        inner = jnp.zeros(gates.shape, F32)
        for e in range(here):
            mine = lane == first + e
            gate = jnp.sum(jnp.where(mine, jnp.maximum(gates, 0.0), 0.0), axis=1, keepdims=True)
            scale = RESIDUAL_SCALE * gate
            gate_pre, up_pre = pre[:, columns_of(e)], pre[:, columns_of(here + e)]
            sigmoid = 1.0 / (1.0 + jnp.exp(-gate_pre))
            silu = gate_pre * sigmoid
            hidden = silu * up_pre
            grad = grad_mixed[:, columns_of(e)]
            share = jnp.sum(hidden * grad, axis=1, keepdims=True)
            inner = jnp.where(mine, RESIDUAL_SCALE * share, inner)
            hidden_ref[rows, columns_of(e)] = (scale * hidden).astype(BF16)
            grad = scale * grad
            back_ref[rows, columns_of(e)] = (
                grad * up_pre * sigmoid * (1.0 + gate_pre * (1.0 - sigmoid))
            ).astype(BF16)
            back_ref[rows, columns_of(here + e)] = (grad * silu).astype(BF16)
        dg_ref[rows, :] = inner
        db_ref[rows, :] = dot(back_ref[rows, :], in_ref[...], (1, 1)).astype(BF16)
        tile_store(i, 1).start()
        out_ref[rows, :] = dot(hidden_ref[rows, :], down_ref[...]).astype(BF16)
        tile_store(i, 0).start()
        return carry

    lax.fori_loop(0, tiles, forward_back, 0)
    parts = 4
    part = model_width // parts

    def part_columns(i):
        return pl.ds(pl.multiple_of(i * part, part), part)

    def down_grad(i, carry):
        grad = dot(hidden_ref[...], dy_ref[:, part_columns(i)], (0, 0))
        for e in range(here):
            down_stage[i, e] = grad[columns_of(e), :].astype(BF16)
        return carry

    def in_grad(i, carry):
        grad = dot(b_ref[:, part_columns(i)], back_ref[...], (0, 0))
        for e in range(here):
            gate_stage[i, e] = grad[:, columns_of(e)].astype(BF16)
            up_stage[i, e] = grad[:, columns_of(here + e)].astype(BF16)
        return carry

    stores = []

    def store(k, stage):
        copy = pltpu.make_async_copy(stage, grad_hbm[k], grad_sem.at[k])
        copy.start()
        stores.append(copy)

    lax.fori_loop(0, parts, down_grad, 0)
    store(2, down_stage)
    lax.fori_loop(0, parts, in_grad, 0)
    store(0, gate_stage)
    store(1, up_stage)
    for copy in stores:
        copy.wait()
    for i in range(tiles):
        for k in range(2):
            tile_store(i, k).wait()


def experts(place, b_all, dy_all, g_all, w_gate, w_up, w_down):
    sources, tokens, model_width = b_all.shape
    here, _, hidden_width = w_gate.shape
    rows_all = sources * tokens
    width = hidden_width
    part = model_width // 4
    tile = 256
    tiles = rows_all // tile
    in_stage, down_stage = (4, here, part, width), (4, here, width, part)
    shapes = [in_stage, in_stage, down_stage]
    flat = (rows_all, model_width)
    out = pl.pallas_call(
        functools.partial(experts_kernel, here, tile),
        out_shape=[
            jax.ShapeDtypeStruct(flat, BF16),
            jax.ShapeDtypeStruct(flat, BF16),
            jax.ShapeDtypeStruct((rows_all, LANES), F32),
        ]
        + [jax.ShapeDtypeStruct(shape, BF16) for shape in shapes],
        in_specs=[pl.BlockSpec(memory_space=pltpu.SMEM)] + anywhere(2) + in_vmem(1) + anywhere(3),
        out_specs=anywhere(2) + in_vmem(1) + anywhere(len(shapes)),
        scratch_shapes=[
            pltpu.VMEM(flat, BF16),
            pltpu.VMEM(flat, BF16),
            pltpu.VMEM((model_width, 2 * here * width), BF16),
            pltpu.VMEM((here * width, model_width), BF16),
            pltpu.VMEM((rows_all, here * width), BF16),
            pltpu.VMEM((rows_all, 2 * here * width), BF16),
            pltpu.VMEM(flat, BF16),
            pltpu.VMEM(flat, BF16),
            pltpu.VMEM(in_stage, BF16),
            pltpu.VMEM(in_stage, BF16),
            pltpu.VMEM(down_stage, BF16),
            pltpu.SemaphoreType.DMA((3 * here,)),
            pltpu.SemaphoreType.DMA((2, tiles)),
            pltpu.SemaphoreType.DMA((2, tiles)),
            pltpu.SemaphoreType.DMA((3,)),
        ],
        compiler_params=pltpu.CompilerParams(vmem_limit_bytes=VMEM_LIMIT),
        cost_estimate=pl.CostEstimate(
            flops=43_000_000_000, bytes_accessed=42_000_000, transcendentals=1_000_000
        ),
        name="experts",
    )(
        place, b_all.reshape(flat), dy_all.reshape(flat), g_all.reshape(rows_all, LANES),
        w_gate, w_up, w_down,
    )
    return [
        out[0].reshape(b_all.shape), out[1].reshape(b_all.shape),
        out[2].reshape(sources, tokens, LANES), *out[3:],
    ]


class Trade:
    def __init__(self, line, stages, nears, came, far, sems):
        self.beside, self.across = beside(line), pair_of(line)
        self.stages, self.nears, self.came, self.far, self.sems = stages, nears, came, far, sems

    def copies(self, e, hop):
        made = []
        for k in range(3):
            source = self.stages[k].at[e, (1, 0, 3)[hop]]
            target = self.far[3 * e + k] if hop == 2 else (self.nears, self.came)[hop][k].at[e]
            peer = self.across if hop == 2 else self.beside
            made.append(
                push(source, target, self.sems.at[0, hop, k, e], self.sems.at[1, hop, k, e], "fsdp", peer)
            )
        return made

    def send(self, e, hop):
        for copy in self.copies(e, hop):
            copy.start()

    def add(self, e):
        for k, copy in enumerate(self.copies(e, 0)):
            copy.wait_recv()
            self.stages[k][e, 3] = (
                self.stages[k][e, 3].astype(F32) + self.nears[k][e].astype(F32)
            ).astype(BF16)

    def finish(self, count):
        for e in range(count):
            for hop in range(3 if e < count - 1 else 2):
                for copy in self.copies(e, hop):
                    copy.wait_send()
                    if hop:
                        copy.wait_recv()


def experts_back_kernel(
    here, tile, lane_of, query_width, router_at,
    b_hbm, dy_hbm, g_ref, gate_hbm, up_hbm, down_hbm,
    middle_ref, marked_ref, win_ref, wout_ref,
    out_hbm, dw_out, dl_out, grad_ref, gain_ref, *rest,
):
    kept_hbm, came_hbm, rest = rest[0:3], rest[3:6], rest[6:]
    far_hbm, rest = rest[: 3 * (here - 1)], rest[3 * (here - 1) :]
    other_hbm, rest = rest[:3], rest[3:]
    (
        b_ref, dy_ref, in_ref, down_ref, hidden_ref, back_ref, out_ref, db_ref, dg_ref,
        down_stage, gate_stage, up_stage, down_near, gate_near, up_near,
        dw_own, dl_own, db_total, dg_total, db_landed, dg_landed,
    ) = rest[:21]
    scratch, rest = rest[21:41], rest[41:]
    (
        weight_sem, tile_sem, out_sem, kept_sem, other_sem, trade_sems, swap_sems,
        scatter_send, scatter_recv, own_sem, send_sem, recv_sem,
    ) = rest
    rows_all, model_width = b_ref.shape
    width = down_ref.shape[1]
    tiles = rows_all // tile
    tokens = middle_ref.shape[0]
    per_tile = tile // tokens
    plane, line = plane_neighbours(), lax.axis_index("fsdp")
    me = plane[0]
    first = me * here + lane_of
    high, low = line // 2, lax.rem(line, 2)
    span = pl.ds(pl.multiple_of(high * width, width), width)

    def weight_loads(e):
        pairs = (
            (gate_hbm.at[e, :, span], in_ref.at[e, :, pl.ds(0, width)]),
            (up_hbm.at[e, :, span], in_ref.at[e, :, pl.ds(width, width)]),
            (down_hbm.at[e, span, :], down_ref.at[e]),
        )
        return [
            pltpu.make_async_copy(source, target, weight_sem.at[e, i])
            for i, (source, target) in enumerate(pairs)
        ]

    def tile_rows(j):
        return pl.ds(pl.multiple_of(j * tile, tile), tile)

    def tile_loads(j):
        return [
            pltpu.make_async_copy(
                source.at[tile_rows(j)], target.at[tile_rows(j)], tile_sem.at[k, j]
            )
            for k, (source, target) in enumerate(((b_hbm, b_ref), (dy_hbm, dy_ref)))
        ]

    def tile_store(j):
        return pltpu.make_async_copy(
            out_ref.at[tile_rows(j)], out_hbm.at[tile_rows(j)], out_sem.at[j]
        )

    def place_of(i):
        return lax.rem(i + tiles // 2, tiles)

    def start_loads(i, carry):
        for load in tile_loads(place_of(i)):
            load.start()
        return carry

    start_loads(0, 0)
    for load in weight_loads(0):
        load.start()
    lax.fori_loop(1, tiles, start_loads, 0)
    for e in range(1, here):
        for load in weight_loads(e):
            load.start()
    meet(plane, line, 4, False)
    trade = Trade(
        line, (down_stage, gate_stage, up_stage), (down_near, gate_near, up_near),
        came_hbm, far_hbm, trade_sems,
    )
    sums = (scatter_send, scatter_recv)
    db_other = Scatter(plane, 0, db_ref, 8, scratch[:5], *sums)
    dg_other = Scatter(plane, 1, dg_ref, 8, scratch[5:10], *sums)
    db = Scatter(plane, 2, db_ref, 0, scratch[10:15], *sums)
    dg = Scatter(plane, 3, dg_ref, 0, scratch[15:20], *sums)
    swap_g = push(dg_total, dg_landed, swap_sems.at[0], swap_sems.at[1], "fsdp", pair_of(line))
    swap_b = push(db_total, db_landed, swap_sems.at[2], swap_sems.at[3], "fsdp", pair_of(line))
    half = tokens // 2
    part = model_width // 4

    def one_expert(e, carry):
        for load in weight_loads(e):
            load.wait()
        last = e == here - 1

        def forward_back(i, carry):
            j = place_of(i)
            rows = tile_rows(j)

            @pl.when(e == 0)
            def _():
                for load in tile_loads(j):
                    load.wait()

            pre = dot(b_ref[rows, :], in_ref[e])
            grad = dot(dy_ref[rows, :], down_ref[e], (1, 1))
            gates = g_ref[rows, :]
            mine = lax.broadcasted_iota(jnp.int32, gates.shape, 1) == first + e
            gate = jnp.sum(jnp.where(mine, jnp.maximum(gates, 0.0), 0.0), axis=1, keepdims=True)
            scale = RESIDUAL_SCALE * gate
            gate_pre, up_pre = pre[:, :width], pre[:, width:]
            sigmoid = 1.0 / (1.0 + jnp.exp(-gate_pre))
            silu = gate_pre * sigmoid
            hidden = silu * up_pre
            share = jnp.sum(hidden * grad, axis=1, keepdims=True)
            inner = jnp.where(mine, RESIDUAL_SCALE * share, 0.0)
            hidden_ref[rows, :] = (scale * hidden).astype(BF16)
            grad = scale * grad
            back_ref[rows, :width] = (
                grad * up_pre * sigmoid * (1.0 + gate_pre * (1.0 - sigmoid))
            ).astype(BF16)
            back_ref[rows, width:] = (grad * silu).astype(BF16)
            made = dot(hidden_ref[rows, :], down_ref[e])
            back = dot(back_ref[rows, :], in_ref[e], (1, 1))

            @pl.when(e == 0)
            def _():
                out_ref[rows, :] = made.astype(BF16)
                for t in range(per_tile):
                    piece = slice(t * tokens, (t + 1) * tokens)
                    db_ref[per_tile * j + t] = back[piece].astype(BF16)
                    dg_ref[per_tile * j + t] = inner[piece]

            @pl.when(e > 0)
            def _():
                out_ref[rows, :] = (out_ref[rows, :].astype(F32) + made).astype(BF16)
                for t in range(per_tile):
                    piece = slice(t * tokens, (t + 1) * tokens)
                    block = per_tile * j + t
                    db_ref[block] = (db_ref[block].astype(F32) + back[piece]).astype(BF16)
                    dg_ref[block] += inner[piece]

            @pl.when(last)
            def _():
                tile_store(j).start()

            @pl.when((e == 1) & (i == tiles - 3))
            def _():
                trade.add(0)
                trade.send(0, 2)

            @pl.when(last & (i == tiles // 2 - 1))
            def _():
                dg_other.begin()
                db_other.begin()

            @pl.when(last & (i == tiles - 2))
            def _():
                dg_other.first()
                db_other.first()

            return carry

        lax.fori_loop(0, tiles, forward_back, 0)

        @pl.when(last)
        def _():
            dg.begin()
            db.begin()
            dg_other.second()
            db_other.second()

        def weight_grads(p, carry):
            i = p + 1 - 2 * lax.rem(p, 2)
            parity = jnp.where(p < 2, 1 - low, low)
            side = jnp.where(lax.rem(i, 2) == 0, high, 1 - high)
            columns = pl.ds(pl.multiple_of((2 * side + parity) * part, part), part)
            down_stage[e, i] = dot(hidden_ref[...], dy_ref[:, columns], (0, 0)).astype(BF16)
            grad = dot(b_ref[:, columns], back_ref[...], (0, 0))
            gate_stage[e, i] = grad[:, :width].astype(BF16)
            up_stage[e, i] = grad[:, width:].astype(BF16)

            @pl.when((p == 0) & (e < here - 1))
            def _():
                trade.send(e, 0)

            @pl.when((p == 1) & (e < here - 2))
            def _():
                trade.send(e, 1)

            @pl.when(last & (p == 1))
            def _():
                for h in range(2):
                    rows = pl.ds(h * half, half)
                    dg_total[rows] = dg_other.total(h)
                    db_total[rows] = db_other.total(h).astype(BF16)
                swap_g.start()
                swap_b.start()

            @pl.when(last & (p == 2))
            def _():
                dg.first()
                db.first()
                trade.add(here - 2)
                trade.send(here - 2, 2)
                trade.send(here - 2, 1)
                trade.send(here - 1, 0)
                trade.send(here - 1, 1)

            return carry

        lax.fori_loop(0, 4, weight_grads, 0)
        return carry

    lax.fori_loop(0, here, one_expert, 0)
    stores = [
        pltpu.make_async_copy(stage.at[e, 2], kept_hbm[k].at[e], kept_sem.at[k, e])
        for k, stage in enumerate((down_stage, gate_stage, up_stage))
        for e in range(here)
    ]
    for store in stores:
        store.start()
    dg.second()
    db.second()
    gain = wout_ref[query_width + 1 : query_width + 2, :].astype(F32)
    router = win_ref[:, router_at : router_at + LANES]
    gain_grad = jnp.zeros((1, model_width), F32)
    sums_g = [dg.total(h) for h in range(2)]
    swap_g.wait_recv()
    swap_b.wait_recv()
    for h in range(2):
        rows = pl.ds(h * half, half)
        gates = jnp.maximum(marked_ref[rows], 0.0)
        grad_gates = sums_g[h] + dg_landed[rows]
        grad_chosen = gates * (
            grad_gates - jnp.sum(gates * grad_gates, axis=1, keepdims=True)
        )
        grad_logits = grad_chosen.astype(BF16)
        dl_own[rows] = grad_logits
        grad_b = dot(grad_logits, router, (1, 1)) + db.total(h) + db_landed[rows].astype(F32)
        middle = middle_ref[rows]
        inverse = lax.rsqrt(jnp.mean(middle * middle, axis=1, keepdims=True) + EPSILON)
        normed = middle * inverse
        gain_grad += jnp.sum(grad_b * normed, axis=0, keepdims=True)
        own = pl.ds(pl.multiple_of(me * tokens + h * half, half), half)
        grad = dy_ref[own].astype(F32) + norm_back(grad_b * gain, normed, inverse)
        grad_ref[rows] = grad
        dw_own[rows] = (RESIDUAL_SCALE * grad).astype(BF16)
    gain_ref[...] = jnp.broadcast_to(gain_grad, gain_ref.shape)
    gathers = (own_sem, send_sem, recv_sem)
    dw = Gather(plane, 0, dw_own, dw_out, 0, *gathers)
    dl = Gather(plane, 1, dl_own, dl_out, 0, *gathers)
    dw.begin()
    dl.begin()
    dw.relay()
    dl.relay()
    dw.relay_diagonal()
    dl.relay_diagonal()
    trade.add(here - 1)
    others = [
        pltpu.make_async_copy(stage.at[here - 1, 3], other_hbm[k], other_sem.at[k])
        for k, stage in enumerate((down_stage, gate_stage, up_stage))
    ]
    for copy in others:
        copy.start()
    for item in (dg_other, db_other, dg, db, dw, dl):
        item.finish()
    swap_b.wait_send()
    swap_g.wait_send()
    for store in stores + others:
        store.wait()
    for j in range(tiles):
        tile_store(j).wait()
    trade.finish(here)


def experts_back(
    b_all, dy_all, g_all, w_gate, w_up, w_down, middle, marked, w_in, w_out,
    lane_of, query_width, router_at, collective_id,
):
    sources, tokens, model_width = b_all.shape
    here, _, hidden_width = w_gate.shape
    rows_all = sources * tokens
    width, part, tile = hidden_width // 2, model_width // 4, 256
    tiles = rows_all // tile
    flat, wide, narrow = (rows_all, model_width), (tokens, model_width), (tokens, LANES)
    slices = [(width, part), (part, width), (part, width)]
    out = pl.pallas_call(
        functools.partial(experts_back_kernel, here, tile, lane_of, query_width, router_at),
        out_shape=[
            jax.ShapeDtypeStruct(flat, BF16),
            jax.ShapeDtypeStruct((8,) + wide, BF16),
            jax.ShapeDtypeStruct((8,) + narrow, BF16),
            jax.ShapeDtypeStruct(wide, F32),
            jax.ShapeDtypeStruct((8, model_width), F32),
        ]
        + [jax.ShapeDtypeStruct((here,) + shape, BF16) for shape in slices * 2]
        + [jax.ShapeDtypeStruct(shape, BF16) for shape in slices * here],
        in_specs=anywhere(2) + in_vmem(1) + anywhere(3) + in_vmem(4),
        out_specs=anywhere(3) + in_vmem(2) + anywhere(6 + 3 * here),
        scratch_shapes=[
            pltpu.VMEM(flat, BF16),
            pltpu.VMEM(flat, BF16),
            pltpu.VMEM((here, model_width, 2 * width), BF16),
            pltpu.VMEM((here, width, model_width), BF16),
            pltpu.VMEM((rows_all, width), BF16),
            pltpu.VMEM((rows_all, 2 * width), BF16),
            pltpu.VMEM(flat, BF16),
            pltpu.VMEM((sources,) + wide, BF16),
            pltpu.VMEM((sources,) + narrow, F32),
        ]
        + [pltpu.VMEM((here, 4) + shape, BF16) for shape in slices]
        + [pltpu.VMEM((here,) + shape, BF16) for shape in slices]
        + [
            pltpu.VMEM(wide, BF16),
            pltpu.VMEM(narrow, BF16),
            pltpu.VMEM(wide, BF16),
            pltpu.VMEM(narrow, F32),
            pltpu.VMEM(wide, BF16),
            pltpu.VMEM(narrow, F32),
        ]
        + (scatter_scratch(*wide, BF16, True) + scatter_scratch(*narrow, F32, True)) * 2
        + [
            pltpu.SemaphoreType.DMA((here, 3)),
            pltpu.SemaphoreType.DMA((2, tiles)),
            pltpu.SemaphoreType.DMA((tiles,)),
            pltpu.SemaphoreType.DMA((3, here)),
            pltpu.SemaphoreType.DMA((3,)),
            pltpu.SemaphoreType.DMA((2, 3, 3, here)),
            pltpu.SemaphoreType.DMA((4,)),
        ]
        + scatter_sems(4)
        + gather_sems(2),
        compiler_params=pltpu.CompilerParams(
            collective_id=collective_id, has_side_effects=True, vmem_limit_bytes=67_000_000
        ),
        cost_estimate=pl.CostEstimate(
            flops=43_000_000_000, bytes_accessed=42_000_000, transcendentals=1_000_000
        ),
        name="experts_back",
    )(
        b_all.reshape(flat), dy_all.reshape(flat), g_all.reshape(rows_all, LANES),
        w_gate, w_up, w_down, middle, marked, w_in, w_out,
    )
    return [out[0].reshape(b_all.shape), *out[1:5], out[5:8], out[8:11], out[11:-3], out[-3:]]


def rotary_tables(length):
    lane = lax.broadcasted_iota(jnp.int32, (length, LANES), 1) % HEAD_DIM
    half = HEAD_DIM // 2
    exponent = (lane % half).astype(F32) * (2.0 / HEAD_DIM)
    position = lax.broadcasted_iota(jnp.int32, (length, LANES), 0).astype(F32)
    angles = position * jnp.power(ROPE_BASE, -exponent)
    return jnp.cos(angles), jnp.where(lane < half, -jnp.sin(angles), jnp.sin(angles))


def finish_kernel(per_group, here, in_ref, out_ref, *refs):
    kept, came, far, refs = refs[:3], refs[3:6], refs[6 : 6 + 3 * here], refs[6 + 3 * here :]
    query_ref, key_ref, value_ref, router_ref, proj_ref, *expert_refs = refs
    query_width = per_group * HEAD_DIM
    groups, out_rows, _ = out_ref.shape
    for j in range(0, groups, 2):
        pair = (in_ref[j].astype(F32), in_ref[j + 1].astype(F32))
        at = 0
        for target, width in ((query_ref, query_width), (key_ref, HEAD_DIM), (value_ref, HEAD_DIM)):
            target[:, j * width : (j + 2) * width] = jnp.concatenate(
                [block[:, at : at + width] for block in pair], axis=1
            )
            at += width
    router_ref[...] = in_ref[0][:, at : at + router_ref.shape[1]].astype(F32)
    for j in range(groups):
        proj_ref[j * out_rows : (j + 1) * out_rows, :] = out_ref[j].astype(F32)
    high = lax.axis_index("fsdp") // 2
    for k, target in enumerate(expert_refs):
        width = kept[k].shape[1 if k == 0 else 2]
        near = pl.ds(pl.multiple_of(high * width, width), width)
        beyond = pl.ds(pl.multiple_of((1 - high) * width, width), width)
        for e in range(here):
            near_sum = kept[k][e].astype(F32) + came[k][e].astype(F32)
            far_sum = far[3 * e + k][...].astype(F32)
            if k == 0:
                target[e, near, :] = near_sum
                target[e, beyond, :] = far_sum
            else:
                target[e, :, near] = near_sum
                target[e, :, beyond] = far_sum


def finish(in_all, out_all, kept, came, far, per_group, experts_all):
    groups, shard, _ = in_all.shape
    here, width, part = kept[0].shape
    query_width = per_group * HEAD_DIM
    shapes = [
        (shard, groups * query_width),
        (shard, groups * HEAD_DIM),
        (shard, groups * HEAD_DIM),
        (shard, experts_all),
        (groups * out_all.shape[1], out_all.shape[2]),
        (here, 2 * width, part),
        (here, part, 2 * width),
        (here, part, 2 * width),
    ]
    operands = (in_all, out_all, *kept, *came, *far)
    return pl.pallas_call(
        functools.partial(finish_kernel, per_group, here),
        out_shape=[jax.ShapeDtypeStruct(shape, F32) for shape in shapes],
        in_specs=in_vmem(len(operands)),
        out_specs=in_vmem(len(shapes)),
        compiler_params=pltpu.CompilerParams(vmem_limit_bytes=VMEM_LIMIT),
        cost_estimate=pl.CostEstimate(flops=0, bytes_accessed=25_000_000, transcendentals=0),
        name="finish",
    )(*operands)


def per_device(
    residual_in, cotangent, gain_attn, w_query, w_key, w_value, w_out, gain_ffn, w_router,
    w_gate, w_up, w_down, route_ids,
):
    me = lax.axis_index("expert")
    line = lax.axis_index("fsdp")
    peers = lax.axis_size("expert")
    lines = lax.axis_size("fsdp")
    tokens, model_width = residual_in.shape[1:]
    length = tokens * peers
    groups = w_key.shape[1] // HEAD_DIM
    per_group = w_query.shape[1] // w_key.shape[1]
    query_width = per_group * HEAD_DIM
    experts_all = w_router.shape[1]
    here = w_gate.shape[0]
    shard = w_query.shape[0]
    turned = query_width + HEAD_DIM
    router_at = turned
    lane_of = HEAD_DIM
    in_width = turned + LANES
    paired = lines == 4 and peers == 8

    w_in_shard = jnp.concatenate(
        [
            lax.dynamic_slice(w_query, (0, me * query_width), (shard, query_width)),
            lax.dynamic_slice(w_key, (0, me * HEAD_DIM), (shard, HEAD_DIM)),
            lax.dynamic_slice(w_value, (0, me * HEAD_DIM), (shard, HEAD_DIM)),
            w_router,
            jnp.zeros((shard, in_width - turned - HEAD_DIM - experts_all), BF16),
        ],
        axis=1,
    )
    w_out_shard = jnp.concatenate(
        [
            lax.dynamic_slice(w_out, (me * query_width, 0), (query_width, shard)),
            gain_attn[None],
            gain_ffn[None],
            jnp.zeros((14, shard), BF16),
        ],
        axis=0,
    )
    chosen = jnp.any(
        route_ids[0][:, :, None]
        == jnp.arange(LANES, dtype=jnp.int32)[None, None, :] - lane_of,
        axis=1,
    ).astype(F32)
    cosine, sine = rotary_tables(length)
    place = jnp.full((1,), me * here + lane_of, jnp.int32)
    own_rows, own_grad = residual_in[0], cotangent[0]
    wide = (peers, tokens, model_width)

    if paired:
        dy_all, w_in, w_out_rows, saved, b_all, g_all, middle, marked = front(
            own_rows, own_grad, w_in_shard, w_out_shard, chosen, cosine, sine, lines, per_group,
            router_at, 0,
        )
        sum_part, dw_all, dl_all, grad_middle, gain_two_grad, kept, came, far, others = experts_back(
            b_all, dy_all, g_all, w_gate, w_up, w_down, middle, marked, w_in, w_out_rows,
            lane_of, query_width, router_at, 2,
        )
        da_part, grad_in, out_low, e_own, e_total, *crossed = attend_back(
            dw_all.reshape(length, model_width), w_in, w_out_rows, cosine, sine, saved,
            b_all.reshape(2 * length, model_width), dl_all.reshape(length, LANES), per_group,
            (sum_part, others), 4,
        )
        outcome, grad_input, in_all, out_all, gains_all, notes_all = close_transfers(
            da_part.reshape(wide), e_own, e_total, own_rows, middle, grad_middle, gain_two_grad,
            w_out_rows, grad_in.reshape(lines, shard, in_width), out_low,
            query_width, 3,
        )
        squares = jnp.sum(notes_all, axis=0)[:5, 0]
        query, key, value, router_grad, proj, down, gate, up = finish(
            in_all, out_all, kept, came, [*far, *crossed], per_group, experts_all
        )
        reduced = [gate, up, down]
        gain_rows = jnp.sum(gains_all[:, :2].astype(F32), axis=0)
    else:
        x_all, dy_all = plane_gather([own_rows, own_grad], 0)
        w_in, w_out_rows = (
            lax.all_gather(w_in_shard, "fsdp", axis=0, tiled=True),
            lax.all_gather(w_out_shard, "fsdp", axis=1, tiled=True),
        )
        part, *saved = attend(
            x_all.reshape(length, model_width), w_in, w_out_rows, cosine, sine, per_group
        )
        (branch,) = plane_scatter([part.reshape(wide)], 1)
        gain_one = w_out_rows[query_width][None].astype(F32)
        gain_two = w_out_rows[query_width + 1][None].astype(F32)
        router = w_in[:, router_at:]
        rows = own_rows.astype(F32)
        inverse_one = lax.rsqrt(jnp.mean(rows * rows, axis=-1, keepdims=True) + EPSILON)
        normed_one = rows * inverse_one
        middle = rows + RESIDUAL_SCALE * branch
        inverse_two = lax.rsqrt(jnp.mean(middle * middle, axis=-1, keepdims=True) + EPSILON)
        normed_two = middle * inverse_two
        routed = (normed_two * gain_two).astype(BF16)
        logits = jnp.where(chosen > 0, dot(routed, router), -1e30)
        lifted = jnp.exp(logits - jnp.max(logits, axis=-1, keepdims=True))
        lifted = jnp.where(chosen > 0, lifted, 0.0)
        gates = lifted / jnp.sum(lifted, axis=-1, keepdims=True)
        b_all, g_all = plane_gather([routed, jnp.where(chosen > 0, gates, -1.0)], 2)
        sum_part, db_part, dg_part, *grads = experts(
            place, b_all, dy_all, g_all, w_gate, w_up, w_down
        )
        db_sum, dg_sum = plane_scatter([db_part, dg_part], 3)
        grad_rows = own_grad.astype(F32)
        grad_chosen = gates * (dg_sum - jnp.sum(gates * dg_sum, axis=-1, keepdims=True))
        grad_logits = grad_chosen.astype(BF16)
        grad_routed = dot(grad_logits, router, (1, 1)) + db_sum
        grad_gain_two = jnp.sum(grad_routed * normed_two, axis=0)
        grad_middle = grad_rows + norm_back(grad_routed * gain_two, normed_two, inverse_two)
        grad_branch = (RESIDUAL_SCALE * grad_middle).astype(BF16)
        dw_all, dl_all = plane_gather([grad_branch, grad_logits], 4)
        da_part, grad_in, grad_out = attend_back(
            dw_all.reshape(length, model_width), w_in, w_out_rows, cosine, sine, saved,
            b_all.reshape(length, model_width), dl_all.reshape(length, LANES), per_group,
        )
        da_sum, expert_sum = plane_scatter([da_part.reshape(wide), sum_part], 5)
        outcome = middle + expert_sum
        grad_gain_one = jnp.sum(da_sum * normed_one, axis=0)
        grad_input = grad_middle + norm_back(da_sum * gain_one, normed_one, inverse_one)
        squares = lax.psum(
            jnp.stack(
                [jnp.sum(v * v) for v in (rows, middle, outcome, grad_middle, grad_input)]
            ),
            ("fsdp", "expert"),
        )
        in_sum = lax.psum_scatter(grad_in, "fsdp", scatter_dimension=0, tiled=True)
        out_sum = lax.psum_scatter(
            grad_out.transpose(1, 0, 2).reshape(query_width, model_width), "fsdp",
            scatter_dimension=1, tiled=True,
        )
        gain_rows = lax.psum_scatter(
            lax.psum(jnp.stack([grad_gain_one, grad_gain_two]), "expert"),
            "fsdp", scatter_dimension=1, tiled=True,
        )
        in_all = lax.all_gather(in_sum, "expert", axis=0)
        out_all = lax.all_gather(out_sum, "expert", axis=0)
        outcome, grad_input = outcome.astype(BF16), grad_input.astype(BF16)
        grads = [
            grads[0].transpose(1, 0, 2, 3).reshape(w_gate.shape),
            grads[1].transpose(1, 0, 2, 3).reshape(w_up.shape),
            grads[2].transpose(1, 2, 0, 3).reshape(w_down.shape),
        ]
        reduced = [
            lax.psum_scatter(array, "fsdp", scatter_dimension=axis, tiled=True).astype(F32)
            for array, axis in zip(grads, (1, 1, 2))
        ]

        def columns_of(start, stop):
            return in_all[:, :, start:stop].transpose(1, 0, 2).reshape(shard, -1).astype(F32)

        query, key = columns_of(0, query_width), columns_of(query_width, turned)
        value = columns_of(turned, turned + HEAD_DIM)
        proj = out_all.reshape(groups * query_width, shard).astype(F32)
        at = turned + HEAD_DIM
        router_grad = in_all[0, :, at : at + experts_all].astype(F32)

    root_means = jnp.sqrt(squares / (tokens * model_width * lines * peers))
    return (
        outcome[None],
        grad_input[None],
        gain_rows[0],
        query,
        key,
        value,
        proj,
        gain_rows[1],
        router_grad,
        reduced[0],
        reduced[1],
        reduced[2],
        root_means,
    )


def solution(mesh):
    in_specs = (
        P("fsdp", "expert", None),
        P("fsdp", "expert", None),
        P("fsdp"),
        P("fsdp", None),
        P("fsdp", None),
        P("fsdp", None),
        P(None, "fsdp"),
        P("fsdp"),
        P("fsdp", None),
        P("expert", None, None),
        P("expert", None, None),
        P("expert", None, None),
        P("fsdp", "expert", None),
    )
    out_specs = (
        P("fsdp", "expert", None),
        P("fsdp", "expert", None),
        P("fsdp"),
        P("fsdp", None),
        P("fsdp", None),
        P("fsdp", None),
        P(None, "fsdp"),
        P("fsdp"),
        P("fsdp", None),
        P("expert", "fsdp", None),
        P("expert", "fsdp", None),
        P("expert", None, "fsdp"),
        P(),
    )
    return jax.shard_map(
        per_device, mesh=mesh, in_specs=in_specs, out_specs=out_specs, check_vma=False
    )
```

```python
import functools

import jax
import jax.numpy as jnp
from jax import lax
from jax.experimental import pallas as pl
from jax.experimental.pallas import tpu as pltpu
from jax.sharding import PartitionSpec as P

HEAD_DIM = 64
BLOCK = 256

EPSILON = 1e-06
RESIDUAL_SCALE = 0.22
ATTENTION_SCALE = 0.015625
ROPE_BASE = 10000.0
HIGHEST = lax.Precision.HIGHEST
MESH = pl.DeviceIdType.MESH
VMEM_LIMIT = 63_000_000
F32 = jnp.float32
BF16 = jnp.bfloat16
LANES = 128


def plane_neighbours():
    me = lax.axis_index("expert")
    core = lax.rem(me, 2)
    x_bit = lax.rem(me // 2, 2)
    y_bit = me // 4
    sibling = me + 1 - 2 * core
    x_peer = me + 2 - 4 * x_bit
    y_peer = me + 4 - 8 * y_bit
    diagonal = x_peer + 4 - 8 * y_bit
    return me, core, x_bit, y_bit, sibling, x_peer, y_peer, diagonal


def greet(axis, peers):
    barrier = pltpu.get_barrier_semaphore()
    for peer in peers:
        pl.semaphore_signal(barrier, inc=1, device_id={axis: peer}, device_id_type=MESH)
    pl.semaphore_wait(barrier, len(peers))


def gather_kernel(count, *refs):
    ins, outs = refs[:count], refs[count : 2 * count]
    own_sem, send_sem, recv_sem = refs[2 * count :]
    me, _, _, _, sibling, x_peer, y_peer, diagonal = plane_neighbours()
    greet("expert", (sibling, x_peer, y_peer))

    def remote(k, slot, source, target, peer):
        return pltpu.make_async_remote_copy(
            src_ref=source,
            dst_ref=target,
            send_sem=send_sem.at[k, slot],
            recv_sem=recv_sem.at[k, slot],
            device_id={"expert": peer},
            device_id_type=MESH,
        )

    plans = []
    for k in range(count):
        half = ins[k].shape[0] // 2
        parts = (pl.ds(0, half), pl.ds(half, half))
        out = outs[k]
        own = pltpu.make_async_copy(ins[k], out.at[me], own_sem.at[k])
        copies = [remote(k, 0, ins[k], out.at[me], sibling)]
        for h in range(2):
            copies.append(remote(k, 1 + h, ins[k].at[parts[h]], out.at[me, parts[h]], x_peer))
        for h in range(2):
            copies.append(remote(k, 3 + h, ins[k].at[parts[h]], out.at[me, parts[h]], y_peer))

        def forward(slot, block, h, peer):
            return remote(k, slot, out.at[block, parts[h]], out.at[block, parts[h]], peer)

        copies.append(forward(5, y_peer, 0, x_peer))
        copies.append(forward(6, x_peer, 1, y_peer))
        for h in range(2):
            copies.append(forward(7 + h, x_peer, h, sibling))
        for h in range(2):
            copies.append(forward(9 + h, y_peer, h, sibling))
        for h in range(2):
            copies.append(forward(11 + h, diagonal, h, sibling))
        plans.append((own, copies))
    for own, copies in plans:
        for slot in (3, 2, 1, 4, 0):
            copies[slot].start()
        own.start()
    for own, copies in plans:
        copies[3].wait_recv()
        copies[5].start()
        copies[2].wait_recv()
        copies[6].start()
        copies[9].start()
        copies[8].start()
        copies[1].wait_recv()
        copies[7].start()
        copies[4].wait_recv()
        copies[10].start()
    for own, copies in plans:
        copies[5].wait_recv()
        copies[11].start()
        copies[6].wait_recv()
        copies[12].start()
    for own, copies in plans:
        for slot in (0, 7, 8, 9, 10, 11, 12):
            copies[slot].wait_recv()
        for copy in copies:
            copy.wait_send()
        own.wait()


def plane_gather(arrays, collective_id):
    if lax.axis_size("expert") != 8:
        return [lax.all_gather(array, "expert", axis=0) for array in arrays]
    count = len(arrays)
    size = sum(array.size * array.dtype.itemsize for array in arrays)
    return pl.pallas_call(
        functools.partial(gather_kernel, count),
        out_shape=[jax.ShapeDtypeStruct((8,) + array.shape, array.dtype) for array in arrays],
        in_specs=[pl.BlockSpec(memory_space=pltpu.VMEM)] * count,
        out_specs=[pl.BlockSpec(memory_space=pl.ANY)] * count,
        scratch_shapes=[
            pltpu.SemaphoreType.DMA((count,)),
            pltpu.SemaphoreType.DMA((count, 13)),
            pltpu.SemaphoreType.DMA((count, 13)),
        ],
        compiler_params=pltpu.CompilerParams(
            collective_id=collective_id, has_side_effects=True, vmem_limit_bytes=VMEM_LIMIT
        ),
        cost_estimate=pl.CostEstimate(flops=0, bytes_accessed=16 * size, transcendentals=0),
        name="plane_gather",
    )(*arrays)


def scatter_kernel(count, *refs):
    ins, outs = refs[:count], refs[count : 2 * count]
    scratch = refs[2 * count : 2 * count + 6 * count]
    send_sem, recv_sem = refs[8 * count :]
    me, core, x_bit, y_bit, sibling, x_peer, y_peer, diagonal = plane_neighbours()
    greet("expert", (sibling, x_peer, y_peer))
    chip = me // 2
    chip_x, chip_y, chip_d = x_peer // 2, y_peer // 2, diagonal // 2
    order = (chip_d, chip_x, chip_y, chip)

    def remote(k, slot, source, target, peer):
        return pltpu.make_async_remote_copy(
            src_ref=source,
            dst_ref=target,
            send_sem=send_sem.at[k, slot],
            recv_sem=recv_sem.at[k, slot],
            device_id={"expert": peer},
            device_id_type=MESH,
        )

    stage0 = []
    for k in range(count):
        pair = scratch[6 * k]
        copies = [
            remote(k, i, ins[k].at[2 * order[i] + 1 - core], pair.at[i], sibling) for i in range(4)
        ]
        stage0.append(copies)
        for copy in copies:
            copy.start()
    later = []
    for k in range(count):
        pair, sums, first_x, first_y, second_x, second_y = scratch[6 * k : 6 * k + 6]
        rows = ins[k].shape[1]
        half = rows // 2
        parts = (pl.ds(0, half), pl.ds(half, half))
        dtype = ins[k].dtype

        def join(i):
            stage0[k][i].wait_recv()
            sums[i] = (ins[k][2 * order[i] + core].astype(F32) + pair[i].astype(F32)).astype(dtype)

        join(0)
        copies = [
            remote(k, 4, sums.at[0, parts[0]], first_x.at[1], x_peer),
            remote(k, 5, sums.at[0, parts[1]], first_y.at[1], y_peer),
        ]
        for copy in copies:
            copy.start()
        join(1)
        copies.append(remote(k, 6, sums.at[1, parts[0]], first_x.at[0], x_peer))
        copies[-1].start()
        join(2)
        copies.append(remote(k, 7, sums.at[2, parts[1]], first_y.at[0], y_peer))
        copies[-1].start()
        join(3)
        later.append(copies)
    for k in range(count):
        pair, sums, first_x, first_y, second_x, second_y = scratch[6 * k : 6 * k + 6]
        half = ins[k].shape[1] // 2
        parts = (pl.ds(0, half), pl.ds(half, half))
        dtype = ins[k].dtype
        copies = later[k]
        copies[0].wait_recv()
        pair[0, parts[0]] = (
            sums[2, parts[0]].astype(F32) + first_x[1].astype(F32)
        ).astype(dtype)
        copies.append(remote(k, 8, pair.at[0, parts[0]], second_y, y_peer))
        copies[-1].start()
        copies[1].wait_recv()
        pair[0, parts[1]] = (
            sums[1, parts[1]].astype(F32) + first_y[1].astype(F32)
        ).astype(dtype)
        copies.append(remote(k, 9, pair.at[0, parts[1]], second_x, x_peer))
        copies[-1].start()
    for k in range(count):
        pair, sums, first_x, first_y, second_x, second_y = scratch[6 * k : 6 * k + 6]
        half = ins[k].shape[1] // 2
        parts = (pl.ds(0, half), pl.ds(half, half))
        copies = later[k]
        copies[2].wait_recv()
        copies[4].wait_recv()
        outs[k][parts[0]] = (
            sums[3, parts[0]].astype(F32) + first_x[0].astype(F32) + second_y[...].astype(F32)
        )
        copies[3].wait_recv()
        copies[5].wait_recv()
        outs[k][parts[1]] = (
            sums[3, parts[1]].astype(F32) + first_y[0].astype(F32) + second_x[...].astype(F32)
        )
        for copy in stage0[k] + copies:
            copy.wait_send()


def plane_scatter(arrays, collective_id):
    if lax.axis_size("expert") != 8:
        return [
            lax.psum_scatter(array, "expert", scatter_dimension=0, tiled=False).astype(F32)
            for array in arrays
        ]
    count = len(arrays)
    scratch = []
    for array in arrays:
        _, rows, columns = array.shape
        half = rows // 2
        for shape in (
            (4, rows, columns),
            (4, rows, columns),
            (2, half, columns),
            (2, half, columns),
            (half, columns),
            (half, columns),
        ):
            scratch.append(pltpu.VMEM(shape, array.dtype))
    size = sum(array.size * array.dtype.itemsize for array in arrays)
    return pl.pallas_call(
        functools.partial(scatter_kernel, count),
        out_shape=[jax.ShapeDtypeStruct(array.shape[1:], F32) for array in arrays],
        in_specs=[pl.BlockSpec(memory_space=pltpu.VMEM)] * count,
        out_specs=[pl.BlockSpec(memory_space=pltpu.VMEM)] * count,
        scratch_shapes=scratch
        + [pltpu.SemaphoreType.DMA((count, 10)), pltpu.SemaphoreType.DMA((count, 10))],
        compiler_params=pltpu.CompilerParams(
            collective_id=collective_id, has_side_effects=True, vmem_limit_bytes=VMEM_LIMIT
        ),
        cost_estimate=pl.CostEstimate(flops=0, bytes_accessed=3 * size, transcendentals=0),
        name="plane_scatter",
    )(*arrays)


def push(source, target, send_sem, recv_sem, axis, peer):
    return pltpu.make_async_remote_copy(
        src_ref=source,
        dst_ref=target,
        send_sem=send_sem,
        recv_sem=recv_sem,
        device_id={axis: peer},
        device_id_type=MESH,
    )


def meet(plane, line, size, with_line):
    barrier = pltpu.get_barrier_semaphore()
    me, _, _, _, sibling, x_peer, y_peer, _ = plane
    for peer in (sibling, x_peer, y_peer):
        pl.semaphore_signal(barrier, inc=1, device_id={"expert": peer}, device_id_type=MESH)
    pl.semaphore_signal(
        barrier, inc=1, device_id={"fsdp": pair_of(line)}, device_id_type=MESH
    )
    if not with_line:
        pl.semaphore_signal(
            barrier, inc=1, device_id={"fsdp": beside(line)}, device_id_type=MESH
        )
        pl.semaphore_wait(barrier, 5)
        return

    @pl.when(line > 0)
    def _():
        pl.semaphore_signal(barrier, inc=1, device_id={"fsdp": line - 1}, device_id_type=MESH)

    @pl.when(line < size - 1)
    def _():
        pl.semaphore_signal(barrier, inc=1, device_id={"fsdp": line + 1}, device_id_type=MESH)

    @pl.when((line > 0) & (line < size - 1))
    def _():
        pl.semaphore_wait(barrier, 6)

    @pl.when((line == 0) | (line == size - 1))
    def _():
        pl.semaphore_wait(barrier, 5)


def pair_of(line):
    return line + 2 - 4 * (line // 2)


def beside(line):
    return line + 1 - 2 * lax.rem(line, 2)


def norm_back(grad_normed, normed, inverse):
    return inverse * (grad_normed - normed * jnp.mean(grad_normed * normed, axis=-1, keepdims=True))


class Gather:
    def __init__(self, plane, k, source, out, base, own_sem, send_sem, recv_sem):
        me, _, _, _, sibling, x_peer, y_peer, diagonal = plane
        half = source.shape[0] // 2
        parts = (pl.ds(0, half), pl.ds(half, half))

        def copy(slot, src, dst, peer):
            return push(src, dst, send_sem.at[k, slot], recv_sem.at[k, slot], "expert", peer)

        def forward(slot, block, h, peer):
            ref = out.at[base + block, parts[h]]
            return copy(slot, ref, ref, peer)

        self.own = pltpu.make_async_copy(source, out.at[base + me], own_sem.at[k])
        copies = [copy(0, source, out.at[base + me], sibling)]
        for slot, peer in ((1, x_peer), (3, y_peer)):
            for h in range(2):
                copies.append(
                    copy(slot + h, source.at[parts[h]], out.at[base + me, parts[h]], peer)
                )
        copies.append(forward(5, y_peer, 0, x_peer))
        copies.append(forward(6, x_peer, 1, y_peer))
        for slot, block in ((7, x_peer), (9, y_peer), (11, diagonal)):
            for h in range(2):
                copies.append(forward(slot + h, block, h, sibling))
        self.copies = copies

    def begin(self):
        for slot in (3, 2, 1, 4, 0):
            self.copies[slot].start()
        self.own.start()

    def relay(self):
        copies = self.copies
        for landed, onward in ((3, (5, 9)), (2, (6, 8)), (1, (7,)), (4, (10,))):
            copies[landed].wait_recv()
            for slot in onward:
                copies[slot].start()

    def relay_diagonal(self):
        for landed, onward in ((5, 11), (6, 12)):
            self.copies[landed].wait_recv()
            self.copies[onward].start()

    def finish(self):
        for slot in (0, 7, 8, 9, 10, 11, 12):
            self.copies[slot].wait_recv()
        for copy in self.copies:
            copy.wait_send()
        self.own.wait()


def gather_sems(count):
    return [
        pltpu.SemaphoreType.DMA((count,)),
        pltpu.SemaphoreType.DMA((count, 13)),
        pltpu.SemaphoreType.DMA((count, 13)),
    ]


class Scatter:
    def __init__(self, plane, k, source, base, scratch, send_sem, recv_sem):
        me, core, _, _, sibling, x_peer, y_peer, diagonal = plane
        self.source, self.base, self.core = source, base, core
        self.pair, self.first_x, self.first_y, self.second_x, self.second_y = scratch[:5]
        self.order = (diagonal // 2, x_peer // 2, y_peer // 2, me // 2)
        self.sums = [
            scratch[5].at[i] if len(scratch) > 5 else source.at[base + 2 * self.order[i] + core]
            for i in range(4)
        ]
        self.dtype = source.dtype
        half = source.shape[1] // 2
        self.parts = parts = (pl.ds(0, half), pl.ds(half, half))

        def copy(slot, src, dst, peer):
            return push(src, dst, send_sem.at[k, slot], recv_sem.at[k, slot], "expert", peer)

        self.stage0 = [
            copy(i, source.at[base + 2 * self.order[i] + 1 - core], self.pair.at[i], sibling)
            for i in range(4)
        ]
        self.stage1 = [
            copy(4, self.sums[0].at[parts[0]], self.first_x.at[1], x_peer),
            copy(5, self.sums[0].at[parts[1]], self.first_y.at[1], y_peer),
            copy(6, self.sums[1].at[parts[0]], self.first_x.at[0], x_peer),
            copy(7, self.sums[2].at[parts[1]], self.first_y.at[0], y_peer),
        ]
        self.stage2 = [
            copy(8, self.pair.at[0, parts[0]], self.second_y, y_peer),
            copy(9, self.pair.at[0, parts[1]], self.second_x, x_peer),
        ]

    def begin(self):
        for copy in self.stage0:
            copy.start()

    def join(self, i):
        self.stage0[i].wait_recv()
        mine = self.source[self.base + 2 * self.order[i] + self.core]
        self.sums[i][...] = (mine.astype(F32) + self.pair[i].astype(F32)).astype(self.dtype)

    def first(self):
        self.join(0)
        self.stage1[0].start()
        self.stage1[1].start()
        self.join(1)
        self.stage1[2].start()
        self.join(2)
        self.stage1[3].start()
        self.join(3)

    def second(self):
        for h, block, landed in ((0, 2, self.first_x), (1, 1, self.first_y)):
            self.stage1[h].wait_recv()
            rows = self.parts[h]
            self.pair[0, rows] = (
                self.sums[block][rows].astype(F32) + landed[1].astype(F32)
            ).astype(self.dtype)
            self.stage2[h].start()

    def total(self, h):
        self.stage1[2 + h].wait_recv()
        self.stage2[h].wait_recv()
        near, far = ((self.first_x, self.second_y), (self.first_y, self.second_x))[h]
        return (
            self.sums[3][self.parts[h]].astype(F32)
            + near[0].astype(F32)
            + far[...].astype(F32)
        )

    def finish(self):
        for copy in self.stage0 + self.stage1 + self.stage2:
            copy.wait_send()


def scatter_scratch(rows, columns, dtype, in_place=False):
    half = rows // 2
    shapes = [
        (4, rows, columns),
        (2, half, columns),
        (2, half, columns),
        (half, columns),
        (half, columns),
        (4, rows, columns),
    ]
    return [pltpu.VMEM(shape, dtype) for shape in shapes[: 5 if in_place else 6]]


def scatter_sems(count):
    return [pltpu.SemaphoreType.DMA((count, 10)), pltpu.SemaphoreType.DMA((count, 10))]


class LineGather:
    def __init__(self, line, size, k, source, out, axis, own_sem, send_sem, recv_sem):
        self.line, self.size, self.k, self.source, self.out = line, size, k, source, out
        self.axis, self.send_sem, self.recv_sem = axis, send_sem, recv_sem
        self.own = pltpu.make_async_copy(source, self.place(line), own_sem.at[k])

    def place(self, owner):
        extent = self.source.shape[self.axis]
        span = pl.ds(pl.multiple_of(owner * extent, extent), extent)
        return self.out.at[span] if self.axis == 0 else self.out.at[:, span]

    def hop(self, side, step, owner, source=None):
        target = self.place(owner)
        return push(
            target if source is None else source,
            target,
            self.send_sem.at[self.k, side, step],
            self.recv_sem.at[self.k, side, step],
            "fsdp",
            self.line + 1 - 2 * side,
        )

    def begin(self):
        for side, there in ((0, self.line < self.size - 1), (1, self.line > 0)):

            @pl.when(there)
            def _():
                self.hop(side, 0, self.line, self.source).start()

        self.own.start()

    def step(self, step):
        line, last = self.line, self.size - 1
        for side, owner in ((0, line - 1 - step), (1, line + 1 + step)):

            @pl.when((owner >= 0) & (owner <= last))
            def _():
                self.hop(side, step, owner).wait_recv()

                @pl.when((line < last) if side == 0 else (line > 0))
                def _():
                    self.hop(side, step + 1, owner).start()

    def finish(self):
        line, last = self.line, self.size - 1
        self.own.wait()
        for step in range(self.size - 1):
            for side, owner, there in ((0, line - step, line < last), (1, line + step, line > 0)):

                @pl.when(there & (owner >= 0) & (owner <= last))
                def _():
                    self.hop(side, step, owner).wait_send()


def line_gather_sems(count, size):
    return [
        pltpu.SemaphoreType.DMA((count,)),
        pltpu.SemaphoreType.DMA((count, 2, size)),
        pltpu.SemaphoreType.DMA((count, 2, size)),
    ]


class LineScatter:
    def __init__(self, line, size, k, source, sums, landed, send_sem, recv_sem):
        self.line, self.size, self.k = line, size, k
        self.source, self.sums, self.landed = source, sums, landed
        self.send_sem, self.recv_sem = send_sem, recv_sem

    def hop(self, side, owner):
        return push(
            self.sums.at[side, owner],
            self.landed.at[side, owner],
            self.send_sem.at[self.k, side, owner],
            self.recv_sem.at[self.k, side, owner],
            "fsdp",
            self.line + 1 - 2 * side,
        )

    def begin(self):
        last = self.size - 1
        for far in range(last):
            for side, owner, end in ((0, last - far, 0), (1, far, last)):

                @pl.when(self.line == end)
                def _():
                    self.sums[side, owner] = self.source[owner]
                    self.hop(side, owner).start()

    def pass_on(self, side, owner):
        self.hop(side, owner).wait_recv()
        self.sums[side, owner] = (
            self.source[owner].astype(F32) + self.landed[side, owner].astype(F32)
        ).astype(self.source.dtype)
        self.hop(side, owner).start()

    def step(self, far):
        line, last = self.line, self.size - 1

        @pl.when((line < last - far) & (line > 0))
        def _():
            self.pass_on(0, last - far)

        @pl.when((line > far) & (line < last))
        def _():
            self.pass_on(1, far)

    def total(self):
        line, last = self.line, self.size - 1
        for side, there, beyond in ((0, line > 0, line == 0), (1, line < last, line == last)):

            @pl.when(there)
            def _():
                self.hop(side, line).wait_recv()

            @pl.when(beyond)
            def _():
                self.landed[side, line] = jnp.zeros(self.source.shape[1:], self.source.dtype)

        return (
            self.source[line].astype(F32)
            + self.landed[0, line].astype(F32)
            + self.landed[1, line].astype(F32)
        )

    def finish(self):
        for owner in range(self.size):

            @pl.when(self.line < owner)
            def _():
                self.hop(0, owner).wait_send()

            @pl.when(self.line > owner)
            def _():
                self.hop(1, owner).wait_send()


def line_scatter_sems(count, size):
    return [
        pltpu.SemaphoreType.DMA((count, 2, size)),
        pltpu.SemaphoreType.DMA((count, 2, size)),
    ]


def in_vmem(count):
    return [pl.BlockSpec(memory_space=pltpu.VMEM)] * count


def anywhere(count):
    return [pl.BlockSpec(memory_space=pl.ANY)] * count


def talk_params(collective_id):
    return pltpu.CompilerParams(
        collective_id=collective_id, has_side_effects=True, vmem_limit_bytes=VMEM_LIMIT
    )


def close_kernel(
    size, query_width, da_ref, e_own, e_total, x_ref, middle_ref, grad_ref,
    gain_two_ref, wout_ref, gin_ref, out_low,
    outcome_ref, input_grad_ref, in_out, out_out, gains_out, notes_out,
    e_landed, gains, notes, notes_line, in_low, gain_low, notes_low, *rest,
):
    scratch, rest = rest[:6], rest[6:]
    line_scratch, rest = rest[:4], rest[4:]
    (
        swap_sems, scatter_send, scatter_recv, sum_send, sum_recv,
        line_own, line_send, line_recv, own_sem, send_sem, recv_sem,
    ) = rest
    plane, line = plane_neighbours(), lax.axis_index("fsdp")
    meet(plane, line, size, True)
    sums = (scatter_send, scatter_recv)
    da = Scatter(plane, 0, da_ref, 0, scratch[:6], *sums)
    swap = push(e_total, e_landed, swap_sems.at[0], swap_sems.at[1], "fsdp", pair_of(line))
    gin = LineScatter(line, size, 0, gin_ref, *line_scratch[0:2], sum_send, sum_recv)
    gain = LineScatter(line, size, 1, gains, *line_scratch[2:4], sum_send, sum_recv)
    gathers = (own_sem, send_sem, recv_sem)
    out_all = Gather(plane, 1, out_low, out_out, 0, *gathers)
    half = x_ref.shape[0] // 2
    gin.begin()
    swap.start()
    da.begin()
    da.first()
    gin.step(0)
    da.second()
    gin.step(1)
    gin.step(2)
    out_all.begin()
    gain_one = wout_ref[query_width : query_width + 1, :].astype(F32)
    grad_gain = jnp.zeros((1, x_ref.shape[1]), F32)
    squares = [jnp.zeros((1, 1), F32)] * 5

    def add_square(i, values):
        squares[i] = squares[i] + jnp.sum(
            jnp.sum(values * values, axis=1, keepdims=True), axis=0, keepdims=True
        )

    for h in range(2):
        rows = pl.ds(h * half, half)
        x = x_ref[rows].astype(F32)
        inverse = lax.rsqrt(jnp.mean(x * x, axis=1, keepdims=True) + EPSILON)
        normed = x * inverse
        grad_a = da.total(h)
        grad_gain += jnp.sum(grad_a * normed, axis=0, keepdims=True)
        grad_middle = grad_ref[rows]
        grad_input = grad_middle + norm_back(grad_a * gain_one, normed, inverse)
        input_grad_ref[rows] = grad_input.astype(BF16)
        add_square(0, x)
        add_square(1, middle_ref[rows])
        add_square(3, grad_middle)
        add_square(4, grad_input)
    width = x_ref.shape[1] // size
    row = lax.broadcasted_iota(jnp.int32, gains.shape[1:], 0)
    for p in range(size):
        columns = slice(p * width, (p + 1) * width)
        gains[p] = jnp.where(
            row == 0, grad_gain[:, columns],
            jnp.where(row == 1, gain_two_ref[0:1, columns], 0.0),
        ).astype(BF16)
    gain.begin()
    gain.step(0)
    gain.step(1)
    gain.step(2)
    out_all.relay()
    swap.wait_recv()
    for h in range(2):
        rows = pl.ds(h * half, half)
        outcome = middle_ref[rows] + e_own[rows] + e_landed[rows].astype(F32)
        outcome_ref[rows] = outcome.astype(BF16)
        add_square(2, outcome)
    row = lax.broadcasted_iota(jnp.int32, notes.shape, 0)
    told = jnp.zeros(notes.shape, F32)
    for i in range(5):
        told = jnp.where(row == i, squares[i], told)
    notes[...] = told
    spread = LineGather(line, size, 0, notes, notes_line, 0, line_own, line_send, line_recv)
    spread.begin()
    in_low[...] = gin.total().astype(BF16)
    in_all = Gather(plane, 0, in_low, in_out, 0, *gathers)
    in_all.begin()
    spread.step(0)
    out_all.relay_diagonal()
    spread.step(1)
    spread.step(2)
    gain_low[...] = gain.total().astype(BF16)
    gain_all = Gather(plane, 2, gain_low, gains_out, 0, *gathers)
    gain_all.begin()
    spread.finish()
    count = notes.shape[0]
    notes_low[...] = (
        notes_line[pl.ds(0, count)] + notes_line[pl.ds(count, count)]
        + notes_line[pl.ds(2 * count, count)] + notes_line[pl.ds(3 * count, count)]
    )
    notes_all = Gather(plane, 3, notes_low, notes_out, 0, *gathers)
    notes_all.begin()
    last = (in_all, gain_all, notes_all)
    for item in last:
        item.relay()
    for item in last:
        item.relay_diagonal()
    for item in last + (out_all, da, gin, gain):
        item.finish()
    swap.wait_send()


def close_transfers(
    da_part, e_own, e_total, x, middle, grad_middle, gain_two, w_out, grad_in, out_low,
    query_width, collective_id,
):
    tokens, model_width = x.shape
    size, in_rows, in_columns = grad_in.shape
    out_rows, out_columns = out_low.shape
    wide = (tokens, model_width)
    gain_shape, note_shape = (16, out_columns), (16, LANES)
    line_scratch = []
    for shape in (grad_in.shape, (size,) + gain_shape):
        line_scratch += [pltpu.VMEM((2,) + shape, BF16)] * 2
    return pl.pallas_call(
        functools.partial(close_kernel, size, query_width),
        out_shape=[
            jax.ShapeDtypeStruct(wide, BF16),
            jax.ShapeDtypeStruct(wide, BF16),
            jax.ShapeDtypeStruct((8, in_rows, in_columns), BF16),
            jax.ShapeDtypeStruct((8, out_rows, out_columns), BF16),
            jax.ShapeDtypeStruct((8,) + gain_shape, BF16),
            jax.ShapeDtypeStruct((8,) + note_shape, F32),
        ],
        in_specs=in_vmem(10),
        out_specs=in_vmem(2) + anywhere(4),
        scratch_shapes=[
            pltpu.VMEM(wide, BF16),
            pltpu.VMEM((size,) + gain_shape, BF16),
            pltpu.VMEM(note_shape, F32),
            pltpu.VMEM((size * note_shape[0], LANES), F32),
            pltpu.VMEM((in_rows, in_columns), BF16),
            pltpu.VMEM(gain_shape, BF16),
            pltpu.VMEM(note_shape, F32),
        ]
        + scatter_scratch(*wide, BF16)
        + line_scratch
        + [pltpu.SemaphoreType.DMA((2,))]
        + scatter_sems(1)
        + line_scatter_sems(2, size)
        + line_gather_sems(1, size)
        + gather_sems(4),
        compiler_params=talk_params(collective_id),
        cost_estimate=pl.CostEstimate(flops=0, bytes_accessed=200_000_000, transcendentals=0),
        name="close_transfers",
    )(da_part, e_own, e_total, x, middle, grad_middle, gain_two, w_out, grad_in, out_low)


def dot(first, second, contract=(1, 0)):
    return lax.dot_general(
        first, second, (((contract[0],), (contract[1],)), ((), ())), preferred_element_type=F32
    )


def spin(values, cosine, sine):
    width = values.shape[1]
    half = HEAD_DIM // 2
    cosine = jnp.concatenate([cosine] * (width // LANES), axis=1)
    sine = jnp.concatenate([sine] * (width // LANES), axis=1)
    lane = lax.broadcasted_iota(jnp.int32, values.shape, 1)
    lower = lax.rem(lane, HEAD_DIM) < half
    swapped = jnp.where(
        lower, pltpu.roll(values, width - half, 1), pltpu.roll(values, half, 1)
    )
    return values * cosine + swapped * sine


def attend_kernel(per_group, x_ref, w_in_ref, w_out_ref, cos_ref, sin_ref, part_ref, *outs):
    def take(rows):
        return x_ref[rows, :]

    def put(i, part):
        part_ref[i * BLOCK : (i + 1) * BLOCK, :] = part

    attend_steps(
        per_group, x_ref.shape[0], take, put, lambda step: None, w_in_ref, w_out_ref, cos_ref,
        sin_ref, *outs,
    )


def attend_steps(
    per_group, length, take, put, hook, w_in_ref, w_out_ref, cos_ref, sin_ref,
    a_ref, q_ref, k_ref, v_ref, o_ref, lse_ref,
):
    query_width = per_group * HEAD_DIM
    turned = query_width + HEAD_DIM
    gain = w_out_ref[query_width : query_width + 1, :].astype(F32)

    def project(i, carry):
        rows = pl.ds(pl.multiple_of(i * BLOCK, BLOCK), BLOCK)
        x = take(rows).astype(F32)
        inverse = lax.rsqrt(jnp.mean(x * x, axis=1, keepdims=True) + EPSILON)
        a = (x * inverse * gain).astype(BF16)
        a_ref[rows, :] = a
        pre = dot(a, w_in_ref[...])
        spun = spin(pre[:, :turned], cos_ref[rows, :], sin_ref[rows, :]).astype(BF16)
        for h in range(per_group):
            q_ref[h, rows, :] = spun[:, h * HEAD_DIM : (h + 1) * HEAD_DIM]
        k_ref[rows, :] = spun[:, query_width:turned]
        v_ref[rows, :] = pre[:, turned : turned + HEAD_DIM].astype(BF16)
        return carry

    lax.fori_loop(0, length // BLOCK, project, 0)
    hook(0)
    for i in range(length // BLOCK):
        seen = (i + 1) * BLOCK
        rows = slice(i * BLOCK, seen)
        keys, values = k_ref[:seen, :], v_ref[:seen, :]
        for h in range(per_group):
            scores = dot(q_ref[h, rows, :], keys, (1, 1)) * ATTENTION_SCALE
            peak = jnp.max(scores, axis=1, keepdims=True)
            lifted = jnp.exp(scores - peak)
            total = jnp.sum(lifted, axis=1, keepdims=True)
            weights = (lifted * (1.0 / total)).astype(BF16)
            mixed = dot(weights, values)
            o_ref[rows, h * HEAD_DIM : (h + 1) * HEAD_DIM] = mixed.astype(BF16)
            lse_ref[h, rows, :] = peak + jnp.log(total)
        put(i, dot(o_ref[rows, :], w_out_ref[:query_width, :]).astype(BF16))
        hook(1 + i)


def saved_shapes(length, model_width, per_group):
    return [
        jax.ShapeDtypeStruct((length, model_width), BF16),
        jax.ShapeDtypeStruct((per_group, length, HEAD_DIM), BF16),
        jax.ShapeDtypeStruct((length, HEAD_DIM), BF16),
        jax.ShapeDtypeStruct((length, HEAD_DIM), BF16),
        jax.ShapeDtypeStruct((length, per_group * HEAD_DIM), BF16),
        jax.ShapeDtypeStruct((per_group, length, 1), F32),
    ]


def front_kernel(
    size, per_group, router_at, x_ref, dy_ref, win_shard, wout_shard, chosen_ref, cos_ref, sin_ref,
    dy_out, win_ref, wout_ref, *rest,
):
    saved, rest = rest[:6], rest[6:]
    b_out, g_out, middle_ref, marked_ref, *rest = rest
    x_all, part_ref, dy_landed, routed, b_landed, g_landed, *rest = rest
    scratch, rest = rest[:5], rest[5:]
    (
        swap_sems, scatter_send, scatter_recv, own_sem, send_sem, recv_sem,
        line_own, line_send, line_recv,
    ) = rest
    plane, line = plane_neighbours(), lax.axis_index("fsdp")
    pair = pair_of(line)
    tokens = x_ref.shape[0]
    half, per_block = tokens // 2, BLOCK // tokens
    query_width = per_group * HEAD_DIM
    meet(plane, line, size, True)
    sems = (own_sem, send_sem, recv_sem)
    line_sems = (line_own, line_send, line_recv)
    x = Gather(plane, 0, x_ref, x_all, 0, *sems)
    dy = Gather(plane, 1, dy_ref, dy_out, 0, *sems)
    other = Gather(plane, 2, dy_landed, dy_out, 8, *sems)
    win = LineGather(line, size, 0, win_shard, win_ref, 0, *line_sems)
    wout = LineGather(line, size, 1, wout_shard, wout_ref, 1, *line_sems)
    scatter = Scatter(plane, 0, part_ref, 0, scratch, scatter_send, scatter_recv)
    swap_dy = push(dy_ref, dy_landed, swap_sems.at[0], swap_sems.at[1], "fsdp", pair)
    swap_b = push(routed, b_landed, swap_sems.at[2], swap_sems.at[3], "fsdp", pair)
    swap_g = push(marked_ref, g_landed, swap_sems.at[4], swap_sems.at[5], "fsdp", pair)
    win.begin()
    x.begin()
    wout.begin()
    x.relay()
    win.step(0)
    x.relay_diagonal()
    wout.step(0)
    dy.begin()
    win.step(1)
    wout.step(1)
    win.step(2)
    wout.step(2)
    swap_dy.start()
    for item in (x, win, wout):
        item.finish()

    def take(rows):
        block = pl.ds(rows.start // tokens, per_block)
        return x_all[block].reshape(BLOCK, x_all.shape[2])

    def put(i, part):
        for t in range(per_block):
            part_ref[per_block * i + t] = part[t * tokens : (t + 1) * tokens]

    def hook(step):
        if step == 0:
            dy.relay()
        elif step == 2:
            dy.relay_diagonal()
        elif step == 3:
            swap_dy.wait_recv()

    attend_steps(
        per_group, x_all.shape[0] * tokens, take, put, hook, win_ref, wout_ref, cos_ref, sin_ref,
        *saved,
    )
    scatter.begin()
    scatter.first()
    scatter.second()
    gain = wout_ref[query_width + 1 : query_width + 2, :].astype(F32)
    router = win_ref[:, router_at : router_at + LANES]
    for h in range(2):
        rows = pl.ds(h * half, half)
        middle = x_ref[rows].astype(F32) + RESIDUAL_SCALE * scatter.total(h)
        middle_ref[rows] = middle
        inverse = lax.rsqrt(jnp.mean(middle * middle, axis=1, keepdims=True) + EPSILON)
        b = (middle * inverse * gain).astype(BF16)
        routed[rows] = b
        chosen = chosen_ref[rows] > 0.0
        logits = jnp.where(chosen, dot(b, router), -1e30)
        lifted = jnp.where(chosen, jnp.exp(logits - jnp.max(logits, axis=1, keepdims=True)), 0.0)
        gates = lifted / jnp.sum(lifted, axis=1, keepdims=True)
        marked_ref[rows] = jnp.where(chosen, gates, -1.0)
    swap_b.start()
    swap_g.start()
    b = Gather(plane, 3, routed, b_out, 0, *sems)
    g = Gather(plane, 4, marked_ref, g_out, 0, *sems)
    b_other = Gather(plane, 5, b_landed, b_out, 8, *sems)
    g_other = Gather(plane, 6, g_landed, g_out, 8, *sems)
    b.begin()
    g.begin()
    b.relay()
    g.relay()
    other.begin()
    b.relay_diagonal()
    g.relay_diagonal()
    other.relay()
    swap_b.wait_recv()
    swap_g.wait_recv()
    b_other.begin()
    g_other.begin()
    other.relay_diagonal()
    b_other.relay()
    g_other.relay()
    b_other.relay_diagonal()
    g_other.relay_diagonal()
    for item in (dy, other, b, g, b_other, g_other, scatter):
        item.finish()
    for swap in (swap_dy, swap_b, swap_g):
        swap.wait_send()


def front(
    x, dy, w_in_shard, w_out_shard, chosen, cosine, sine, size, per_group, router_at, collective_id
):
    tokens, model_width = x.shape
    rows, columns = w_in_shard.shape
    out_rows, out_columns = w_out_shard.shape
    wide, narrow = (tokens, model_width), (tokens, LANES)
    out = pl.pallas_call(
        functools.partial(front_kernel, size, per_group, router_at),
        out_shape=[
            jax.ShapeDtypeStruct((16,) + wide, BF16),
            jax.ShapeDtypeStruct((rows * size, columns), BF16),
            jax.ShapeDtypeStruct((out_rows, out_columns * size), BF16),
        ]
        + saved_shapes(8 * tokens, model_width, per_group)
        + [
            jax.ShapeDtypeStruct((16,) + wide, BF16),
            jax.ShapeDtypeStruct((16,) + narrow, F32),
            jax.ShapeDtypeStruct(wide, F32),
            jax.ShapeDtypeStruct(narrow, F32),
        ],
        in_specs=in_vmem(7),
        out_specs=anywhere(1) + in_vmem(8) + anywhere(2) + in_vmem(2),
        scratch_shapes=[
            pltpu.VMEM((8,) + wide, BF16),
            pltpu.VMEM((8,) + wide, BF16),
            pltpu.VMEM(wide, BF16),
            pltpu.VMEM(wide, BF16),
            pltpu.VMEM(wide, BF16),
            pltpu.VMEM(narrow, F32),
        ]
        + scatter_scratch(*wide, BF16, True)
        + [pltpu.SemaphoreType.DMA((6,))]
        + scatter_sems(1)
        + gather_sems(7)
        + line_gather_sems(2, size),
        compiler_params=talk_params(collective_id),
        cost_estimate=pl.CostEstimate(
            flops=8_000_000_000, bytes_accessed=150_000_000, transcendentals=2_000_000
        ),
        name="front",
    )(x, dy, w_in_shard, w_out_shard, chosen, cosine, sine)
    return [*out[:3], out[3:9], *out[9:]]


def attend(x_all, w_in, w_out, cosine, sine, per_group):
    length, model_width = x_all.shape
    shapes = [jax.ShapeDtypeStruct((length, model_width), BF16)]
    shapes += saved_shapes(length, model_width, per_group)
    return pl.pallas_call(
        functools.partial(attend_kernel, per_group),
        out_shape=shapes,
        in_specs=[pl.BlockSpec(memory_space=pltpu.VMEM)] * 5,
        out_specs=[pl.BlockSpec(memory_space=pltpu.VMEM)] * len(shapes),
        compiler_params=pltpu.CompilerParams(vmem_limit_bytes=VMEM_LIMIT),
        cost_estimate=pl.CostEstimate(
            flops=8_000_000_000, bytes_accessed=16_000_000, transcendentals=2_000_000
        ),
        name="attend",
    )(x_all, w_in, w_out, cosine, sine)


def attend_back_kernel(per_group, *refs):
    attend_back_steps(per_group, lambda step: None, *refs)


def attend_back_talk_kernel(per_group, size, swaps, *refs):
    ins, refs = refs[:13], refs[13:]
    sum_ref, sent, refs = refs[0], refs[1 : 1 + swaps], refs[1 + swaps :]
    part_ref, gin_ref, out_low, e_own, e_other = refs[:5]
    came, refs = refs[5 : 5 + swaps], refs[5 + swaps :]
    scratch, stage_a, stage_b, refs = refs[:5], refs[5:11], refs[11:17], refs[17:]
    gout_ref, line_sums, line_landed, sends, receives, swap_sems, line_send, line_recv = refs
    plane, line = plane_neighbours(), lax.axis_index("fsdp")
    other = Scatter(plane, 0, sum_ref, 8, stage_a, sends, receives)
    mine = Scatter(plane, 1, sum_ref, 0, stage_b, sends, receives)
    gout = LineScatter(line, size, 0, gout_ref, line_sums, line_landed, line_send, line_recv)
    across = [
        push(source, target, swap_sems.at[0, i], swap_sems.at[1, i], "fsdp", pair_of(line))
        for i, (source, target) in enumerate(zip(sent, came))
    ]
    half = e_own.shape[0] // 2

    def hook(step):
        if step == 0:
            meet(plane, line, size, True)
            other.begin()
            mine.begin()
            gout.begin()
            across[0].start()
        elif step == 1:
            other.first()
            gout.step(0)
            for copy in across[1:2]:
                copy.start()
        elif step == 2:
            mine.first()
            gout.step(1)
            for copy in across[2:]:
                copy.start()
        elif step == 3:
            other.second()
            gout.step(2)
        elif step == 4:
            mine.second()
        elif step == 6:
            for h in range(2):
                e_other[pl.ds(h * half, half)] = other.total(h).astype(BF16)
                e_own[pl.ds(h * half, half)] = mine.total(h)
            out_low[...] = gout.total().astype(BF16)
            for item in (other, mine, gout):
                item.finish()
            for copy in across:
                copy.wait()

    attend_back_steps(per_group, hook, *ins, part_ref, gin_ref, gout_ref, *scratch)


def attend_back_steps(
    per_group, hook, dw_ref, w_in_ref, w_out_ref, cos_ref, sin_ref,
    a_ref, q_ref, k_ref, v_ref, o_ref, lse_ref, b_all_ref, dl_ref,
    part_ref, gin_ref, gout_ref,
    turn_ref, dv_ref, back_ref, b_ref, b_sem,
):
    length, model_width = dw_ref.shape
    fetch = pltpu.make_async_copy(b_all_ref.at[pl.ds(0, length)], b_ref, b_sem)
    fetch.start()
    query_width = per_group * HEAD_DIM
    turned = query_width + HEAD_DIM
    blocks = length // BLOCK
    chunk = 384

    def out_grads(i, carry):
        columns = pl.ds(pl.multiple_of(i * chunk, chunk), chunk)
        gout_ref[i] = dot(o_ref[...], dw_ref[:, columns], (0, 0)).astype(BF16)
        return carry

    lax.fori_loop(0, model_width // chunk, out_grads, 0)
    hook(0)
    turn_ref[...] = jnp.zeros_like(turn_ref)
    dv_ref[...] = jnp.zeros_like(dv_ref)
    for i in range(blocks):
        seen = (i + 1) * BLOCK
        rows = slice(i * BLOCK, seen)
        keys, values = k_ref[:seen, :], v_ref[:seen, :]
        grad = dot(dw_ref[rows, :], w_out_ref[:query_width, :], (1, 1)).astype(BF16)
        for h in range(per_group):
            columns = slice(h * HEAD_DIM, (h + 1) * HEAD_DIM)
            queries = q_ref[h, rows, :]
            grad_head = grad[:, columns]
            scores = dot(queries, keys, (1, 1)) * ATTENTION_SCALE
            probs = jnp.exp(scores - lse_ref[h, rows, :])
            dv_ref[:seen, :] += dot(probs.astype(BF16), grad_head, (0, 0))
            grad_probs = dot(grad_head, values, (1, 1))
            inner = jnp.sum(probs * grad_probs, axis=1, keepdims=True)
            grad_scores = (probs * (grad_probs - inner)).astype(BF16)
            turn_ref[rows, columns] = dot(grad_scores, keys) * ATTENTION_SCALE
            turn_ref[:seen, query_width:turned] += (
                dot(grad_scores, queries, (0, 0)) * ATTENTION_SCALE
            )
        hook(1 + i)

    def unturn(i, carry):
        rows = pl.ds(pl.multiple_of(i * BLOCK, BLOCK), BLOCK)
        back_ref[rows, :turned] = spin(
            turn_ref[rows, :], cos_ref[rows, :], -sin_ref[rows, :]
        ).astype(BF16)
        back_ref[rows, turned:] = jnp.concatenate(
            [dv_ref[rows, :].astype(BF16), jnp.zeros((BLOCK, LANES - HEAD_DIM), BF16)], axis=1
        )
        part_ref[rows, :] = dot(
            back_ref[rows, : turned + HEAD_DIM], w_in_ref[:, : turned + HEAD_DIM], (1, 1)
        ).astype(BF16)
        return carry

    lax.fori_loop(0, blocks, unturn, 0)
    hook(5)
    fetch.wait()

    def weight_grads(i, carry):
        columns = pl.ds(pl.multiple_of(i * chunk, chunk), chunk)
        a = a_ref[:, columns]
        gin_ref[columns, :turned] = dot(a, back_ref[:, :turned], (0, 0)).astype(BF16)
        gin_ref[columns, turned:] = (
            dot(a, back_ref[:, turned:], (0, 0)) + dot(b_ref[:, columns], dl_ref[...], (0, 0))
        ).astype(BF16)
        return carry

    lax.fori_loop(0, model_width // chunk, weight_grads, 0)
    hook(6)


def attend_back(
    dw_all, w_in, w_out, cosine, sine, saved, b_all, dl_all, per_group, talk=None, collective_id=None
):
    length, model_width = dw_all.shape
    query_width = per_group * HEAD_DIM
    turned = query_width + HEAD_DIM
    shapes = [
        jax.ShapeDtypeStruct((length, model_width), BF16),
        jax.ShapeDtypeStruct((model_width, w_in.shape[1]), BF16),
        jax.ShapeDtypeStruct((model_width // 384, query_width, 384), BF16),
    ]
    scratch = [
        pltpu.VMEM((length, turned), F32),
        pltpu.VMEM((length, HEAD_DIM), F32),
        pltpu.VMEM((length, w_in.shape[1]), BF16),
        pltpu.VMEM((length, model_width), BF16),
        pltpu.SemaphoreType.DMA,
    ]
    operands = (dw_all, w_in, w_out, cosine, sine, *saved, b_all, dl_all)
    in_specs, out_specs = in_vmem(11) + anywhere(1) + in_vmem(1), in_vmem(len(shapes))
    kernel = functools.partial(attend_back_kernel, per_group)
    params = pltpu.CompilerParams(vmem_limit_bytes=VMEM_LIMIT)
    if talk is not None:
        sum_part, sent = talk
        wide = sum_part.shape[1:]
        shapes = shapes + [jax.ShapeDtypeStruct(wide, F32), jax.ShapeDtypeStruct(wide, BF16)]
        shapes += [jax.ShapeDtypeStruct(array.shape, array.dtype) for array in sent]
        gout_shape, size = shapes[2].shape, lax.axis_size("fsdp")
        shapes[2] = jax.ShapeDtypeStruct(gout_shape[1:], BF16)
        scratch = scratch + scatter_scratch(*wide, BF16) * 2
        scratch += [pltpu.VMEM(gout_shape, BF16)] + [pltpu.VMEM((2,) + gout_shape, BF16)] * 2
        scratch += scatter_sems(2) + [pltpu.SemaphoreType.DMA((2, len(sent)))]
        scratch += line_scatter_sems(1, size)
        operands += (sum_part, *sent)
        in_specs = in_specs + in_vmem(1) + anywhere(len(sent))
        out_specs = out_specs + in_vmem(2) + anywhere(len(sent))
        kernel = functools.partial(attend_back_talk_kernel, per_group, size, len(sent))
        params = talk_params(collective_id)
    return pl.pallas_call(
        kernel,
        out_shape=shapes,
        in_specs=in_specs,
        out_specs=out_specs,
        scratch_shapes=scratch,
        compiler_params=params,
        cost_estimate=pl.CostEstimate(
            flops=20_000_000_000, bytes_accessed=30_000_000, transcendentals=2_000_000
        ),
        name="attend_back",
    )(*operands)


def experts_kernel(
    here, tile,
    place_ref, b_hbm, dy_hbm, g_ref, gate_hbm, up_hbm, down_hbm, *rest,
):
    out_hbm, db_hbm, dg_ref = rest[:3]
    grad_hbm, rest = rest[3:6], rest[6:]
    (
        b_ref, dy_ref, in_ref, down_ref, hidden_ref, back_ref, out_ref, db_ref,
        gate_stage, up_stage, down_stage, weight_sem, tile_sem, out_sem, grad_sem,
    ) = rest
    rows_all, model_width = b_ref.shape
    width = down_ref.shape[0] // here
    tiles = rows_all // tile
    first = place_ref[0]

    def columns_of(e):
        return slice(e * width, (e + 1) * width)

    loads = []
    for e in range(here):
        loads.append((gate_hbm.at[e], in_ref.at[:, columns_of(e)]))
        loads.append((up_hbm.at[e], in_ref.at[:, columns_of(here + e)]))
    for e in range(here):
        loads.append((down_hbm.at[e], down_ref.at[columns_of(e), :]))
    loads = [
        pltpu.make_async_copy(source, target, weight_sem.at[i])
        for i, (source, target) in enumerate(loads)
    ]

    def tile_rows(i):
        return pl.ds(pl.multiple_of(i * tile, tile), tile)

    def tile_load(i, k):
        source, target = ((b_hbm, b_ref), (dy_hbm, dy_ref))[k]
        return pltpu.make_async_copy(
            source.at[tile_rows(i)], target.at[tile_rows(i)], tile_sem.at[k, i]
        )

    def tile_store(i, k):
        source, target = ((out_ref, out_hbm), (db_ref, db_hbm))[k]
        return pltpu.make_async_copy(
            source.at[tile_rows(i)], target.at[tile_rows(i)], out_sem.at[k, i]
        )

    for k in range(2):
        tile_load(0, k).start()
    for load in loads:
        load.start()
    for i in range(1, tiles):
        for k in range(2):
            tile_load(i, k).start()
    for load in loads:
        load.wait()

    def forward_back(i, carry):
        rows = tile_rows(i)
        tile_load(i, 0).wait()
        tile_load(i, 1).wait()
        pre = dot(b_ref[rows, :], in_ref[...])
        grad_mixed = dot(dy_ref[rows, :], down_ref[...], (1, 1))
        gates = g_ref[rows, :]
        lane = lax.broadcasted_iota(jnp.int32, gates.shape, 1)
        inner = jnp.zeros(gates.shape, F32)
        for e in range(here):
            mine = lane == first + e
            gate = jnp.sum(jnp.where(mine, jnp.maximum(gates, 0.0), 0.0), axis=1, keepdims=True)
            scale = RESIDUAL_SCALE * gate
            gate_pre, up_pre = pre[:, columns_of(e)], pre[:, columns_of(here + e)]
            sigmoid = 1.0 / (1.0 + jnp.exp(-gate_pre))
            silu = gate_pre * sigmoid
            hidden = silu * up_pre
            grad = grad_mixed[:, columns_of(e)]
            share = jnp.sum(hidden * grad, axis=1, keepdims=True)
            inner = jnp.where(mine, RESIDUAL_SCALE * share, inner)
            hidden_ref[rows, columns_of(e)] = (scale * hidden).astype(BF16)
            grad = scale * grad
            back_ref[rows, columns_of(e)] = (
                grad * up_pre * sigmoid * (1.0 + gate_pre * (1.0 - sigmoid))
            ).astype(BF16)
            back_ref[rows, columns_of(here + e)] = (grad * silu).astype(BF16)
        dg_ref[rows, :] = inner
        db_ref[rows, :] = dot(back_ref[rows, :], in_ref[...], (1, 1)).astype(BF16)
        tile_store(i, 1).start()
        out_ref[rows, :] = dot(hidden_ref[rows, :], down_ref[...]).astype(BF16)
        tile_store(i, 0).start()
        return carry

    lax.fori_loop(0, tiles, forward_back, 0)
    parts = 4
    part = model_width // parts

    def part_columns(i):
        return pl.ds(pl.multiple_of(i * part, part), part)

    def down_grad(i, carry):
        grad = dot(hidden_ref[...], dy_ref[:, part_columns(i)], (0, 0))
        for e in range(here):
            down_stage[i, e] = grad[columns_of(e), :].astype(BF16)
        return carry

    def in_grad(i, carry):
        grad = dot(b_ref[:, part_columns(i)], back_ref[...], (0, 0))
        for e in range(here):
            gate_stage[i, e] = grad[:, columns_of(e)].astype(BF16)
            up_stage[i, e] = grad[:, columns_of(here + e)].astype(BF16)
        return carry

    stores = []

    def store(k, stage):
        copy = pltpu.make_async_copy(stage, grad_hbm[k], grad_sem.at[k])
        copy.start()
        stores.append(copy)

    lax.fori_loop(0, parts, down_grad, 0)
    store(2, down_stage)
    lax.fori_loop(0, parts, in_grad, 0)
    store(0, gate_stage)
    store(1, up_stage)
    for copy in stores:
        copy.wait()
    for i in range(tiles):
        for k in range(2):
            tile_store(i, k).wait()


def experts(place, b_all, dy_all, g_all, w_gate, w_up, w_down):
    sources, tokens, model_width = b_all.shape
    here, _, hidden_width = w_gate.shape
    rows_all = sources * tokens
    width = hidden_width
    part = model_width // 4
    tile = 256
    tiles = rows_all // tile
    in_stage, down_stage = (4, here, part, width), (4, here, width, part)
    shapes = [in_stage, in_stage, down_stage]
    flat = (rows_all, model_width)
    out = pl.pallas_call(
        functools.partial(experts_kernel, here, tile),
        out_shape=[
            jax.ShapeDtypeStruct(flat, BF16),
            jax.ShapeDtypeStruct(flat, BF16),
            jax.ShapeDtypeStruct((rows_all, LANES), F32),
        ]
        + [jax.ShapeDtypeStruct(shape, BF16) for shape in shapes],
        in_specs=[pl.BlockSpec(memory_space=pltpu.SMEM)] + anywhere(2) + in_vmem(1) + anywhere(3),
        out_specs=anywhere(2) + in_vmem(1) + anywhere(len(shapes)),
        scratch_shapes=[
            pltpu.VMEM(flat, BF16),
            pltpu.VMEM(flat, BF16),
            pltpu.VMEM((model_width, 2 * here * width), BF16),
            pltpu.VMEM((here * width, model_width), BF16),
            pltpu.VMEM((rows_all, here * width), BF16),
            pltpu.VMEM((rows_all, 2 * here * width), BF16),
            pltpu.VMEM(flat, BF16),
            pltpu.VMEM(flat, BF16),
            pltpu.VMEM(in_stage, BF16),
            pltpu.VMEM(in_stage, BF16),
            pltpu.VMEM(down_stage, BF16),
            pltpu.SemaphoreType.DMA((3 * here,)),
            pltpu.SemaphoreType.DMA((2, tiles)),
            pltpu.SemaphoreType.DMA((2, tiles)),
            pltpu.SemaphoreType.DMA((3,)),
        ],
        compiler_params=pltpu.CompilerParams(vmem_limit_bytes=VMEM_LIMIT),
        cost_estimate=pl.CostEstimate(
            flops=43_000_000_000, bytes_accessed=42_000_000, transcendentals=1_000_000
        ),
        name="experts",
    )(
        place, b_all.reshape(flat), dy_all.reshape(flat), g_all.reshape(rows_all, LANES),
        w_gate, w_up, w_down,
    )
    return [
        out[0].reshape(b_all.shape), out[1].reshape(b_all.shape),
        out[2].reshape(sources, tokens, LANES), *out[3:],
    ]


class Trade:
    def __init__(self, line, stages, nears, came, far, sems):
        self.beside, self.across = beside(line), pair_of(line)
        self.stages, self.nears, self.came, self.far, self.sems = stages, nears, came, far, sems

    def copies(self, e, hop):
        made = []
        for k in range(3):
            source = self.stages[k].at[e, (1, 0, 3)[hop]]
            target = self.far[3 * e + k] if hop == 2 else (self.nears, self.came)[hop][k].at[e]
            peer = self.across if hop == 2 else self.beside
            made.append(
                push(source, target, self.sems.at[0, hop, k, e], self.sems.at[1, hop, k, e], "fsdp", peer)
            )
        return made

    def send(self, e, hop):
        for copy in self.copies(e, hop):
            copy.start()

    def add(self, e):
        for k, copy in enumerate(self.copies(e, 0)):
            copy.wait_recv()
            self.stages[k][e, 3] = (
                self.stages[k][e, 3].astype(F32) + self.nears[k][e].astype(F32)
            ).astype(BF16)

    def finish(self, count):
        for e in range(count):
            for hop in range(3 if e < count - 1 else 2):
                for copy in self.copies(e, hop):
                    copy.wait_send()
                    if hop:
                        copy.wait_recv()


def experts_back_kernel(
    here, tile, lane_of, query_width, router_at,
    b_hbm, dy_hbm, g_ref, gate_hbm, up_hbm, down_hbm,
    middle_ref, marked_ref, win_ref, wout_ref,
    out_hbm, dw_out, dl_out, grad_ref, gain_ref, *rest,
):
    kept_hbm, came_hbm, rest = rest[0:3], rest[3:6], rest[6:]
    far_hbm, rest = rest[: 3 * (here - 1)], rest[3 * (here - 1) :]
    other_hbm, rest = rest[:3], rest[3:]
    (
        b_ref, dy_ref, in_ref, down_ref, hidden_ref, back_ref, out_ref, db_ref, dg_ref,
        down_stage, gate_stage, up_stage, down_near, gate_near, up_near,
        dw_own, dl_own, db_total, dg_total, db_landed, dg_landed,
    ) = rest[:21]
    scratch, rest = rest[21:41], rest[41:]
    (
        weight_sem, tile_sem, out_sem, kept_sem, other_sem, trade_sems, swap_sems,
        scatter_send, scatter_recv, own_sem, send_sem, recv_sem,
    ) = rest
    rows_all, model_width = b_ref.shape
    width = down_ref.shape[1]
    tiles = rows_all // tile
    tokens = middle_ref.shape[0]
    per_tile = tile // tokens
    plane, line = plane_neighbours(), lax.axis_index("fsdp")
    me = plane[0]
    first = me * here + lane_of
    high, low = line // 2, lax.rem(line, 2)
    span = pl.ds(pl.multiple_of(high * width, width), width)

    def weight_loads(e):
        pairs = (
            (gate_hbm.at[e, :, span], in_ref.at[e, :, pl.ds(0, width)]),
            (up_hbm.at[e, :, span], in_ref.at[e, :, pl.ds(width, width)]),
            (down_hbm.at[e, span, :], down_ref.at[e]),
        )
        return [
            pltpu.make_async_copy(source, target, weight_sem.at[e, i])
            for i, (source, target) in enumerate(pairs)
        ]

    def tile_rows(j):
        return pl.ds(pl.multiple_of(j * tile, tile), tile)

    def tile_loads(j):
        return [
            pltpu.make_async_copy(
                source.at[tile_rows(j)], target.at[tile_rows(j)], tile_sem.at[k, j]
            )
            for k, (source, target) in enumerate(((b_hbm, b_ref), (dy_hbm, dy_ref)))
        ]

    def tile_store(j):
        return pltpu.make_async_copy(
            out_ref.at[tile_rows(j)], out_hbm.at[tile_rows(j)], out_sem.at[j]
        )

    def place_of(i):
        return lax.rem(i + tiles // 2, tiles)

    def start_loads(i, carry):
        for load in tile_loads(place_of(i)):
            load.start()
        return carry

    start_loads(0, 0)
    for load in weight_loads(0):
        load.start()
    lax.fori_loop(1, tiles, start_loads, 0)
    for e in range(1, here):
        for load in weight_loads(e):
            load.start()
    meet(plane, line, 4, False)
    trade = Trade(
        line, (down_stage, gate_stage, up_stage), (down_near, gate_near, up_near),
        came_hbm, far_hbm, trade_sems,
    )
    sums = (scatter_send, scatter_recv)
    db_other = Scatter(plane, 0, db_ref, 8, scratch[:5], *sums)
    dg_other = Scatter(plane, 1, dg_ref, 8, scratch[5:10], *sums)
    db = Scatter(plane, 2, db_ref, 0, scratch[10:15], *sums)
    dg = Scatter(plane, 3, dg_ref, 0, scratch[15:20], *sums)
    swap_g = push(dg_total, dg_landed, swap_sems.at[0], swap_sems.at[1], "fsdp", pair_of(line))
    swap_b = push(db_total, db_landed, swap_sems.at[2], swap_sems.at[3], "fsdp", pair_of(line))
    half = tokens // 2
    part = model_width // 4

    def one_expert(e, carry):
        for load in weight_loads(e):
            load.wait()
        last = e == here - 1

        def forward_back(i, carry):
            j = place_of(i)
            rows = tile_rows(j)

            @pl.when(e == 0)
            def _():
                for load in tile_loads(j):
                    load.wait()

            pre = dot(b_ref[rows, :], in_ref[e])
            grad = dot(dy_ref[rows, :], down_ref[e], (1, 1))
            gates = g_ref[rows, :]
            mine = lax.broadcasted_iota(jnp.int32, gates.shape, 1) == first + e
            gate = jnp.sum(jnp.where(mine, jnp.maximum(gates, 0.0), 0.0), axis=1, keepdims=True)
            scale = RESIDUAL_SCALE * gate
            gate_pre, up_pre = pre[:, :width], pre[:, width:]
            sigmoid = 1.0 / (1.0 + jnp.exp(-gate_pre))
            silu = gate_pre * sigmoid
            hidden = silu * up_pre
            share = jnp.sum(hidden * grad, axis=1, keepdims=True)
            inner = jnp.where(mine, RESIDUAL_SCALE * share, 0.0)
            hidden_ref[rows, :] = (scale * hidden).astype(BF16)
            grad = scale * grad
            back_ref[rows, :width] = (
                grad * up_pre * sigmoid * (1.0 + gate_pre * (1.0 - sigmoid))
            ).astype(BF16)
            back_ref[rows, width:] = (grad * silu).astype(BF16)
            made = dot(hidden_ref[rows, :], down_ref[e])
            back = dot(back_ref[rows, :], in_ref[e], (1, 1))

            @pl.when(e == 0)
            def _():
                out_ref[rows, :] = made.astype(BF16)
                for t in range(per_tile):
                    piece = slice(t * tokens, (t + 1) * tokens)
                    db_ref[per_tile * j + t] = back[piece].astype(BF16)
                    dg_ref[per_tile * j + t] = inner[piece]

            @pl.when(e > 0)
            def _():
                out_ref[rows, :] = (out_ref[rows, :].astype(F32) + made).astype(BF16)
                for t in range(per_tile):
                    piece = slice(t * tokens, (t + 1) * tokens)
                    block = per_tile * j + t
                    db_ref[block] = (db_ref[block].astype(F32) + back[piece]).astype(BF16)
                    dg_ref[block] += inner[piece]

            @pl.when(last)
            def _():
                tile_store(j).start()

            @pl.when((e == 1) & (i == tiles - 3))
            def _():
                trade.add(0)
                trade.send(0, 2)

            @pl.when(last & (i == tiles // 2 - 1))
            def _():
                dg_other.begin()
                db_other.begin()

            @pl.when(last & (i == tiles - 2))
            def _():
                dg_other.first()
                db_other.first()

            return carry

        lax.fori_loop(0, tiles, forward_back, 0)

        @pl.when(last)
        def _():
            dg.begin()
            db.begin()
            dg_other.second()
            db_other.second()

        def weight_grads(p, carry):
            i = p + 1 - 2 * lax.rem(p, 2)
            parity = jnp.where(p < 2, 1 - low, low)
            side = jnp.where(lax.rem(i, 2) == 0, high, 1 - high)
            columns = pl.ds(pl.multiple_of((2 * side + parity) * part, part), part)
            down_stage[e, i] = dot(hidden_ref[...], dy_ref[:, columns], (0, 0)).astype(BF16)
            grad = dot(b_ref[:, columns], back_ref[...], (0, 0))
            gate_stage[e, i] = grad[:, :width].astype(BF16)
            up_stage[e, i] = grad[:, width:].astype(BF16)

            @pl.when((p == 0) & (e < here - 1))
            def _():
                trade.send(e, 0)

            @pl.when((p == 1) & (e < here - 2))
            def _():
                trade.send(e, 1)

            @pl.when(last & (p == 1))
            def _():
                for h in range(2):
                    rows = pl.ds(h * half, half)
                    dg_total[rows] = dg_other.total(h)
                    db_total[rows] = db_other.total(h).astype(BF16)
                swap_g.start()
                swap_b.start()

            @pl.when(last & (p == 2))
            def _():
                dg.first()
                db.first()
                trade.add(here - 2)
                trade.send(here - 2, 2)
                trade.send(here - 2, 1)
                trade.send(here - 1, 0)
                trade.send(here - 1, 1)

            return carry

        lax.fori_loop(0, 4, weight_grads, 0)
        return carry

    lax.fori_loop(0, here, one_expert, 0)
    stores = [
        pltpu.make_async_copy(stage.at[e, 2], kept_hbm[k].at[e], kept_sem.at[k, e])
        for k, stage in enumerate((down_stage, gate_stage, up_stage))
        for e in range(here)
    ]
    for store in stores:
        store.start()
    dg.second()
    db.second()
    gain = wout_ref[query_width + 1 : query_width + 2, :].astype(F32)
    router = win_ref[:, router_at : router_at + LANES]
    gain_grad = jnp.zeros((1, model_width), F32)
    sums_g = [dg.total(h) for h in range(2)]
    swap_g.wait_recv()
    swap_b.wait_recv()
    for h in range(2):
        rows = pl.ds(h * half, half)
        gates = jnp.maximum(marked_ref[rows], 0.0)
        grad_gates = sums_g[h] + dg_landed[rows]
        grad_chosen = gates * (
            grad_gates - jnp.sum(gates * grad_gates, axis=1, keepdims=True)
        )
        grad_logits = grad_chosen.astype(BF16)
        dl_own[rows] = grad_logits
        grad_b = dot(grad_logits, router, (1, 1)) + db.total(h) + db_landed[rows].astype(F32)
        middle = middle_ref[rows]
        inverse = lax.rsqrt(jnp.mean(middle * middle, axis=1, keepdims=True) + EPSILON)
        normed = middle * inverse
        gain_grad += jnp.sum(grad_b * normed, axis=0, keepdims=True)
        own = pl.ds(pl.multiple_of(me * tokens + h * half, half), half)
        grad = dy_ref[own].astype(F32) + norm_back(grad_b * gain, normed, inverse)
        grad_ref[rows] = grad
        dw_own[rows] = (RESIDUAL_SCALE * grad).astype(BF16)
    gain_ref[...] = jnp.broadcast_to(gain_grad, gain_ref.shape)
    gathers = (own_sem, send_sem, recv_sem)
    dw = Gather(plane, 0, dw_own, dw_out, 0, *gathers)
    dl = Gather(plane, 1, dl_own, dl_out, 0, *gathers)
    dw.begin()
    dl.begin()
    dw.relay()
    dl.relay()
    dw.relay_diagonal()
    dl.relay_diagonal()
    trade.add(here - 1)
    others = [
        pltpu.make_async_copy(stage.at[here - 1, 3], other_hbm[k], other_sem.at[k])
        for k, stage in enumerate((down_stage, gate_stage, up_stage))
    ]
    for copy in others:
        copy.start()
    for item in (dg_other, db_other, dg, db, dw, dl):
        item.finish()
    swap_b.wait_send()
    swap_g.wait_send()
    for store in stores + others:
        store.wait()
    for j in range(tiles):
        tile_store(j).wait()
    trade.finish(here)


def experts_back(
    b_all, dy_all, g_all, w_gate, w_up, w_down, middle, marked, w_in, w_out,
    lane_of, query_width, router_at, collective_id,
):
    sources, tokens, model_width = b_all.shape
    here, _, hidden_width = w_gate.shape
    rows_all = sources * tokens
    width, part, tile = hidden_width // 2, model_width // 4, 256
    tiles = rows_all // tile
    flat, wide, narrow = (rows_all, model_width), (tokens, model_width), (tokens, LANES)
    slices = [(width, part), (part, width), (part, width)]
    out = pl.pallas_call(
        functools.partial(experts_back_kernel, here, tile, lane_of, query_width, router_at),
        out_shape=[
            jax.ShapeDtypeStruct(flat, BF16),
            jax.ShapeDtypeStruct((8,) + wide, BF16),
            jax.ShapeDtypeStruct((8,) + narrow, BF16),
            jax.ShapeDtypeStruct(wide, F32),
            jax.ShapeDtypeStruct((8, model_width), F32),
        ]
        + [jax.ShapeDtypeStruct((here,) + shape, BF16) for shape in slices * 2]
        + [jax.ShapeDtypeStruct(shape, BF16) for shape in slices * here],
        in_specs=anywhere(2) + in_vmem(1) + anywhere(3) + in_vmem(4),
        out_specs=anywhere(3) + in_vmem(2) + anywhere(6 + 3 * here),
        scratch_shapes=[
            pltpu.VMEM(flat, BF16),
            pltpu.VMEM(flat, BF16),
            pltpu.VMEM((here, model_width, 2 * width), BF16),
            pltpu.VMEM((here, width, model_width), BF16),
            pltpu.VMEM((rows_all, width), BF16),
            pltpu.VMEM((rows_all, 2 * width), BF16),
            pltpu.VMEM(flat, BF16),
            pltpu.VMEM((sources,) + wide, BF16),
            pltpu.VMEM((sources,) + narrow, F32),
        ]
        + [pltpu.VMEM((here, 4) + shape, BF16) for shape in slices]
        + [pltpu.VMEM((here,) + shape, BF16) for shape in slices]
        + [
            pltpu.VMEM(wide, BF16),
            pltpu.VMEM(narrow, BF16),
            pltpu.VMEM(wide, BF16),
            pltpu.VMEM(narrow, F32),
            pltpu.VMEM(wide, BF16),
            pltpu.VMEM(narrow, F32),
        ]
        + (scatter_scratch(*wide, BF16, True) + scatter_scratch(*narrow, F32, True)) * 2
        + [
            pltpu.SemaphoreType.DMA((here, 3)),
            pltpu.SemaphoreType.DMA((2, tiles)),
            pltpu.SemaphoreType.DMA((tiles,)),
            pltpu.SemaphoreType.DMA((3, here)),
            pltpu.SemaphoreType.DMA((3,)),
            pltpu.SemaphoreType.DMA((2, 3, 3, here)),
            pltpu.SemaphoreType.DMA((4,)),
        ]
        + scatter_sems(4)
        + gather_sems(2),
        compiler_params=pltpu.CompilerParams(
            collective_id=collective_id, has_side_effects=True, vmem_limit_bytes=67_000_000
        ),
        cost_estimate=pl.CostEstimate(
            flops=43_000_000_000, bytes_accessed=42_000_000, transcendentals=1_000_000
        ),
        name="experts_back",
    )(
        b_all.reshape(flat), dy_all.reshape(flat), g_all.reshape(rows_all, LANES),
        w_gate, w_up, w_down, middle, marked, w_in, w_out,
    )
    return [out[0].reshape(b_all.shape), *out[1:5], out[5:8], out[8:11], out[11:-3], out[-3:]]


def rotary_tables(length):
    lane = lax.broadcasted_iota(jnp.int32, (length, LANES), 1) % HEAD_DIM
    half = HEAD_DIM // 2
    exponent = (lane % half).astype(F32) * (2.0 / HEAD_DIM)
    position = lax.broadcasted_iota(jnp.int32, (length, LANES), 0).astype(F32)
    angles = position * jnp.power(ROPE_BASE, -exponent)
    return jnp.cos(angles), jnp.where(lane < half, -jnp.sin(angles), jnp.sin(angles))


def finish_kernel(per_group, here, in_ref, out_ref, *refs):
    kept, came, far, refs = refs[:3], refs[3:6], refs[6 : 6 + 3 * here], refs[6 + 3 * here :]
    query_ref, key_ref, value_ref, router_ref, proj_ref, *expert_refs = refs
    query_width = per_group * HEAD_DIM
    groups, out_rows, _ = out_ref.shape
    for j in range(0, groups, 2):
        pair = (in_ref[j].astype(F32), in_ref[j + 1].astype(F32))
        at = 0
        for target, width in ((query_ref, query_width), (key_ref, HEAD_DIM), (value_ref, HEAD_DIM)):
            target[:, j * width : (j + 2) * width] = jnp.concatenate(
                [block[:, at : at + width] for block in pair], axis=1
            )
            at += width
    router_ref[...] = in_ref[0][:, at : at + router_ref.shape[1]].astype(F32)
    for j in range(groups):
        proj_ref[j * out_rows : (j + 1) * out_rows, :] = out_ref[j].astype(F32)
    high = lax.axis_index("fsdp") // 2
    for k, target in enumerate(expert_refs):
        width = kept[k].shape[1 if k == 0 else 2]
        near = pl.ds(pl.multiple_of(high * width, width), width)
        beyond = pl.ds(pl.multiple_of((1 - high) * width, width), width)
        for e in range(here):
            near_sum = kept[k][e].astype(F32) + came[k][e].astype(F32)
            far_sum = far[3 * e + k][...].astype(F32)
            if k == 0:
                target[e, near, :] = near_sum
                target[e, beyond, :] = far_sum
            else:
                target[e, :, near] = near_sum
                target[e, :, beyond] = far_sum


def finish(in_all, out_all, kept, came, far, per_group, experts_all):
    groups, shard, _ = in_all.shape
    here, width, part = kept[0].shape
    query_width = per_group * HEAD_DIM
    shapes = [
        (shard, groups * query_width),
        (shard, groups * HEAD_DIM),
        (shard, groups * HEAD_DIM),
        (shard, experts_all),
        (groups * out_all.shape[1], out_all.shape[2]),
        (here, 2 * width, part),
        (here, part, 2 * width),
        (here, part, 2 * width),
    ]
    operands = (in_all, out_all, *kept, *came, *far)
    return pl.pallas_call(
        functools.partial(finish_kernel, per_group, here),
        out_shape=[jax.ShapeDtypeStruct(shape, F32) for shape in shapes],
        in_specs=in_vmem(len(operands)),
        out_specs=in_vmem(len(shapes)),
        compiler_params=pltpu.CompilerParams(vmem_limit_bytes=VMEM_LIMIT),
        cost_estimate=pl.CostEstimate(flops=0, bytes_accessed=25_000_000, transcendentals=0),
        name="finish",
    )(*operands)


def per_device(
    residual_in, cotangent, gain_attn, w_query, w_key, w_value, w_out, gain_ffn, w_router,
    w_gate, w_up, w_down, route_ids,
):
    me = lax.axis_index("expert")
    line = lax.axis_index("fsdp")
    peers = lax.axis_size("expert")
    lines = lax.axis_size("fsdp")
    tokens, model_width = residual_in.shape[1:]
    length = tokens * peers
    groups = w_key.shape[1] // HEAD_DIM
    per_group = w_query.shape[1] // w_key.shape[1]
    query_width = per_group * HEAD_DIM
    experts_all = w_router.shape[1]
    here = w_gate.shape[0]
    shard = w_query.shape[0]
    turned = query_width + HEAD_DIM
    router_at = turned
    lane_of = HEAD_DIM
    in_width = turned + LANES
    paired = lines == 4 and peers == 8

    w_in_shard = jnp.concatenate(
        [
            lax.dynamic_slice(w_query, (0, me * query_width), (shard, query_width)),
            lax.dynamic_slice(w_key, (0, me * HEAD_DIM), (shard, HEAD_DIM)),
            lax.dynamic_slice(w_value, (0, me * HEAD_DIM), (shard, HEAD_DIM)),
            w_router,
            jnp.zeros((shard, in_width - turned - HEAD_DIM - experts_all), BF16),
        ],
        axis=1,
    )
    w_out_shard = jnp.concatenate(
        [
            lax.dynamic_slice(w_out, (me * query_width, 0), (query_width, shard)),
            gain_attn[None],
            gain_ffn[None],
            jnp.zeros((14, shard), BF16),
        ],
        axis=0,
    )
    chosen = jnp.any(
        route_ids[0][:, :, None]
        == jnp.arange(LANES, dtype=jnp.int32)[None, None, :] - lane_of,
        axis=1,
    ).astype(F32)
    cosine, sine = rotary_tables(length)
    place = jnp.full((1,), me * here + lane_of, jnp.int32)
    own_rows, own_grad = residual_in[0], cotangent[0]
    wide = (peers, tokens, model_width)

    if paired:
        dy_all, w_in, w_out_rows, saved, b_all, g_all, middle, marked = front(
            own_rows, own_grad, w_in_shard, w_out_shard, chosen, cosine, sine, lines, per_group,
            router_at, 0,
        )
        sum_part, dw_all, dl_all, grad_middle, gain_two_grad, kept, came, far, others = experts_back(
            b_all, dy_all, g_all, w_gate, w_up, w_down, middle, marked, w_in, w_out_rows,
            lane_of, query_width, router_at, 2,
        )
        da_part, grad_in, out_low, e_own, e_total, *crossed = attend_back(
            dw_all.reshape(length, model_width), w_in, w_out_rows, cosine, sine, saved,
            b_all.reshape(2 * length, model_width), dl_all.reshape(length, LANES), per_group,
            (sum_part, others), 4,
        )
        outcome, grad_input, in_all, out_all, gains_all, notes_all = close_transfers(
            da_part.reshape(wide), e_own, e_total, own_rows, middle, grad_middle, gain_two_grad,
            w_out_rows, grad_in.reshape(lines, shard, in_width), out_low,
            query_width, 3,
        )
        squares = jnp.sum(notes_all, axis=0)[:5, 0]
        query, key, value, router_grad, proj, down, gate, up = finish(
            in_all, out_all, kept, came, [*far, *crossed], per_group, experts_all
        )
        reduced = [gate, up, down]
        gain_rows = jnp.sum(gains_all[:, :2].astype(F32), axis=0)
    else:
        x_all, dy_all = plane_gather([own_rows, own_grad], 0)
        w_in, w_out_rows = (
            lax.all_gather(w_in_shard, "fsdp", axis=0, tiled=True),
            lax.all_gather(w_out_shard, "fsdp", axis=1, tiled=True),
        )
        part, *saved = attend(
            x_all.reshape(length, model_width), w_in, w_out_rows, cosine, sine, per_group
        )
        (branch,) = plane_scatter([part.reshape(wide)], 1)
        gain_one = w_out_rows[query_width][None].astype(F32)
        gain_two = w_out_rows[query_width + 1][None].astype(F32)
        router = w_in[:, router_at:]
        rows = own_rows.astype(F32)
        inverse_one = lax.rsqrt(jnp.mean(rows * rows, axis=-1, keepdims=True) + EPSILON)
        normed_one = rows * inverse_one
        middle = rows + RESIDUAL_SCALE * branch
        inverse_two = lax.rsqrt(jnp.mean(middle * middle, axis=-1, keepdims=True) + EPSILON)
        normed_two = middle * inverse_two
        routed = (normed_two * gain_two).astype(BF16)
        logits = jnp.where(chosen > 0, dot(routed, router), -1e30)
        lifted = jnp.exp(logits - jnp.max(logits, axis=-1, keepdims=True))
        lifted = jnp.where(chosen > 0, lifted, 0.0)
        gates = lifted / jnp.sum(lifted, axis=-1, keepdims=True)
        b_all, g_all = plane_gather([routed, jnp.where(chosen > 0, gates, -1.0)], 2)
        sum_part, db_part, dg_part, *grads = experts(
            place, b_all, dy_all, g_all, w_gate, w_up, w_down
        )
        db_sum, dg_sum = plane_scatter([db_part, dg_part], 3)
        grad_rows = own_grad.astype(F32)
        grad_chosen = gates * (dg_sum - jnp.sum(gates * dg_sum, axis=-1, keepdims=True))
        grad_logits = grad_chosen.astype(BF16)
        grad_routed = dot(grad_logits, router, (1, 1)) + db_sum
        grad_gain_two = jnp.sum(grad_routed * normed_two, axis=0)
        grad_middle = grad_rows + norm_back(grad_routed * gain_two, normed_two, inverse_two)
        grad_branch = (RESIDUAL_SCALE * grad_middle).astype(BF16)
        dw_all, dl_all = plane_gather([grad_branch, grad_logits], 4)
        da_part, grad_in, grad_out = attend_back(
            dw_all.reshape(length, model_width), w_in, w_out_rows, cosine, sine, saved,
            b_all.reshape(length, model_width), dl_all.reshape(length, LANES), per_group,
        )
        da_sum, expert_sum = plane_scatter([da_part.reshape(wide), sum_part], 5)
        outcome = middle + expert_sum
        grad_gain_one = jnp.sum(da_sum * normed_one, axis=0)
        grad_input = grad_middle + norm_back(da_sum * gain_one, normed_one, inverse_one)
        squares = lax.psum(
            jnp.stack(
                [jnp.sum(v * v) for v in (rows, middle, outcome, grad_middle, grad_input)]
            ),
            ("fsdp", "expert"),
        )
        in_sum = lax.psum_scatter(grad_in, "fsdp", scatter_dimension=0, tiled=True)
        out_sum = lax.psum_scatter(
            grad_out.transpose(1, 0, 2).reshape(query_width, model_width), "fsdp",
            scatter_dimension=1, tiled=True,
        )
        gain_rows = lax.psum_scatter(
            lax.psum(jnp.stack([grad_gain_one, grad_gain_two]), "expert"),
            "fsdp", scatter_dimension=1, tiled=True,
        )
        in_all = lax.all_gather(in_sum, "expert", axis=0)
        out_all = lax.all_gather(out_sum, "expert", axis=0)
        outcome, grad_input = outcome.astype(BF16), grad_input.astype(BF16)
        grads = [
            grads[0].transpose(1, 0, 2, 3).reshape(w_gate.shape),
            grads[1].transpose(1, 0, 2, 3).reshape(w_up.shape),
            grads[2].transpose(1, 2, 0, 3).reshape(w_down.shape),
        ]
        reduced = [
            lax.psum_scatter(array, "fsdp", scatter_dimension=axis, tiled=True).astype(F32)
            for array, axis in zip(grads, (1, 1, 2))
        ]

        def columns_of(start, stop):
            return in_all[:, :, start:stop].transpose(1, 0, 2).reshape(shard, -1).astype(F32)

        query, key = columns_of(0, query_width), columns_of(query_width, turned)
        value = columns_of(turned, turned + HEAD_DIM)
        proj = out_all.reshape(groups * query_width, shard).astype(F32)
        at = turned + HEAD_DIM
        router_grad = in_all[0, :, at : at + experts_all].astype(F32)

    root_means = jnp.sqrt(squares / (tokens * model_width * lines * peers))
    return (
        outcome[None],
        grad_input[None],
        gain_rows[0],
        query,
        key,
        value,
        proj,
        gain_rows[1],
        router_grad,
        reduced[0],
        reduced[1],
        reduced[2],
        root_means,
    )


def solution(mesh):
    in_specs = (
        P("fsdp", "expert", None),
        P("fsdp", "expert", None),
        P("fsdp"),
        P("fsdp", None),
        P("fsdp", None),
        P("fsdp", None),
        P(None, "fsdp"),
        P("fsdp"),
        P("fsdp", None),
        P("expert", None, None),
        P("expert", None, None),
        P("expert", None, None),
        P("fsdp", "expert", None),
    )
    out_specs = (
        P("fsdp", "expert", None),
        P("fsdp", "expert", None),
        P("fsdp"),
        P("fsdp", None),
        P("fsdp", None),
        P("fsdp", None),
        P(None, "fsdp"),
        P("fsdp"),
        P("fsdp", None),
        P("expert", "fsdp", None),
        P("expert", "fsdp", None),
        P("expert", None, "fsdp"),
        P(),
    )
    return jax.shard_map(
        per_device, mesh=mesh, in_specs=in_specs, out_specs=out_specs, check_vma=False
    )
```
